32 devices in a mesh: dp: 2 (over x), fsdp: 16 (over z, y, core).
Axes of the slice: x: 2, y: 2, z: 4, core: 2. Of those that a mesh axis runs over, the one named last changes fastest.
Arguments:
- image_tokens: bfloat16 [1024, 50, 768], P(('dp', 'fsdp')), may hold values from -6 to 6
- text_tokens: bfloat16 [1024, 16, 768], P(('dp', 'fsdp')), may hold values from -6 to 6
- image_qkv: bfloat16 [768, 2304], replicated, may hold values from -0.21875 to 0.21875
- image_out: bfloat16 [768, 768], replicated, may hold values from -1.25 to 1.25
- image_up: bfloat16 [768, 3072], replicated, may hold values from -0.21875 to 0.21875
- image_down: bfloat16 [3072, 768], replicated, may hold values from -0.109375 to 0.109375
- image_vectors: bfloat16 [8, 768], replicated, may hold values from -1.2 to 1.5
- image_up_bias: bfloat16 [3072], replicated, may hold values from -2 to 2
- text_qkv: bfloat16 [768, 2304], P('fsdp', 'dp'), may hold values from -0.21875 to 0.21875
- text_out: bfloat16 [768, 768], P('fsdp', 'dp'), may hold values from -0.875 to 0.875
- text_up: bfloat16 [768, 3072], P('fsdp', 'dp'), may hold values from -0.21875 to 0.21875
- text_down: bfloat16 [3072, 768], P('fsdp', 'dp'), may hold values from -0.109375 to 0.109375
- text_vectors: bfloat16 [8, 768], P(None, 'fsdp'), may hold values from -1.2 to 1.5
- text_up_bias: bfloat16 [3072], P('fsdp'), may hold values from -2 to 2
- pair_counts: int32 [32], replicated, may hold values from 8 to 32, as said below
- pair_groups: int32 [1024], replicated, may hold values from 0 to 511
Outputs:
- loss_value: float32 [], replicated
- grad_text_tokens: float32 [1024, 16, 768], P(('dp', 'fsdp'))
- grad_text_qkv: float32 [768, 2304], P('fsdp', 'dp')
- grad_text_out: float32 [768, 768], P('fsdp', 'dp')
- grad_text_up: float32 [768, 3072], P('fsdp', 'dp')
- grad_text_down: float32 [3072, 768], P('fsdp', 'dp')
- grad_text_vectors: float32 [8, 768], P(None, 'fsdp')
- grad_text_up_bias: float32 [3072], P('fsdp')
The draws below stay inside these ranges and needn't reach their ends.
Inputs may be any that keep to these rules, and one draw needn't show every extreme that they name: Device d (index over dp+fsdp, dp slowest) has its first pair_counts[d] of its 32 pair slots live; some device is full.
All inputs are finite; a program needn't handle non-finite values.
Results may differ from the reference program's by a relative error of at most 0.024.
Values may be sent and summed in bfloat16 or wider, within the bound.
No kernel may reach another device: no remote copies, remote signals or barrier semaphores. Data moves between devices by JAX's collectives and lax.ppermute only.
A program may use at most 192 MiB of HBM per device.

```python
import math
import jax
import jax.numpy as jnp
from jax import lax

D = 768
HEAD_DIM = 64
F = 3072
IMG_TOK = 50
TXT_TOK = 16
CAP = 32
MINP = 8
PAIRS = 1024
DEVICES = 32


def vector_rows(key):
    gain_key, shift_key = jax.random.split(key)
    gains = jnp.clip(1.0 + 0.15 * jax.random.normal(gain_key, (8, D), jnp.float32), 0.5, 1.5)
    shifts = jnp.clip(0.3 * jax.random.normal(shift_key, (8, D), jnp.float32), -1.2, 1.2)
    row_index = jnp.arange(8)[:, None]
    gain_rows = (row_index == 0) | (row_index == 5)
    return jnp.where(gain_rows, gains, shifts)


def draw_image_vectors(key, part):
    return vector_rows(jax.random.fold_in(key, 11)).astype(jnp.bfloat16)


def draw_text_vectors(key, part):
    return vector_rows(jax.random.fold_in(key, 12)).astype(jnp.bfloat16)


def draw_pair_counts(key, part):
    spread = CAP - MINP
    draw_one, draw_two, draw_pick = jax.random.split(jax.random.fold_in(key, 13), 3)
    left_factor = jax.random.randint(draw_one, (DEVICES,), 0, spread + 1)
    right_factor = jax.random.randint(draw_two, (DEVICES,), 0, spread + 1)
    surplus = jnp.minimum(spread, left_factor * right_factor * 2 // spread)
    chosen = jax.random.randint(draw_pick, (), 0, DEVICES)
    counts = MINP + surplus
    return jnp.where(jnp.arange(DEVICES) == chosen, CAP, counts).astype(jnp.int32)


def with_ends(drawn, own_key, smallest, high):
    place = [jax.random.randint(jax.random.fold_in(own_key, axis), (), 0, length) for axis, length in enumerate(drawn.shape)]
    longest = drawn.shape.index(max(drawn.shape))
    beside = place[:longest] + [(place[longest] + 1) % drawn.shape[longest]] + place[longest + 1:]
    return drawn.at[tuple(place)].set(smallest).at[tuple(beside)].set(high)


def steps_of(key, shape, pieces, low, largest):
    factor_of = 1.0
    for dim, shards_of in pieces:
        draws = jax.random.uniform(jax.random.fold_in(jax.random.fold_in(key, 6), dim), (shards_of,), jnp.float32, low / len(pieces), largest / len(pieces))
        factor_of = factor_of * jnp.repeat(jnp.exp(draws), shape[dim] // shards_of).reshape((-1,) + (1,) * (len(shape) - 1 - dim))
    return factor_of


def noise(rng, extent, deviation, bound, shards=(), kind=jnp.bfloat16):
    values = deviation * jax.random.normal(rng, extent, jnp.float32)
    if shards:
        values = values * steps_of(rng, extent, shards, -0.22, 0.18)
    return jnp.clip(values, -bound, bound).astype(kind)


def setup_inputs(seed: int = 0) -> dict:
    key_list = jax.random.split(jax.random.key(seed), 17)
    return {
        "image_tokens": noise(key_list[0], (PAIRS, IMG_TOK, D), 1.0, 6.0, ((0, 32),)),
        "text_tokens": noise(key_list[1], (PAIRS, TXT_TOK, D), 1.0, 6.0, ((0, 32),)),
        "image_qkv": noise(key_list[2], (D, 3 * D), D ** -0.5, 0.21875),
        "image_out": noise(key_list[3], (D, D), (D // 32) ** -0.5, 1.25),
        "image_up": noise(key_list[4], (D, F), D ** -0.5, 0.21875),
        "image_down": noise(key_list[5], (F, D), F ** -0.5, 0.109375),
        "image_vectors": draw_image_vectors(jax.random.fold_in(key_list[16], 71), 0),
        "image_up_bias": noise(key_list[7], (F,), 0.5, 2.0),
        "text_qkv": noise(key_list[8], (D, 3 * D), D ** -0.5, 0.21875, ((0, 16), (1, 2))),
        "text_out": noise(key_list[9], (D, D), (D // 16) ** -0.5, 0.875, ((0, 16), (1, 2))),
        "text_up": noise(key_list[10], (D, F), D ** -0.5, 0.21875, ((0, 16), (1, 2))),
        "text_down": noise(key_list[11], (F, D), F ** -0.5, 0.109375, ((0, 16), (1, 2))),
        "text_vectors": draw_text_vectors(jax.random.fold_in(key_list[16], 71), 0),
        "text_up_bias": noise(key_list[13], (F,), 0.5, 2.0, ((0, 16),)),
        "pair_counts": draw_pair_counts(jax.random.fold_in(key_list[16], 71), 0),
        "pair_groups": with_ends(jax.random.randint(key_list[15], (PAIRS,), 0, PAIRS // 2), jax.random.fold_in(key_list[15], 1), 0, (PAIRS // 2) - 1).astype(jnp.int32),
    }


@jax.custom_vjp
def low(v):
    return lax.optimization_barrier(v.astype(jnp.bfloat16)).astype(jnp.float32)

@jax.custom_vjp
def low_back(v):
    return v

def low_keep(v):
    return (low(v), None)

def low_pass(kept, grad):
    return (grad,)

def back_keep(v):
    return (v, None)

def back_low(kept, grad):
    return (low(grad),)
low.defvjp(low_keep, low_pass)
low_back.defvjp(back_keep, back_low)
highest = lax.Precision.HIGHEST
logit_scale = 50.0
loss_weight = 32768.0

def layer_norm(values, gain_row, shift_row):
    centered = values - lax.optimization_barrier(jnp.mean(values, axis=-1, keepdims=True))
    variance = lax.optimization_barrier(jnp.mean(centered * centered, axis=-1, keepdims=True))
    return centered * lax.rsqrt(variance + 1e-05) * gain_row + shift_row

def matmul(left_side, right_side):
    return jnp.einsum('bld,de->ble', left_side, right_side, precision=highest, preferred_element_type=jnp.float32)

def block(tokens, qkv_weight, out_weight, up_weight, down_weight, vectors, up_bias):
    batch_size, length, model_width = tokens.shape
    head_count = model_width // HEAD_DIM
    head_scale = HEAD_DIM ** (-0.5)
    first_low = low(layer_norm(tokens, vectors[0], vectors[1]))
    qkv_bias = jnp.concatenate([vectors[2], jnp.zeros_like(vectors[2]), vectors[3]])
    packed = low_back(low(matmul(first_low, qkv_weight) + qkv_bias))
    packed = packed.reshape(batch_size, length, 3, head_count, HEAD_DIM)
    scores = low_back(jnp.einsum('blhd,bmhd->bhlm', packed[:, :, 0], packed[:, :, 1], precision=highest) * head_scale)
    attend = low(jax.nn.softmax(scores, axis=-1))
    mixed_low = jnp.einsum('bhlm,bmhd->blhd', attend, packed[:, :, 2], precision=highest)
    mixed_low = low_back(low(mixed_low.reshape(batch_size, length, model_width)))
    middle = tokens + low_back(matmul(mixed_low, out_weight) + vectors[4])
    second = low(layer_norm(middle, vectors[5], vectors[6]))
    hidden = low(jax.nn.gelu(low_back(matmul(second, up_weight) + up_bias), approximate=False))
    return middle + low_back(matmul(hidden, down_weight) + vectors[7])

def embed(tokens, params):
    block_rows = block(tokens.astype(jnp.float32), params[0], params[1], params[2], params[3], params[4], params[5])
    pooled = lax.optimization_barrier(jnp.mean(block_rows, axis=1))
    return pooled * lax.rsqrt(lax.optimization_barrier(jnp.sum(pooled * pooled, axis=-1, keepdims=True)) + 1e-06)

def contrast(image_low, text_low, live, groups, same_count):
    pairs_all = live.shape[0]
    block_rows = math.gcd(pairs_all, 512)

    def block_step(totals, offset):
        col_sum, col_lin, row_part = totals
        image_part = lax.dynamic_slice_in_dim(image_low, offset, block_rows, 0)
        live_part = lax.dynamic_slice_in_dim(live, offset, block_rows, 0)
        group_part = lax.dynamic_slice_in_dim(groups, offset, block_rows, 0)
        count_part = lax.dynamic_slice_in_dim(same_count, offset, block_rows, 0)
        scores = low_back(logit_scale * jnp.einsum('id,jd->ij', image_part, text_low, precision=highest))
        exponent = jnp.exp(scores)
        matched = (group_part[:, None] == groups[None, :]).astype(scores.dtype)
        row_sum = lax.optimization_barrier(jnp.sum(exponent * live[None, :], axis=1))
        row_lin = lax.optimization_barrier(jnp.sum(matched * scores * live[None, :], axis=1))
        row_part = row_part + jnp.sum(live_part * (jnp.log(row_sum) - row_lin / count_part))
        col_sum = col_sum + lax.optimization_barrier(jnp.sum(exponent * live_part[:, None], axis=0))
        col_lin = col_lin + lax.optimization_barrier(jnp.sum(matched * scores * live_part[:, None], axis=0))
        return ((col_sum, col_lin, row_part), None)
    offsets = jnp.arange(pairs_all // block_rows, dtype=jnp.int32) * block_rows
    zeros_col = jnp.zeros((pairs_all,), image_low.dtype)
    initial = (zeros_col, zeros_col, jnp.zeros((), image_low.dtype))
    totals, unused = lax.scan(jax.checkpoint(block_step), initial, offsets)
    col_sum, col_lin, row_part = totals
    col_part = jnp.sum(live * (jnp.log(col_sum) - col_lin / same_count))
    return (row_part + col_part) / (2.0 * jnp.sum(live))

def reference(image_tokens, text_tokens, image_qkv, image_out, image_up, image_down, image_vectors, image_up_bias, text_qkv, text_out, text_up, text_down, text_vectors, text_up_bias, pair_counts, pair_groups):
    pairs_all = text_tokens.shape[0]
    model_width = text_tokens.shape[2]
    slots = jnp.arange(CAP, dtype=jnp.int32)
    live = (slots[None, :] < pair_counts[:, None]).reshape(pairs_all).astype(jnp.float32)
    count_rows = math.gcd(pairs_all, 512)

    def count_block(group_part):
        return lax.optimization_barrier(jnp.sum(jnp.where(group_part[:, None] == pair_groups[None, :], live[None, :], 0.0), axis=1))
    same_count = lax.map(count_block, pair_groups.reshape(pairs_all // count_rows, count_rows))
    same_count = jnp.maximum(same_count.reshape(pairs_all), 1.0)
    image_params = (image_qkv.astype(jnp.float32), image_out.astype(jnp.float32), image_up.astype(jnp.float32), image_down.astype(jnp.float32), image_vectors.astype(jnp.float32), image_up_bias.astype(jnp.float32))
    image_rows = math.gcd(pairs_all, 64)
    image_blocks = image_tokens.reshape(pairs_all // image_rows, image_rows, IMG_TOK, model_width)
    image_emb = lax.map(lambda segment: embed(segment, image_params), image_blocks)
    image_low = low(image_emb.reshape(pairs_all, model_width))
    text_rows = math.gcd(pairs_all, 256)
    embed_saved = jax.checkpoint(embed)

    def objective(tokens, qkv_weight, out_weight, up_weight, down_weight, vectors, up_bias):
        params = (qkv_weight, out_weight, up_weight, down_weight, vectors, up_bias)
        text_blocks = tokens.reshape(pairs_all // text_rows, text_rows, TXT_TOK, model_width)
        text_emb = lax.map(lambda segment: embed_saved(segment, params), text_blocks)
        text_low = low(text_emb.reshape(pairs_all, model_width))
        return contrast(image_low, text_low, live, pair_groups, same_count)
    loss_value, pullback = jax.vjp(objective, text_tokens.astype(jnp.float32), text_qkv.astype(jnp.float32), text_out.astype(jnp.float32), text_up.astype(jnp.float32), text_down.astype(jnp.float32), text_vectors.astype(jnp.float32), text_up_bias.astype(jnp.float32))
    grads = pullback(jnp.asarray(loss_weight, loss_value.dtype))
    return (loss_value, grads[0], grads[1], grads[2], grads[3], grads[4], grads[5], grads[6])
```

```python
import functools

import jax
import jax.numpy as jnp
from jax import lax
from jax.experimental import pallas as pl
from jax.experimental.pallas import tpu as pltpu
from jax.sharding import PartitionSpec as P

HEAD_DIM = 64
LOGIT_SCALE = 50.0
LOSS_WEIGHT = 32768.0
BF = jnp.bfloat16
F32 = jnp.float32
AXES = ("dp", "fsdp")
PX, PF = 2, 16
VMEM_LIMIT = 62 * 1024 * 1024

ANY = pl.BlockSpec(memory_space=pl.ANY)
WHOLE = pl.BlockSpec(memory_space=pltpu.VMEM)


def params(**more):
    return pltpu.CompilerParams(vmem_limit_bytes=VMEM_LIMIT, **more)


def dot(a, b, ca=1, cb=0):
    return lax.dot_general(a, b, (((ca,), (cb,)), ((), ())), preferred_element_type=F32)


def normalize(values):
    centered = values - jnp.mean(values, axis=-1, keepdims=True)
    inverse = lax.rsqrt(jnp.mean(centered * centered, axis=-1, keepdims=True) + 1e-05)
    return centered * inverse, inverse


def norm_back(grad, hat, inverse, gain):
    scaled = grad * gain
    return inverse * (
        scaled
        - jnp.mean(scaled, axis=-1, keepdims=True)
        - hat * jnp.mean(scaled * hat, axis=-1, keepdims=True)
    )


def gauss_tail(u):
    size = jnp.abs(u)
    t = 1.0 / (1.0 + (0.3275911 * 0.7071067811865476) * size)
    bell = jnp.exp(-0.5 * (u * u))
    poly = 0.5 * 1.061405429 * t - 0.5 * 1.453152027
    poly = poly * t + 0.5 * 1.421413741
    poly = poly * t - 0.5 * 0.284496736
    poly = poly * t + 0.5 * 0.254829592
    return poly * t * bell, bell, size


def head_pair(block, low_lane):
    zero = jnp.zeros_like(block)
    return jnp.concatenate(
        [jnp.where(low_lane, block, zero), jnp.where(low_lane, zero, block)], axis=0
    )


def softmax_half(scores, bias):
    scores = scores + bias
    top = jnp.max(scores, axis=-1, keepdims=True)
    powers = jnp.exp(scores - top)
    return powers * (1.0 / jnp.sum(powers, axis=-1, keepdims=True))


def unit_rows(pooled):
    return pooled * lax.rsqrt(jnp.sum(pooled * pooled, axis=-1, keepdims=True) + 1e-06)


def mean_down(total, count, down):
    mean = total * (1.0 / count)
    high = mean.astype(BF)
    low = (mean - high.astype(F32)).astype(BF)
    return dot(high, down) + dot(low, down)


def image_kernel(
    tok, wq_h, wo_h, wu_h, wd_h, vec, ub, out, wq, wo, wu, wd, x, h, qkv, att, act_sum, r1_sum, sem
):
    step, steps = pl.program_id(0), pl.num_programs(0)
    group, length, width = tok.shape
    rows = group * length
    hidden = wu.shape[1]
    copies = [
        pltpu.make_async_copy(src, dst, sem.at[i])
        for i, (src, dst) in enumerate(((wq_h, wq), (wo_h, wo), (wu_h, wu), (wd_h, wd)))
    ]

    @pl.when(step == 0)
    def _():
        for copy in copies:
            copy.start()

    def arrived(i):
        @pl.when(step == 0)
        def _():
            copies[i].wait()

    v = vec[...].astype(F32)
    for i in range(group):
        x[pl.ds(i * length, length), :] = tok[i].astype(F32)
    blk = 80
    for r in range(0, rows, blk):
        hat, _ = normalize(x[r : r + blk, :])
        h[r : r + blk, :] = (hat * v[0:1] + v[1:2]).astype(BF)
    arrived(0)
    for c in range(0, 3 * width, 256):
        part = dot(h[...], wq[:, c : c + 256])
        if c < width:
            part = part + v[2:3, c : c + 256]
        if c >= 2 * width:
            part = part + v[3:4, c - 2 * width : c - 2 * width + 256]
        qkv[:, c : c + 256] = part.astype(BF)

    wins = rows // (2 * length)
    q_at = [(2 * length * w) // 16 * 16 for w in range(wins)]
    k_at = [min(q, rows - 128) for q in q_at]
    q_len = 112
    low_lane = lax.broadcasted_iota(jnp.int32, (128, 128), 1) < HEAD_DIM
    for w in range(wins):
        qi = q_at[w] + lax.broadcasted_iota(jnp.int32, (q_len, 128), 0)
        ki = k_at[w] + lax.broadcasted_iota(jnp.int32, (q_len, 128), 1)
        lo, mid, hi = 2 * w * length, (2 * w + 1) * length, (2 * w + 2) * length
        first = (qi >= lo) & (qi < mid) & (ki >= lo) & (ki < mid)
        second = (qi >= mid) & (qi < hi) & (ki >= mid) & (ki < hi)
        allowed = first | second
        bias = jnp.where(allowed, 0.0, -1e30)
        inside = jnp.where((qi >= lo) & (qi < hi), 1.0, 0.0)
        for p in range(width // 128):
            c = p * 128
            q2 = qkv[q_at[w] : q_at[w] + q_len, c : c + 128] * 0.125
            k2 = head_pair(qkv[k_at[w] : k_at[w] + 128, width + c : width + c + 128], low_lane)
            v2 = head_pair(
                qkv[k_at[w] : k_at[w] + 128, 2 * width + c : 2 * width + c + 128], low_lane
            )
            scores = dot(q2, k2, 1, 1)
            probs = jnp.concatenate(
                [
                    (softmax_half(scores[:, :128], bias) * inside).astype(BF),
                    (softmax_half(scores[:, 128:], bias) * inside).astype(BF),
                ],
                axis=1,
            )
            mixed = dot(probs, v2)
            a = q_at[w]
            if w == 0:
                att[a : a + q_len, c : c + 128] = mixed.astype(BF)
            else:
                prev_end = q_at[w - 1] + q_len
                over = prev_end - a
                if over > 0:
                    old = att[a : a + over, c : c + 128].astype(F32)
                    att[a : a + over, c : c + 128] = (old + mixed[:over]).astype(BF)
                att[a + over : a + q_len, c : c + 128] = mixed[over:].astype(BF)

    arrived(1)
    for c in range(0, width, 256):
        x[:, c : c + 256] = x[:, c : c + 256] + (dot(att[...], wo[:, c : c + 256]) + v[4:5, c : c + 256])
    for r in range(0, rows, blk):
        hat, _ = normalize(x[r : r + blk, :])
        h[r : r + blk, :] = (hat * v[5:6] + v[6:7]).astype(BF)

    def image_sums(values):
        sums = []
        for i in range(group):
            lo, hi = i * length, (i + 1) * length
            a, b = lo // 8 * 8, -(-hi // 8) * 8
            part = values[a:b]
            row = a + lax.broadcasted_iota(jnp.int32, (b - a, 1), 0)
            if lo % 8 or hi % 8:
                part = jnp.where((row >= lo) & (row < hi), part, 0.0)
            sums.append(jnp.sum(part, axis=0, keepdims=True))
        return jnp.concatenate(sums, axis=0)

    place = pl.ds(pl.multiple_of(step * group, group), group)
    for c in range(0, width, 256):
        r1_sum[place, c : c + 256] = image_sums(x[:, c : c + 256])
    arrived(2)
    for c in range(0, hidden, 256):
        u = dot(h[...], wu[:, c : c + 256]) + ub[:, c : c + 256].astype(F32)
        tail, _, size = gauss_tail(u)
        act_sum[place, c : c + 256] = image_sums(jnp.maximum(u, 0.0) - size * tail)
    arrived(3)

    @pl.when(step == steps - 1)
    def _():
        pooled = r1_sum[...] * (1.0 / length) + mean_down(act_sum[...], length, wd[...]) + v[7:8]
        out[...] = unit_rows(pooled).astype(BF)


def image_forward(tokens, wq, wo, wu, wd, vec, ub):
    pairs, length, width = tokens.shape
    hidden = wu.shape[1]
    group = 8
    rows = group * length
    return pl.pallas_call(
        image_kernel,
        name="image_forward",
        grid=(pairs // group,),
        in_specs=[
            pl.BlockSpec((group, length, width), lambda i: (i, 0, 0)),
            ANY,
            ANY,
            ANY,
            ANY,
            pl.BlockSpec((8, width), lambda i: (0, 0)),
            pl.BlockSpec((1, hidden), lambda i: (0, 0)),
        ],
        out_specs=pl.BlockSpec((pairs, width), lambda i: (0, 0)),
        out_shape=jax.ShapeDtypeStruct((pairs, width), BF),
        scratch_shapes=[
            pltpu.VMEM((width, 3 * width), BF),
            pltpu.VMEM((width, width), BF),
            pltpu.VMEM((width, hidden), BF),
            pltpu.VMEM((hidden, width), BF),
            pltpu.VMEM((rows, width), F32),
            pltpu.VMEM((rows, width), BF),
            pltpu.VMEM((rows, 3 * width), BF),
            pltpu.VMEM((rows, width), BF),
            pltpu.VMEM((pairs, hidden), F32),
            pltpu.VMEM((pairs, width), F32),
            pltpu.SemaphoreType.DMA((4,)),
        ],
        compiler_params=params(),
        cost_estimate=pl.CostEstimate(
            flops=2 * pairs * length * width * (4 * width + hidden),
            bytes_accessed=2 * (4 * width * width + 2 * width * hidden + pairs * length * width),
            transcendentals=pairs * length * hidden,
        ),
    )(tokens, wq, wo, wu, wd, vec, ub.reshape(1, hidden))


def pack_rows(width, hidden):
    piece, rows = width // PX, width // PF
    return piece, rows, hidden // PF


def weight_copies(packed, which, dst, sem, base, width, hidden):
    piece, rows, frows = pack_rows(width, hidden)
    q_pieces, u_pieces = 3, hidden // width
    spans = {
        "qkv": (0, q_pieces, rows),
        "out": (q_pieces * rows, 1, rows),
        "up": ((q_pieces + 1) * rows, u_pieces, rows),
        "down": ((q_pieces + 1 + u_pieces) * rows, 1, frows),
    }
    start, count, tall = spans[which]
    copies = []
    for x in range(PX):
        for p in range(count):
            copies.append(
                pltpu.make_async_copy(
                    packed.at[pl.ds(x * PF, PF), pl.ds(start + p * tall, tall), :],
                    dst.at[:, :, pl.ds((x * count + p) * piece, piece)],
                    sem.at[base + len(copies)],
                )
            )
    return copies


def natural(ref):
    blocks, rows, cols = ref.shape
    return ref[...].reshape(blocks * rows, cols)


def weight_scratch(which, width, hidden):
    rows, frows = width // PF, hidden // PF
    shape = {
        "qkv": (PF, rows, 3 * width),
        "out": (PF, rows, width),
        "up": (PF, rows, hidden),
        "down": (PF, frows, width),
    }[which]
    return pltpu.VMEM(shape, BF)


def text_mask(size, length):
    row = lax.broadcasted_iota(jnp.int32, (size, size), 0) // length
    col = lax.broadcasted_iota(jnp.int32, (size, size), 1) // length
    return jnp.where(row == col, 0.0, -1e30)


def text_forward_kernel(
    length, tok, packed, vec, ub, h1, qkv, att, r1, h2, slope, acts, pooled_out, low, wq, wo, wu, wd, total, sem
):
    rows, width = tok.shape
    hidden = slope.shape[1]
    texts = rows // length
    load = {}
    base = 0
    for which, dst in (("qkv", wq), ("out", wo), ("up", wu), ("down", wd)):
        load[which] = weight_copies(packed, which, dst, sem, base, width, hidden)
        base += len(load[which])
        for copy in load[which]:
            copy.start()
    v = vec[...].astype(F32)
    blk = 128
    for r in range(0, rows, blk):
        hat, _ = normalize(tok[r : r + blk, :].astype(F32))
        h1[r : r + blk, :] = (hat * v[0:1] + v[1:2]).astype(BF)
    for copy in load["qkv"]:
        copy.wait()
    for c in range(0, 3 * width, 256):
        part = dot(h1[...], wq[:, :, c : c + 256].reshape(width, 256))
        if c < width:
            part = part + v[2:3, c : c + 256]
        if c >= 2 * width:
            part = part + v[3:4, c - 2 * width : c - 2 * width + 256]
        qkv[:, c : c + 256] = part.astype(BF)
    low_lane = lax.broadcasted_iota(jnp.int32, (blk, 128), 1) < HEAD_DIM
    bias = text_mask(blk, length)
    for r in range(0, rows, blk):
        for c in range(0, width, 128):
            q2 = qkv[r : r + blk, c : c + 128] * 0.125
            k2 = head_pair(qkv[r : r + blk, width + c : width + c + 128], low_lane)
            v2 = head_pair(qkv[r : r + blk, 2 * width + c : 2 * width + c + 128], low_lane)
            scores = dot(q2, k2, 1, 1)
            probs = jnp.concatenate(
                [
                    softmax_half(scores[:, :blk], bias).astype(BF),
                    softmax_half(scores[:, blk:], bias).astype(BF),
                ],
                axis=1,
            )
            att[r : r + blk, c : c + 128] = dot(probs, v2).astype(BF)
    for copy in load["out"]:
        copy.wait()
    for c in range(0, width, 256):
        r1[:, c : c + 256] = tok[:, c : c + 256].astype(F32) + (
            dot(att[...], wo[:, :, c : c + 256].reshape(width, 256)) + v[4:5, c : c + 256]
        )
    for r in range(0, rows, blk):
        hat, _ = normalize(r1[r : r + blk, :])
        h2[r : r + blk, :] = (hat * v[5:6] + v[6:7]).astype(BF)
    for copy in load["up"]:
        copy.wait()
    for c in range(0, hidden, 256):
        u = dot(h2[...], wu[:, :, c : c + 256].reshape(width, 256)) + ub[:, c : c + 256].astype(F32)
        tail, bell, size = gauss_tail(u)
        act = jnp.maximum(u, 0.0) - size * tail
        phi = jnp.where(u >= 0.0, 1.0 - tail, tail)
        slope[:, c : c + 256] = (phi + u * (bell * 0.3989422804014327)).astype(BF)
        sums = jnp.sum(act.reshape(texts, length, 256), axis=1)
        total[:, c : c + 256] = sums
        acts[:, c : c + 256] = sums.astype(BF)
    for copy in load["down"]:
        copy.wait()
    mean_r1 = jnp.sum(r1[...].reshape(texts, length, width), axis=1) * (1.0 / length)
    pooled = mean_r1 + mean_down(total[...], length, natural(wd)) + v[7:8]
    pooled_out[...] = pooled
    low[...] = unit_rows(pooled).astype(BF)


def text_forward(tokens, packed, vec, ub, length, hidden):
    rows, width = tokens.shape
    texts = rows // length
    shape = jax.ShapeDtypeStruct
    copies = PX * (3 + 1 + hidden // width + 1)
    return pl.pallas_call(
        functools.partial(text_forward_kernel, length),
        name="text_forward",
        in_specs=[WHOLE, ANY, WHOLE, WHOLE],
        out_specs=[WHOLE] * 9,
        out_shape=[
            shape((rows, width), BF),
            shape((rows, 3 * width), BF),
            shape((rows, width), BF),
            shape((rows, width), F32),
            shape((rows, width), BF),
            shape((rows, hidden), BF),
            shape((texts, hidden), BF),
            shape((texts, width), F32),
            shape((texts, width), BF),
        ],
        scratch_shapes=[weight_scratch(w, width, hidden) for w in ("qkv", "out", "up", "down")]
        + [pltpu.VMEM((texts, hidden), F32), pltpu.SemaphoreType.DMA((copies,))],
        compiler_params=params(),
        cost_estimate=pl.CostEstimate(
            flops=2 * rows * width * (4 * width + hidden),
            bytes_accessed=2 * (4 * width * width + 2 * width * hidden + 12 * rows * width),
            transcendentals=rows * hidden,
        ),
    )(tokens, packed, vec, ub)


def contrast_kernel(low, images, live, same, groups, own, own_group, power, row_part, col_sum, loss_part):
    scores = LOGIT_SCALE * dot(low[...], images[...], 1, 1)
    exps = jnp.exp(scores)
    live_own, same_own = own[:, 0:1], own[:, 1:2]
    power[...] = exps
    rows = jnp.sum(exps * live_own, axis=0, keepdims=True)
    for k in range(row_part.shape[0]):
        row_part[k : k + 1, :] = rows[:, k * 128 : (k + 1) * 128]
    cols = jnp.sum(exps * live[...], axis=1, keepdims=True)
    col_sum[...] = cols
    pair = jnp.where(own_group[...] == groups[...], live_own * live[...], 0.0)
    linear = pair * scores * (1.0 / same_own + 1.0 / same[...])
    losses = live_own * jnp.log(cols) - jnp.sum(linear, axis=1, keepdims=True)
    loss_part[...] = jnp.broadcast_to(jnp.sum(losses, axis=0, keepdims=True), loss_part.shape)


def contrast(low, images, live, same, groups, own, own_group):
    texts = low.shape[0]
    pairs = images.shape[0]
    shape = jax.ShapeDtypeStruct
    return pl.pallas_call(
        contrast_kernel,
        name="contrast",
        in_specs=[WHOLE] * 7,
        out_specs=[WHOLE] * 4,
        out_shape=[
            shape((texts, pairs), F32),
            shape((pairs // 128, 128), F32),
            shape((texts, 1), F32),
            shape((8, 128), F32),
        ],
        compiler_params=params(),
    )(low, images, live, same, groups, own, own_group)


def back_first_kernel(
    length,
    power, row_all, col_sum, images, live, same, groups, own, own_group, factor, pooled, packed, slope, h2,
    dy_out, dm_out, du, grad_up, bias_up, down_bias, wd, dact, sem,
):
    rows, hidden = slope.shape
    texts = rows // length
    width = h2.shape[1]
    loads = weight_copies(packed, "down", wd, sem, 0, width, hidden)
    for copy in loads:
        copy.start()
    sums = row_all[...]
    if sums.ndim == 3:
        sums = jnp.sum(sums, axis=0)
    row_sum = jnp.concatenate([sums[k : k + 1] for k in range(sums.shape[0])], axis=1)
    live_own, same_own = own[:, 0:1], own[:, 1:2]
    pair = factor[0:1, 0:1] * live_own * live[...]
    match = jnp.where(own_group[...] == groups[...], 1.0 / same_own + 1.0 / same[...], 0.0)
    grad_scores = pair * (power[...] * (1.0 / row_sum + 1.0 / col_sum[...]) - match)
    grad_low = LOGIT_SCALE * dot(grad_scores.astype(BF), images[...])
    pool = pooled[...]
    inverse = lax.rsqrt(jnp.sum(pool * pool, axis=-1, keepdims=True) + 1e-06)
    along = jnp.sum(pool * grad_low, axis=-1, keepdims=True)
    dy = inverse * (grad_low - pool * (inverse * inverse * along)) * (1.0 / length)
    dm = dy.astype(BF)
    dy_out[...] = dy
    dm_out[...] = dm
    down_bias[...] = length * jnp.sum(dm.astype(F32), axis=0, keepdims=True)
    for copy in loads:
        copy.wait()
    dact[...] = dot(dm, natural(wd), 1, 1)
    half = hidden // PX
    for c in range(0, hidden, 256):
        spread = jnp.broadcast_to(dact[:, c : c + 256].reshape(texts, 1, 256), (texts, length, 256))
        part = spread.reshape(rows, 256) * slope[:, c : c + 256].astype(F32)
        part = part.astype(BF)
        du[:, c : c + 256] = part
        bias_up[:, c : c + 256] = jnp.sum(part.astype(F32), axis=0, keepdims=True)
        grad_up[c // half, :, c % half : c % half + 256] = dot(h2[...], part, 0, 0).astype(BF)


def back_first(power, row_all, col_sum, images, live, same, groups, own, own_group, factor, pooled, packed, slope, h2, length):
    rows, hidden = slope.shape
    width = h2.shape[1]
    texts = rows // length
    shape = jax.ShapeDtypeStruct
    return pl.pallas_call(
        functools.partial(back_first_kernel, length),
        name="back_first",
        in_specs=[WHOLE] * 11 + [ANY, WHOLE, WHOLE],
        out_specs=[WHOLE] * 6,
        out_shape=[
            shape((texts, width), F32),
            shape((texts, width), BF),
            shape((rows, hidden), BF),
            shape((PX, width, hidden // PX), BF),
            shape((1, hidden), F32),
            shape((1, width), F32),
        ],
        scratch_shapes=[
            weight_scratch("down", width, hidden),
            pltpu.VMEM((texts, hidden), F32),
            pltpu.SemaphoreType.DMA((PX,)),
        ],
        compiler_params=params(),
        cost_estimate=pl.CostEstimate(
            flops=2 * rows * width * hidden, bytes_accessed=12 * width * hidden, transcendentals=0
        ),
    )(power, row_all, col_sum, images, live, same, groups, own, own_group, factor, pooled, packed, slope, h2)


def back_second_kernel(
    length,
    dy, du, r1, h1, qkv, att, packed, vec,
    dr1, dqkv, grad_attn, sums, wu, wo, dz_s, da_s, sem,
):
    rows, width = r1.shape
    hidden = du.shape[1]
    texts = rows // length
    up = weight_copies(packed, "up", wu, sem, 0, width, hidden)
    out = weight_copies(packed, "out", wo, sem, len(up), width, hidden)
    for copy in up + out:
        copy.start()
    v = vec[...].astype(F32)
    blk = 128
    for copy in up:
        copy.wait()
    dr1[...] = dot(du[...], natural(wu), 1, 1)
    gain_sum = jnp.zeros((1, width), F32)
    shift_sum = jnp.zeros((1, width), F32)
    out_sum = jnp.zeros((1, width), F32)
    for r in range(0, rows, blk):
        hat, inverse = normalize(r1[r : r + blk, :])
        grad = dr1[r : r + blk, :]
        gain_sum = gain_sum + jnp.sum(grad * hat, axis=0, keepdims=True)
        shift_sum = shift_sum + jnp.sum(grad, axis=0, keepdims=True)
        some = blk // length
        spread = jnp.broadcast_to(
            dy[r // length : r // length + some, :].reshape(some, 1, width), (some, length, width)
        ).reshape(blk, width)
        grad = spread + norm_back(grad, hat, inverse, v[5:6])
        dr1[r : r + blk, :] = grad
        low = grad.astype(BF)
        dz_s[r : r + blk, :] = low
        out_sum = out_sum + jnp.sum(low.astype(F32), axis=0, keepdims=True)
    for copy in out:
        copy.wait()
    piece = width // PX
    q_cols = 3 * piece
    da_s[...] = dot(dz_s[...], natural(wo), 1, 1).astype(BF)
    for c in range(0, width, 128):
        grad_attn[c // piece, :, q_cols + c % piece : q_cols + c % piece + 128] = dot(
            att[...], dz_s[:, c : c + 128], 0, 0
        ).astype(BF)
    low_lane = lax.broadcasted_iota(jnp.int32, (blk, 128), 1) < HEAD_DIM
    bias = text_mask(blk, length)
    for r in range(0, rows, blk):
        for c in range(0, width, 128):
            q2 = qkv[r : r + blk, c : c + 128] * 0.125
            k2 = head_pair(qkv[r : r + blk, width + c : width + c + 128], low_lane)
            v2 = head_pair(qkv[r : r + blk, 2 * width + c : 2 * width + c + 128], low_lane)
            da = da_s[r : r + blk, c : c + 128]
            scores = dot(q2, k2, 1, 1)
            grads = dot(da, v2, 1, 1)
            probs, deltas = [], []
            for half in range(2):
                soft = softmax_half(scores[:, half * blk : (half + 1) * blk], bias)
                grad = grads[:, half * blk : (half + 1) * blk]
                probs.append(soft.astype(BF))
                deltas.append(
                    (soft * (grad - jnp.sum(grad * soft, axis=-1, keepdims=True))).astype(BF)
                )
            probs = jnp.concatenate(probs, axis=1)
            deltas = jnp.concatenate(deltas, axis=1)
            dq = dot(deltas, k2) * 0.125
            dk = dot(deltas, q2, 0, 0)
            dv = dot(probs, da, 0, 0)
            dqkv[r : r + blk, c : c + 128] = dq.astype(BF)
            dqkv[r : r + blk, width + c : width + c + 128] = jnp.where(
                low_lane, dk[:blk], dk[blk:]
            ).astype(BF)
            dqkv[r : r + blk, 2 * width + c : 2 * width + c + 128] = jnp.where(
                low_lane, dv[:blk], dv[blk:]
            ).astype(BF)
    for c in range(0, 3 * width, 128):
        grad_attn[c // q_cols, :, c % q_cols : c % q_cols + 128] = dot(
            h1[...], dqkv[:, c : c + 128], 0, 0
        ).astype(BF)
    sums[0:1, :] = jnp.sum(dqkv[:, :width].astype(F32), axis=0, keepdims=True)
    sums[1:2, :] = jnp.sum(dqkv[:, 2 * width :].astype(F32), axis=0, keepdims=True)
    sums[2:3, :] = out_sum
    sums[3:4, :] = gain_sum
    sums[4:5, :] = shift_sum
    sums[5:8, :] = jnp.zeros((3, width), F32)


def back_second(dy, du, r1, h1, qkv, att, packed, vec, length):
    rows, width = r1.shape
    hidden = du.shape[1]
    shape = jax.ShapeDtypeStruct
    return pl.pallas_call(
        functools.partial(back_second_kernel, length),
        name="back_second",
        in_specs=[WHOLE] * 6 + [ANY, WHOLE],
        out_specs=[WHOLE] * 4,
        out_shape=[
            shape((rows, width), F32),
            shape((rows, 3 * width), BF),
            shape((PX, width, 4 * width // PX), BF),
            shape((8, width), F32),
        ],
        scratch_shapes=[
            weight_scratch("up", width, hidden),
            weight_scratch("out", width, hidden),
            pltpu.VMEM((rows, width), BF),
            pltpu.VMEM((rows, width), BF),
            pltpu.SemaphoreType.DMA((PX * (1 + hidden // width),)),
        ],
        compiler_params=params(),
        cost_estimate=pl.CostEstimate(
            flops=2 * rows * width * (hidden + 5 * width),
            bytes_accessed=12 * width * hidden,
            transcendentals=0,
        ),
    )(dy, du, r1, h1, qkv, att, packed, vec)


def back_third_kernel(dr1, dqkv, tok, packed, vec, sums, down_bias, dx, all_sums, wq, sem):
    rows, width = tok.shape
    loads = weight_copies(packed, "qkv", wq, sem, 0, width, width)
    for copy in loads:
        copy.start()
    v = vec[...].astype(F32)
    for copy in loads:
        copy.wait()
    dx[...] = dot(dqkv[...], natural(wq), 1, 1)
    gain_sum = jnp.zeros((1, width), F32)
    shift_sum = jnp.zeros((1, width), F32)
    blk = 128
    for r in range(0, rows, blk):
        hat, inverse = normalize(tok[r : r + blk, :].astype(F32))
        grad = dx[r : r + blk, :]
        gain_sum = gain_sum + jnp.sum(grad * hat, axis=0, keepdims=True)
        shift_sum = shift_sum + jnp.sum(grad, axis=0, keepdims=True)
        dx[r : r + blk, :] = dr1[r : r + blk, :] + norm_back(grad, hat, inverse, v[0:1])
    all_sums[0:1, :] = gain_sum
    all_sums[1:2, :] = shift_sum
    all_sums[2:7, :] = sums[0:5, :]
    all_sums[7:8, :] = down_bias[...]


def back_third(dr1, dqkv, tok, packed, vec, sums, down_bias):
    rows, width = tok.shape
    shape = jax.ShapeDtypeStruct
    return pl.pallas_call(
        back_third_kernel,
        name="back_third",
        in_specs=[WHOLE, WHOLE, WHOLE, ANY, WHOLE, WHOLE, WHOLE],
        out_specs=[WHOLE] * 2,
        out_shape=[shape((rows, width), F32), shape((8, width), F32)],
        scratch_shapes=[
            weight_scratch("qkv", width, width),
            pltpu.SemaphoreType.DMA((PX * 3,)),
        ],
        compiler_params=params(),
        cost_estimate=pl.CostEstimate(
            flops=6 * rows * width * width, bytes_accessed=14 * width * width, transcendentals=0
        ),
    )(dr1, dqkv, tok, packed, vec, sums, down_bias)


def pack_block(qkv, out, up, down):
    piece = out.shape[1]
    parts = [qkv[:, i : i + piece] for i in range(0, qkv.shape[1], piece)] + [out]
    parts += [up[:, i : i + piece] for i in range(0, up.shape[1], piece)] + [down]
    return jnp.concatenate(parts, axis=0)


def gather_packed(qkv, out, up, down, dp, fsdp):
    if (dp, fsdp) == (PX, PF):
        return lax.all_gather(pack_block(qkv, out, up, down), AXES, axis=0)
    full = [
        lax.all_gather(lax.all_gather(w, "dp", axis=1, tiled=True), "fsdp", axis=0, tiled=True)
        for w in (qkv, out, up, down)
    ]
    blocks = []
    for x in range(PX):
        for f in range(PF):
            some = []
            for w in full:
                rows, cols = w.shape[0] // PF, w.shape[1] // PX
                some.append(w[f * rows : (f + 1) * rows, x * cols : (x + 1) * cols])
            blocks.append(pack_block(*some))
    return jnp.stack(blocks)


def scatter_columns(grad, dp, fsdp):
    parts, rows, cols = grad.shape
    if dp != parts:
        grad = jnp.swapaxes(grad, 0, 1).reshape(rows, dp, parts * cols // dp)
        grad = jnp.swapaxes(grad, 0, 1)
    return lax.psum_scatter(
        grad.reshape(dp * rows, -1), AXES, scatter_dimension=0, tiled=True
    ).astype(F32)


def body(
    image_tokens,
    text_tokens,
    image_qkv,
    image_out,
    image_up,
    image_down,
    image_vectors,
    image_up_bias,
    text_qkv,
    text_out,
    text_up,
    text_down,
    text_vectors,
    text_up_bias,
    pair_counts,
    pair_groups,
):
    dp, fsdp = lax.axis_size("dp"), lax.axis_size("fsdp")
    devices = dp * fsdp
    cap, length, width = text_tokens.shape
    hidden = image_up.shape[1]
    pairs = pair_groups.shape[0]
    me = lax.axis_index("dp") * fsdp + lax.axis_index("fsdp")

    packed = gather_packed(text_qkv, text_out, text_up, text_down, dp, fsdp)
    part = width // fsdp
    small = jnp.concatenate([text_vectors, text_up_bias.reshape(8, -1)], axis=1)
    small = lax.all_gather(small, "fsdp", axis=0)
    vec = jnp.swapaxes(small[:, :, :part], 0, 1).reshape(8, width)
    ub = small[:, :, part:].reshape(1, hidden)

    image_low = image_forward(
        image_tokens, image_qkv, image_out, image_up, image_down, image_vectors, image_up_bias
    )
    images = lax.all_gather(image_low, AXES, axis=0, tiled=True)

    slots = jnp.arange(cap, dtype=jnp.int32)
    live = (slots[None, :] < pair_counts[:, None]).reshape(pairs).astype(F32)
    same = jnp.maximum(
        jnp.sum(jnp.where(pair_groups[:, None] == pair_groups[None, :], live[None, :], 0.0), axis=1), 1.0
    )
    own_of = lambda array: lax.dynamic_slice_in_dim(array, me * cap, cap)
    own = jnp.stack([own_of(live), own_of(same)], axis=1)
    own_group = own_of(pair_groups).reshape(cap, 1)
    live_row, same_row, group_row = (a.reshape(1, pairs) for a in (live, same, pair_groups))
    live_total = jnp.sum(pair_counts).astype(F32)
    factor = jnp.broadcast_to(LOSS_WEIGHT / (2.0 * live_total), (1, 128))

    tokens = text_tokens.reshape(cap * length, width)
    h1, qkv, att, r1, h2, slope, acts, pooled, low = text_forward(tokens, packed, vec, ub, length, hidden)
    power, row_part, col_sum, loss_part = contrast(
        low, images, live_row, same_row, group_row, own, own_group
    )
    if devices <= 32:
        row_all = lax.all_to_all(
            jnp.broadcast_to(row_part[None], (devices,) + row_part.shape), AXES, 0, 0, tiled=True
        )
        row_sum = jnp.sum(row_all, axis=0)
    else:
        row_all = lax.psum(row_part, AXES)
        row_sum = row_all
    dy, dm, du, grad_up, bias_up, down_bias = back_first(
        power, row_all, col_sum, images, live_row, same_row, group_row, own, own_group, factor, pooled,
        packed, slope, h2, length,
    )
    dr1, dqkv, grad_attn, sums = back_second(dy, du, r1, h1, qkv, att, packed, vec, length)
    dx, vec_grads = back_third(dr1, dqkv, tokens, packed, vec, sums, down_bias)

    if dp == PX:
        grad_up = scatter_columns(grad_up, dp, fsdp)
        grad_attn = scatter_columns(grad_attn, dp, fsdp)
        grad_qkv, grad_out = grad_attn[:, : 3 * width // dp], grad_attn[:, 3 * width // dp :]
    else:
        grad_up = scatter_columns(grad_up, dp, fsdp)
        grad_qkv = scatter_columns(grad_attn[:, :, : 3 * width // PX], dp, fsdp)
        grad_out = scatter_columns(grad_attn[:, :, 3 * width // PX :], dp, fsdp)

    rows_of = hidden // fsdp
    cols_of = width // dp
    left = jnp.swapaxes(acts.reshape(cap, fsdp, rows_of), 0, 1)
    left = jnp.broadcast_to(left[None], (dp, fsdp, cap, rows_of)).reshape(devices, cap, rows_of)
    right = jnp.swapaxes(dm.reshape(cap, dp, cols_of), 0, 1)
    right = jnp.broadcast_to(right[:, None], (dp, fsdp, cap, cols_of)).reshape(devices, cap, cols_of)
    both = lax.all_to_all(jnp.concatenate([left, right], axis=2), AXES, 0, 0, tiled=True)
    both = both.reshape(pairs, rows_of + cols_of)
    grad_down = dot(both[:, :rows_of], both[:, rows_of:], 0, 0)

    share = jnp.concatenate(
        [
            jnp.swapaxes(vec_grads.reshape(8, fsdp, part), 0, 1).reshape(fsdp, 8 * part),
            bias_up.reshape(fsdp, rows_of),
            jnp.broadcast_to(loss_part[0, 0].reshape(1, 1), (fsdp, 1)),
        ],
        axis=1,
    )
    used = share.shape[1]
    padded = -(-used // 128) * 128
    share = jnp.pad(share, ((0, 0), (0, padded - used))).reshape(fsdp, padded // 128, 128)
    share = jnp.broadcast_to(share[None], (dp,) + share.shape).reshape(devices, padded // 128, 128)
    share = jnp.sum(lax.all_to_all(share, AXES, 0, 0, tiled=True), axis=0).reshape(padded)
    grad_vec = share[: 8 * part].reshape(8, part)
    grad_bias = share[8 * part : 8 * part + rows_of]
    loss = (share[used - 1] + jnp.sum(live * jnp.log(row_sum.reshape(pairs)))) / (2.0 * live_total)

    return (
        loss,
        dx.reshape(text_tokens.shape),
        grad_qkv,
        grad_out,
        grad_up,
        grad_down,
        grad_vec,
        grad_bias,
    )


def solution(mesh):
    return jax.shard_map(
        body,
        mesh=mesh,
        in_specs=(
            P(AXES, None, None),
            P(AXES, None, None),
            P(),
            P(),
            P(),
            P(),
            P(),
            P(),
            P("fsdp", "dp"),
            P("fsdp", "dp"),
            P("fsdp", "dp"),
            P("fsdp", "dp"),
            P(None, "fsdp"),
            P("fsdp"),
            P(),
            P(),
        ),
        out_specs=(
            P(),
            P(AXES, None, None),
            P("fsdp", "dp"),
            P("fsdp", "dp"),
            P("fsdp", "dp"),
            P("fsdp", "dp"),
            P(None, "fsdp"),
            P("fsdp"),
        ),
        check_vma=False,
    )
```

```python
import functools

import jax
import jax.numpy as jnp
from jax import lax
from jax.experimental import pallas as pl
from jax.experimental.pallas import tpu as pltpu
from jax.sharding import PartitionSpec as P

HEAD_DIM = 64
LOGIT_SCALE = 50.0
LOSS_WEIGHT = 32768.0
BF = jnp.bfloat16
F32 = jnp.float32
AXES = ("dp", "fsdp")
PX, PF = 2, 16
VMEM_LIMIT = 62 * 1024 * 1024

ANY = pl.BlockSpec(memory_space=pl.ANY)
WHOLE = pl.BlockSpec(memory_space=pltpu.VMEM)


def params(**more):
    return pltpu.CompilerParams(vmem_limit_bytes=VMEM_LIMIT, **more)


def dot(a, b, ca=1, cb=0):
    return lax.dot_general(a, b, (((ca,), (cb,)), ((), ())), preferred_element_type=F32)


def normalize(values):
    centered = values - jnp.mean(values, axis=-1, keepdims=True)
    inverse = lax.rsqrt(jnp.mean(centered * centered, axis=-1, keepdims=True) + 1e-05)
    return centered * inverse, inverse


def norm_back(grad, hat, inverse, gain):
    scaled = grad * gain
    return inverse * (
        scaled
        - jnp.mean(scaled, axis=-1, keepdims=True)
        - hat * jnp.mean(scaled * hat, axis=-1, keepdims=True)
    )


def gauss_tail(u):
    size = jnp.abs(u)
    t = 1.0 / (1.0 + (0.3275911 * 0.7071067811865476) * size)
    bell = jnp.exp(-0.5 * (u * u))
    poly = 0.5 * 1.061405429 * t - 0.5 * 1.453152027
    poly = poly * t + 0.5 * 1.421413741
    poly = poly * t - 0.5 * 0.284496736
    poly = poly * t + 0.5 * 0.254829592
    return poly * t * bell, bell, size


def head_pair(block, low_lane):
    zero = jnp.zeros_like(block)
    return jnp.concatenate(
        [jnp.where(low_lane, block, zero), jnp.where(low_lane, zero, block)], axis=0
    )


def softmax_half(scores, bias):
    scores = scores + bias
    top = jnp.max(scores, axis=-1, keepdims=True)
    powers = jnp.exp(scores - top)
    return powers * (1.0 / jnp.sum(powers, axis=-1, keepdims=True))


def unit_rows(pooled):
    return pooled * lax.rsqrt(jnp.sum(pooled * pooled, axis=-1, keepdims=True) + 1e-06)


def mean_down(total, count, down):
    mean = total * (1.0 / count)
    high = mean.astype(BF)
    low = (mean - high.astype(F32)).astype(BF)
    return dot(high, down) + dot(low, down)


def image_kernel(
    tok, wq_h, wo_h, wu_h, wd_h, vec, ub, out, wq, wo, wu, wd, x, h, qkv, att, act_sum, r1_sum, sem
):
    step, steps = pl.program_id(0), pl.num_programs(0)
    group, length, width = tok.shape
    rows = group * length
    hidden = wu.shape[1]
    copies = [
        pltpu.make_async_copy(src, dst, sem.at[i])
        for i, (src, dst) in enumerate(((wq_h, wq), (wo_h, wo), (wu_h, wu), (wd_h, wd)))
    ]

    @pl.when(step == 0)
    def _():
        for copy in copies:
            copy.start()

    def arrived(i):
        @pl.when(step == 0)
        def _():
            copies[i].wait()

    v = vec[...].astype(F32)
    for i in range(group):
        x[pl.ds(i * length, length), :] = tok[i].astype(F32)
    blk = 80
    for r in range(0, rows, blk):
        hat, _ = normalize(x[r : r + blk, :])
        h[r : r + blk, :] = (hat * v[0:1] + v[1:2]).astype(BF)
    arrived(0)
    for c in range(0, 3 * width, 256):
        part = dot(h[...], wq[:, c : c + 256])
        if c < width:
            part = part + v[2:3, c : c + 256]
        if c >= 2 * width:
            part = part + v[3:4, c - 2 * width : c - 2 * width + 256]
        qkv[:, c : c + 256] = part.astype(BF)

    wins = rows // (2 * length)
    q_at = [(2 * length * w) // 16 * 16 for w in range(wins)]
    k_at = [min(q, rows - 128) for q in q_at]
    q_len = 112
    low_lane = lax.broadcasted_iota(jnp.int32, (128, 128), 1) < HEAD_DIM
    for w in range(wins):
        qi = q_at[w] + lax.broadcasted_iota(jnp.int32, (q_len, 128), 0)
        ki = k_at[w] + lax.broadcasted_iota(jnp.int32, (q_len, 128), 1)
        lo, mid, hi = 2 * w * length, (2 * w + 1) * length, (2 * w + 2) * length
        first = (qi >= lo) & (qi < mid) & (ki >= lo) & (ki < mid)
        second = (qi >= mid) & (qi < hi) & (ki >= mid) & (ki < hi)
        allowed = first | second
        bias = jnp.where(allowed, 0.0, -1e30)
        inside = jnp.where((qi >= lo) & (qi < hi), 1.0, 0.0)
        for p in range(width // 128):
            c = p * 128
            q2 = qkv[q_at[w] : q_at[w] + q_len, c : c + 128] * 0.125
            k2 = head_pair(qkv[k_at[w] : k_at[w] + 128, width + c : width + c + 128], low_lane)
            v2 = head_pair(
                qkv[k_at[w] : k_at[w] + 128, 2 * width + c : 2 * width + c + 128], low_lane
            )
            scores = dot(q2, k2, 1, 1)
            probs = jnp.concatenate(
                [
                    (softmax_half(scores[:, :128], bias) * inside).astype(BF),
                    (softmax_half(scores[:, 128:], bias) * inside).astype(BF),
                ],
                axis=1,
            )
            mixed = dot(probs, v2)
            a = q_at[w]
            if w == 0:
                att[a : a + q_len, c : c + 128] = mixed.astype(BF)
            else:
                prev_end = q_at[w - 1] + q_len
                over = prev_end - a
                if over > 0:
                    old = att[a : a + over, c : c + 128].astype(F32)
                    att[a : a + over, c : c + 128] = (old + mixed[:over]).astype(BF)
                att[a + over : a + q_len, c : c + 128] = mixed[over:].astype(BF)

    arrived(1)
    for c in range(0, width, 256):
        x[:, c : c + 256] = x[:, c : c + 256] + (dot(att[...], wo[:, c : c + 256]) + v[4:5, c : c + 256])
    for r in range(0, rows, blk):
        hat, _ = normalize(x[r : r + blk, :])
        h[r : r + blk, :] = (hat * v[5:6] + v[6:7]).astype(BF)

    def image_sums(values):
        sums = []
        for i in range(group):
            lo, hi = i * length, (i + 1) * length
            a, b = lo // 8 * 8, -(-hi // 8) * 8
            part = values[a:b]
            row = a + lax.broadcasted_iota(jnp.int32, (b - a, 1), 0)
            if lo % 8 or hi % 8:
                part = jnp.where((row >= lo) & (row < hi), part, 0.0)
            sums.append(jnp.sum(part, axis=0, keepdims=True))
        return jnp.concatenate(sums, axis=0)

    place = pl.ds(pl.multiple_of(step * group, group), group)
    for c in range(0, width, 256):
        r1_sum[place, c : c + 256] = image_sums(x[:, c : c + 256])
    arrived(2)
    for c in range(0, hidden, 256):
        u = dot(h[...], wu[:, c : c + 256]) + ub[:, c : c + 256].astype(F32)
        tail, _, size = gauss_tail(u)
        act_sum[place, c : c + 256] = image_sums(jnp.maximum(u, 0.0) - size * tail)
    arrived(3)

    @pl.when(step == steps - 1)
    def _():
        pooled = r1_sum[...] * (1.0 / length) + mean_down(act_sum[...], length, wd[...]) + v[7:8]
        out[...] = unit_rows(pooled).astype(BF)


def image_forward(tokens, wq, wo, wu, wd, vec, ub):
    pairs, length, width = tokens.shape
    hidden = wu.shape[1]
    group = 8
    rows = group * length
    return pl.pallas_call(
        image_kernel,
        name="image_forward",
        grid=(pairs // group,),
        in_specs=[
            pl.BlockSpec((group, length, width), lambda i: (i, 0, 0)),
            ANY,
            ANY,
            ANY,
            ANY,
            pl.BlockSpec((8, width), lambda i: (0, 0)),
            pl.BlockSpec((1, hidden), lambda i: (0, 0)),
        ],
        out_specs=pl.BlockSpec((pairs, width), lambda i: (0, 0)),
        out_shape=jax.ShapeDtypeStruct((pairs, width), BF),
        scratch_shapes=[
            pltpu.VMEM((width, 3 * width), BF),
            pltpu.VMEM((width, width), BF),
            pltpu.VMEM((width, hidden), BF),
            pltpu.VMEM((hidden, width), BF),
            pltpu.VMEM((rows, width), F32),
            pltpu.VMEM((rows, width), BF),
            pltpu.VMEM((rows, 3 * width), BF),
            pltpu.VMEM((rows, width), BF),
            pltpu.VMEM((pairs, hidden), F32),
            pltpu.VMEM((pairs, width), F32),
            pltpu.SemaphoreType.DMA((4,)),
        ],
        compiler_params=params(),
        cost_estimate=pl.CostEstimate(
            flops=2 * pairs * length * width * (4 * width + hidden),
            bytes_accessed=2 * (4 * width * width + 2 * width * hidden + pairs * length * width),
            transcendentals=pairs * length * hidden,
        ),
    )(tokens, wq, wo, wu, wd, vec, ub.reshape(1, hidden))


def pack_rows(width, hidden):
    piece, rows = width // PX, width // PF
    return piece, rows, hidden // PF


def weight_copies(packed, which, dst, sem, base, width, hidden):
    piece, rows, frows = pack_rows(width, hidden)
    q_pieces, u_pieces = 3, hidden // width
    spans = {
        "qkv": (0, q_pieces, rows),
        "out": (q_pieces * rows, 1, rows),
        "up": ((q_pieces + 1) * rows, u_pieces, rows),
        "down": ((q_pieces + 1 + u_pieces) * rows, 1, frows),
    }
    start, count, tall = spans[which]
    copies = []
    for x in range(PX):
        for p in range(count):
            copies.append(
                pltpu.make_async_copy(
                    packed.at[pl.ds(x * PF, PF), pl.ds(start + p * tall, tall), :],
                    dst.at[:, :, pl.ds((x * count + p) * piece, piece)],
                    sem.at[base + len(copies)],
                )
            )
    return copies


def natural(ref):
    blocks, rows, cols = ref.shape
    return ref[...].reshape(blocks * rows, cols)


def weight_scratch(which, width, hidden):
    rows, frows = width // PF, hidden // PF
    shape = {
        "qkv": (PF, rows, 3 * width),
        "out": (PF, rows, width),
        "up": (PF, rows, hidden),
        "down": (PF, frows, width),
    }[which]
    return pltpu.VMEM(shape, BF)


def text_mask(size, length):
    row = lax.broadcasted_iota(jnp.int32, (size, size), 0) // length
    col = lax.broadcasted_iota(jnp.int32, (size, size), 1) // length
    return jnp.where(row == col, 0.0, -1e30)


def text_forward_kernel(
    length, tok, packed, vec, ub, h1, qkv, att, r1, h2, slope, acts, pooled_out, low, wq, wo, wu, wd, total, sem
):
    rows, width = tok.shape
    hidden = slope.shape[1]
    texts = rows // length
    load = {}
    base = 0
    for which, dst in (("qkv", wq), ("out", wo), ("up", wu), ("down", wd)):
        load[which] = weight_copies(packed, which, dst, sem, base, width, hidden)
        base += len(load[which])
        for copy in load[which]:
            copy.start()
    v = vec[...].astype(F32)
    blk = 128
    for r in range(0, rows, blk):
        hat, _ = normalize(tok[r : r + blk, :].astype(F32))
        h1[r : r + blk, :] = (hat * v[0:1] + v[1:2]).astype(BF)
    for copy in load["qkv"]:
        copy.wait()
    for c in range(0, 3 * width, 256):
        part = dot(h1[...], wq[:, :, c : c + 256].reshape(width, 256))
        if c < width:
            part = part + v[2:3, c : c + 256]
        if c >= 2 * width:
            part = part + v[3:4, c - 2 * width : c - 2 * width + 256]
        qkv[:, c : c + 256] = part.astype(BF)
    low_lane = lax.broadcasted_iota(jnp.int32, (blk, 128), 1) < HEAD_DIM
    bias = text_mask(blk, length)
    for r in range(0, rows, blk):
        for c in range(0, width, 128):
            q2 = qkv[r : r + blk, c : c + 128] * 0.125
            k2 = head_pair(qkv[r : r + blk, width + c : width + c + 128], low_lane)
            v2 = head_pair(qkv[r : r + blk, 2 * width + c : 2 * width + c + 128], low_lane)
            scores = dot(q2, k2, 1, 1)
            probs = jnp.concatenate(
                [
                    softmax_half(scores[:, :blk], bias).astype(BF),
                    softmax_half(scores[:, blk:], bias).astype(BF),
                ],
                axis=1,
            )
            att[r : r + blk, c : c + 128] = dot(probs, v2).astype(BF)
    for copy in load["out"]:
        copy.wait()
    for c in range(0, width, 256):
        r1[:, c : c + 256] = tok[:, c : c + 256].astype(F32) + (
            dot(att[...], wo[:, :, c : c + 256].reshape(width, 256)) + v[4:5, c : c + 256]
        )
    for r in range(0, rows, blk):
        hat, _ = normalize(r1[r : r + blk, :])
        h2[r : r + blk, :] = (hat * v[5:6] + v[6:7]).astype(BF)
    for copy in load["up"]:
        copy.wait()
    for c in range(0, hidden, 256):
        u = dot(h2[...], wu[:, :, c : c + 256].reshape(width, 256)) + ub[:, c : c + 256].astype(F32)
        tail, bell, size = gauss_tail(u)
        act = jnp.maximum(u, 0.0) - size * tail
        phi = jnp.where(u >= 0.0, 1.0 - tail, tail)
        slope[:, c : c + 256] = (phi + u * (bell * 0.3989422804014327)).astype(BF)
        sums = jnp.sum(act.reshape(texts, length, 256), axis=1)
        total[:, c : c + 256] = sums
        acts[:, c : c + 256] = sums.astype(BF)
    for copy in load["down"]:
        copy.wait()
    mean_r1 = jnp.sum(r1[...].reshape(texts, length, width), axis=1) * (1.0 / length)
    pooled = mean_r1 + mean_down(total[...], length, natural(wd)) + v[7:8]
    pooled_out[...] = pooled
    low[...] = unit_rows(pooled).astype(BF)


def text_forward(tokens, packed, vec, ub, length, hidden):
    rows, width = tokens.shape
    texts = rows // length
    shape = jax.ShapeDtypeStruct
    copies = PX * (3 + 1 + hidden // width + 1)
    return pl.pallas_call(
        functools.partial(text_forward_kernel, length),
        name="text_forward",
        in_specs=[WHOLE, ANY, WHOLE, WHOLE],
        out_specs=[WHOLE] * 9,
        out_shape=[
            shape((rows, width), BF),
            shape((rows, 3 * width), BF),
            shape((rows, width), BF),
            shape((rows, width), F32),
            shape((rows, width), BF),
            shape((rows, hidden), BF),
            shape((texts, hidden), BF),
            shape((texts, width), F32),
            shape((texts, width), BF),
        ],
        scratch_shapes=[weight_scratch(w, width, hidden) for w in ("qkv", "out", "up", "down")]
        + [pltpu.VMEM((texts, hidden), F32), pltpu.SemaphoreType.DMA((copies,))],
        compiler_params=params(),
        cost_estimate=pl.CostEstimate(
            flops=2 * rows * width * (4 * width + hidden),
            bytes_accessed=2 * (4 * width * width + 2 * width * hidden + 12 * rows * width),
            transcendentals=rows * hidden,
        ),
    )(tokens, packed, vec, ub)


def contrast_kernel(low, images, live, same, groups, own, own_group, power, row_part, col_sum, loss_part):
    scores = LOGIT_SCALE * dot(low[...], images[...], 1, 1)
    exps = jnp.exp(scores)
    live_own, same_own = own[:, 0:1], own[:, 1:2]
    power[...] = exps
    rows = jnp.sum(exps * live_own, axis=0, keepdims=True)
    for k in range(row_part.shape[0]):
        row_part[k : k + 1, :] = rows[:, k * 128 : (k + 1) * 128]
    cols = jnp.sum(exps * live[...], axis=1, keepdims=True)
    col_sum[...] = cols
    pair = jnp.where(own_group[...] == groups[...], live_own * live[...], 0.0)
    linear = pair * scores * (1.0 / same_own + 1.0 / same[...])
    losses = live_own * jnp.log(cols) - jnp.sum(linear, axis=1, keepdims=True)
    loss_part[...] = jnp.broadcast_to(jnp.sum(losses, axis=0, keepdims=True), loss_part.shape)


def contrast(low, images, live, same, groups, own, own_group):
    texts = low.shape[0]
    pairs = images.shape[0]
    shape = jax.ShapeDtypeStruct
    return pl.pallas_call(
        contrast_kernel,
        name="contrast",
        in_specs=[WHOLE] * 7,
        out_specs=[WHOLE] * 4,
        out_shape=[
            shape((texts, pairs), F32),
            shape((pairs // 128, 128), F32),
            shape((texts, 1), F32),
            shape((8, 128), F32),
        ],
        compiler_params=params(),
    )(low, images, live, same, groups, own, own_group)


def relative_kernel(where, h1, h2, att, h1_t, h2_t, att_t):
    width = h1.shape[1]
    block = width // PF
    my, mz, mc = where[1], where[2], where[3]
    for src, dst in ((h2, h2_t), (h1, h1_t), (att, att_t)):
        turned = src[...].T
        for z in range(4):
            for y in range(2):
                for c in range(2):
                    f = (z * 2 + y) * 2 + c
                    place = (((c ^ mc) * 2 + (y ^ my)) * 4 + (z ^ mz)) * block
                    dst[pl.ds(pl.multiple_of(place, block), block), :] = turned[
                        f * block : (f + 1) * block
                    ]


SMEM = pl.BlockSpec(memory_space=pltpu.SMEM)


def relative_rows(where, h1, h2, att):
    rows, width = h1.shape
    return pl.pallas_call(
        relative_kernel,
        name="relative_rows",
        in_specs=[SMEM, WHOLE, WHOLE, WHOLE],
        out_specs=[WHOLE] * 3,
        out_shape=[jax.ShapeDtypeStruct((width, rows), BF)] * 3,
        compiler_params=params(),
        cost_estimate=pl.CostEstimate(flops=0, bytes_accessed=12 * rows * width, transcendentals=0),
    )(where, h1, h2, att)


def grad_shapes(width):
    block, half = width // PF, width
    return [jax.ShapeDtypeStruct((2, 2, 4, block, half), BF)] * 4


def put_grad(values, outs, x_rel, col):
    width = values.shape[0]
    block, cols = width // PF, values.shape[1]
    half = width
    at = col % half
    low = values.astype(BF)
    for c in range(2):
        for y in range(2):
            piece = low[(c * 2 + y) * 4 * block : (c * 2 + y + 1) * 4 * block].reshape(4, block, cols)
            if col < half:
                outs[2 * 0 + c][x_rel, y, :, :, at : at + cols] = piece
            else:
                outs[2 * 1 + c][y, x_rel, :, :, at : at + cols] = piece


def back_first_kernel(
    length,
    where, power, row_all, col_sum, images, live, same, groups, own, own_group, factor, pooled, packed, slope,
    h2_t, dy_out, dm_out, du, keep_a, send_a, keep_b, send_b, bias_up, down_bias, wd, dact, sem,
):
    rows, hidden = slope.shape
    texts = rows // length
    width = h2_t.shape[0]
    loads = weight_copies(packed, "down", wd, sem, 0, width, hidden)
    for copy in loads:
        copy.start()
    sums = row_all[...]
    if sums.ndim == 3:
        sums = jnp.sum(sums, axis=0)
    row_sum = jnp.concatenate([sums[k : k + 1] for k in range(sums.shape[0])], axis=1)
    live_own, same_own = own[:, 0:1], own[:, 1:2]
    pair = factor[0:1, 0:1] * live_own * live[...]
    match = jnp.where(own_group[...] == groups[...], 1.0 / same_own + 1.0 / same[...], 0.0)
    grad_scores = pair * (power[...] * (1.0 / row_sum + 1.0 / col_sum[...]) - match)
    grad_low = LOGIT_SCALE * dot(grad_scores.astype(BF), images[...])
    pool = pooled[...]
    inverse = lax.rsqrt(jnp.sum(pool * pool, axis=-1, keepdims=True) + 1e-06)
    along = jnp.sum(pool * grad_low, axis=-1, keepdims=True)
    dy = inverse * (grad_low - pool * (inverse * inverse * along)) * (1.0 / length)
    dm = dy.astype(BF)
    dy_out[...] = dy
    dm_out[...] = dm
    down_bias[...] = length * jnp.sum(dm.astype(F32), axis=0, keepdims=True)
    for copy in loads:
        copy.wait()
    dact[...] = dot(dm, natural(wd), 1, 1)
    for c in range(0, hidden, 256):
        spread = jnp.broadcast_to(dact[:, c : c + 256].reshape(texts, 1, 256), (texts, length, 256))
        part = spread.reshape(rows, 256) * slope[:, c : c + 256].astype(F32)
        part = part.astype(BF)
        du[:, c : c + 256] = part
        bias_up[:, c : c + 256] = jnp.sum(part.astype(F32), axis=0, keepdims=True)
    half = hidden // PX
    for x in range(PX):
        first = (x ^ where[0]) * half
        for c in range(0, half, 256):
            part = du[:, pl.ds(pl.multiple_of(first + c, 256), 256)]
            put_grad(dot(h2_t[...], part), (keep_a, send_a, keep_b, send_b), x, c)


def back_first(
    where, power, row_all, col_sum, images, live, same, groups, own, own_group, factor, pooled, packed, slope,
    h2_t, length,
):
    rows, hidden = slope.shape
    width = h2_t.shape[0]
    texts = rows // length
    shape = jax.ShapeDtypeStruct
    return pl.pallas_call(
        functools.partial(back_first_kernel, length),
        name="back_first",
        in_specs=[SMEM] + [WHOLE] * 11 + [ANY, WHOLE, WHOLE],
        out_specs=[WHOLE] * 9,
        out_shape=[
            shape((texts, width), F32),
            shape((texts, width), BF),
            shape((rows, hidden), BF),
            *grad_shapes(width),
            shape((1, hidden), F32),
            shape((1, width), F32),
        ],
        scratch_shapes=[
            weight_scratch("down", width, hidden),
            pltpu.VMEM((texts, hidden), F32),
            pltpu.SemaphoreType.DMA((PX,)),
        ],
        compiler_params=params(),
        cost_estimate=pl.CostEstimate(
            flops=2 * rows * width * hidden, bytes_accessed=12 * width * hidden, transcendentals=0
        ),
    )(
        where, power, row_all, col_sum, images, live, same, groups, own, own_group, factor, pooled, packed, slope,
        h2_t,
    )


def back_norm_kernel(length, dy, du, r1, packed, vec, dr1, dz_s, da_s, sums, wu, wo, sem):
    rows, width = r1.shape
    hidden = du.shape[1]
    up = weight_copies(packed, "up", wu, sem, 0, width, hidden)
    out = weight_copies(packed, "out", wo, sem, len(up), width, hidden)
    for copy in up + out:
        copy.start()
    v = vec[...].astype(F32)
    blk = 128
    for copy in up:
        copy.wait()
    dr1[...] = dot(du[...], natural(wu), 1, 1)
    gain_sum = jnp.zeros((1, width), F32)
    shift_sum = jnp.zeros((1, width), F32)
    out_sum = jnp.zeros((1, width), F32)
    for r in range(0, rows, blk):
        hat, inverse = normalize(r1[r : r + blk, :])
        grad = dr1[r : r + blk, :]
        gain_sum = gain_sum + jnp.sum(grad * hat, axis=0, keepdims=True)
        shift_sum = shift_sum + jnp.sum(grad, axis=0, keepdims=True)
        some = blk // length
        spread = jnp.broadcast_to(
            dy[r // length : r // length + some, :].reshape(some, 1, width), (some, length, width)
        ).reshape(blk, width)
        grad = spread + norm_back(grad, hat, inverse, v[5:6])
        dr1[r : r + blk, :] = grad
        low = grad.astype(BF)
        dz_s[r : r + blk, :] = low
        out_sum = out_sum + jnp.sum(low.astype(F32), axis=0, keepdims=True)
    for copy in out:
        copy.wait()
    da_s[...] = dot(dz_s[...], natural(wo), 1, 1).astype(BF)
    sums[0:1, :] = out_sum
    sums[1:2, :] = gain_sum
    sums[2:3, :] = shift_sum
    sums[3:8, :] = jnp.zeros((5, width), F32)


def back_norm(dy, du, r1, packed, vec, length):
    rows, width = r1.shape
    hidden = du.shape[1]
    shape = jax.ShapeDtypeStruct
    return pl.pallas_call(
        functools.partial(back_norm_kernel, length),
        name="back_norm",
        in_specs=[WHOLE] * 3 + [ANY, WHOLE],
        out_specs=[WHOLE] * 4,
        out_shape=[
            shape((rows, width), F32),
            shape((rows, width), BF),
            shape((rows, width), BF),
            shape((8, width), F32),
        ],
        scratch_shapes=[
            weight_scratch("up", width, hidden),
            weight_scratch("out", width, hidden),
            pltpu.SemaphoreType.DMA((PX * (1 + hidden // width),)),
        ],
        compiler_params=params(),
        cost_estimate=pl.CostEstimate(
            flops=2 * rows * width * (hidden + width), bytes_accessed=6 * width * hidden, transcendentals=0
        ),
    )(dy, du, r1, packed, vec)


def back_attention_kernel(length, qkv, da_s, dqkv, sums):
    rows, width = da_s.shape
    blk = 128
    low_lane = lax.broadcasted_iota(jnp.int32, (blk, 128), 1) < HEAD_DIM
    bias = text_mask(blk, length)
    cols = range(0, width, 128)
    for r in range(0, rows, blk):
        take = lambda base, c: qkv[r : r + blk, base + c : base + c + 128]
        q2 = [take(0, c) * 0.125 for c in cols]
        k2 = [head_pair(take(width, c), low_lane) for c in cols]
        v2 = [head_pair(take(2 * width, c), low_lane) for c in cols]
        da = [da_s[r : r + blk, c : c + 128] for c in cols]
        scores = [dot(k, q, 1, 1) for k, q in zip(k2, q2)]
        grads = [dot(v, d, 1, 1) for v, d in zip(v2, da)]
        probs, deltas = [], []
        for score, grad in zip(scores, grads):
            p_low, d_low = [], []
            for half in range(2):
                s = score[half * blk : (half + 1) * blk] + bias
                g = grad[half * blk : (half + 1) * blk]
                powers = jnp.exp(s - jnp.max(s, axis=0, keepdims=True))
                soft = powers * (1.0 / jnp.sum(powers, axis=0, keepdims=True))
                p_low.append(soft.astype(BF))
                d_low.append((soft * (g - jnp.sum(g * soft, axis=0, keepdims=True))).astype(BF))
            probs.append(jnp.concatenate(p_low, axis=0))
            deltas.append(jnp.concatenate(d_low, axis=0))
        for i, c in enumerate(cols):
            dq = dot(deltas[i], k2[i], 0, 0) * 0.125
            dk = dot(deltas[i], q2[i])
            dv = dot(probs[i], da[i])
            dqkv[r : r + blk, c : c + 128] = dq.astype(BF)
            dqkv[r : r + blk, width + c : width + c + 128] = jnp.where(
                low_lane, dk[:blk], dk[blk:]
            ).astype(BF)
            dqkv[r : r + blk, 2 * width + c : 2 * width + c + 128] = jnp.where(
                low_lane, dv[:blk], dv[blk:]
            ).astype(BF)
    sums[0:1, :] = jnp.sum(dqkv[:, :width].astype(F32), axis=0, keepdims=True)
    sums[1:2, :] = jnp.sum(dqkv[:, 2 * width :].astype(F32), axis=0, keepdims=True)
    sums[2:8, :] = jnp.zeros((6, width), F32)


def back_attention(qkv, da, length):
    rows, width = da.shape
    shape = jax.ShapeDtypeStruct
    return pl.pallas_call(
        functools.partial(back_attention_kernel, length),
        name="back_attention",
        in_specs=[WHOLE] * 2,
        out_specs=[WHOLE] * 2,
        out_shape=[shape((rows, 3 * width), BF), shape((8, width), F32)],
        compiler_params=params(),
        cost_estimate=pl.CostEstimate(
            flops=2 * rows * width * 1280, bytes_accessed=20 * rows * width, transcendentals=rows * width
        ),
    )(qkv, da)


def attention_grads_kernel(where, h1_t, att_t, dqkv, dz, keep_a, send_a, keep_b, send_b):
    width = h1_t.shape[0]
    piece = width // PX
    outs = (keep_a, send_a, keep_b, send_b)
    for x in range(PX):
        other = x ^ where[0]
        first = other * (3 * piece)
        for c in range(0, width, 256):
            part = dqkv[:, pl.ds(pl.multiple_of(first + c, 128), 256)]
            put_grad(dot(h1_t[...], part), outs, x, c)
        part = dqkv[:, pl.ds(pl.multiple_of(first + width, 128), piece)]
        put_grad(dot(h1_t[...], part), outs, x, width)
        part = dz[:, pl.ds(pl.multiple_of(other * piece, 128), piece)]
        put_grad(dot(att_t[...], part), outs, x, width + piece)


def attention_grads(where, h1_t, att_t, dqkv, dz):
    width, rows = h1_t.shape
    return pl.pallas_call(
        attention_grads_kernel,
        name="attention_grads",
        in_specs=[SMEM] + [WHOLE] * 4,
        out_specs=[WHOLE] * 4,
        out_shape=grad_shapes(width),
        compiler_params=params(),
        cost_estimate=pl.CostEstimate(
            flops=8 * rows * width * width, bytes_accessed=8 * width * width + 12 * rows * width, transcendentals=0
        ),
    )(where, h1_t, att_t, dqkv, dz)


def back_third_kernel(dr1, dqkv, tok, packed, vec, sums, bias_sums, down_bias, dx, all_sums, wq, sem):
    rows, width = tok.shape
    loads = weight_copies(packed, "qkv", wq, sem, 0, width, width)
    for copy in loads:
        copy.start()
    v = vec[...].astype(F32)
    for copy in loads:
        copy.wait()
    dx[...] = dot(dqkv[...], natural(wq), 1, 1)
    gain_sum = jnp.zeros((1, width), F32)
    shift_sum = jnp.zeros((1, width), F32)
    blk = 128
    for r in range(0, rows, blk):
        hat, inverse = normalize(tok[r : r + blk, :].astype(F32))
        grad = dx[r : r + blk, :]
        gain_sum = gain_sum + jnp.sum(grad * hat, axis=0, keepdims=True)
        shift_sum = shift_sum + jnp.sum(grad, axis=0, keepdims=True)
        dx[r : r + blk, :] = dr1[r : r + blk, :] + norm_back(grad, hat, inverse, v[0:1])
    all_sums[0:1, :] = gain_sum
    all_sums[1:2, :] = shift_sum
    all_sums[2:4, :] = bias_sums[0:2, :]
    all_sums[4:7, :] = sums[0:3, :]
    all_sums[7:8, :] = down_bias[...]


def back_third(dr1, dqkv, tok, packed, vec, sums, bias_sums, down_bias):
    rows, width = tok.shape
    shape = jax.ShapeDtypeStruct
    return pl.pallas_call(
        back_third_kernel,
        name="back_third",
        in_specs=[WHOLE, WHOLE, WHOLE, ANY, WHOLE, WHOLE, WHOLE, WHOLE],
        out_specs=[WHOLE] * 2,
        out_shape=[shape((rows, width), F32), shape((8, width), F32)],
        scratch_shapes=[
            weight_scratch("qkv", width, width),
            pltpu.SemaphoreType.DMA((PX * 3,)),
        ],
        compiler_params=params(),
        cost_estimate=pl.CostEstimate(
            flops=6 * rows * width * width, bytes_accessed=14 * width * width, transcendentals=0
        ),
    )(dr1, dqkv, tok, packed, vec, sums, bias_sums, down_bias)


def fold_kernel(a_own, a_new, b_own, b_new, a_keep, a_send, b_keep, b_send):
    for own, new, keep, send in ((a_own, a_new, a_keep, a_send), (b_own, b_new, b_keep, b_send)):
        total = own[...].astype(F32) + new[...].astype(F32)
        keep[...] = total[0].astype(BF)
        send[...] = total[1].astype(BF)


def fold(a_own, a_new, b_own, b_new):
    shape = a_own.shape
    rest = 1
    for n in shape[1:-2]:
        rest *= n
    rows, cols = shape[-2:]
    view = lambda a: a.reshape(2, rest, rows, cols)
    steps = 2 if rest > 4 else 1
    pair = pl.BlockSpec((2, rest // steps, rows, cols), lambda i: (0, i, 0, 0))
    one = pl.BlockSpec((rest // steps, rows, cols), lambda i: (i, 0, 0))
    outs = pl.pallas_call(
        fold_kernel,
        name="fold",
        grid=(steps,),
        in_specs=[pair] * 4,
        out_specs=[one] * 4,
        out_shape=[jax.ShapeDtypeStruct((rest, rows, cols), BF)] * 4,
        compiler_params=params(),
        cost_estimate=pl.CostEstimate(
            flops=4 * rest * rows * cols, bytes_accessed=24 * rest * rows * cols, transcendentals=0
        ),
    )(*(view(a) for a in (a_own, a_new, b_own, b_new)))
    return [o.reshape(shape[1:]) for o in outs]


def join_kernel(a_own, a_new, b_own, b_new, stay, one, two, three):
    half = a_own.shape[-1]
    for at, own, new in ((0, a_own, a_new), (half, b_own, b_new)):
        total = own[...].astype(F32) + new[...].astype(F32)
        for k, dst in enumerate((stay, one, two, three)):
            dst[:, at : at + half] = total[k].astype(dst.dtype)


def join(a_own, a_new, b_own, b_new):
    blocks, rows, cols = a_own.shape
    shape = jax.ShapeDtypeStruct
    return pl.pallas_call(
        join_kernel,
        name="join",
        in_specs=[WHOLE] * 4,
        out_specs=[WHOLE] * 4,
        out_shape=[shape((rows, 2 * cols), F32)] + [shape((rows, 2 * cols), BF)] * 3,
        compiler_params=params(),
        cost_estimate=pl.CostEstimate(
            flops=16 * rows * cols, bytes_accessed=40 * rows * cols, transcendentals=0
        ),
    )(a_own, a_new, b_own, b_new)


def shifted(x, y, z, core):
    change = x * 16 + z * 4 + y * 2 + core
    return [(i, i ^ change) for i in range(32)]


def hop(array, x=0, y=0, z=0, core=0):
    return lax.ppermute(array, AXES, shifted(x, y, z, core))


def after(values, *others):
    return lax.optimization_barrier((tuple(values), others))[0]


def core_step(parts, *wait):
    keep_a, send_a, keep_b, send_b = parts
    new_a, new_b = hop(send_a, core=1), hop(send_b, core=1)
    keep_a, keep_b = after((keep_a, keep_b), *wait)
    return fold(keep_a, new_a, keep_b, new_b)


def first_step(parts, *wait):
    keep_a, send_a, keep_b, send_b = parts
    new_a, new_b = hop(send_a, x=1), hop(send_b, y=1)
    keep_a, keep_b = after((keep_a, keep_b), *wait)
    return fold(keep_a, new_a, keep_b, new_b)


def second_step(parts, *wait):
    keep_a, send_a, keep_b, send_b = parts
    new_a, new_b = hop(send_a, y=1), hop(send_b, x=1)
    keep_a, keep_b = after((keep_a, keep_b), *wait)
    return join(keep_a, new_a, keep_b, new_b)


def third_step(parts):
    stay, one, two, three = parts
    others = [hop(one, z=1), hop(two, z=2), hop(three, z=3)]
    return stay + sum(o.astype(F32) for o in others)


def natural_grad(keep_a, send_a, keep_b, send_b):
    first = jnp.stack([keep_a, send_a])
    second = jnp.swapaxes(jnp.stack([keep_b, send_b]), 1, 2)
    whole = jnp.concatenate([first, second], axis=-1)
    core, x, y, z, rows, cols = whole.shape
    return whole.transpose(1, 3, 2, 0, 4, 5).reshape(x, z * y * core * rows, cols)


def pack_block(qkv, out, up, down):
    piece = out.shape[1]
    parts = [qkv[:, i : i + piece] for i in range(0, qkv.shape[1], piece)] + [out]
    parts += [up[:, i : i + piece] for i in range(0, up.shape[1], piece)] + [down]
    return jnp.concatenate(parts, axis=0)


def gather_packed(qkv, out, up, down, dp, fsdp):
    if (dp, fsdp) == (PX, PF):
        return lax.all_gather(pack_block(qkv, out, up, down), AXES, axis=0)
    full = [
        lax.all_gather(lax.all_gather(w, "dp", axis=1, tiled=True), "fsdp", axis=0, tiled=True)
        for w in (qkv, out, up, down)
    ]
    blocks = []
    for x in range(PX):
        for f in range(PF):
            some = []
            for w in full:
                rows, cols = w.shape[0] // PF, w.shape[1] // PX
                some.append(w[f * rows : (f + 1) * rows, x * cols : (x + 1) * cols])
            blocks.append(pack_block(*some))
    return jnp.stack(blocks)


def scatter_columns(grad, dp, fsdp):
    parts, rows, cols = grad.shape
    if dp != parts:
        grad = jnp.swapaxes(grad, 0, 1).reshape(rows, dp, parts * cols // dp)
        grad = jnp.swapaxes(grad, 0, 1)
    return lax.psum_scatter(
        grad.reshape(dp * rows, -1), AXES, scatter_dimension=0, tiled=True
    ).astype(F32)


def body(
    image_tokens,
    text_tokens,
    image_qkv,
    image_out,
    image_up,
    image_down,
    image_vectors,
    image_up_bias,
    text_qkv,
    text_out,
    text_up,
    text_down,
    text_vectors,
    text_up_bias,
    pair_counts,
    pair_groups,
):
    dp, fsdp = lax.axis_size("dp"), lax.axis_size("fsdp")
    devices = dp * fsdp
    cap, length, width = text_tokens.shape
    hidden = image_up.shape[1]
    pairs = pair_groups.shape[0]
    me = lax.axis_index("dp") * fsdp + lax.axis_index("fsdp")

    grid_mesh = (dp, fsdp) == (PX, PF)
    packed = gather_packed(text_qkv, text_out, text_up, text_down, dp, fsdp)
    part = width // fsdp
    small = jnp.concatenate([text_vectors, text_up_bias.reshape(8, -1)], axis=1)
    if grid_mesh:
        small = jnp.broadcast_to(small[None], (fsdp,) + small.shape)
        small = lax.all_to_all(small, "fsdp", 0, 0, tiled=True)
    else:
        small = lax.all_gather(small, "fsdp", axis=0)
    vec = jnp.swapaxes(small[:, :, :part], 0, 1).reshape(8, width)
    ub = small[:, :, part:].reshape(1, hidden)
    bits = [lax.shift_right_logical(me, k) & 1 for k in range(5)]
    where = jnp.stack([bits[4], bits[1], 2 * bits[3] + bits[2], bits[0]])
    where = where if grid_mesh else jnp.zeros_like(where)

    image_low = image_forward(
        image_tokens, image_qkv, image_out, image_up, image_down, image_vectors, image_up_bias
    )
    if grid_mesh:
        images = image_low
        for change in (dict(z=1), dict(z=2), dict(x=1), dict(y=1), dict(core=1)):
            images = jnp.concatenate([images, hop(images, **change)], axis=0)
        far = jnp.arange(devices, dtype=jnp.int32) ^ me
        bit = lambda k: lax.shift_right_logical(far, k) & 1
        order = bit(2) + 2 * bit(3) + 4 * bit(4) + 8 * bit(1) + 16 * bit(0)
        images = jnp.take(images.reshape(devices, cap, width), order, axis=0).reshape(pairs, width)
    else:
        images = lax.all_gather(image_low, AXES, axis=0, tiled=True)

    slots = jnp.arange(cap, dtype=jnp.int32)
    live = (slots[None, :] < pair_counts[:, None]).reshape(pairs).astype(F32)
    same = jnp.maximum(
        jnp.sum(jnp.where(pair_groups[:, None] == pair_groups[None, :], live[None, :], 0.0), axis=1), 1.0
    )
    own_of = lambda array: lax.dynamic_slice_in_dim(array, me * cap, cap)
    own = jnp.stack([own_of(live), own_of(same)], axis=1)
    own_group = own_of(pair_groups).reshape(cap, 1)
    live_row, same_row, group_row = (a.reshape(1, pairs) for a in (live, same, pair_groups))
    live_total = jnp.sum(pair_counts).astype(F32)
    factor = jnp.broadcast_to(LOSS_WEIGHT / (2.0 * live_total), (1, 128))

    tokens = text_tokens.reshape(cap * length, width)
    h1, qkv, att, r1, h2, slope, acts, pooled, low = text_forward(tokens, packed, vec, ub, length, hidden)
    power, row_part, col_sum, loss_part = contrast(
        low, images, live_row, same_row, group_row, own, own_group
    )
    if devices <= 32:
        row_all = lax.all_to_all(
            jnp.broadcast_to(row_part[None], (devices,) + row_part.shape), AXES, 0, 0, tiled=True
        )
        row_sum = jnp.sum(row_all, axis=0)
    else:
        row_all = lax.psum(row_part, AXES)
        row_sum = row_all
    h1_t, h2_t, att_t = relative_rows(where, h1, h2, att)
    dy, dm, du, *up_parts, bias_up, down_bias = back_first(
        where, power, row_all, col_sum, images, live_row, same_row, group_row, own, own_group, factor, pooled,
        packed, slope, h2_t, length,
    )
    dr1, dz, da, sums = back_norm(dy, du, r1, packed, vec, length)
    if grid_mesh:
        up_parts = core_step(up_parts, da)
        (da,) = after((da,), *up_parts)
    dqkv, bias_sums = back_attention(qkv, da, length)
    att_parts = attention_grads(where, h1_t, att_t, dqkv, dz)
    if grid_mesh:
        up_parts = first_step(up_parts, *att_parts)
        dqkv, *att_parts = after((dqkv, *att_parts), *up_parts)
    dx, vec_grads = back_third(dr1, dqkv, tokens, packed, vec, sums, bias_sums, down_bias)
    rows_of = hidden // fsdp
    cols_of = width // dp
    left = jnp.swapaxes(acts.reshape(cap, fsdp, rows_of), 0, 1)
    left = jnp.broadcast_to(left[None], (dp, fsdp, cap, rows_of)).reshape(devices, cap, rows_of)
    right = jnp.swapaxes(dm.reshape(cap, dp, cols_of), 0, 1)
    right = jnp.broadcast_to(right[:, None], (dp, fsdp, cap, cols_of)).reshape(devices, cap, cols_of)
    both = lax.all_to_all(jnp.concatenate([left, right], axis=2), AXES, 0, 0, tiled=True)
    both = both.reshape(pairs, rows_of + cols_of)
    grad_down = dot(both[:, :rows_of], both[:, rows_of:], 0, 0)

    if grid_mesh:
        att_parts = core_step(att_parts, dx)
        up_parts = second_step(up_parts, *att_parts)
        att_parts = first_step(att_parts, grad_down, *up_parts)
        (vec_grads,) = after((vec_grads,), *att_parts)
        grad_up = third_step(up_parts)
        grad_attn = third_step(second_step(att_parts))
        grad_qkv, grad_out = grad_attn[:, : 3 * width // dp], grad_attn[:, 3 * width // dp :]
    else:
        grad_attn = natural_grad(*att_parts)
        grad_up = scatter_columns(natural_grad(*up_parts), dp, fsdp)
        grad_qkv = scatter_columns(grad_attn[:, :, : 3 * width // PX], dp, fsdp)
        grad_out = scatter_columns(grad_attn[:, :, 3 * width // PX :], dp, fsdp)

    share = jnp.concatenate(
        [
            jnp.swapaxes(vec_grads.reshape(8, fsdp, part), 0, 1).reshape(fsdp, 8 * part),
            bias_up.reshape(fsdp, rows_of),
            jnp.broadcast_to(loss_part[0, 0].reshape(1, 1), (fsdp, 1)),
        ],
        axis=1,
    )
    used = share.shape[1]
    padded = -(-used // 128) * 128
    share = jnp.pad(share, ((0, 0), (0, padded - used))).reshape(fsdp, padded // 128, 128)
    share = jnp.broadcast_to(share[None], (dp,) + share.shape).reshape(devices, padded // 128, 128)
    share = jnp.sum(lax.all_to_all(share, AXES, 0, 0, tiled=True), axis=0).reshape(padded)
    grad_vec = share[: 8 * part].reshape(8, part)
    grad_bias = share[8 * part : 8 * part + rows_of]
    loss = (share[used - 1] + jnp.sum(live * jnp.log(row_sum.reshape(pairs)))) / (2.0 * live_total)

    return (
        loss,
        dx.reshape(text_tokens.shape),
        grad_qkv,
        grad_out,
        grad_up,
        grad_down,
        grad_vec,
        grad_bias,
    )


def solution(mesh):
    return jax.shard_map(
        body,
        mesh=mesh,
        in_specs=(
            P(AXES, None, None),
            P(AXES, None, None),
            P(),
            P(),
            P(),
            P(),
            P(),
            P(),
            P("fsdp", "dp"),
            P("fsdp", "dp"),
            P("fsdp", "dp"),
            P("fsdp", "dp"),
            P(None, "fsdp"),
            P("fsdp"),
            P(),
            P(),
        ),
        out_specs=(
            P(),
            P(AXES, None, None),
            P("fsdp", "dp"),
            P("fsdp", "dp"),
            P("fsdp", "dp"),
            P("fsdp", "dp"),
            P(None, "fsdp"),
            P("fsdp"),
        ),
        check_vma=False,
    )
```

```python
import functools

import jax
import jax.numpy as jnp
from jax import lax
from jax.experimental import pallas as pl
from jax.experimental.pallas import tpu as pltpu
from jax.sharding import PartitionSpec as P

HEAD_DIM = 64
LOGIT_SCALE = 50.0
LOSS_WEIGHT = 32768.0
BF = jnp.bfloat16
F32 = jnp.float32
AXES = ("dp", "fsdp")
PX, PF = 2, 16
VMEM_LIMIT = 62 * 1024 * 1024

ANY = pl.BlockSpec(memory_space=pl.ANY)
WHOLE = pl.BlockSpec(memory_space=pltpu.VMEM)


def params(**more):
    return pltpu.CompilerParams(vmem_limit_bytes=VMEM_LIMIT, **more)


def dot(a, b, ca=1, cb=0):
    return lax.dot_general(a, b, (((ca,), (cb,)), ((), ())), preferred_element_type=F32)


def repeat(count, step, together=1):
    def turn(j, _):
        for k in range(together):
            step(j * together + k)
        return 0

    if together >= count:
        for i in range(count):
            step(i)
    else:
        lax.fori_loop(0, count // together, turn, 0)


def normalize(values):
    centered = values - jnp.mean(values, axis=-1, keepdims=True)
    inverse = lax.rsqrt(jnp.mean(centered * centered, axis=-1, keepdims=True) + 1e-05)
    return centered * inverse, inverse


def norm_back(grad, hat, inverse, gain):
    scaled = grad * gain
    return inverse * (
        scaled
        - jnp.mean(scaled, axis=-1, keepdims=True)
        - hat * jnp.mean(scaled * hat, axis=-1, keepdims=True)
    )


def gauss_tail(u):
    size = jnp.abs(u)
    t = 1.0 / (1.0 + (0.3275911 * 0.7071067811865476) * size)
    bell = jnp.exp(-0.5 * (u * u))
    poly = 0.5 * 1.061405429 * t - 0.5 * 1.453152027
    poly = poly * t + 0.5 * 1.421413741
    poly = poly * t - 0.5 * 0.284496736
    poly = poly * t + 0.5 * 0.254829592
    return poly * t * bell, bell, size


def head_pair(block, low_lane):
    zero = jnp.zeros_like(block)
    return jnp.concatenate(
        [jnp.where(low_lane, block, zero), jnp.where(low_lane, zero, block)], axis=0
    )


def softmax_half(scores, bias):
    scores = scores + bias
    top = jnp.max(scores, axis=-1, keepdims=True)
    powers = jnp.exp(scores - top)
    return powers * (1.0 / jnp.sum(powers, axis=-1, keepdims=True))


def unit_rows(pooled):
    return pooled * lax.rsqrt(jnp.sum(pooled * pooled, axis=-1, keepdims=True) + 1e-06)


def mean_down(total, count, down):
    mean = total * (1.0 / count)
    high = mean.astype(BF)
    low = (mean - high.astype(F32)).astype(BF)
    both = dot(jnp.concatenate([high, low], axis=0), down)
    return both[: mean.shape[0]] + both[mean.shape[0] :]


def image_kernel(
    tok, wq_h, wo_h, wu_h, wd_h, vec, ub, out, wq, wo, wu, wd, x, h, qkv, att, act_sum, r1_sum, bias_row, stage, sem
):
    step, steps = pl.program_id(0), pl.num_programs(0)
    length, group, width = tok.shape
    rows = group * length
    hidden = wu.shape[1]
    copies = [
        pltpu.make_async_copy(src, dst, sem.at[i])
        for i, (src, dst) in enumerate(((wq_h, wq), (wo_h, wo), (wu_h, wu), (wd_h, wd)))
    ]

    @pl.when(step == 0)
    def _():
        for copy in copies:
            copy.start()

    def arrived(i):
        @pl.when(step == 0)
        def _():
            copies[i].wait()

    v = vec[...].astype(F32)
    bias_row[:, :width] = v[2:3]
    bias_row[:, width : 2 * width] = jnp.zeros((1, width), F32)
    bias_row[:, 2 * width :] = v[3:4]
    for k in range(width // 128):
        stage[k] = tok[:, :, k * 128 : (k + 1) * 128].astype(F32).reshape(rows, 128)
        for i in range(group):
            x[pl.ds(i * length, length), k * 128 : (k + 1) * 128] = stage[k, pl.ds(i, length, stride=group), :]

    def norm_rows(gain, shift):
        blk = 80

        def one(i):
            at = pl.ds(pl.multiple_of(i * blk, blk), blk)
            hat, _ = normalize(x[at, :])
            h[at, :] = (hat * gain + shift).astype(BF)

        repeat(rows // blk, one, 5)

    norm_rows(v[0:1], v[1:2])
    arrived(0)

    def project(i):
        at = pl.ds(pl.multiple_of(i * 256, 256), 256)
        qkv[:, at] = (dot(h[...], wq[:, at]) + bias_row[:, at]).astype(BF)

    repeat(3 * width // 256, project, 3)

    wins = rows // (2 * length)
    q_len = 112
    low_lane = lax.broadcasted_iota(jnp.int32, (128, 128), 1) < HEAD_DIM
    cols = range(0, width, 128)

    def window(w):
        q_at = pl.multiple_of((2 * length * w) // 16 * 16, 16)
        k_at = pl.multiple_of(jnp.minimum(q_at, rows - 128), 16)
        lo, mid, hi = 2 * w * length, (2 * w + 1) * length, (2 * w + 2) * length
        qi = q_at + lax.broadcasted_iota(jnp.int32, (q_len, 128), 0)
        ki = k_at + lax.broadcasted_iota(jnp.int32, (q_len, 128), 1)
        first = (qi >= lo) & (qi < mid) & (ki >= lo) & (ki < mid)
        second = (qi >= mid) & (qi < hi) & (ki >= mid) & (ki < hi)
        bias = jnp.where(first | second, 0.0, -1e30)
        q_rows, k_rows = pl.ds(q_at, q_len), pl.ds(k_at, 128)
        q2 = [qkv[q_rows, c : c + 128] * 0.125 for c in cols]
        k2 = [head_pair(qkv[k_rows, width + c : width + c + 128], low_lane) for c in cols]
        v2 = [head_pair(qkv[k_rows, 2 * width + c : 2 * width + c + 128], low_lane) for c in cols]
        scores = [dot(q, k, 1, 1) for q, k in zip(q2, k2)]
        probs = [
            jnp.concatenate(
                [softmax_half(s[:, :128], bias).astype(BF), softmax_half(s[:, 128:], bias).astype(BF)],
                axis=1,
            )
            for s in scores
        ]
        mine = (q_at + lax.broadcasted_iota(jnp.int32, (16, 128), 0)) >= lo
        for c, p, values in zip(cols, probs, v2):
            mixed = dot(p, values)
            old = att[pl.ds(q_at, 16), c : c + 128].astype(F32)
            att[pl.ds(q_at, 16), c : c + 128] = jnp.where(mine, mixed[:16], old).astype(BF)
            att[pl.ds(q_at + 16, q_len - 16), c : c + 128] = mixed[16:].astype(BF)

    repeat(wins, window, 2)

    arrived(1)
    for c in range(0, width, 256):
        x[:, c : c + 256] = x[:, c : c + 256] + (dot(att[...], wo[:, c : c + 256]) + v[4:5, c : c + 256])
    norm_rows(v[5:6], v[6:7])

    def image_sums(values):
        sums = []
        for i in range(group):
            lo, hi = i * length, (i + 1) * length
            a, b = lo // 8 * 8, -(-hi // 8) * 8
            part = values[a:b]
            row = a + lax.broadcasted_iota(jnp.int32, (b - a, 1), 0)
            if lo % 8 or hi % 8:
                part = jnp.where((row >= lo) & (row < hi), part, 0.0)
            sums.append(jnp.sum(part, axis=0, keepdims=True))
        return jnp.concatenate(sums, axis=0)

    place = pl.ds(pl.multiple_of(step * group, group), group)
    for c in range(0, width, 256):
        r1_sum[place, c : c + 256] = image_sums(x[:, c : c + 256])
    arrived(2)

    def expand(i):
        at = pl.ds(pl.multiple_of(i * 256, 256), 256)
        u = dot(h[...], wu[:, at]) + ub[:, at].astype(F32)
        tail, _, size = gauss_tail(u)
        act_sum[place, at] = image_sums(jnp.maximum(u, 0.0) - size * tail)

    repeat(hidden // 256, expand, 3)
    arrived(3)

    @pl.when(step == steps - 1)
    def _():
        pooled = r1_sum[...] * (1.0 / length) + mean_down(act_sum[...], length, wd[...]) + v[7:8]
        out[...] = unit_rows(pooled).astype(BF)


def image_forward(tokens, wq, wo, wu, wd, vec, ub):
    pairs, length, width = tokens.shape
    hidden = wu.shape[1]
    group = 16
    rows = group * length
    return pl.pallas_call(
        image_kernel,
        name="image_forward",
        grid=(pairs // group,),
        in_specs=[
            pl.BlockSpec((length, group, width), lambda i: (0, i, 0)),
            ANY,
            ANY,
            ANY,
            ANY,
            pl.BlockSpec((8, width), lambda i: (0, 0)),
            pl.BlockSpec((1, hidden), lambda i: (0, 0)),
        ],
        out_specs=pl.BlockSpec((pairs, width), lambda i: (0, 0)),
        out_shape=jax.ShapeDtypeStruct((pairs, width), BF),
        scratch_shapes=[
            pltpu.VMEM((width, 3 * width), BF),
            pltpu.VMEM((width, width), BF),
            pltpu.VMEM((width, hidden), BF),
            pltpu.VMEM((hidden, width), BF),
            pltpu.VMEM((rows, width), F32),
            pltpu.VMEM((rows, width), BF),
            pltpu.VMEM((rows, 3 * width), BF),
            pltpu.VMEM((rows, width), BF),
            pltpu.VMEM((pairs, hidden), F32),
            pltpu.VMEM((pairs, width), F32),
            pltpu.VMEM((1, 3 * width), F32),
            pltpu.VMEM((width // 128, rows, 128), F32),
            pltpu.SemaphoreType.DMA((4,)),
        ],
        compiler_params=params(),
        cost_estimate=pl.CostEstimate(
            flops=2 * pairs * length * width * (4 * width + hidden),
            bytes_accessed=2 * (4 * width * width + 2 * width * hidden + pairs * length * width),
            transcendentals=pairs * length * hidden,
        ),
    )(jnp.swapaxes(tokens, 0, 1), wq, wo, wu, wd, vec, ub.reshape(1, hidden))


def pack_rows(width, hidden):
    piece, rows = width // PX, width // PF
    return piece, rows, hidden // PF


def weight_copies(packed, which, dst, sem, base, width, hidden):
    piece, rows, frows = pack_rows(width, hidden)
    q_pieces, u_pieces = 3, hidden // width
    spans = {
        "qkv": (0, q_pieces, rows),
        "out": (q_pieces * rows, 1, rows),
        "up": ((q_pieces + 1) * rows, u_pieces, rows),
        "down": ((q_pieces + 1 + u_pieces) * rows, 1, frows),
    }
    start, count, tall = spans[which]
    copies = []
    for x in range(PX):
        for p in range(count):
            copies.append(
                pltpu.make_async_copy(
                    packed.at[pl.ds(x * PF, PF), pl.ds(start + p * tall, tall), :],
                    dst.at[:, :, pl.ds((x * count + p) * piece, piece)],
                    sem.at[base + len(copies)],
                )
            )
    return copies


def natural(ref):
    blocks, rows, cols = ref.shape
    return ref[...].reshape(blocks * rows, cols)


def weight_scratch(which, width, hidden):
    rows, frows = width // PF, hidden // PF
    shape = {
        "qkv": (PF, rows, 3 * width),
        "out": (PF, rows, width),
        "up": (PF, rows, hidden),
        "down": (PF, frows, width),
    }[which]
    return pltpu.VMEM(shape, BF)


def text_mask(size, length):
    row = lax.broadcasted_iota(jnp.int32, (size, size), 0) // length
    col = lax.broadcasted_iota(jnp.int32, (size, size), 1) // length
    return jnp.where(row == col, 0.0, -1e30)


def text_forward_kernel(
    length, tok, packed, vec, ub, h1, qkv, att, r1, h2, slope, acts, pooled_out, low, wq, wo, wu, wd, total,
    bias_row, sem
):
    rows, width = tok.shape
    hidden = slope.shape[1]
    texts = rows // length
    load = {}
    base = 0
    for which, dst in (("qkv", wq), ("out", wo), ("up", wu), ("down", wd)):
        load[which] = weight_copies(packed, which, dst, sem, base, width, hidden)
        base += len(load[which])
        for copy in load[which]:
            copy.start()
    v = vec[...].astype(F32)
    bias_row[:, :width] = v[2:3]
    bias_row[:, width : 2 * width] = jnp.zeros((1, width), F32)
    bias_row[:, 2 * width :] = v[3:4]
    blk = 128

    def norm_rows(src, dst, gain, shift):
        def one(i):
            at = pl.ds(pl.multiple_of(i * blk, blk), blk)
            hat, _ = normalize(src[at, :].astype(F32))
            dst[at, :] = (hat * gain + shift).astype(BF)

        repeat(rows // blk, one, 2)

    norm_rows(tok, h1, v[0:1], v[1:2])
    for copy in load["qkv"]:
        copy.wait()

    def project(i):
        at = pl.ds(pl.multiple_of(i * 256, 256), 256)
        qkv[:, at] = (dot(h1[...], wq[:, :, at].reshape(width, 256)) + bias_row[:, at]).astype(BF)

    repeat(3 * width // 256, project, 3)
    low_lane = lax.broadcasted_iota(jnp.int32, (blk, 128), 1) < HEAD_DIM
    bias = text_mask(blk, length)
    cols = range(0, width, 128)

    def attend(i):
        at = pl.ds(pl.multiple_of(i * blk, blk), blk)
        q2 = [qkv[at, c : c + 128] * 0.125 for c in cols]
        k2 = [head_pair(qkv[at, width + c : width + c + 128], low_lane) for c in cols]
        v2 = [head_pair(qkv[at, 2 * width + c : 2 * width + c + 128], low_lane) for c in cols]
        scores = [dot(q, k, 1, 1) for q, k in zip(q2, k2)]
        probs = [
            jnp.concatenate(
                [softmax_half(s[:, :blk], bias).astype(BF), softmax_half(s[:, blk:], bias).astype(BF)],
                axis=1,
            )
            for s in scores
        ]
        for c, p, values in zip(cols, probs, v2):
            att[at, c : c + 128] = dot(p, values).astype(BF)

    repeat(rows // blk, attend, 2)
    for copy in load["out"]:
        copy.wait()
    for c in range(0, width, 256):
        r1[:, c : c + 256] = tok[:, c : c + 256].astype(F32) + (
            dot(att[...], wo[:, :, c : c + 256].reshape(width, 256)) + v[4:5, c : c + 256]
        )
    norm_rows(r1, h2, v[5:6], v[6:7])
    for copy in load["up"]:
        copy.wait()

    def expand(i):
        at = pl.ds(pl.multiple_of(i * 256, 256), 256)
        u = dot(h2[...], wu[:, :, at].reshape(width, 256)) + ub[:, at].astype(F32)
        tail, bell, size = gauss_tail(u)
        act = jnp.maximum(u, 0.0) - size * tail
        phi = jnp.where(u >= 0.0, 1.0 - tail, tail)
        slope[:, at] = (phi + u * (bell * 0.3989422804014327)).astype(BF)
        sums = jnp.sum(act.reshape(texts, length, 256), axis=1)
        total[:, at] = sums
        acts[:, at] = sums.astype(BF)

    repeat(hidden // 256, expand, 3)
    for copy in load["down"]:
        copy.wait()
    mean_r1 = jnp.sum(r1[...].reshape(texts, length, width), axis=1) * (1.0 / length)
    pooled = mean_r1 + mean_down(total[...], length, natural(wd)) + v[7:8]
    pooled_out[...] = pooled
    low[...] = unit_rows(pooled).astype(BF)


def text_forward(tokens, packed, vec, ub, length, hidden):
    rows, width = tokens.shape
    texts = rows // length
    shape = jax.ShapeDtypeStruct
    copies = PX * (3 + 1 + hidden // width + 1)
    return pl.pallas_call(
        functools.partial(text_forward_kernel, length),
        name="text_forward",
        in_specs=[WHOLE, ANY, WHOLE, WHOLE],
        out_specs=[WHOLE] * 9,
        out_shape=[
            shape((rows, width), BF),
            shape((rows, 3 * width), BF),
            shape((rows, width), BF),
            shape((rows, width), F32),
            shape((rows, width), BF),
            shape((rows, hidden), BF),
            shape((texts, hidden), BF),
            shape((texts, width), F32),
            shape((texts, width), BF),
        ],
        scratch_shapes=[weight_scratch(w, width, hidden) for w in ("qkv", "out", "up", "down")]
        + [
            pltpu.VMEM((texts, hidden), F32),
            pltpu.VMEM((1, 3 * width), F32),
            pltpu.SemaphoreType.DMA((copies,)),
        ],
        compiler_params=params(),
        cost_estimate=pl.CostEstimate(
            flops=2 * rows * width * (4 * width + hidden),
            bytes_accessed=2 * (4 * width * width + 2 * width * hidden + 12 * rows * width),
            transcendentals=rows * hidden,
        ),
    )(tokens, packed, vec, ub)


def contrast_kernel(low, images, live, same, groups, own, own_group, power, row_part, col_sum, loss_part):
    scores = LOGIT_SCALE * dot(low[...], images[...], 1, 1)
    exps = jnp.exp(scores)
    live_own, same_own = own[:, 0:1], own[:, 1:2]
    power[...] = exps
    rows = jnp.sum(exps * live_own, axis=0, keepdims=True)
    for k in range(row_part.shape[0]):
        row_part[k : k + 1, :] = rows[:, k * 128 : (k + 1) * 128]
    cols = jnp.sum(exps * live[...], axis=1, keepdims=True)
    col_sum[...] = cols
    pair = jnp.where(own_group[...] == groups[...], live_own * live[...], 0.0)
    linear = pair * scores * (1.0 / same_own + 1.0 / same[...])
    losses = live_own * jnp.log(cols) - jnp.sum(linear, axis=1, keepdims=True)
    loss_part[...] = jnp.broadcast_to(jnp.sum(losses, axis=0, keepdims=True), loss_part.shape)


def contrast(low, images, live, same, groups, own, own_group):
    texts = low.shape[0]
    pairs = images.shape[0]
    shape = jax.ShapeDtypeStruct
    return pl.pallas_call(
        contrast_kernel,
        name="contrast",
        in_specs=[WHOLE] * 7,
        out_specs=[WHOLE] * 4,
        out_shape=[
            shape((texts, pairs), F32),
            shape((pairs // 128, 128), F32),
            shape((texts, 1), F32),
            shape((8, 128), F32),
        ],
        compiler_params=params(),
    )(low, images, live, same, groups, own, own_group)


def relative_kernel(where, h1, h2, att, h1_t, h2_t, att_t):
    width = h1.shape[1]
    block = width // PF
    my, mz, mc = where[1], where[2], where[3]
    for src, dst in ((h2, h2_t), (h1, h1_t), (att, att_t)):
        turned = src[...].T
        for z in range(4):
            for y in range(2):
                for c in range(2):
                    f = (z * 2 + y) * 2 + c
                    place = (((c ^ mc) * 2 + (y ^ my)) * 4 + (z ^ mz)) * block
                    dst[pl.ds(pl.multiple_of(place, block), block), :] = turned[
                        f * block : (f + 1) * block
                    ]


SMEM = pl.BlockSpec(memory_space=pltpu.SMEM)


def relative_rows(where, h1, h2, att):
    rows, width = h1.shape
    return pl.pallas_call(
        relative_kernel,
        name="relative_rows",
        in_specs=[SMEM, WHOLE, WHOLE, WHOLE],
        out_specs=[WHOLE] * 3,
        out_shape=[jax.ShapeDtypeStruct((width, rows), BF)] * 3,
        compiler_params=params(),
        cost_estimate=pl.CostEstimate(flops=0, bytes_accessed=12 * rows * width, transcendentals=0),
    )(where, h1, h2, att)


def grad_shapes(width):
    block, half = width // PF, width
    return [jax.ShapeDtypeStruct((2, 2, 4, block, half), BF)] * 4


def put_grad(values, outs, x_rel, at, second):
    width, cols = values.shape
    block = width // PF
    low = values.astype(BF)
    for c in range(2):
        for y in range(2):
            piece = low[(c * 2 + y) * 4 * block : (c * 2 + y + 1) * 4 * block].reshape(4, block, cols)
            if second:
                outs[2 + c][y, x_rel, :, :, pl.ds(at, cols)] = piece
            else:
                outs[c][x_rel, y, :, :, pl.ds(at, cols)] = piece


def back_first_kernel(
    length,
    where, power, row_all, col_sum, images, live, same, groups, own, own_group, factor, pooled, packed, slope,
    h2_t, dy_out, dm_out, du, keep_a, send_a, keep_b, send_b, bias_up, down_bias, wd, dact, sem,
):
    rows, hidden = slope.shape
    texts = rows // length
    width = h2_t.shape[0]
    loads = weight_copies(packed, "down", wd, sem, 0, width, hidden)
    for copy in loads:
        copy.start()
    sums = row_all[...]
    if sums.ndim == 3:
        sums = jnp.sum(sums, axis=0)
    row_sum = jnp.concatenate([sums[k : k + 1] for k in range(sums.shape[0])], axis=1)
    live_own, same_own = own[:, 0:1], own[:, 1:2]
    pair = factor[0:1, 0:1] * live_own * live[...]
    match = jnp.where(own_group[...] == groups[...], 1.0 / same_own + 1.0 / same[...], 0.0)
    grad_scores = pair * (power[...] * (1.0 / row_sum + 1.0 / col_sum[...]) - match)
    grad_low = LOGIT_SCALE * dot(grad_scores.astype(BF), images[...])
    pool = pooled[...]
    inverse = lax.rsqrt(jnp.sum(pool * pool, axis=-1, keepdims=True) + 1e-06)
    along = jnp.sum(pool * grad_low, axis=-1, keepdims=True)
    dy = inverse * (grad_low - pool * (inverse * inverse * along)) * (1.0 / length)
    dm = dy.astype(BF)
    dy_out[...] = dy
    dm_out[...] = dm
    down_bias[...] = length * jnp.sum(dm.astype(F32), axis=0, keepdims=True)
    for copy in loads:
        copy.wait()
    dact[...] = dot(dm, natural(wd), 1, 1)

    def slopes(i):
        at = pl.ds(pl.multiple_of(i * 256, 256), 256)
        spread = jnp.broadcast_to(dact[:, at].reshape(texts, 1, 256), (texts, length, 256))
        part = (spread.reshape(rows, 256) * slope[:, at].astype(F32)).astype(BF)
        du[:, at] = part
        bias_up[:, at] = jnp.sum(part.astype(F32), axis=0, keepdims=True)

    repeat(hidden // 256, slopes, 3)
    half = hidden // PX

    def grads(i):
        x, c = i // (width // 256), pl.multiple_of(i % (width // 256) * 256, 256)
        first = (x ^ where[0]) * half + c
        for second in range(2):
            part = du[:, pl.ds(pl.multiple_of(first + second * width, 256), 256)]
            put_grad(dot(h2_t[...], part), (keep_a, send_a, keep_b, send_b), x, c, second)

    repeat(PX * width // 256, grads, 2)


def back_first(
    where, power, row_all, col_sum, images, live, same, groups, own, own_group, factor, pooled, packed, slope,
    h2_t, length,
):
    rows, hidden = slope.shape
    width = h2_t.shape[0]
    texts = rows // length
    shape = jax.ShapeDtypeStruct
    return pl.pallas_call(
        functools.partial(back_first_kernel, length),
        name="back_first",
        in_specs=[SMEM] + [WHOLE] * 11 + [ANY, WHOLE, WHOLE],
        out_specs=[WHOLE] * 9,
        out_shape=[
            shape((texts, width), F32),
            shape((texts, width), BF),
            shape((rows, hidden), BF),
            *grad_shapes(width),
            shape((1, hidden), F32),
            shape((1, width), F32),
        ],
        scratch_shapes=[
            weight_scratch("down", width, hidden),
            pltpu.VMEM((texts, hidden), F32),
            pltpu.SemaphoreType.DMA((PX,)),
        ],
        compiler_params=params(),
        cost_estimate=pl.CostEstimate(
            flops=2 * rows * width * hidden, bytes_accessed=12 * width * hidden, transcendentals=0
        ),
    )(
        where, power, row_all, col_sum, images, live, same, groups, own, own_group, factor, pooled, packed, slope,
        h2_t,
    )


def back_norm_kernel(length, dy, du, r1, packed, vec, dr1, dz_s, da_s, sums, wu, wo, sem):
    rows, width = r1.shape
    hidden = du.shape[1]
    up = weight_copies(packed, "up", wu, sem, 0, width, hidden)
    out = weight_copies(packed, "out", wo, sem, len(up), width, hidden)
    for copy in up + out:
        copy.start()
    v = vec[...].astype(F32)
    blk = 128
    for copy in up:
        copy.wait()
    half = rows // 2

    def product(i):
        at = pl.ds(pl.multiple_of(i * half, half), half)
        dr1[at, :] = dot(du[at, :], natural(wu), 1, 1)

    repeat(2, product)
    sums[...] = jnp.zeros((8, width), F32)
    some = blk // length

    def back(i):
        at = pl.ds(pl.multiple_of(i * blk, blk), blk)
        hat, inverse = normalize(r1[at, :])
        grad = dr1[at, :]
        sums[1:2, :] += jnp.sum(grad * hat, axis=0, keepdims=True)
        sums[2:3, :] += jnp.sum(grad, axis=0, keepdims=True)
        spread = jnp.broadcast_to(
            dy[pl.ds(pl.multiple_of(i * some, some), some), :].reshape(some, 1, width), (some, length, width)
        ).reshape(blk, width)
        grad = spread + norm_back(grad, hat, inverse, v[5:6])
        dr1[at, :] = grad
        low = grad.astype(BF)
        dz_s[at, :] = low
        sums[0:1, :] += jnp.sum(low.astype(F32), axis=0, keepdims=True)

    repeat(rows // blk, back, 2)
    for copy in out:
        copy.wait()
    da_s[...] = dot(dz_s[...], natural(wo), 1, 1).astype(BF)


def back_norm(dy, du, r1, packed, vec, length):
    rows, width = r1.shape
    hidden = du.shape[1]
    shape = jax.ShapeDtypeStruct
    return pl.pallas_call(
        functools.partial(back_norm_kernel, length),
        name="back_norm",
        in_specs=[WHOLE] * 3 + [ANY, WHOLE],
        out_specs=[WHOLE] * 4,
        out_shape=[
            shape((rows, width), F32),
            shape((rows, width), BF),
            shape((rows, width), BF),
            shape((8, width), F32),
        ],
        scratch_shapes=[
            weight_scratch("up", width, hidden),
            weight_scratch("out", width, hidden),
            pltpu.SemaphoreType.DMA((PX * (1 + hidden // width),)),
        ],
        compiler_params=params(),
        cost_estimate=pl.CostEstimate(
            flops=2 * rows * width * (hidden + width), bytes_accessed=6 * width * hidden, transcendentals=0
        ),
    )(dy, du, r1, packed, vec)


def back_attention_kernel(length, qkv, da_s, dqkv, sums):
    rows, width = da_s.shape
    blk = 128
    low_lane = lax.broadcasted_iota(jnp.int32, (blk, 128), 1) < HEAD_DIM
    bias = text_mask(blk, length)
    cols = range(0, width, 128)
    def group(i):
        at = pl.ds(pl.multiple_of(i * blk, blk), blk)
        take = lambda base, c: qkv[at, base + c : base + c + 128]
        q2 = [take(0, c) * 0.125 for c in cols]
        k2 = [head_pair(take(width, c), low_lane) for c in cols]
        v2 = [head_pair(take(2 * width, c), low_lane) for c in cols]
        da = [da_s[at, c : c + 128] for c in cols]
        scores = [dot(k, q, 1, 1) for k, q in zip(k2, q2)]
        grads = [dot(v, d, 1, 1) for v, d in zip(v2, da)]
        probs, deltas = [], []
        for score, grad in zip(scores, grads):
            p_low, d_low = [], []
            for half in range(2):
                s = score[half * blk : (half + 1) * blk] + bias
                g = grad[half * blk : (half + 1) * blk]
                powers = jnp.exp(s - jnp.max(s, axis=0, keepdims=True))
                soft = powers * (1.0 / jnp.sum(powers, axis=0, keepdims=True))
                p_low.append(soft.astype(BF))
                d_low.append((soft * (g - jnp.sum(g * soft, axis=0, keepdims=True))).astype(BF))
            probs.append(jnp.concatenate(p_low, axis=0))
            deltas.append(jnp.concatenate(d_low, axis=0))
        for n, c in enumerate(cols):
            dq = dot(deltas[n], k2[n], 0, 0) * 0.125
            dk = dot(deltas[n], q2[n])
            dv = dot(probs[n], da[n])
            dqkv[at, c : c + 128] = dq.astype(BF)
            dqkv[at, width + c : width + c + 128] = jnp.where(
                low_lane, dk[:blk], dk[blk:]
            ).astype(BF)
            dqkv[at, 2 * width + c : 2 * width + c + 128] = jnp.where(
                low_lane, dv[:blk], dv[blk:]
            ).astype(BF)

    repeat(rows // blk, group, 2)
    sums[0:1, :] = jnp.sum(dqkv[:, :width].astype(F32), axis=0, keepdims=True)
    sums[1:2, :] = jnp.sum(dqkv[:, 2 * width :].astype(F32), axis=0, keepdims=True)
    sums[2:8, :] = jnp.zeros((6, width), F32)


def back_attention(qkv, da, length):
    rows, width = da.shape
    shape = jax.ShapeDtypeStruct
    return pl.pallas_call(
        functools.partial(back_attention_kernel, length),
        name="back_attention",
        in_specs=[WHOLE] * 2,
        out_specs=[WHOLE] * 2,
        out_shape=[shape((rows, 3 * width), BF), shape((8, width), F32)],
        compiler_params=params(),
        cost_estimate=pl.CostEstimate(
            flops=2 * rows * width * 1280, bytes_accessed=20 * rows * width, transcendentals=rows * width
        ),
    )(qkv, da)


def attention_grads_kernel(where, h1_t, att_t, dqkv, dz, keep_a, send_a, keep_b, send_b):
    width = h1_t.shape[0]
    piece = width // PX
    outs = (keep_a, send_a, keep_b, send_b)

    def part_of(x):
        other = x ^ where[0]
        first = other * (3 * piece)

        def chunk(i):
            c = pl.multiple_of(i * 256, 256)
            part = dqkv[:, pl.ds(pl.multiple_of(first + c, 128), 256)]
            put_grad(dot(h1_t[...], part), outs, x, c, 0)

        repeat(width // 256, chunk, 3)
        part = dqkv[:, pl.ds(pl.multiple_of(first + width, 128), piece)]
        put_grad(dot(h1_t[...], part), outs, x, 0, 1)
        part = dz[:, pl.ds(pl.multiple_of(other * piece, 128), piece)]
        put_grad(dot(att_t[...], part), outs, x, piece, 1)

    repeat(PX, part_of)


def attention_grads(where, h1_t, att_t, dqkv, dz):
    width, rows = h1_t.shape
    return pl.pallas_call(
        attention_grads_kernel,
        name="attention_grads",
        in_specs=[SMEM] + [WHOLE] * 4,
        out_specs=[WHOLE] * 4,
        out_shape=grad_shapes(width),
        compiler_params=params(),
        cost_estimate=pl.CostEstimate(
            flops=8 * rows * width * width, bytes_accessed=8 * width * width + 12 * rows * width, transcendentals=0
        ),
    )(where, h1_t, att_t, dqkv, dz)


def back_third_kernel(dr1, dqkv, tok, packed, vec, sums, bias_sums, down_bias, dx, all_sums, wq, sem):
    rows, width = tok.shape
    loads = weight_copies(packed, "qkv", wq, sem, 0, width, width)
    for copy in loads:
        copy.start()
    v = vec[...].astype(F32)
    for copy in loads:
        copy.wait()
    half = rows // 2

    def product(i):
        at = pl.ds(pl.multiple_of(i * half, half), half)
        dx[at, :] = dot(dqkv[at, :], natural(wq), 1, 1)

    repeat(2, product)
    all_sums[0:2, :] = jnp.zeros((2, width), F32)
    blk = 128

    def back(i):
        at = pl.ds(pl.multiple_of(i * blk, blk), blk)
        hat, inverse = normalize(tok[at, :].astype(F32))
        grad = dx[at, :]
        all_sums[0:1, :] += jnp.sum(grad * hat, axis=0, keepdims=True)
        all_sums[1:2, :] += jnp.sum(grad, axis=0, keepdims=True)
        dx[at, :] = dr1[at, :] + norm_back(grad, hat, inverse, v[0:1])

    repeat(rows // blk, back, 2)
    all_sums[2:4, :] = bias_sums[0:2, :]
    all_sums[4:7, :] = sums[0:3, :]
    all_sums[7:8, :] = down_bias[...]


def back_third(dr1, dqkv, tok, packed, vec, sums, bias_sums, down_bias):
    rows, width = tok.shape
    shape = jax.ShapeDtypeStruct
    return pl.pallas_call(
        back_third_kernel,
        name="back_third",
        in_specs=[WHOLE, WHOLE, WHOLE, ANY, WHOLE, WHOLE, WHOLE, WHOLE],
        out_specs=[WHOLE] * 2,
        out_shape=[shape((rows, width), F32), shape((8, width), F32)],
        scratch_shapes=[
            weight_scratch("qkv", width, width),
            pltpu.SemaphoreType.DMA((PX * 3,)),
        ],
        compiler_params=params(),
        cost_estimate=pl.CostEstimate(
            flops=6 * rows * width * width, bytes_accessed=14 * width * width, transcendentals=0
        ),
    )(dr1, dqkv, tok, packed, vec, sums, bias_sums, down_bias)


def fold_kernel(a_own, a_new, b_own, b_new, a_keep, a_send, b_keep, b_send):
    for own, new, keep, send in ((a_own, a_new, a_keep, a_send), (b_own, b_new, b_keep, b_send)):
        total = own[...].astype(F32) + new[...].astype(F32)
        keep[...] = total[0].astype(BF)
        send[...] = total[1].astype(BF)


def fold(a_own, a_new, b_own, b_new):
    shape = a_own.shape
    rest = 1
    for n in shape[1:-2]:
        rest *= n
    rows, cols = shape[-2:]
    view = lambda a: a.reshape(2, rest, rows, cols)
    steps = 2 if rest > 4 else 1
    pair = pl.BlockSpec((2, rest // steps, rows, cols), lambda i: (0, i, 0, 0))
    one = pl.BlockSpec((rest // steps, rows, cols), lambda i: (i, 0, 0))
    outs = pl.pallas_call(
        fold_kernel,
        name="fold",
        grid=(steps,),
        in_specs=[pair] * 4,
        out_specs=[one] * 4,
        out_shape=[jax.ShapeDtypeStruct((rest, rows, cols), BF)] * 4,
        compiler_params=params(),
        cost_estimate=pl.CostEstimate(
            flops=4 * rest * rows * cols, bytes_accessed=24 * rest * rows * cols, transcendentals=0
        ),
    )(*(view(a) for a in (a_own, a_new, b_own, b_new)))
    return [o.reshape(shape[1:]) for o in outs]


def join_kernel(a_own, a_new, b_own, b_new, stay, one, two, three):
    half = a_own.shape[-1]
    for at, own, new in ((0, a_own, a_new), (half, b_own, b_new)):
        total = own[...].astype(F32) + new[...].astype(F32)
        for k, dst in enumerate((stay, one, two, three)):
            dst[:, at : at + half] = total[k].astype(dst.dtype)


def join(a_own, a_new, b_own, b_new):
    blocks, rows, cols = a_own.shape
    shape = jax.ShapeDtypeStruct
    return pl.pallas_call(
        join_kernel,
        name="join",
        in_specs=[WHOLE] * 4,
        out_specs=[WHOLE] * 4,
        out_shape=[shape((rows, 2 * cols), F32)] + [shape((rows, 2 * cols), BF)] * 3,
        compiler_params=params(),
        cost_estimate=pl.CostEstimate(
            flops=16 * rows * cols, bytes_accessed=40 * rows * cols, transcendentals=0
        ),
    )(a_own, a_new, b_own, b_new)


def shifted(x, y, z, core):
    change = x * 16 + z * 4 + y * 2 + core
    return [(i, i ^ change) for i in range(32)]


def hop(array, x=0, y=0, z=0, core=0):
    return lax.ppermute(array, AXES, shifted(x, y, z, core))


def after(values, *others):
    return lax.optimization_barrier((tuple(values), others))[0]


def core_step(parts, *wait):
    keep_a, send_a, keep_b, send_b = parts
    new_a, new_b = hop(send_a, core=1), hop(send_b, core=1)
    keep_a, keep_b = after((keep_a, keep_b), *wait)
    return fold(keep_a, new_a, keep_b, new_b)


def first_step(parts, *wait):
    keep_a, send_a, keep_b, send_b = parts
    new_a, new_b = hop(send_a, x=1), hop(send_b, y=1)
    keep_a, keep_b = after((keep_a, keep_b), *wait)
    return fold(keep_a, new_a, keep_b, new_b)


def second_step(parts, *wait):
    keep_a, send_a, keep_b, send_b = parts
    new_a, new_b = hop(send_a, y=1), hop(send_b, x=1)
    keep_a, keep_b = after((keep_a, keep_b), *wait)
    return join(keep_a, new_a, keep_b, new_b)


def third_step(parts):
    stay, one, two, three = parts
    others = [hop(one, z=1), hop(two, z=2), hop(three, z=3)]
    return stay + sum(o.astype(F32) for o in others)


def natural_grad(keep_a, send_a, keep_b, send_b):
    first = jnp.stack([keep_a, send_a])
    second = jnp.swapaxes(jnp.stack([keep_b, send_b]), 1, 2)
    whole = jnp.concatenate([first, second], axis=-1)
    core, x, y, z, rows, cols = whole.shape
    return whole.transpose(1, 3, 2, 0, 4, 5).reshape(x, z * y * core * rows, cols)


def pack_kernel(qkv, out, up, down, packed):
    rows, piece = out.shape
    at = 0
    for ref in (qkv, out, up, down):
        for c in range(0, ref.shape[1], piece):
            packed[at : at + ref.shape[0], :] = ref[:, c : c + piece]
            at += ref.shape[0]


def pack_block(qkv, out, up, down):
    piece = out.shape[1]
    total = sum(w.shape[0] * w.shape[1] for w in (qkv, out, up, down)) // piece
    return pl.pallas_call(
        pack_kernel,
        name="pack_block",
        in_specs=[WHOLE] * 4,
        out_specs=WHOLE,
        out_shape=jax.ShapeDtypeStruct((total, piece), BF),
        compiler_params=params(),
    )(qkv, out, up, down)


def gather_packed(qkv, out, up, down, dp, fsdp):
    if (dp, fsdp) == (PX, PF):
        return lax.all_gather(pack_block(qkv, out, up, down), AXES, axis=0)
    full = [
        lax.all_gather(lax.all_gather(w, "dp", axis=1, tiled=True), "fsdp", axis=0, tiled=True)
        for w in (qkv, out, up, down)
    ]
    blocks = []
    for x in range(PX):
        for f in range(PF):
            some = []
            for w in full:
                rows, cols = w.shape[0] // PF, w.shape[1] // PX
                some.append(w[f * rows : (f + 1) * rows, x * cols : (x + 1) * cols])
            blocks.append(pack_block(*some))
    return jnp.stack(blocks)


def scatter_columns(grad, dp, fsdp):
    parts, rows, cols = grad.shape
    if dp != parts:
        grad = jnp.swapaxes(grad, 0, 1).reshape(rows, dp, parts * cols // dp)
        grad = jnp.swapaxes(grad, 0, 1)
    return lax.psum_scatter(
        grad.reshape(dp * rows, -1), AXES, scatter_dimension=0, tiled=True
    ).astype(F32)


def body(
    image_tokens,
    text_tokens,
    image_qkv,
    image_out,
    image_up,
    image_down,
    image_vectors,
    image_up_bias,
    text_qkv,
    text_out,
    text_up,
    text_down,
    text_vectors,
    text_up_bias,
    pair_counts,
    pair_groups,
):
    dp, fsdp = lax.axis_size("dp"), lax.axis_size("fsdp")
    devices = dp * fsdp
    cap, length, width = text_tokens.shape
    hidden = image_up.shape[1]
    pairs = pair_groups.shape[0]
    me = lax.axis_index("dp") * fsdp + lax.axis_index("fsdp")

    grid_mesh = (dp, fsdp) == (PX, PF)
    packed = gather_packed(text_qkv, text_out, text_up, text_down, dp, fsdp)
    part = width // fsdp
    small = jnp.concatenate([text_vectors, text_up_bias.reshape(8, -1)], axis=1)
    if grid_mesh:
        small = jnp.broadcast_to(small[None], (fsdp,) + small.shape)
        small = lax.all_to_all(small, "fsdp", 0, 0, tiled=True)
    else:
        small = lax.all_gather(small, "fsdp", axis=0)
    vec = jnp.swapaxes(small[:, :, :part], 0, 1).reshape(8, width)
    ub = small[:, :, part:].reshape(1, hidden)
    bits = [lax.shift_right_logical(me, k) & 1 for k in range(5)]
    where = jnp.stack([bits[4], bits[1], 2 * bits[3] + bits[2], bits[0]])
    where = where if grid_mesh else jnp.zeros_like(where)

    image_low = image_forward(
        image_tokens, image_qkv, image_out, image_up, image_down, image_vectors, image_up_bias
    )
    if grid_mesh:
        images = image_low
        for change in (dict(z=1), dict(z=2), dict(x=1), dict(y=1), dict(core=1)):
            images = jnp.concatenate([images, hop(images, **change)], axis=0)
        far = jnp.arange(devices, dtype=jnp.int32) ^ me
        bit = lambda k: lax.shift_right_logical(far, k) & 1
        order = bit(2) + 2 * bit(3) + 4 * bit(4) + 8 * bit(1) + 16 * bit(0)
        images = jnp.take(images.reshape(devices, cap, width), order, axis=0).reshape(pairs, width)
    else:
        images = lax.all_gather(image_low, AXES, axis=0, tiled=True)

    slots = jnp.arange(cap, dtype=jnp.int32)
    live = (slots[None, :] < pair_counts[:, None]).reshape(pairs).astype(F32)
    same = jnp.maximum(
        jnp.sum(jnp.where(pair_groups[:, None] == pair_groups[None, :], live[None, :], 0.0), axis=1), 1.0
    )
    own_of = lambda array: lax.dynamic_slice_in_dim(array, me * cap, cap)
    own = jnp.stack([own_of(live), own_of(same)], axis=1)
    own_group = own_of(pair_groups).reshape(cap, 1)
    live_row, same_row, group_row = (a.reshape(1, pairs) for a in (live, same, pair_groups))
    live_total = jnp.sum(pair_counts).astype(F32)
    factor = jnp.broadcast_to(LOSS_WEIGHT / (2.0 * live_total), (1, 128))

    tokens = text_tokens.reshape(cap * length, width)
    h1, qkv, att, r1, h2, slope, acts, pooled, low = text_forward(tokens, packed, vec, ub, length, hidden)
    power, row_part, col_sum, loss_part = contrast(
        low, images, live_row, same_row, group_row, own, own_group
    )
    if devices <= 32:
        row_all = lax.all_to_all(
            jnp.broadcast_to(row_part[None], (devices,) + row_part.shape), AXES, 0, 0, tiled=True
        )
        row_sum = jnp.sum(row_all, axis=0)
    else:
        row_all = lax.psum(row_part, AXES)
        row_sum = row_all
    h1_t, h2_t, att_t = relative_rows(where, h1, h2, att)
    dy, dm, du, *up_parts, bias_up, down_bias = back_first(
        where, power, row_all, col_sum, images, live_row, same_row, group_row, own, own_group, factor, pooled,
        packed, slope, h2_t, length,
    )
    dr1, dz, da, sums = back_norm(dy, du, r1, packed, vec, length)
    if grid_mesh:
        up_parts = core_step(up_parts, da)
        (da,) = after((da,), *up_parts)
    dqkv, bias_sums = back_attention(qkv, da, length)
    att_parts = attention_grads(where, h1_t, att_t, dqkv, dz)
    if grid_mesh:
        up_parts = first_step(up_parts, *att_parts)
        dqkv, *att_parts = after((dqkv, *att_parts), *up_parts)
    dx, vec_grads = back_third(dr1, dqkv, tokens, packed, vec, sums, bias_sums, down_bias)
    rows_of = hidden // fsdp
    cols_of = width // dp
    left = jnp.swapaxes(acts.reshape(cap, fsdp, rows_of), 0, 1)
    left = jnp.broadcast_to(left[None], (dp, fsdp, cap, rows_of)).reshape(devices, cap, rows_of)
    right = jnp.swapaxes(dm.reshape(cap, dp, cols_of), 0, 1)
    right = jnp.broadcast_to(right[:, None], (dp, fsdp, cap, cols_of)).reshape(devices, cap, cols_of)
    both = lax.all_to_all(jnp.concatenate([left, right], axis=2), AXES, 0, 0, tiled=True)
    both = both.reshape(pairs, rows_of + cols_of)
    grad_down = dot(both[:, :rows_of], both[:, rows_of:], 0, 0)

    if grid_mesh:
        att_parts = core_step(att_parts, dx)
        up_parts = second_step(up_parts, *att_parts)
        att_parts = first_step(att_parts, grad_down, *up_parts)
        (vec_grads,) = after((vec_grads,), *att_parts)
        grad_up = third_step(up_parts)
        grad_attn = third_step(second_step(att_parts))
        grad_qkv, grad_out = grad_attn[:, : 3 * width // dp], grad_attn[:, 3 * width // dp :]
    else:
        grad_attn = natural_grad(*att_parts)
        grad_up = scatter_columns(natural_grad(*up_parts), dp, fsdp)
        grad_qkv = scatter_columns(grad_attn[:, :, : 3 * width // PX], dp, fsdp)
        grad_out = scatter_columns(grad_attn[:, :, 3 * width // PX :], dp, fsdp)

    share = jnp.concatenate(
        [
            jnp.swapaxes(vec_grads.reshape(8, fsdp, part), 0, 1).reshape(fsdp, 8 * part),
            bias_up.reshape(fsdp, rows_of),
            jnp.broadcast_to(loss_part[0, 0].reshape(1, 1), (fsdp, 1)),
        ],
        axis=1,
    )
    used = share.shape[1]
    padded = -(-used // 128) * 128
    share = jnp.pad(share, ((0, 0), (0, padded - used))).reshape(fsdp, padded // 128, 128)
    share = jnp.broadcast_to(share[None], (dp,) + share.shape).reshape(devices, padded // 128, 128)
    share = jnp.sum(lax.all_to_all(share, AXES, 0, 0, tiled=True), axis=0).reshape(padded)
    grad_vec = share[: 8 * part].reshape(8, part)
    grad_bias = share[8 * part : 8 * part + rows_of]
    loss = (share[used - 1] + jnp.sum(live * jnp.log(row_sum.reshape(pairs)))) / (2.0 * live_total)

    return (
        loss,
        dx.reshape(text_tokens.shape),
        grad_qkv,
        grad_out,
        grad_up,
        grad_down,
        grad_vec,
        grad_bias,
    )


def solution(mesh):
    return jax.shard_map(
        body,
        mesh=mesh,
        in_specs=(
            P(AXES, None, None),
            P(AXES, None, None),
            P(),
            P(),
            P(),
            P(),
            P(),
            P(),
            P("fsdp", "dp"),
            P("fsdp", "dp"),
            P("fsdp", "dp"),
            P("fsdp", "dp"),
            P(None, "fsdp"),
            P("fsdp"),
            P(),
            P(),
        ),
        out_specs=(
            P(),
            P(AXES, None, None),
            P("fsdp", "dp"),
            P("fsdp", "dp"),
            P("fsdp", "dp"),
            P("fsdp", "dp"),
            P(None, "fsdp"),
            P("fsdp"),
        ),
        check_vma=False,
    )
```

```python
import functools

import jax
import jax.numpy as jnp
from jax import lax
from jax.experimental import pallas as pl
from jax.experimental.pallas import tpu as pltpu
from jax.sharding import PartitionSpec as P

HEAD_DIM = 64
LOGIT_SCALE = 50.0
LOSS_WEIGHT = 32768.0
BF = jnp.bfloat16
F32 = jnp.float32
AXES = ("dp", "fsdp")
PX, PF = 2, 16

ANY = pl.BlockSpec(memory_space=pltpu.HBM)
WHOLE = pl.BlockSpec(memory_space=pltpu.VMEM)


def params(mebibytes=62):
    return pltpu.CompilerParams(vmem_limit_bytes=mebibytes * 1024 * 1024)


def dot(a, b, ca=1, cb=0):
    return lax.dot_general(a, b, (((ca,), (cb,)), ((), ())), preferred_element_type=F32)


def repeat(count, step, together=1):
    def turn(j, _):
        for k in range(together):
            step(j * together + k)
        return 0

    if together >= count:
        for i in range(count):
            step(i)
    else:
        lax.fori_loop(0, count // together, turn, 0)


def move(pairs, sem, base=0):
    copies = [pltpu.make_async_copy(a, b, sem.at[base + i]) for i, (a, b) in enumerate(pairs)]
    for copy in copies:
        copy.start()
    return copies


def normalize(values):
    centered = values - jnp.mean(values, axis=-1, keepdims=True)
    inverse = lax.rsqrt(jnp.mean(centered * centered, axis=-1, keepdims=True) + 1e-05)
    return centered * inverse, inverse


def norm_back(grad, hat, inverse, gain):
    scaled = grad * gain
    return inverse * (
        scaled
        - jnp.mean(scaled, axis=-1, keepdims=True)
        - hat * jnp.mean(scaled * hat, axis=-1, keepdims=True)
    )


def gauss_tail(u):
    size = jnp.abs(u)
    t = 1.0 / (1.0 + (0.3275911 * 0.7071067811865476) * size)
    bell = jnp.exp(-0.5 * (u * u))
    poly = 0.5 * 1.061405429 * t - 0.5 * 1.453152027
    poly = poly * t + 0.5 * 1.421413741
    poly = poly * t - 0.5 * 0.284496736
    poly = poly * t + 0.5 * 0.254829592
    return poly * t * bell, bell, size


def head_pair(block, low_lane):
    zero = jnp.zeros_like(block)
    return jnp.concatenate(
        [jnp.where(low_lane, block, zero), jnp.where(low_lane, zero, block)], axis=0
    )


def softmax_half(scores, bias):
    scores = scores + bias
    top = jnp.max(scores, axis=-1, keepdims=True)
    powers = jnp.exp(scores - top)
    return powers * (1.0 / jnp.sum(powers, axis=-1, keepdims=True))


def unit_rows(pooled):
    return pooled * lax.rsqrt(jnp.sum(pooled * pooled, axis=-1, keepdims=True) + 1e-06)


def mean_down(total, count, down):
    mean = total * (1.0 / count)
    high = mean.astype(BF)
    low = (mean - high.astype(F32)).astype(BF)
    both = dot(jnp.concatenate([high, low], axis=0), down)
    return both[: mean.shape[0]] + both[mean.shape[0] :]


def image_kernel(
    tok, wq_h, wo_h, wu_h, wd_h, vec, ub, out, wq, wo, wu, wd, x, h, qkv, att, act_sum, r1_sum, bias_row, stage, sem
):
    step, steps = pl.program_id(0), pl.num_programs(0)
    length, group, width = tok.shape
    rows = group * length
    hidden = wu.shape[1]
    copies = [
        pltpu.make_async_copy(src, dst, sem.at[i])
        for i, (src, dst) in enumerate(((wq_h, wq), (wo_h, wo), (wu_h, wu), (wd_h, wd)))
    ]

    @pl.when(step == 0)
    def _():
        for copy in copies:
            copy.start()

    def arrived(i):
        @pl.when(step == 0)
        def _():
            copies[i].wait()

    v = vec[...].astype(F32)
    bias_row[:, :width] = v[2:3]
    bias_row[:, width : 2 * width] = jnp.zeros((1, width), F32)
    bias_row[:, 2 * width :] = v[3:4]
    for k in range(width // 128):
        stage[k] = tok[:, :, k * 128 : (k + 1) * 128].astype(F32).reshape(rows, 128)
        for i in range(group):
            x[pl.ds(i * length, length), k * 128 : (k + 1) * 128] = stage[k, pl.ds(i, length, stride=group), :]

    def norm_rows(gain, shift):
        blk = 80

        def one(i):
            at = pl.ds(pl.multiple_of(i * blk, blk), blk)
            hat, _ = normalize(x[at, :])
            h[at, :] = (hat * gain + shift).astype(BF)

        repeat(rows // blk, one, 5)

    norm_rows(v[0:1], v[1:2])
    arrived(0)

    def project(i):
        at = pl.ds(pl.multiple_of(i * 256, 256), 256)
        qkv[:, at] = (dot(h[...], wq[:, at]) + bias_row[:, at]).astype(BF)

    repeat(3 * width // 256, project, 3)

    wins = rows // (2 * length)
    q_len = 112
    low_lane = lax.broadcasted_iota(jnp.int32, (128, 128), 1) < HEAD_DIM
    cols = range(0, width, 128)

    def window(w):
        q_at = pl.multiple_of((2 * length * w) // 16 * 16, 16)
        k_at = pl.multiple_of(jnp.minimum(q_at, rows - 128), 16)
        lo, mid, hi = 2 * w * length, (2 * w + 1) * length, (2 * w + 2) * length
        qi = q_at + lax.broadcasted_iota(jnp.int32, (q_len, 128), 0)
        ki = k_at + lax.broadcasted_iota(jnp.int32, (q_len, 128), 1)
        first = (qi >= lo) & (qi < mid) & (ki >= lo) & (ki < mid)
        second = (qi >= mid) & (qi < hi) & (ki >= mid) & (ki < hi)
        bias = jnp.where(first | second, 0.0, -1e30)
        q_rows, k_rows = pl.ds(q_at, q_len), pl.ds(k_at, 128)
        q2 = [qkv[q_rows, c : c + 128] * 0.125 for c in cols]
        k2 = [head_pair(qkv[k_rows, width + c : width + c + 128], low_lane) for c in cols]
        v2 = [head_pair(qkv[k_rows, 2 * width + c : 2 * width + c + 128], low_lane) for c in cols]
        scores = [dot(q, k, 1, 1) for q, k in zip(q2, k2)]
        probs = [
            jnp.concatenate(
                [softmax_half(s[:, :128], bias).astype(BF), softmax_half(s[:, 128:], bias).astype(BF)],
                axis=1,
            )
            for s in scores
        ]
        mine = (q_at + lax.broadcasted_iota(jnp.int32, (16, 128), 0)) >= lo
        for c, p, values in zip(cols, probs, v2):
            mixed = dot(p, values)
            old = att[pl.ds(q_at, 16), c : c + 128].astype(F32)
            att[pl.ds(q_at, 16), c : c + 128] = jnp.where(mine, mixed[:16], old).astype(BF)
            att[pl.ds(q_at + 16, q_len - 16), c : c + 128] = mixed[16:].astype(BF)

    repeat(wins, window, 2)

    arrived(1)
    for c in range(0, width, 256):
        x[:, c : c + 256] = x[:, c : c + 256] + (dot(att[...], wo[:, c : c + 256]) + v[4:5, c : c + 256])
    norm_rows(v[5:6], v[6:7])

    def image_sums(values):
        sums = []
        for i in range(group):
            lo, hi = i * length, (i + 1) * length
            a, b = lo // 8 * 8, -(-hi // 8) * 8
            part = values[a:b]
            row = a + lax.broadcasted_iota(jnp.int32, (b - a, 1), 0)
            if lo % 8 or hi % 8:
                part = jnp.where((row >= lo) & (row < hi), part, 0.0)
            sums.append(jnp.sum(part, axis=0, keepdims=True))
        return jnp.concatenate(sums, axis=0)

    place = pl.ds(pl.multiple_of(step * group, group), group)
    for c in range(0, width, 256):
        r1_sum[place, c : c + 256] = image_sums(x[:, c : c + 256])
    arrived(2)

    def expand(i):
        at = pl.ds(pl.multiple_of(i * 256, 256), 256)
        u = dot(h[...], wu[:, at]) + ub[:, at].astype(F32)
        tail, _, size = gauss_tail(u)
        act_sum[place, at] = image_sums(jnp.maximum(u, 0.0) - size * tail)

    repeat(hidden // 256, expand, 3)
    arrived(3)

    @pl.when(step == steps - 1)
    def _():
        pooled = r1_sum[...] * (1.0 / length) + mean_down(act_sum[...], length, wd[...]) + v[7:8]
        out[...] = unit_rows(pooled).astype(BF)


def image_forward(tokens, wq, wo, wu, wd, vec, ub):
    pairs, length, width = tokens.shape
    hidden = wu.shape[1]
    group = 16
    rows = group * length
    return pl.pallas_call(
        image_kernel,
        name="image_forward",
        grid=(pairs // group,),
        in_specs=[
            pl.BlockSpec((length, group, width), lambda i: (0, i, 0)),
            ANY,
            ANY,
            ANY,
            ANY,
            pl.BlockSpec((8, width), lambda i: (0, 0)),
            pl.BlockSpec((1, hidden), lambda i: (0, 0)),
        ],
        out_specs=pl.BlockSpec((pairs, width), lambda i: (0, 0)),
        out_shape=jax.ShapeDtypeStruct((pairs, width), BF),
        scratch_shapes=[
            pltpu.VMEM((width, 3 * width), BF),
            pltpu.VMEM((width, width), BF),
            pltpu.VMEM((width, hidden), BF),
            pltpu.VMEM((hidden, width), BF),
            pltpu.VMEM((rows, width), F32),
            pltpu.VMEM((rows, width), BF),
            pltpu.VMEM((rows, 3 * width), BF),
            pltpu.VMEM((rows, width), BF),
            pltpu.VMEM((pairs, hidden), F32),
            pltpu.VMEM((pairs, width), F32),
            pltpu.VMEM((1, 3 * width), F32),
            pltpu.VMEM((width // 128, rows, 128), F32),
            pltpu.SemaphoreType.DMA((4,)),
        ],
        compiler_params=params(),
        cost_estimate=pl.CostEstimate(
            flops=2 * pairs * length * width * (4 * width + hidden),
            bytes_accessed=2 * (4 * width * width + 2 * width * hidden + pairs * length * width),
            transcendentals=pairs * length * hidden,
        ),
    )(jnp.swapaxes(tokens, 0, 1), wq, wo, wu, wd, vec, ub.reshape(1, hidden))


def pack_rows(width, hidden):
    piece, rows = width // PX, width // PF
    return piece, rows, hidden // PF


def weight_copies(packed, which, dst, sem, base, width, hidden):
    piece, rows, frows = pack_rows(width, hidden)
    q_pieces, u_pieces = 3, hidden // width
    spans = {
        "qkv": (0, q_pieces, rows),
        "out": (q_pieces * rows, 1, rows),
        "up": ((q_pieces + 1) * rows, u_pieces, rows),
        "down": ((q_pieces + 1 + u_pieces) * rows, 1, frows),
    }
    start, count, tall = spans[which]
    copies = []
    for x in range(PX):
        for p in range(count):
            copies.append(
                pltpu.make_async_copy(
                    packed.at[pl.ds(x * PF, PF), pl.ds(start + p * tall, tall), :],
                    dst.at[:, :, pl.ds((x * count + p) * piece, piece)],
                    sem.at[base + len(copies)],
                )
            )
    return copies


def natural(ref):
    blocks, rows, cols = ref.shape
    return ref[...].reshape(blocks * rows, cols)


def weight_scratch(which, width, hidden):
    rows, frows = width // PF, hidden // PF
    shape = {
        "qkv": (PF, rows, 3 * width),
        "out": (PF, rows, width),
        "up": (PF, rows, hidden),
        "down": (PF, frows, width),
    }[which]
    return pltpu.VMEM(shape, BF)


def contrast(low, images, live, same, groups, own, own_group, power, row_part, col_sum, loss_part):
    scores = LOGIT_SCALE * dot(low, images[...], 1, 1)
    exps = jnp.exp(scores)
    live_own, same_own = own[:, 0:1], own[:, 1:2]
    power[...] = exps
    rows = jnp.sum(exps * live_own, axis=0, keepdims=True)
    tiled = jnp.concatenate(
        [rows[:, k * 128 : (k + 1) * 128] for k in range(rows.shape[1] // 128)], axis=0
    )
    for d in range(row_part.shape[0]):
        row_part[d] = tiled
    cols = jnp.sum(exps * live[...], axis=1, keepdims=True)
    col_sum[...] = cols
    pair = jnp.where(own_group[...] == groups[...], live_own * live[...], 0.0)
    linear = pair * scores * (1.0 / same_own + 1.0 / same[...])
    losses = live_own * jnp.log(cols) - jnp.sum(linear, axis=1, keepdims=True)
    loss_part[...] = jnp.broadcast_to(jnp.sum(losses, axis=0, keepdims=True), loss_part.shape)


def text_mask(size, length):
    row = lax.broadcasted_iota(jnp.int32, (size, size), 0) // length
    col = lax.broadcasted_iota(jnp.int32, (size, size), 1) // length
    return jnp.where(row == col, 0.0, -1e30)


def text_forward_kernel(
    length, tok, packed, vec, ub, images_i, live, same, groups, own, own_group,
    h1_o, qkv_o, att_o, r1_o, h2_o, slope_o, acts, pooled_out, power, row_part, col_sum, loss_part,
    wq, wo, wu, wd, total, bias_row, h1, qkv, att, r1, h2, slope, sem, images, out_sem
):
    rows, width = tok.shape
    hidden = slope.shape[1]
    texts = rows // length
    load = {}
    base = 0
    for which, dst in (("qkv", wq), ("out", wo), ("up", wu), ("down", wd)):
        load[which] = weight_copies(packed, which, dst, sem, base, width, hidden)
        base += len(load[which])
        for copy in load[which]:
            copy.start()
    v = vec[...].astype(F32)
    bias_row[:, :width] = v[2:3]
    bias_row[:, width : 2 * width] = jnp.zeros((1, width), F32)
    bias_row[:, 2 * width :] = v[3:4]
    blk = 128

    def norm_rows(src, dst, gain, shift):
        def one(i):
            at = pl.ds(pl.multiple_of(i * blk, blk), blk)
            hat, _ = normalize(src[at, :].astype(F32))
            dst[at, :] = (hat * gain + shift).astype(BF)

        repeat(rows // blk, one, 2)

    norm_rows(tok, h1, v[0:1], v[1:2])
    saves = move([(h1, h1_o)], out_sem)
    (gathered,) = move([(images_i, images)], out_sem, 6)
    for copy in load["qkv"]:
        copy.wait()

    def project(i):
        at = pl.ds(pl.multiple_of(i * 256, 256), 256)
        qkv[:, at] = (dot(h1[...], wq[:, :, at].reshape(width, 256)) + bias_row[:, at]).astype(BF)

    repeat(3 * width // 256, project, 3)
    saves += move([(qkv, qkv_o)], out_sem, 1)
    low_lane = lax.broadcasted_iota(jnp.int32, (blk, 128), 1) < HEAD_DIM
    bias = text_mask(blk, length)
    cols = range(0, width, 128)

    def attend(i):
        at = pl.ds(pl.multiple_of(i * blk, blk), blk)
        q2 = [qkv[at, c : c + 128] * 0.125 for c in cols]
        k2 = [head_pair(qkv[at, width + c : width + c + 128], low_lane) for c in cols]
        v2 = [head_pair(qkv[at, 2 * width + c : 2 * width + c + 128], low_lane) for c in cols]
        scores = [dot(q, k, 1, 1) for q, k in zip(q2, k2)]
        probs = [
            jnp.concatenate(
                [softmax_half(s[:, :blk], bias).astype(BF), softmax_half(s[:, blk:], bias).astype(BF)],
                axis=1,
            )
            for s in scores
        ]
        for c, p, values in zip(cols, probs, v2):
            att[at, c : c + 128] = dot(p, values).astype(BF)

    repeat(rows // blk, attend, 2)
    saves += move([(att, att_o)], out_sem, 2)
    for copy in load["out"]:
        copy.wait()
    for c in range(0, width, 256):
        r1[:, c : c + 256] = tok[:, c : c + 256].astype(F32) + (
            dot(att[...], wo[:, :, c : c + 256].reshape(width, 256)) + v[4:5, c : c + 256]
        )
    saves += move([(r1, r1_o)], out_sem, 3)
    norm_rows(r1, h2, v[5:6], v[6:7])
    saves += move([(h2, h2_o)], out_sem, 4)
    for copy in load["up"]:
        copy.wait()

    def expand(i):
        at = pl.ds(pl.multiple_of(i * 256, 256), 256)
        u = dot(h2[...], wu[:, :, at].reshape(width, 256)) + ub[:, at].astype(F32)
        tail, bell, size = gauss_tail(u)
        act = jnp.maximum(u, 0.0) - size * tail
        phi = jnp.where(u >= 0.0, 1.0 - tail, tail)
        slope[:, at] = (phi + u * (bell * 0.3989422804014327)).astype(BF)
        sums = jnp.sum(act.reshape(texts, length, 256), axis=1)
        total[:, at] = sums
        acts[:, at] = sums.astype(BF)

    repeat(hidden // 256, expand, 3)
    saves += move([(slope, slope_o)], out_sem, 5)
    for copy in load["down"]:
        copy.wait()
    mean_r1 = jnp.sum(r1[...].reshape(texts, length, width), axis=1) * (1.0 / length)
    pooled = mean_r1 + mean_down(total[...], length, natural(wd)) + v[7:8]
    pooled_out[...] = pooled
    gathered.wait()
    contrast(
        unit_rows(pooled).astype(BF), images, live, same, groups, own, own_group, power, row_part, col_sum, loss_part
    )
    for copy in saves:
        copy.wait()


def text_forward(
    tokens, packed, vec, ub, images, live, same, groups, own, own_group, length, hidden, copies_of
):
    rows, width = tokens.shape
    texts = rows // length
    pairs = images.shape[0]
    shape = jax.ShapeDtypeStruct
    copies = PX * (3 + 1 + hidden // width + 1)
    return pl.pallas_call(
        functools.partial(text_forward_kernel, length),
        name="text_forward",
        in_specs=[WHOLE, ANY, WHOLE, WHOLE, ANY] + [WHOLE] * 5,
        out_specs=[ANY] * 6 + [WHOLE] * 6,
        out_shape=[
            shape((rows, width), BF),
            shape((rows, 3 * width), BF),
            shape((rows, width), BF),
            shape((rows, width), F32),
            shape((rows, width), BF),
            shape((rows, hidden), BF),
            shape((texts, hidden), BF),
            shape((texts, width), F32),
            shape((texts, pairs), F32),
            shape((copies_of, pairs // 128, 128), F32),
            shape((texts, 1), F32),
            shape((8, 128), F32),
        ],
        scratch_shapes=[weight_scratch(w, width, hidden) for w in ("qkv", "out", "up", "down")]
        + [
            pltpu.VMEM((texts, hidden), F32),
            pltpu.VMEM((1, 3 * width), F32),
            pltpu.VMEM((rows, width), BF),
            pltpu.VMEM((rows, 3 * width), BF),
            pltpu.VMEM((rows, width), BF),
            pltpu.VMEM((rows, width), F32),
            pltpu.VMEM((rows, width), BF),
            pltpu.VMEM((rows, hidden), BF),
            pltpu.SemaphoreType.DMA((copies,)),
            pltpu.VMEM((pairs, width), BF),
            pltpu.SemaphoreType.DMA((7,)),
        ],
        compiler_params=params(),
        cost_estimate=pl.CostEstimate(
            flops=2 * rows * width * (4 * width + hidden),
            bytes_accessed=2 * (4 * width * width + 2 * width * hidden + 12 * rows * width),
            transcendentals=rows * hidden,
        ),
    )(tokens, packed, vec, ub, images, live, same, groups, own, own_group)


def relative_kernel(where, h1_i, h2_i, att_i, h1_o, h2_o, att_o, h1, h2, att, h1_t, h2_t, att_t, sem):
    width = h1.shape[1]
    block = width // PF
    my, mz, mc = where[1], where[2], where[3]
    loads = move([(h2_i, h2), (h1_i, h1), (att_i, att)], sem)
    saves = []
    for n, (src, dst, out) in enumerate(((h2, h2_t, h2_o), (h1, h1_t, h1_o), (att, att_t, att_o))):
        loads[n].wait()
        turned = src[...].T
        for z in range(4):
            for y in range(2):
                for c in range(2):
                    f = (z * 2 + y) * 2 + c
                    place = (((c ^ mc) * 2 + (y ^ my)) * 4 + (z ^ mz)) * block
                    dst[pl.ds(pl.multiple_of(place, block), block), :] = turned[
                        f * block : (f + 1) * block
                    ]
        saves += move([(dst, out)], sem, 3 + n)
    for copy in saves:
        copy.wait()


SMEM = pl.BlockSpec(memory_space=pltpu.SMEM)


def relative_rows(where, h1, h2, att):
    rows, width = h1.shape
    return pl.pallas_call(
        relative_kernel,
        name="relative_rows",
        in_specs=[SMEM, ANY, ANY, ANY],
        out_specs=[ANY] * 3,
        out_shape=[jax.ShapeDtypeStruct((width, rows), BF)] * 3,
        scratch_shapes=[pltpu.VMEM((rows, width), BF)] * 3
        + [pltpu.VMEM((width, rows), BF)] * 3
        + [pltpu.SemaphoreType.DMA((6,))],
        compiler_params=params(),
        cost_estimate=pl.CostEstimate(flops=0, bytes_accessed=12 * rows * width, transcendentals=0),
    )(where, h1, h2, att)


def grad_shapes(width):
    block, half = width // PF, width
    return [jax.ShapeDtypeStruct((2, 2, 4, block, half), BF)] * 4


def put_grad(values, outs, x_rel, at, second):
    width, cols = values.shape
    block = width // PF
    low = values.astype(BF)
    for c in range(2):
        for y in range(2):
            piece = low[(c * 2 + y) * 4 * block : (c * 2 + y + 1) * 4 * block].reshape(4, block, cols)
            if second:
                outs[2 + c, y, x_rel, :, :, pl.ds(at, cols)] = piece
            else:
                outs[c, x_rel, y, :, :, pl.ds(at, cols)] = piece


def start_grads(parts, outs, sem, x):
    return move(
        [(parts.at[n, x], outs[n].at[x]) for n in range(2)]
        + [(parts.at[n, :, x], outs[n].at[:, x]) for n in range(2, 4)],
        sem,
        4 * x,
    )


def back_one_kernel(
    length, shard,
    where, power, row_all, col_sum, images_i, live, same, groups, own, own_group, factor, pooled, packed, vec,
    slope_i, h2_i, r1_i, acts,
    factors_o, keep_a, send_a, keep_b, send_b, bias_up, down_bias, dr1_o, dz_o, da_o, sums, loss_rows,
    factors, wd, wu, wo, dact, images, slope, h2_t, r1, du, dr1, dz_s, da_s, dy, parts, sem, in_sem, out_sem,
):
    rows, hidden = slope.shape
    texts = rows // length
    width = h2_t.shape[0]
    (gathered,) = move([(images_i, images)], in_sem)
    down = weight_copies(packed, "down", wd, sem, 0, width, hidden)
    up = weight_copies(packed, "up", wu, sem, len(down), width, hidden)
    out = weight_copies(packed, "out", wo, sem, len(down) + len(up), width, hidden)
    for copy in down:
        copy.start()
    saved = move([(slope_i, slope), (h2_i, h2_t)], in_sem, 1)
    for copy in up + out:
        copy.start()
    saved += move([(r1_i, r1)], in_sem, 3)
    totals = jnp.sum(row_all[...], axis=0)
    row_sum = jnp.concatenate([totals[k : k + 1] for k in range(totals.shape[0])], axis=1)
    live_own, same_own = own[:, 0:1], own[:, 1:2]
    pair = factor[0:1, 0:1] * live_own * live[...]
    match = jnp.where(own_group[...] == groups[...], 1.0 / same_own + 1.0 / same[...], 0.0)
    grad_scores = pair * (power[...] * (1.0 / row_sum + 1.0 / col_sum[...]) - match)
    gathered.wait()
    grad_low = LOGIT_SCALE * dot(grad_scores.astype(BF), images[...])
    pool = pooled[...]
    inverse = lax.rsqrt(jnp.sum(pool * pool, axis=-1, keepdims=True) + 1e-06)
    along = jnp.sum(pool * grad_low, axis=-1, keepdims=True)
    dy[...] = inverse * (grad_low - pool * (inverse * inverse * along)) * (1.0 / length)
    dm = dy[...].astype(BF)
    loss_rows[...] = jnp.broadcast_to(
        jnp.sum(live[...] * jnp.log(row_sum), axis=1, keepdims=True), loss_rows.shape
    )
    parts_x, parts_f = shard
    piece_x, piece_f = width // parts_x, hidden // parts_f
    for f in range(parts_f):
        left = acts[:, f * piece_f : (f + 1) * piece_f]
        for x in range(parts_x):
            factors[x * parts_f + f, :, piece_x:] = left
            factors[x * parts_f + f, :, :piece_x] = dm[:, x * piece_x : (x + 1) * piece_x]
    sent = move([(factors, factors_o)], out_sem, 11)
    down_bias[...] = length * jnp.sum(dm.astype(F32), axis=0, keepdims=True)
    for copy in down:
        copy.wait()
    dact[...] = dot(dm, natural(wd), 1, 1)
    saved[0].wait()

    def slopes(i):
        at = pl.ds(pl.multiple_of(i * 256, 256), 256)
        spread = jnp.broadcast_to(dact[:, at].reshape(texts, 1, 256), (texts, length, 256))
        part = (spread.reshape(rows, 256) * slope[:, at].astype(F32)).astype(BF)
        du[:, at] = part
        bias_up[:, at] = jnp.sum(part.astype(F32), axis=0, keepdims=True)

    repeat(hidden // 256, slopes, 3)
    saved[1].wait()
    half = hidden // PX
    outs = (keep_a, send_a, keep_b, send_b)
    for x in range(PX):
        first = (x ^ where[0]) * half

        def grads(i):
            c = pl.multiple_of(i * 256, 256)
            for second in range(2):
                part = du[:, pl.ds(pl.multiple_of(first + c + second * width, 256), 256)]
                put_grad(dot(h2_t[...], part), parts, x, c, second)

        repeat(width // 256, grads)
        sent += start_grads(parts, outs, out_sem, x)

    v = vec[...].astype(F32)
    blk = 128
    for copy in up:
        copy.wait()

    def product(i):
        at = pl.ds(pl.multiple_of(i * (rows // 2), rows // 2), rows // 2)
        dr1[at, :] = dot(du[at, :], natural(wu), 1, 1)

    repeat(2, product)
    sums[...] = jnp.zeros((8, width), F32)
    some = blk // length
    saved[2].wait()

    def back(i):
        at = pl.ds(pl.multiple_of(i * blk, blk), blk)
        hat, inverse = normalize(r1[at, :])
        grad = dr1[at, :]
        sums[1:2, :] += jnp.sum(grad * hat, axis=0, keepdims=True)
        sums[2:3, :] += jnp.sum(grad, axis=0, keepdims=True)
        spread = jnp.broadcast_to(
            dy[pl.ds(pl.multiple_of(i * some, some), some), :].reshape(some, 1, width), (some, length, width)
        ).reshape(blk, width)
        grad = spread + norm_back(grad, hat, inverse, v[5:6])
        dr1[at, :] = grad
        low = grad.astype(BF)
        dz_s[at, :] = low
        sums[0:1, :] += jnp.sum(low.astype(F32), axis=0, keepdims=True)

    repeat(rows // blk, back, 2)
    sent += move([(dr1, dr1_o), (dz_s, dz_o)], out_sem, 8)
    for copy in out:
        copy.wait()
    da_s[...] = dot(dz_s[...], natural(wo), 1, 1).astype(BF)
    sent += move([(da_s, da_o)], out_sem, 10)
    for copy in sent:
        copy.wait()


def back_one(
    where, power, row_all, col_sum, images, live, same, groups, own, own_group, factor, pooled, packed, vec, slope,
    h2_t, r1, acts, length, shard,
):
    rows, hidden = slope.shape
    width = h2_t.shape[0]
    texts = rows // length
    payload = (shard[0] * shard[1], texts, width // shard[0] + hidden // shard[1])
    shape = jax.ShapeDtypeStruct
    return pl.pallas_call(
        functools.partial(back_one_kernel, length, shard),
        name="back_one",
        in_specs=[SMEM] + [WHOLE] * 3 + [ANY] + [WHOLE] * 7 + [ANY, WHOLE, ANY, ANY, ANY, WHOLE],
        out_specs=[ANY] * 5 + [WHOLE] * 2 + [ANY] * 3 + [WHOLE] * 2,
        out_shape=[
            shape(payload, BF),
            *grad_shapes(width),
            shape((1, hidden), F32),
            shape((1, width), F32),
            shape((rows, width), F32),
            shape((rows, width), BF),
            shape((rows, width), BF),
            shape((8, width), F32),
            shape((8, 128), F32),
        ],
        scratch_shapes=[
            pltpu.VMEM(payload, BF),
            weight_scratch("down", width, hidden),
            weight_scratch("up", width, hidden),
            weight_scratch("out", width, hidden),
            pltpu.VMEM((texts, hidden), F32),
            pltpu.VMEM(images.shape, BF),
            pltpu.VMEM((rows, hidden), BF),
            pltpu.VMEM((width, rows), BF),
            pltpu.VMEM((rows, width), F32),
            pltpu.VMEM((rows, hidden), BF),
            pltpu.VMEM((rows, width), F32),
            pltpu.VMEM((rows, width), BF),
            pltpu.VMEM((rows, width), BF),
            pltpu.VMEM((texts, width), F32),
            pltpu.VMEM((4,) + grad_shapes(width)[0].shape, BF),
            pltpu.SemaphoreType.DMA((PX * (2 + hidden // width),)),
            pltpu.SemaphoreType.DMA((4,)),
            pltpu.SemaphoreType.DMA((12,)),
        ],
        compiler_params=params(),
        cost_estimate=pl.CostEstimate(
            flops=2 * rows * width * (2 * hidden + width), bytes_accessed=16 * width * hidden, transcendentals=0
        ),
    )(
        where, power, row_all, col_sum, images, live, same, groups, own, own_group, factor, pooled, packed, vec,
        slope, h2_t, r1, acts,
    )


def back_two_kernel(
    length, where, qkv_i, da_i, dz_i, h1_i, att_i, dqkv_o, keep_a, send_a, keep_b, send_b, sums,
    qkv, da_s, dz, h1_t, att_t, dqkv, parts, sem, out_sem,
):
    rows, width = da_s.shape
    blk = 128
    loads = move([(qkv_i, qkv), (da_i, da_s), (att_i, att_t), (dz_i, dz), (h1_i, h1_t)], sem)
    for copy in loads[:2]:
        copy.wait()
    low_lane = lax.broadcasted_iota(jnp.int32, (blk, 128), 1) < HEAD_DIM
    bias = text_mask(blk, length)
    cols = range(0, width, 128)
    def group(i):
        at = pl.ds(pl.multiple_of(i * blk, blk), blk)
        take = lambda base, c: qkv[at, base + c : base + c + 128]
        q2 = [take(0, c) * 0.125 for c in cols]
        k2 = [head_pair(take(width, c), low_lane) for c in cols]
        v2 = [head_pair(take(2 * width, c), low_lane) for c in cols]
        da = [da_s[at, c : c + 128] for c in cols]
        scores = [dot(k, q, 1, 1) for k, q in zip(k2, q2)]
        grads = [dot(v, d, 1, 1) for v, d in zip(v2, da)]
        probs, deltas = [], []
        for score, grad in zip(scores, grads):
            p_low, d_low = [], []
            for half in range(2):
                s = score[half * blk : (half + 1) * blk] + bias
                g = grad[half * blk : (half + 1) * blk]
                powers = jnp.exp(s - jnp.max(s, axis=0, keepdims=True))
                soft = powers * (1.0 / jnp.sum(powers, axis=0, keepdims=True))
                p_low.append(soft.astype(BF))
                d_low.append((soft * (g - jnp.sum(g * soft, axis=0, keepdims=True))).astype(BF))
            probs.append(jnp.concatenate(p_low, axis=0))
            deltas.append(jnp.concatenate(d_low, axis=0))
        for n, c in enumerate(cols):
            dq = dot(deltas[n], k2[n], 0, 0) * 0.125
            dk = dot(deltas[n], q2[n])
            dv = dot(probs[n], da[n])
            dqkv[at, c : c + 128] = dq.astype(BF)
            dqkv[at, width + c : width + c + 128] = jnp.where(
                low_lane, dk[:blk], dk[blk:]
            ).astype(BF)
            dqkv[at, 2 * width + c : 2 * width + c + 128] = jnp.where(
                low_lane, dv[:blk], dv[blk:]
            ).astype(BF)

    repeat(rows // blk, group, 2)
    sums[0:1, :] = jnp.sum(dqkv[:, :width].astype(F32), axis=0, keepdims=True)
    sums[1:2, :] = jnp.sum(dqkv[:, 2 * width :].astype(F32), axis=0, keepdims=True)
    sums[2:8, :] = jnp.zeros((6, width), F32)
    sent = move([(dqkv, dqkv_o)], out_sem, 8)
    for copy in loads[2:]:
        copy.wait()
    piece = width // PX
    outs = (keep_a, send_a, keep_b, send_b)
    for x in range(PX):
        other = x ^ where[0]
        first = other * (3 * piece)

        def chunk(i):
            c = pl.multiple_of(i * 256, 256)
            part = dqkv[:, pl.ds(pl.multiple_of(first + c, 128), 256)]
            put_grad(dot(h1_t[...], part), parts, x, c, 0)

        repeat(width // 256, chunk)
        part = dqkv[:, pl.ds(pl.multiple_of(first + width, 128), piece)]
        put_grad(dot(h1_t[...], part), parts, x, 0, 1)
        part = dz[:, pl.ds(pl.multiple_of(other * piece, 128), piece)]
        put_grad(dot(att_t[...], part), parts, x, piece, 1)
        sent += start_grads(parts, outs, out_sem, x)
    for copy in sent:
        copy.wait()


def back_two(where, qkv, da, dz, h1_t, att_t, length):
    rows, width = da.shape
    shape = jax.ShapeDtypeStruct
    return pl.pallas_call(
        functools.partial(back_two_kernel, length),
        name="back_two",
        in_specs=[SMEM] + [ANY] * 5,
        out_specs=[ANY] * 5 + [WHOLE],
        out_shape=[shape((rows, 3 * width), BF), *grad_shapes(width), shape((8, width), F32)],
        scratch_shapes=[
            pltpu.VMEM((rows, 3 * width), BF),
            pltpu.VMEM((rows, width), BF),
            pltpu.VMEM((rows, width), BF),
            pltpu.VMEM((width, rows), BF),
            pltpu.VMEM((width, rows), BF),
            pltpu.VMEM((rows, 3 * width), BF),
            pltpu.VMEM((4,) + grad_shapes(width)[0].shape, BF),
            pltpu.SemaphoreType.DMA((5,)),
            pltpu.SemaphoreType.DMA((9,)),
        ],
        compiler_params=params(),
        cost_estimate=pl.CostEstimate(
            flops=2 * rows * width * (1280 + 4 * width), bytes_accessed=20 * rows * width, transcendentals=rows * width
        ),
    )(where, qkv, da, dz, h1_t, att_t)


def back_third_kernel(
    parts_f, dr1_i, dqkv_i, tok_i, packed, vec, sums, bias_sums, down_bias, bias_up, loss_part, dx_o, share, all_sums, wq, dr1, tok, dx, sem, dqkv, own_sem
):
    rows, width = tok.shape
    loads = weight_copies(packed, "qkv", wq, sem, 0, width, width)
    for copy in loads:
        copy.start()
    saved = move([(dqkv_i, dqkv), (dr1_i, dr1), (tok_i, tok)], own_sem)
    saved[0].wait()
    v = vec[...].astype(F32)
    for copy in loads:
        copy.wait()
    half = rows // 2

    def product(i):
        at = pl.ds(pl.multiple_of(i * half, half), half)
        dx[at, :] = dot(dqkv[at, :], natural(wq), 1, 1)

    repeat(2, product)
    for copy in saved[1:]:
        copy.wait()
    all_sums[0:2, :] = jnp.zeros((2, width), F32)
    blk = 128

    def back(i):
        at = pl.ds(pl.multiple_of(i * blk, blk), blk)
        hat, inverse = normalize(tok[at, :].astype(F32))
        grad = dx[at, :]
        all_sums[0:1, :] += jnp.sum(grad * hat, axis=0, keepdims=True)
        all_sums[1:2, :] += jnp.sum(grad, axis=0, keepdims=True)
        dx[at, :] = dr1[at, :] + norm_back(grad, hat, inverse, v[0:1])

    repeat(rows // blk, back, 2)
    (save,) = move([(dx, dx_o)], own_sem, 3)
    all_sums[2:4, :] = bias_sums[0:2, :]
    all_sums[4:7, :] = sums[0:3, :]
    all_sums[7:8, :] = down_bias[...]
    every = all_sums[...]
    piece, tall = width // parts_f, bias_up.shape[1] // parts_f
    devices = share.shape[0]
    used = piece + tall // 8
    for f in range(parts_f):
        bias = bias_up[:, f * tall : (f + 1) * tall]
        bias = jnp.concatenate([bias[:, r * tall // 8 : (r + 1) * tall // 8] for r in range(8)], axis=0)
        block = jnp.concatenate(
            [every[:, f * piece : (f + 1) * piece], bias, loss_part[:, : 128 - used]], axis=1
        )
        for x in range(devices // parts_f):
            share[x * parts_f + f] = block
    save.wait()


def back_third(dr1, dqkv, tok, packed, vec, sums, bias_sums, down_bias, bias_up, loss_part, shard):
    rows, width = tok.shape
    shape = jax.ShapeDtypeStruct
    return pl.pallas_call(
        functools.partial(back_third_kernel, shard[1]),
        name="back_third",
        in_specs=[ANY, ANY, ANY, ANY] + [WHOLE] * 6,
        out_specs=[ANY, WHOLE],
        out_shape=[shape((rows, width), F32), shape((shard[0] * shard[1], 8, 128), F32)],
        scratch_shapes=[
            pltpu.VMEM((8, width), F32),
            weight_scratch("qkv", width, width),
            pltpu.VMEM((rows, width), F32),
            pltpu.VMEM((rows, width), BF),
            pltpu.VMEM((rows, width), F32),
            pltpu.SemaphoreType.DMA((PX * 3,)),
            pltpu.VMEM((rows, 3 * width), BF),
            pltpu.SemaphoreType.DMA((4,)),
        ],
        compiler_params=params(),
        cost_estimate=pl.CostEstimate(
            flops=6 * rows * width * width, bytes_accessed=14 * width * width, transcendentals=0
        ),
    )(dr1, dqkv, tok, packed, vec, sums, bias_sums, down_bias, bias_up, loss_part)


def fold_kernel(a_own, a_new, b_own, b_new, a_keep, a_send, b_keep, b_send):
    for own, new, keep, send in ((a_own, a_new, a_keep, a_send), (b_own, b_new, b_keep, b_send)):
        total = own[...].astype(F32) + new[...].astype(F32)
        keep[...] = total[0].astype(BF)
        send[...] = total[1].astype(BF)


def fold(a_own, a_new, b_own, b_new):
    shape = a_own.shape
    rest = 1
    for n in shape[1:-2]:
        rest *= n
    rows, cols = shape[-2:]
    view = lambda a: a.reshape(2, rest, rows, cols)
    steps = 2 if rest > 4 else 1
    pair = pl.BlockSpec((2, rest // steps, rows, cols), lambda i: (0, i, 0, 0))
    one = pl.BlockSpec((rest // steps, rows, cols), lambda i: (i, 0, 0))
    outs = pl.pallas_call(
        fold_kernel,
        name="fold",
        grid=(steps,),
        in_specs=[pair] * 4,
        out_specs=[one] * 4,
        out_shape=[jax.ShapeDtypeStruct((rest, rows, cols), BF)] * 4,
        compiler_params=params(18),
        cost_estimate=pl.CostEstimate(
            flops=4 * rest * rows * cols, bytes_accessed=24 * rest * rows * cols, transcendentals=0
        ),
    )(*(view(a) for a in (a_own, a_new, b_own, b_new)))
    return [o.reshape(shape[1:]) for o in outs]


def join_kernel(a_own, a_new, b_own, b_new, stay, one, two, three):
    half = a_own.shape[-1]
    for at, own, new in ((0, a_own, a_new), (half, b_own, b_new)):
        total = own[...].astype(F32) + new[...].astype(F32)
        for k, dst in enumerate((stay, one, two, three)):
            dst[:, at : at + half] = total[k].astype(dst.dtype)


def join(a_own, a_new, b_own, b_new):
    blocks, rows, cols = a_own.shape
    shape = jax.ShapeDtypeStruct
    return pl.pallas_call(
        join_kernel,
        name="join",
        in_specs=[WHOLE] * 4,
        out_specs=[WHOLE] * 4,
        out_shape=[shape((rows, 2 * cols), F32)] + [shape((rows, 2 * cols), BF)] * 3,
        compiler_params=params(6),
        cost_estimate=pl.CostEstimate(
            flops=16 * rows * cols, bytes_accessed=40 * rows * cols, transcendentals=0
        ),
    )(a_own, a_new, b_own, b_new)


def shifted(x, y, z, core):
    change = x * 16 + z * 4 + y * 2 + core
    return [(i, i ^ change) for i in range(32)]


def hop(array, x=0, y=0, z=0, core=0):
    return lax.ppermute(array, AXES, shifted(x, y, z, core))


def after(values, *others):
    return lax.optimization_barrier((tuple(values), others))[0]


def core_step(parts, *wait):
    keep_a, send_a, keep_b, send_b = parts
    new_a, new_b = hop(send_a, core=1), hop(send_b, core=1)
    keep_a, keep_b = after((keep_a, keep_b), *wait)
    return fold(keep_a, new_a, keep_b, new_b)


def first_step(parts, *wait):
    keep_a, send_a, keep_b, send_b = parts
    new_a, new_b = hop(send_a, x=1), hop(send_b, y=1)
    keep_a, keep_b = after((keep_a, keep_b), *wait)
    return fold(keep_a, new_a, keep_b, new_b)


def second_step(parts, *wait):
    keep_a, send_a, keep_b, send_b = parts
    new_a, new_b = hop(send_a, y=1), hop(send_b, x=1)
    keep_a, keep_b = after((keep_a, keep_b), *wait)
    return join(keep_a, new_a, keep_b, new_b)


def total_kernel(stay, one, two, three, *outs):
    total = stay[...] + one[...].astype(F32) + two[...].astype(F32) + three[...].astype(F32)
    at = 0
    for out in outs:
        out[...] = total[:, at : at + out.shape[1]]
        at += out.shape[1]


def third_step(parts, splits):
    stay, one, two, three = parts
    return pl.pallas_call(
        total_kernel,
        name="total",
        in_specs=[WHOLE] * 4,
        out_specs=[WHOLE] * len(splits),
        out_shape=[jax.ShapeDtypeStruct((stay.shape[0], n), F32) for n in splits],
        compiler_params=params(4),
    )(stay, hop(one, z=1), hop(two, z=2), hop(three, z=3))


def natural_grad(keep_a, send_a, keep_b, send_b):
    first = jnp.stack([keep_a, send_a])
    second = jnp.swapaxes(jnp.stack([keep_b, send_b]), 1, 2)
    whole = jnp.concatenate([first, second], axis=-1)
    core, x, y, z, rows, cols = whole.shape
    return whole.transpose(1, 3, 2, 0, 4, 5).reshape(x, z * y * core * rows, cols)


def pack_kernel(qkv, out, up, down, packed):
    rows, piece = out.shape
    at = 0
    for ref in (qkv, out, up, down):
        for c in range(0, ref.shape[1], piece):
            packed[at : at + ref.shape[0], :] = ref[:, c : c + piece]
            at += ref.shape[0]


def pack_block(qkv, out, up, down):
    piece = out.shape[1]
    total = sum(w.shape[0] * w.shape[1] for w in (qkv, out, up, down)) // piece
    return pl.pallas_call(
        pack_kernel,
        name="pack_block",
        in_specs=[WHOLE] * 4,
        out_specs=WHOLE,
        out_shape=jax.ShapeDtypeStruct((total, piece), BF),
        compiler_params=params(),
    )(qkv, out, up, down)


def gather_packed(qkv, out, up, down, dp, fsdp):
    if (dp, fsdp) == (PX, PF):
        return lax.all_gather(pack_block(qkv, out, up, down), AXES, axis=0)
    full = [
        lax.all_gather(lax.all_gather(w, "dp", axis=1, tiled=True), "fsdp", axis=0, tiled=True)
        for w in (qkv, out, up, down)
    ]
    blocks = []
    for x in range(PX):
        for f in range(PF):
            some = []
            for w in full:
                rows, cols = w.shape[0] // PF, w.shape[1] // PX
                some.append(w[f * rows : (f + 1) * rows, x * cols : (x + 1) * cols])
            blocks.append(pack_block(*some))
    return jnp.stack(blocks)


def scatter_columns(grad, dp, fsdp):
    parts, rows, cols = grad.shape
    if dp != parts:
        grad = jnp.swapaxes(grad, 0, 1).reshape(rows, dp, parts * cols // dp)
        grad = jnp.swapaxes(grad, 0, 1)
    return lax.psum_scatter(
        grad.reshape(dp * rows, -1), AXES, scatter_dimension=0, tiled=True
    ).astype(F32)


def body(
    image_tokens,
    text_tokens,
    image_qkv,
    image_out,
    image_up,
    image_down,
    image_vectors,
    image_up_bias,
    text_qkv,
    text_out,
    text_up,
    text_down,
    text_vectors,
    text_up_bias,
    pair_counts,
    pair_groups,
):
    dp, fsdp = lax.axis_size("dp"), lax.axis_size("fsdp")
    devices = dp * fsdp
    cap, length, width = text_tokens.shape
    hidden = image_up.shape[1]
    pairs = pair_groups.shape[0]
    me = lax.axis_index("dp") * fsdp + lax.axis_index("fsdp")

    grid_mesh = (dp, fsdp) == (PX, PF)
    packed = gather_packed(text_qkv, text_out, text_up, text_down, dp, fsdp)
    part = width // fsdp
    small = jnp.concatenate([text_vectors, text_up_bias.reshape(8, -1)], axis=1)
    if grid_mesh:
        small = jnp.broadcast_to(small[None], (fsdp,) + small.shape)
        small = lax.all_to_all(small, "fsdp", 0, 0, tiled=True)
    else:
        small = lax.all_gather(small, "fsdp", axis=0)
    vec = jnp.swapaxes(small[:, :, :part], 0, 1).reshape(8, width)
    ub = small[:, :, part:].reshape(1, hidden)
    bits = [lax.shift_right_logical(me, k) & 1 for k in range(5)]
    where = jnp.stack([bits[4], bits[1], 2 * bits[3] + bits[2], bits[0]])
    where = where if grid_mesh else jnp.zeros_like(where)

    image_low = image_forward(
        image_tokens, image_qkv, image_out, image_up, image_down, image_vectors, image_up_bias
    )
    if grid_mesh:
        images = image_low
        for change in (dict(z=1), dict(z=2), dict(x=1), dict(y=1), dict(core=1)):
            images = jnp.concatenate([images, hop(images, **change)], axis=0)
        far = jnp.arange(devices, dtype=jnp.int32) ^ me
        bit = lambda k: lax.shift_right_logical(far, k) & 1
        order = bit(2) + 2 * bit(3) + 4 * bit(4) + 8 * bit(1) + 16 * bit(0)
        images = jnp.take(images.reshape(devices, cap, width), order, axis=0).reshape(pairs, width)
    else:
        images = lax.all_gather(image_low, AXES, axis=0, tiled=True)

    slots = jnp.arange(cap, dtype=jnp.int32)
    live = (slots[None, :] < pair_counts[:, None]).reshape(pairs).astype(F32)
    same = jnp.maximum(
        jnp.sum(jnp.where(pair_groups[:, None] == pair_groups[None, :], live[None, :], 0.0), axis=1), 1.0
    )
    own_of = lambda array: lax.dynamic_slice_in_dim(array, me * cap, cap)
    own = jnp.stack([own_of(live), own_of(same)], axis=1)
    own_group = own_of(pair_groups).reshape(cap, 1)
    live_row, same_row, group_row = (a.reshape(1, pairs) for a in (live, same, pair_groups))
    live_total = jnp.sum(pair_counts).astype(F32)
    factor = jnp.broadcast_to(LOSS_WEIGHT / (2.0 * live_total), (1, 128))

    tokens = text_tokens.reshape(cap * length, width)
    h1, qkv, att, r1, h2, slope, acts, pooled, power, row_part, col_sum, loss_part = text_forward(
        tokens, packed, vec, ub, images, live_row, same_row, group_row, own, own_group, length, hidden,
        devices if grid_mesh else 1,
    )
    if grid_mesh:
        row_all = lax.all_to_all(row_part, AXES, 0, 0, tiled=True)
    else:
        row_all = lax.psum(row_part, AXES)
    h1_t, h2_t, att_t = relative_rows(where, h1, h2, att)
    factors, *up_parts, bias_up, down_bias, dr1, dz, da, sums, loss_rows = back_one(
        where, power, row_all, col_sum, images, live_row, same_row, group_row, own, own_group, factor, pooled,
        packed, vec, slope, h2_t, r1, acts, length, (dp, fsdp),
    )
    dqkv, *att_parts, bias_sums = back_two(where, qkv, da, dz, h1_t, att_t, length)

    both = lax.all_to_all(factors, AXES, 0, 0, tiled=True).reshape(pairs, width // dp + hidden // fsdp)
    grad_down = dot(both[:, width // dp :], both[:, : width // dp], 0, 0)

    if grid_mesh:
        up_parts = core_step(up_parts, *att_parts)
        (att_keep,) = after((att_parts[0],), *up_parts)
        att_parts = core_step([att_keep] + att_parts[1:])
        (dqkv,) = after((dqkv,), *att_parts)
        dx, share = back_third(
            dr1, dqkv, tokens, packed, vec, sums, bias_sums, down_bias, bias_up, loss_part, (dp, fsdp)
        )
        up_parts = first_step(up_parts, dx)
        att_parts = first_step(att_parts, grad_down, *up_parts)
        up_parts = second_step(up_parts, *att_parts)
        (share,) = after((share,), *att_parts)
        att_parts = second_step(att_parts, *up_parts)
        (grad_up,) = third_step(up_parts, (hidden // dp,))
        grad_qkv, grad_out = third_step(att_parts, (3 * width // dp, width // dp))
    else:
        dx, share = back_third(
            dr1, dqkv, tokens, packed, vec, sums, bias_sums, down_bias, bias_up, loss_part, (dp, fsdp)
        )
        grad_attn = natural_grad(*att_parts)
        grad_up = scatter_columns(natural_grad(*up_parts), dp, fsdp)
        grad_qkv = scatter_columns(grad_attn[:, :, : 3 * width // PX], dp, fsdp)
        grad_out = scatter_columns(grad_attn[:, :, 3 * width // PX :], dp, fsdp)

    share = jnp.sum(lax.all_to_all(share, AXES, 0, 0, tiled=True), axis=0)
    grad_vec = share[:, :part]
    tall = hidden // fsdp // 8
    grad_bias = share[:, part : part + tall].reshape(hidden // fsdp)
    loss = (share[0, part + tall] + loss_rows[0, 0]) / (2.0 * live_total)

    return (
        loss,
        dx.reshape(text_tokens.shape),
        grad_qkv,
        grad_out,
        grad_up,
        grad_down,
        grad_vec,
        grad_bias,
    )


def solution(mesh):
    return jax.shard_map(
        body,
        mesh=mesh,
        in_specs=(
            P(AXES, None, None),
            P(AXES, None, None),
            P(),
            P(),
            P(),
            P(),
            P(),
            P(),
            P("fsdp", "dp"),
            P("fsdp", "dp"),
            P("fsdp", "dp"),
            P("fsdp", "dp"),
            P(None, "fsdp"),
            P("fsdp"),
            P(),
            P(),
        ),
        out_specs=(
            P(),
            P(AXES, None, None),
            P("fsdp", "dp"),
            P("fsdp", "dp"),
            P("fsdp", "dp"),
            P("fsdp", "dp"),
            P(None, "fsdp"),
            P("fsdp"),
        ),
        check_vma=False,
    )
```

```python
import functools

import jax
import jax.numpy as jnp
from jax import lax
from jax.experimental import pallas as pl
from jax.experimental.pallas import tpu as pltpu
from jax.sharding import PartitionSpec as P

HEAD_DIM = 64
LOGIT_SCALE = 50.0
LOSS_WEIGHT = 32768.0
BF = jnp.bfloat16
F32 = jnp.float32
AXES = ("dp", "fsdp")
PX, PF = 2, 16

ANY = pl.BlockSpec(memory_space=pltpu.HBM)
WHOLE = pl.BlockSpec(memory_space=pltpu.VMEM)


def params(mebibytes=62):
    return pltpu.CompilerParams(vmem_limit_bytes=mebibytes * 1024 * 1024)


def dot(a, b, ca=1, cb=0):
    return lax.dot_general(a, b, (((ca,), (cb,)), ((), ())), preferred_element_type=F32)


def repeat(count, step, together=1):
    def turn(j, _):
        for k in range(together):
            step(j * together + k)
        return 0

    if together >= count:
        for i in range(count):
            step(i)
    else:
        lax.fori_loop(0, count // together, turn, 0)


def move(pairs, sem, base=0):
    copies = [pltpu.make_async_copy(a, b, sem.at[base + i]) for i, (a, b) in enumerate(pairs)]
    for copy in copies:
        copy.start()
    return copies


def normalize(values):
    centered = values - jnp.mean(values, axis=-1, keepdims=True)
    inverse = lax.rsqrt(jnp.mean(centered * centered, axis=-1, keepdims=True) + 1e-05)
    return centered * inverse, inverse


def norm_back(grad, hat, inverse, gain):
    scaled = grad * gain
    return inverse * (
        scaled
        - jnp.mean(scaled, axis=-1, keepdims=True)
        - hat * jnp.mean(scaled * hat, axis=-1, keepdims=True)
    )


def gauss_tail(u):
    size = jnp.abs(u)
    t = 1.0 / (1.0 + (0.3275911 * 0.7071067811865476) * size)
    bell = jnp.exp(-0.5 * (u * u))
    poly = 0.5 * 1.061405429 * t - 0.5 * 1.453152027
    poly = poly * t + 0.5 * 1.421413741
    poly = poly * t - 0.5 * 0.284496736
    poly = poly * t + 0.5 * 0.254829592
    return poly * t * bell, bell, size


def head_pair(block, low_lane):
    zero = jnp.zeros_like(block)
    return jnp.concatenate(
        [jnp.where(low_lane, block, zero), jnp.where(low_lane, zero, block)], axis=0
    )


def softmax_half(scores, bias):
    scores = scores + bias
    top = jnp.max(scores, axis=-1, keepdims=True)
    powers = jnp.exp(scores - top)
    return powers * (1.0 / jnp.sum(powers, axis=-1, keepdims=True))


def unit_rows(pooled):
    return pooled * lax.rsqrt(jnp.sum(pooled * pooled, axis=-1, keepdims=True) + 1e-06)


def mean_down(total, count, down):
    mean = total * (1.0 / count)
    high = mean.astype(BF)
    low = (mean - high.astype(F32)).astype(BF)
    both = dot(jnp.concatenate([high, low], axis=0), down)
    return both[: mean.shape[0]] + both[mean.shape[0] :]


def image_kernel(
    tok, wq_h, wo_h, wu_h, wd_h, vec, ub, out, wq, wo, wu, wd, x, h, qkv, att, act_sum, r1_sum, bias_row, stage, sem
):
    step, steps = pl.program_id(0), pl.num_programs(0)
    length, group, width = tok.shape
    rows = group * length
    hidden = wu.shape[1]
    copies = [
        pltpu.make_async_copy(src, dst, sem.at[i])
        for i, (src, dst) in enumerate(((wq_h, wq), (wo_h, wo), (wu_h, wu), (wd_h, wd)))
    ]

    @pl.when(step == 0)
    def _():
        for copy in copies:
            copy.start()

    def arrived(i):
        @pl.when(step == 0)
        def _():
            copies[i].wait()

    v = vec[...].astype(F32)
    bias_row[:, :width] = v[2:3]
    bias_row[:, width : 2 * width] = jnp.zeros((1, width), F32)
    bias_row[:, 2 * width :] = v[3:4]
    for k in range(width // 128):
        stage[k] = tok[:, :, k * 128 : (k + 1) * 128].astype(F32).reshape(rows, 128)
        for i in range(group):
            x[pl.ds(i * length, length), k * 128 : (k + 1) * 128] = stage[k, pl.ds(i, length, stride=group), :]

    def norm_rows(gain, shift):
        blk = 80

        def one(i):
            at = pl.ds(pl.multiple_of(i * blk, blk), blk)
            hat, _ = normalize(x[at, :])
            h[at, :] = (hat * gain + shift).astype(BF)

        repeat(rows // blk, one, 5)

    norm_rows(v[0:1], v[1:2])
    arrived(0)

    def project(i):
        at = pl.ds(pl.multiple_of(i * 256, 256), 256)
        qkv[:, at] = (dot(h[...], wq[:, at]) + bias_row[:, at]).astype(BF)

    repeat(3 * width // 256, project, 3)

    wins = rows // (2 * length)
    q_len = 112
    low_lane = lax.broadcasted_iota(jnp.int32, (128, 128), 1) < HEAD_DIM
    cols = range(0, width, 128)

    def window(w):
        q_at = pl.multiple_of((2 * length * w) // 16 * 16, 16)
        k_at = pl.multiple_of(jnp.minimum(q_at, rows - 128), 16)
        lo, mid, hi = 2 * w * length, (2 * w + 1) * length, (2 * w + 2) * length
        qi = q_at + lax.broadcasted_iota(jnp.int32, (q_len, 128), 0)
        ki = k_at + lax.broadcasted_iota(jnp.int32, (q_len, 128), 1)
        first = (qi >= lo) & (qi < mid) & (ki >= lo) & (ki < mid)
        second = (qi >= mid) & (qi < hi) & (ki >= mid) & (ki < hi)
        bias = jnp.where(first | second, 0.0, -1e30)
        q_rows, k_rows = pl.ds(q_at, q_len), pl.ds(k_at, 128)
        q2 = [qkv[q_rows, c : c + 128] * 0.125 for c in cols]
        k2 = [head_pair(qkv[k_rows, width + c : width + c + 128], low_lane) for c in cols]
        v2 = [head_pair(qkv[k_rows, 2 * width + c : 2 * width + c + 128], low_lane) for c in cols]
        scores = [dot(q, k, 1, 1) for q, k in zip(q2, k2)]
        probs = [
            jnp.concatenate(
                [softmax_half(s[:, :128], bias).astype(BF), softmax_half(s[:, 128:], bias).astype(BF)],
                axis=1,
            )
            for s in scores
        ]
        mine = (q_at + lax.broadcasted_iota(jnp.int32, (16, 128), 0)) >= lo
        for c, p, values in zip(cols, probs, v2):
            mixed = dot(p, values)
            old = att[pl.ds(q_at, 16), c : c + 128].astype(F32)
            att[pl.ds(q_at, 16), c : c + 128] = jnp.where(mine, mixed[:16], old).astype(BF)
            att[pl.ds(q_at + 16, q_len - 16), c : c + 128] = mixed[16:].astype(BF)

    repeat(wins, window, 2)

    arrived(1)
    for c in range(0, width, 256):
        x[:, c : c + 256] = x[:, c : c + 256] + (dot(att[...], wo[:, c : c + 256]) + v[4:5, c : c + 256])
    norm_rows(v[5:6], v[6:7])

    def image_sums(values):
        sums = []
        for i in range(group):
            lo, hi = i * length, (i + 1) * length
            a, b = lo // 8 * 8, -(-hi // 8) * 8
            part = values[a:b]
            row = a + lax.broadcasted_iota(jnp.int32, (b - a, 1), 0)
            if lo % 8 or hi % 8:
                part = jnp.where((row >= lo) & (row < hi), part, 0.0)
            sums.append(jnp.sum(part, axis=0, keepdims=True))
        return jnp.concatenate(sums, axis=0)

    place = pl.ds(pl.multiple_of(step * group, group), group)
    for c in range(0, width, 256):
        r1_sum[place, c : c + 256] = image_sums(x[:, c : c + 256])
    arrived(2)

    def expand(i):
        at = pl.ds(pl.multiple_of(i * 256, 256), 256)
        u = dot(h[...], wu[:, at]) + ub[:, at].astype(F32)
        tail, _, size = gauss_tail(u)
        act_sum[place, at] = image_sums(jnp.maximum(u, 0.0) - size * tail)

    repeat(hidden // 256, expand, 3)
    arrived(3)

    @pl.when(step == steps - 1)
    def _():
        pooled = r1_sum[...] * (1.0 / length) + mean_down(act_sum[...], length, wd[...]) + v[7:8]
        out[...] = unit_rows(pooled).astype(BF)


def image_forward(tokens, wq, wo, wu, wd, vec, ub):
    pairs, length, width = tokens.shape
    hidden = wu.shape[1]
    group = 16
    rows = group * length
    return pl.pallas_call(
        image_kernel,
        name="image_forward",
        grid=(pairs // group,),
        in_specs=[
            pl.BlockSpec((length, group, width), lambda i: (0, i, 0)),
            ANY,
            ANY,
            ANY,
            ANY,
            pl.BlockSpec((8, width), lambda i: (0, 0)),
            pl.BlockSpec((1, hidden), lambda i: (0, 0)),
        ],
        out_specs=pl.BlockSpec((pairs, width), lambda i: (0, 0)),
        out_shape=jax.ShapeDtypeStruct((pairs, width), BF),
        scratch_shapes=[
            pltpu.VMEM((width, 3 * width), BF),
            pltpu.VMEM((width, width), BF),
            pltpu.VMEM((width, hidden), BF),
            pltpu.VMEM((hidden, width), BF),
            pltpu.VMEM((rows, width), F32),
            pltpu.VMEM((rows, width), BF),
            pltpu.VMEM((rows, 3 * width), BF),
            pltpu.VMEM((rows, width), BF),
            pltpu.VMEM((pairs, hidden), F32),
            pltpu.VMEM((pairs, width), F32),
            pltpu.VMEM((1, 3 * width), F32),
            pltpu.VMEM((width // 128, rows, 128), F32),
            pltpu.SemaphoreType.DMA((4,)),
        ],
        compiler_params=params(),
        cost_estimate=pl.CostEstimate(
            flops=2 * pairs * length * width * (4 * width + hidden),
            bytes_accessed=2 * (4 * width * width + 2 * width * hidden + pairs * length * width),
            transcendentals=pairs * length * hidden,
        ),
    )(jnp.swapaxes(tokens, 0, 1), wq, wo, wu, wd, vec, ub.reshape(1, hidden))


def pack_rows(width, hidden):
    piece, rows = width // PX, width // PF
    return piece, rows, hidden // PF


def weight_copies(packed, which, dst, sem, base, width, hidden):
    piece, rows, frows = pack_rows(width, hidden)
    q_pieces, u_pieces = 3, hidden // width
    spans = {
        "qkv": (0, q_pieces, rows),
        "out": (q_pieces * rows, 1, rows),
        "up": ((q_pieces + 1) * rows, u_pieces, rows),
        "down": ((q_pieces + 1 + u_pieces) * rows, 1, frows),
    }
    start, count, tall = spans[which]
    copies = []
    for x in range(PX):
        for p in range(count):
            copies.append(
                pltpu.make_async_copy(
                    packed.at[pl.ds(x * PF, PF), pl.ds(start + p * tall, tall), :],
                    dst.at[:, :, pl.ds((x * count + p) * piece, piece)],
                    sem.at[base + len(copies)],
                )
            )
    return copies


def natural(ref):
    blocks, rows, cols = ref.shape
    return ref[...].reshape(blocks * rows, cols)


def weight_scratch(which, width, hidden):
    rows, frows = width // PF, hidden // PF
    shape = {
        "qkv": (PF, rows, 3 * width),
        "out": (PF, rows, width),
        "up": (PF, rows, hidden),
        "down": (PF, frows, width),
    }[which]
    return pltpu.VMEM(shape, BF)


def contrast(low, images, live, same, groups, own, own_group, power, row_part, col_sum, loss_part):
    scores = LOGIT_SCALE * dot(low, images[...], 1, 1)
    exps = jnp.exp(scores)
    live_own, same_own = own[:, 0:1], own[:, 1:2]
    power[...] = exps
    rows = jnp.sum(exps * live_own, axis=0, keepdims=True)
    tiled = jnp.concatenate(
        [rows[:, k * 128 : (k + 1) * 128] for k in range(rows.shape[1] // 128)], axis=0
    )
    for d in range(row_part.shape[0]):
        row_part[d] = tiled
    cols = jnp.sum(exps * live[...], axis=1, keepdims=True)
    col_sum[...] = cols
    pair = jnp.where(own_group[...] == groups[...], live_own * live[...], 0.0)
    linear = pair * scores * (1.0 / same_own + 1.0 / same[...])
    losses = live_own * jnp.log(cols) - jnp.sum(linear, axis=1, keepdims=True)
    loss_part[...] = jnp.broadcast_to(jnp.sum(losses, axis=0, keepdims=True), loss_part.shape)


def text_mask(size, length):
    row = lax.broadcasted_iota(jnp.int32, (size, size), 0) // length
    col = lax.broadcasted_iota(jnp.int32, (size, size), 1) // length
    return jnp.where(row == col, 0.0, -1e30)


def text_forward_kernel(
    length, tok, packed, vec, ub, images_i, live, same, groups, own, own_group,
    h1_o, qkv_o, att_o, r1_o, h2_o, slope_o, acts, pooled_out, power, row_part, col_sum, loss_part,
    wq, wo, wu, wd, total, bias_row, h1, qkv, att, r1, h2, slope, sem, images, out_sem
):
    rows, width = tok.shape
    hidden = slope.shape[1]
    texts = rows // length
    load = {}
    base = 0
    for which, dst in (("qkv", wq), ("out", wo), ("up", wu), ("down", wd)):
        load[which] = weight_copies(packed, which, dst, sem, base, width, hidden)
        base += len(load[which])
        for copy in load[which]:
            copy.start()
    v = vec[...].astype(F32)
    bias_row[:, :width] = v[2:3]
    bias_row[:, width : 2 * width] = jnp.zeros((1, width), F32)
    bias_row[:, 2 * width :] = v[3:4]
    blk = 128

    def norm_rows(src, dst, gain, shift):
        def one(i):
            at = pl.ds(pl.multiple_of(i * blk, blk), blk)
            hat, _ = normalize(src[at, :].astype(F32))
            dst[at, :] = (hat * gain + shift).astype(BF)

        repeat(rows // blk, one, 2)

    norm_rows(tok, h1, v[0:1], v[1:2])
    saves = move([(h1, h1_o)], out_sem)
    (gathered,) = move([(images_i, images)], out_sem, 6)
    for copy in load["qkv"]:
        copy.wait()

    def project(i):
        at = pl.ds(pl.multiple_of(i * 256, 256), 256)
        qkv[:, at] = (dot(h1[...], wq[:, :, at].reshape(width, 256)) + bias_row[:, at]).astype(BF)

    repeat(3 * width // 256, project, 3)
    saves += move([(qkv, qkv_o)], out_sem, 1)
    low_lane = lax.broadcasted_iota(jnp.int32, (blk, 128), 1) < HEAD_DIM
    bias = text_mask(blk, length)
    cols = range(0, width, 128)

    def attend(i):
        at = pl.ds(pl.multiple_of(i * blk, blk), blk)
        q2 = [qkv[at, c : c + 128] * 0.125 for c in cols]
        k2 = [head_pair(qkv[at, width + c : width + c + 128], low_lane) for c in cols]
        v2 = [head_pair(qkv[at, 2 * width + c : 2 * width + c + 128], low_lane) for c in cols]
        scores = [dot(q, k, 1, 1) for q, k in zip(q2, k2)]
        probs = [
            jnp.concatenate(
                [softmax_half(s[:, :blk], bias).astype(BF), softmax_half(s[:, blk:], bias).astype(BF)],
                axis=1,
            )
            for s in scores
        ]
        for c, p, values in zip(cols, probs, v2):
            att[at, c : c + 128] = dot(p, values).astype(BF)

    repeat(rows // blk, attend, 2)
    saves += move([(att, att_o)], out_sem, 2)
    for copy in load["out"]:
        copy.wait()
    for c in range(0, width, 256):
        r1[:, c : c + 256] = tok[:, c : c + 256].astype(F32) + (
            dot(att[...], wo[:, :, c : c + 256].reshape(width, 256)) + v[4:5, c : c + 256]
        )
    saves += move([(r1, r1_o)], out_sem, 3)
    norm_rows(r1, h2, v[5:6], v[6:7])
    saves += move([(h2, h2_o)], out_sem, 4)
    for copy in load["up"]:
        copy.wait()

    def expand(i):
        at = pl.ds(pl.multiple_of(i * 256, 256), 256)
        u = dot(h2[...], wu[:, :, at].reshape(width, 256)) + ub[:, at].astype(F32)
        tail, bell, size = gauss_tail(u)
        act = jnp.maximum(u, 0.0) - size * tail
        phi = jnp.where(u >= 0.0, 1.0 - tail, tail)
        slope[:, at] = (phi + u * (bell * 0.3989422804014327)).astype(BF)
        sums = jnp.sum(act.reshape(texts, length, 256), axis=1)
        total[:, at] = sums
        acts[:, at] = sums.astype(BF)

    repeat(hidden // 256, expand, 3)
    saves += move([(slope, slope_o)], out_sem, 5)
    for copy in load["down"]:
        copy.wait()
    mean_r1 = jnp.sum(r1[...].reshape(texts, length, width), axis=1) * (1.0 / length)
    pooled = mean_r1 + mean_down(total[...], length, natural(wd)) + v[7:8]
    pooled_out[...] = pooled
    gathered.wait()
    contrast(
        unit_rows(pooled).astype(BF), images, live, same, groups, own, own_group, power, row_part, col_sum, loss_part
    )
    for copy in saves:
        copy.wait()


def text_forward(
    tokens, packed, vec, ub, images, live, same, groups, own, own_group, length, hidden, copies_of
):
    rows, width = tokens.shape
    texts = rows // length
    pairs = images.shape[0]
    shape = jax.ShapeDtypeStruct
    copies = PX * (3 + 1 + hidden // width + 1)
    return pl.pallas_call(
        functools.partial(text_forward_kernel, length),
        name="text_forward",
        in_specs=[WHOLE, ANY, WHOLE, WHOLE, ANY] + [WHOLE] * 5,
        out_specs=[ANY] * 6 + [WHOLE] * 6,
        out_shape=[
            shape((rows, width), BF),
            shape((rows, 3 * width), BF),
            shape((rows, width), BF),
            shape((rows, width), F32),
            shape((rows, width), BF),
            shape((rows, hidden), BF),
            shape((texts, hidden), BF),
            shape((texts, width), F32),
            shape((texts, pairs), F32),
            shape((copies_of, pairs // 128, 128), F32),
            shape((texts, 1), F32),
            shape((8, 128), F32),
        ],
        scratch_shapes=[weight_scratch(w, width, hidden) for w in ("qkv", "out", "up", "down")]
        + [
            pltpu.VMEM((texts, hidden), F32),
            pltpu.VMEM((1, 3 * width), F32),
            pltpu.VMEM((rows, width), BF),
            pltpu.VMEM((rows, 3 * width), BF),
            pltpu.VMEM((rows, width), BF),
            pltpu.VMEM((rows, width), F32),
            pltpu.VMEM((rows, width), BF),
            pltpu.VMEM((rows, hidden), BF),
            pltpu.SemaphoreType.DMA((copies,)),
            pltpu.VMEM((pairs, width), BF),
            pltpu.SemaphoreType.DMA((7,)),
        ],
        compiler_params=params(),
        cost_estimate=pl.CostEstimate(
            flops=2 * rows * width * (4 * width + hidden),
            bytes_accessed=2 * (4 * width * width + 2 * width * hidden + 12 * rows * width),
            transcendentals=rows * hidden,
        ),
    )(tokens, packed, vec, ub, images, live, same, groups, own, own_group)


def relative_kernel(where, h1_i, h2_i, att_i, h1_o, h2_o, att_o, h1, h2, att, h1_t, h2_t, att_t, sem):
    width = h1.shape[1]
    block = width // PF
    my, mz, mc = where[1], where[2], where[3]
    loads = move([(h2_i, h2), (h1_i, h1), (att_i, att)], sem)
    saves = []
    for n, (src, dst, out) in enumerate(((h2, h2_t, h2_o), (h1, h1_t, h1_o), (att, att_t, att_o))):
        loads[n].wait()
        turned = src[...].T
        for z in range(4):
            for y in range(2):
                for c in range(2):
                    f = (z * 2 + y) * 2 + c
                    place = (((c ^ mc) * 2 + (y ^ my)) * 4 + (z ^ mz)) * block
                    dst[pl.ds(pl.multiple_of(place, block), block), :] = turned[
                        f * block : (f + 1) * block
                    ]
        saves += move([(dst, out)], sem, 3 + n)
    for copy in saves:
        copy.wait()


SMEM = pl.BlockSpec(memory_space=pltpu.SMEM)


def relative_rows(where, h1, h2, att):
    rows, width = h1.shape
    return pl.pallas_call(
        relative_kernel,
        name="relative_rows",
        in_specs=[SMEM, ANY, ANY, ANY],
        out_specs=[ANY] * 3,
        out_shape=[jax.ShapeDtypeStruct((width, rows), BF)] * 3,
        scratch_shapes=[pltpu.VMEM((rows, width), BF)] * 3
        + [pltpu.VMEM((width, rows), BF)] * 3
        + [pltpu.SemaphoreType.DMA((6,))],
        compiler_params=params(),
        cost_estimate=pl.CostEstimate(flops=0, bytes_accessed=12 * rows * width, transcendentals=0),
    )(where, h1, h2, att)


def grad_shapes(width):
    block, half = width // PF, width
    return [jax.ShapeDtypeStruct((2, 2, 4, block, half), BF)] * 4


def put_grad(values, outs, x_rel, at, second):
    width, cols = values.shape
    block = width // PF
    low = values.astype(BF)
    for c in range(2):
        for y in range(2):
            piece = low[(c * 2 + y) * 4 * block : (c * 2 + y + 1) * 4 * block].reshape(4, block, cols)
            if second:
                outs[2 + c, y, x_rel, :, :, pl.ds(at, cols)] = piece
            else:
                outs[c, x_rel, y, :, :, pl.ds(at, cols)] = piece


def start_grads(parts, outs, sem, x):
    return move(
        [(parts.at[n, x], outs[n].at[x]) for n in range(2)]
        + [(parts.at[n, :, x], outs[n].at[:, x]) for n in range(2, 4)],
        sem,
        4 * x,
    )


def back_one_kernel(
    length, shard,
    where, power, row_all, col_sum, images_i, live, same, groups, own, own_group, factor, pooled, packed, vec,
    slope_i, h2_i, r1_i, acts,
    factors_o, keep_a, send_a, keep_b, send_b, bias_up, down_bias, dr1_o, dz_o, da_o, sums, loss_rows,
    factors, wd, wu, wo, dact, images, slope, h2_t, r1, du, dr1, dz_s, da_s, dy, parts, sem, in_sem, out_sem,
):
    rows, hidden = slope.shape
    texts = rows // length
    width = h2_t.shape[0]
    (gathered,) = move([(images_i, images)], in_sem)
    down = weight_copies(packed, "down", wd, sem, 0, width, hidden)
    up = weight_copies(packed, "up", wu, sem, len(down), width, hidden)
    out = weight_copies(packed, "out", wo, sem, len(down) + len(up), width, hidden)
    for copy in down:
        copy.start()
    saved = move([(slope_i, slope), (h2_i, h2_t)], in_sem, 1)
    for copy in up + out:
        copy.start()
    saved += move([(r1_i, r1)], in_sem, 3)
    totals = jnp.sum(row_all[...], axis=0)
    row_sum = jnp.concatenate([totals[k : k + 1] for k in range(totals.shape[0])], axis=1)
    live_own, same_own = own[:, 0:1], own[:, 1:2]
    pair = factor[0:1, 0:1] * live_own * live[...]
    match = jnp.where(own_group[...] == groups[...], 1.0 / same_own + 1.0 / same[...], 0.0)
    grad_scores = pair * (power[...] * (1.0 / row_sum + 1.0 / col_sum[...]) - match)
    gathered.wait()
    grad_low = LOGIT_SCALE * dot(grad_scores.astype(BF), images[...])
    pool = pooled[...]
    inverse = lax.rsqrt(jnp.sum(pool * pool, axis=-1, keepdims=True) + 1e-06)
    along = jnp.sum(pool * grad_low, axis=-1, keepdims=True)
    dy[...] = inverse * (grad_low - pool * (inverse * inverse * along)) * (1.0 / length)
    dm = dy[...].astype(BF)
    loss_rows[...] = jnp.broadcast_to(
        jnp.sum(live[...] * jnp.log(row_sum), axis=1, keepdims=True), loss_rows.shape
    )
    parts_x, parts_f = shard
    piece_x, piece_f = width // parts_x, hidden // parts_f
    for f in range(parts_f):
        left = acts[:, f * piece_f : (f + 1) * piece_f]
        for x in range(parts_x):
            factors[x * parts_f + f, :, piece_x:] = left
            factors[x * parts_f + f, :, :piece_x] = dm[:, x * piece_x : (x + 1) * piece_x]
    sent = move([(factors, factors_o)], out_sem, 11)
    down_bias[...] = length * jnp.sum(dm.astype(F32), axis=0, keepdims=True)
    for copy in down:
        copy.wait()
    dact[...] = dot(dm, natural(wd), 1, 1)
    saved[0].wait()

    def slopes(i):
        at = pl.ds(pl.multiple_of(i * 256, 256), 256)
        spread = jnp.broadcast_to(dact[:, at].reshape(texts, 1, 256), (texts, length, 256))
        part = (spread.reshape(rows, 256) * slope[:, at].astype(F32)).astype(BF)
        du[:, at] = part
        bias_up[:, at] = jnp.sum(part.astype(F32), axis=0, keepdims=True)

    repeat(hidden // 256, slopes, 3)
    saved[1].wait()
    half = hidden // PX
    outs = (keep_a, send_a, keep_b, send_b)
    for x in range(PX):
        first = (x ^ where[0]) * half

        def grads(i):
            c = pl.multiple_of(i * 256, 256)
            for second in range(2):
                part = du[:, pl.ds(pl.multiple_of(first + c + second * width, 256), 256)]
                put_grad(dot(h2_t[...], part), parts, x, c, second)

        repeat(width // 256, grads)
        sent += start_grads(parts, outs, out_sem, x)

    v = vec[...].astype(F32)
    blk = 128
    for copy in up:
        copy.wait()

    def product(i):
        at = pl.ds(pl.multiple_of(i * (rows // 2), rows // 2), rows // 2)
        dr1[at, :] = dot(du[at, :], natural(wu), 1, 1)

    repeat(2, product)
    sums[...] = jnp.zeros((8, width), F32)
    some = blk // length
    saved[2].wait()

    def back(i):
        at = pl.ds(pl.multiple_of(i * blk, blk), blk)
        hat, inverse = normalize(r1[at, :])
        grad = dr1[at, :]
        sums[1:2, :] += jnp.sum(grad * hat, axis=0, keepdims=True)
        sums[2:3, :] += jnp.sum(grad, axis=0, keepdims=True)
        spread = jnp.broadcast_to(
            dy[pl.ds(pl.multiple_of(i * some, some), some), :].reshape(some, 1, width), (some, length, width)
        ).reshape(blk, width)
        grad = spread + norm_back(grad, hat, inverse, v[5:6])
        dr1[at, :] = grad
        low = grad.astype(BF)
        dz_s[at, :] = low
        sums[0:1, :] += jnp.sum(low.astype(F32), axis=0, keepdims=True)

    repeat(rows // blk, back, 2)
    sent += move([(dr1, dr1_o), (dz_s, dz_o)], out_sem, 8)
    for copy in out:
        copy.wait()
    da_s[...] = dot(dz_s[...], natural(wo), 1, 1).astype(BF)
    sent += move([(da_s, da_o)], out_sem, 10)
    for copy in sent:
        copy.wait()


def back_one(
    where, power, row_all, col_sum, images, live, same, groups, own, own_group, factor, pooled, packed, vec, slope,
    h2_t, r1, acts, length, shard,
):
    rows, hidden = slope.shape
    width = h2_t.shape[0]
    texts = rows // length
    payload = (shard[0] * shard[1], texts, width // shard[0] + hidden // shard[1])
    shape = jax.ShapeDtypeStruct
    return pl.pallas_call(
        functools.partial(back_one_kernel, length, shard),
        name="back_one",
        in_specs=[SMEM] + [WHOLE] * 3 + [ANY] + [WHOLE] * 7 + [ANY, WHOLE, ANY, ANY, ANY, WHOLE],
        out_specs=[ANY] * 5 + [WHOLE] * 2 + [ANY] * 3 + [WHOLE] * 2,
        out_shape=[
            shape(payload, BF),
            *grad_shapes(width),
            shape((1, hidden), F32),
            shape((1, width), F32),
            shape((rows, width), F32),
            shape((rows, width), BF),
            shape((rows, width), BF),
            shape((8, width), F32),
            shape((8, 128), F32),
        ],
        scratch_shapes=[
            pltpu.VMEM(payload, BF),
            weight_scratch("down", width, hidden),
            weight_scratch("up", width, hidden),
            weight_scratch("out", width, hidden),
            pltpu.VMEM((texts, hidden), F32),
            pltpu.VMEM(images.shape, BF),
            pltpu.VMEM((rows, hidden), BF),
            pltpu.VMEM((width, rows), BF),
            pltpu.VMEM((rows, width), F32),
            pltpu.VMEM((rows, hidden), BF),
            pltpu.VMEM((rows, width), F32),
            pltpu.VMEM((rows, width), BF),
            pltpu.VMEM((rows, width), BF),
            pltpu.VMEM((texts, width), F32),
            pltpu.VMEM((4,) + grad_shapes(width)[0].shape, BF),
            pltpu.SemaphoreType.DMA((PX * (2 + hidden // width),)),
            pltpu.SemaphoreType.DMA((4,)),
            pltpu.SemaphoreType.DMA((12,)),
        ],
        compiler_params=params(),
        cost_estimate=pl.CostEstimate(
            flops=2 * rows * width * (2 * hidden + width), bytes_accessed=16 * width * hidden, transcendentals=0
        ),
    )(
        where, power, row_all, col_sum, images, live, same, groups, own, own_group, factor, pooled, packed, vec,
        slope, h2_t, r1, acts,
    )


def back_two_kernel(
    length, where, qkv_i, da_i, dz_i, h1_i, att_i, dqkv_o, keep_a, send_a, keep_b, send_b, sums,
    qkv, da_s, dz, h1_t, att_t, dqkv, parts, sem, out_sem,
):
    rows, width = da_s.shape
    blk = 128
    loads = move([(qkv_i, qkv), (da_i, da_s), (att_i, att_t), (dz_i, dz), (h1_i, h1_t)], sem)
    for copy in loads[:2]:
        copy.wait()
    low_lane = lax.broadcasted_iota(jnp.int32, (blk, 128), 1) < HEAD_DIM
    bias = text_mask(blk, length)
    cols = range(0, width, 128)
    def group(i):
        at = pl.ds(pl.multiple_of(i * blk, blk), blk)
        take = lambda base, c: qkv[at, base + c : base + c + 128]
        q2 = [take(0, c) * 0.125 for c in cols]
        k2 = [head_pair(take(width, c), low_lane) for c in cols]
        v2 = [head_pair(take(2 * width, c), low_lane) for c in cols]
        da = [da_s[at, c : c + 128] for c in cols]
        scores = [dot(k, q, 1, 1) for k, q in zip(k2, q2)]
        grads = [dot(v, d, 1, 1) for v, d in zip(v2, da)]
        probs, deltas = [], []
        for score, grad in zip(scores, grads):
            p_low, d_low = [], []
            for half in range(2):
                s = score[half * blk : (half + 1) * blk] + bias
                g = grad[half * blk : (half + 1) * blk]
                powers = jnp.exp(s - jnp.max(s, axis=0, keepdims=True))
                soft = powers * (1.0 / jnp.sum(powers, axis=0, keepdims=True))
                p_low.append(soft.astype(BF))
                d_low.append((soft * (g - jnp.sum(g * soft, axis=0, keepdims=True))).astype(BF))
            probs.append(jnp.concatenate(p_low, axis=0))
            deltas.append(jnp.concatenate(d_low, axis=0))
        for n, c in enumerate(cols):
            dq = dot(deltas[n], k2[n], 0, 0) * 0.125
            dk = dot(deltas[n], q2[n])
            dv = dot(probs[n], da[n])
            dqkv[at, c : c + 128] = dq.astype(BF)
            dqkv[at, width + c : width + c + 128] = jnp.where(
                low_lane, dk[:blk], dk[blk:]
            ).astype(BF)
            dqkv[at, 2 * width + c : 2 * width + c + 128] = jnp.where(
                low_lane, dv[:blk], dv[blk:]
            ).astype(BF)

    repeat(rows // blk, group, 2)
    sums[0:1, :] = jnp.sum(dqkv[:, :width].astype(F32), axis=0, keepdims=True)
    sums[1:2, :] = jnp.sum(dqkv[:, 2 * width :].astype(F32), axis=0, keepdims=True)
    sums[2:8, :] = jnp.zeros((6, width), F32)
    sent = move([(dqkv, dqkv_o)], out_sem, 8)
    for copy in loads[2:]:
        copy.wait()
    piece = width // PX
    outs = (keep_a, send_a, keep_b, send_b)
    for x in range(PX):
        other = x ^ where[0]
        first = other * (3 * piece)

        def chunk(i):
            c = pl.multiple_of(i * 256, 256)
            part = dqkv[:, pl.ds(pl.multiple_of(first + c, 128), 256)]
            put_grad(dot(h1_t[...], part), parts, x, c, 0)

        repeat(width // 256, chunk)
        part = dqkv[:, pl.ds(pl.multiple_of(first + width, 128), piece)]
        put_grad(dot(h1_t[...], part), parts, x, 0, 1)
        part = dz[:, pl.ds(pl.multiple_of(other * piece, 128), piece)]
        put_grad(dot(att_t[...], part), parts, x, piece, 1)
        sent += start_grads(parts, outs, out_sem, x)
    for copy in sent:
        copy.wait()


def back_two(where, qkv, da, dz, h1_t, att_t, length):
    rows, width = da.shape
    shape = jax.ShapeDtypeStruct
    return pl.pallas_call(
        functools.partial(back_two_kernel, length),
        name="back_two",
        in_specs=[SMEM] + [ANY] * 5,
        out_specs=[ANY] * 5 + [WHOLE],
        out_shape=[shape((rows, 3 * width), BF), *grad_shapes(width), shape((8, width), F32)],
        scratch_shapes=[
            pltpu.VMEM((rows, 3 * width), BF),
            pltpu.VMEM((rows, width), BF),
            pltpu.VMEM((rows, width), BF),
            pltpu.VMEM((width, rows), BF),
            pltpu.VMEM((width, rows), BF),
            pltpu.VMEM((rows, 3 * width), BF),
            pltpu.VMEM((4,) + grad_shapes(width)[0].shape, BF),
            pltpu.SemaphoreType.DMA((5,)),
            pltpu.SemaphoreType.DMA((9,)),
        ],
        compiler_params=params(),
        cost_estimate=pl.CostEstimate(
            flops=2 * rows * width * (1280 + 4 * width), bytes_accessed=20 * rows * width, transcendentals=rows * width
        ),
    )(where, qkv, da, dz, h1_t, att_t)


def back_third_kernel(
    parts_f, dr1_i, dqkv_i, tok_i, packed, vec, sums, bias_sums, down_bias, bias_up, loss_part, dx_o, share, all_sums, wq, dr1, tok, dx, sem, dqkv, own_sem
):
    rows, width = tok.shape
    loads = weight_copies(packed, "qkv", wq, sem, 0, width, width)
    for copy in loads:
        copy.start()
    saved = move([(dqkv_i, dqkv), (dr1_i, dr1), (tok_i, tok)], own_sem)
    saved[0].wait()
    v = vec[...].astype(F32)
    for copy in loads:
        copy.wait()
    half = rows // 2

    def product(i):
        at = pl.ds(pl.multiple_of(i * half, half), half)
        dx[at, :] = dot(dqkv[at, :], natural(wq), 1, 1)

    repeat(2, product)
    for copy in saved[1:]:
        copy.wait()
    all_sums[0:2, :] = jnp.zeros((2, width), F32)
    blk = 128

    def back(i):
        at = pl.ds(pl.multiple_of(i * blk, blk), blk)
        hat, inverse = normalize(tok[at, :].astype(F32))
        grad = dx[at, :]
        all_sums[0:1, :] += jnp.sum(grad * hat, axis=0, keepdims=True)
        all_sums[1:2, :] += jnp.sum(grad, axis=0, keepdims=True)
        dx[at, :] = dr1[at, :] + norm_back(grad, hat, inverse, v[0:1])

    repeat(rows // blk, back, 2)
    (save,) = move([(dx, dx_o)], own_sem, 3)
    all_sums[2:4, :] = bias_sums[0:2, :]
    all_sums[4:7, :] = sums[0:3, :]
    all_sums[7:8, :] = down_bias[...]
    every = all_sums[...]
    piece, tall = width // parts_f, bias_up.shape[1] // parts_f
    devices = share.shape[0]
    used = piece + tall // 8
    for f in range(parts_f):
        bias = bias_up[:, f * tall : (f + 1) * tall]
        bias = jnp.concatenate([bias[:, r * tall // 8 : (r + 1) * tall // 8] for r in range(8)], axis=0)
        block = jnp.concatenate(
            [every[:, f * piece : (f + 1) * piece], bias, loss_part[:, : 128 - used]], axis=1
        )
        for x in range(devices // parts_f):
            share[x * parts_f + f] = block
    save.wait()


def back_third(dr1, dqkv, tok, packed, vec, sums, bias_sums, down_bias, bias_up, loss_part, shard):
    rows, width = tok.shape
    shape = jax.ShapeDtypeStruct
    return pl.pallas_call(
        functools.partial(back_third_kernel, shard[1]),
        name="back_third",
        in_specs=[ANY, ANY, ANY, ANY] + [WHOLE] * 6,
        out_specs=[ANY, WHOLE],
        out_shape=[shape((rows, width), F32), shape((shard[0] * shard[1], 8, 128), F32)],
        scratch_shapes=[
            pltpu.VMEM((8, width), F32),
            weight_scratch("qkv", width, width),
            pltpu.VMEM((rows, width), F32),
            pltpu.VMEM((rows, width), BF),
            pltpu.VMEM((rows, width), F32),
            pltpu.SemaphoreType.DMA((PX * 3,)),
            pltpu.VMEM((rows, 3 * width), BF),
            pltpu.SemaphoreType.DMA((4,)),
        ],
        compiler_params=params(),
        cost_estimate=pl.CostEstimate(
            flops=6 * rows * width * width, bytes_accessed=14 * width * width, transcendentals=0
        ),
    )(dr1, dqkv, tok, packed, vec, sums, bias_sums, down_bias, bias_up, loss_part)


def fold_kernel(a_own, a_new, b_own, b_new, a_keep, a_send, b_keep, b_send):
    for own, new, keep, send in ((a_own, a_new, a_keep, a_send), (b_own, b_new, b_keep, b_send)):
        total = own[...].astype(F32) + new[...].astype(F32)
        keep[...] = total[0].astype(BF)
        send[...] = total[1].astype(BF)


def fold(a_own, a_new, b_own, b_new):
    shape = a_own.shape
    rest = 1
    for n in shape[1:-2]:
        rest *= n
    rows, cols = shape[-2:]
    view = lambda a: a.reshape(2, rest, rows, cols)
    steps = 2 if rest > 4 else 1
    pair = pl.BlockSpec((2, rest // steps, rows, cols), lambda i: (0, i, 0, 0))
    one = pl.BlockSpec((rest // steps, rows, cols), lambda i: (i, 0, 0))
    outs = pl.pallas_call(
        fold_kernel,
        name="fold",
        grid=(steps,),
        in_specs=[pair] * 4,
        out_specs=[one] * 4,
        out_shape=[jax.ShapeDtypeStruct((rest, rows, cols), BF)] * 4,
        compiler_params=params(18),
        cost_estimate=pl.CostEstimate(
            flops=4 * rest * rows * cols, bytes_accessed=24 * rest * rows * cols, transcendentals=0
        ),
    )(*(view(a) for a in (a_own, a_new, b_own, b_new)))
    return [o.reshape(shape[1:]) for o in outs]


def join_kernel(a_own, a_new, b_own, b_new, keep, send):
    half = a_own.shape[-1]
    for at, own, new in ((0, a_own, a_new), (half, b_own, b_new)):
        total = own[...].astype(F32) + new[...].astype(F32)
        for k in range(2):
            keep[k, :, at : at + half] = total[2 * k]
            send[k, :, at : at + half] = total[2 * k + 1].astype(BF)


def join(a_own, a_new, b_own, b_new):
    blocks, rows, cols = a_own.shape
    shape = jax.ShapeDtypeStruct
    return pl.pallas_call(
        join_kernel,
        name="join",
        in_specs=[WHOLE] * 4,
        out_specs=[WHOLE] * 2,
        out_shape=[shape((2, rows, 2 * cols), F32), shape((2, rows, 2 * cols), BF)],
        compiler_params=params(6),
        cost_estimate=pl.CostEstimate(
            flops=16 * rows * cols, bytes_accessed=40 * rows * cols, transcendentals=0
        ),
    )(a_own, a_new, b_own, b_new)


def turn_kernel(keep, new, stay, send):
    stay[...] = keep[0] + new[0].astype(F32)
    send[...] = (keep[1] + new[1].astype(F32)).astype(BF)


def turn(keep, new):
    blocks, rows, cols = keep.shape
    shape = jax.ShapeDtypeStruct
    return pl.pallas_call(
        turn_kernel,
        name="turn",
        in_specs=[WHOLE] * 2,
        out_specs=[WHOLE] * 2,
        out_shape=[shape((rows, cols), F32), shape((rows, cols), BF)],
        compiler_params=params(6),
        cost_estimate=pl.CostEstimate(
            flops=4 * rows * cols, bytes_accessed=18 * rows * cols, transcendentals=0
        ),
    )(keep, new)


def shifted(x, y, z, core):
    change = x * 16 + z * 4 + y * 2 + core
    return [(i, i ^ change) for i in range(32)]


def hop(array, x=0, y=0, z=0, core=0):
    return lax.ppermute(array, AXES, shifted(x, y, z, core))


def after(values, *others):
    return lax.optimization_barrier((tuple(values), others))[0]


def core_step(parts, *wait):
    keep_a, send_a, keep_b, send_b = parts
    new_a, new_b = hop(send_a, core=1), hop(send_b, core=1)
    keep_a, keep_b = after((keep_a, keep_b), *wait)
    return fold(keep_a, new_a, keep_b, new_b)


def first_step(parts, *wait):
    keep_a, send_a, keep_b, send_b = parts
    new_a, new_b = hop(send_a, x=1), hop(send_b, y=1)
    keep_a, keep_b = after((keep_a, keep_b), *wait)
    return fold(keep_a, new_a, keep_b, new_b)


def second_step(parts, *wait):
    keep_a, send_a, keep_b, send_b = parts
    new_a, new_b = hop(send_a, y=1), hop(send_b, x=1)
    keep_a, keep_b = after((keep_a, keep_b), *wait)
    return join(keep_a, new_a, keep_b, new_b)


def total_kernel(stay, new, *outs):
    total = stay[...] + new[...].astype(F32)
    at = 0
    for out in outs:
        out[...] = total[:, at : at + out.shape[1]]
        at += out.shape[1]


def third_step(parts, *wait):
    keep, send = parts
    new = hop(send, z=1)
    (keep,) = after((keep,), *wait)
    return turn(keep, new)


def last_step(parts, splits):
    stay, send = parts
    return pl.pallas_call(
        total_kernel,
        name="total",
        in_specs=[WHOLE] * 2,
        out_specs=[WHOLE] * len(splits),
        out_shape=[jax.ShapeDtypeStruct((stay.shape[0], n), F32) for n in splits],
        compiler_params=params(4),
    )(stay, hop(send, z=2))


def natural_grad(keep_a, send_a, keep_b, send_b):
    first = jnp.stack([keep_a, send_a])
    second = jnp.swapaxes(jnp.stack([keep_b, send_b]), 1, 2)
    whole = jnp.concatenate([first, second], axis=-1)
    core, x, y, z, rows, cols = whole.shape
    return whole.transpose(1, 3, 2, 0, 4, 5).reshape(x, z * y * core * rows, cols)


def pack_kernel(qkv, out, up, down, packed):
    rows, piece = out.shape
    at = 0
    for ref in (qkv, out, up, down):
        for c in range(0, ref.shape[1], piece):
            packed[at : at + ref.shape[0], :] = ref[:, c : c + piece]
            at += ref.shape[0]


def pack_block(qkv, out, up, down):
    piece = out.shape[1]
    total = sum(w.shape[0] * w.shape[1] for w in (qkv, out, up, down)) // piece
    return pl.pallas_call(
        pack_kernel,
        name="pack_block",
        in_specs=[WHOLE] * 4,
        out_specs=WHOLE,
        out_shape=jax.ShapeDtypeStruct((total, piece), BF),
        compiler_params=params(),
    )(qkv, out, up, down)


def gather_packed(qkv, out, up, down, dp, fsdp):
    if (dp, fsdp) == (PX, PF):
        return lax.all_gather(pack_block(qkv, out, up, down), AXES, axis=0)
    full = [
        lax.all_gather(lax.all_gather(w, "dp", axis=1, tiled=True), "fsdp", axis=0, tiled=True)
        for w in (qkv, out, up, down)
    ]
    blocks = []
    for x in range(PX):
        for f in range(PF):
            some = []
            for w in full:
                rows, cols = w.shape[0] // PF, w.shape[1] // PX
                some.append(w[f * rows : (f + 1) * rows, x * cols : (x + 1) * cols])
            blocks.append(pack_block(*some))
    return jnp.stack(blocks)


def scatter_columns(grad, dp, fsdp):
    parts, rows, cols = grad.shape
    if dp != parts:
        grad = jnp.swapaxes(grad, 0, 1).reshape(rows, dp, parts * cols // dp)
        grad = jnp.swapaxes(grad, 0, 1)
    return lax.psum_scatter(
        grad.reshape(dp * rows, -1), AXES, scatter_dimension=0, tiled=True
    ).astype(F32)


def body(
    image_tokens,
    text_tokens,
    image_qkv,
    image_out,
    image_up,
    image_down,
    image_vectors,
    image_up_bias,
    text_qkv,
    text_out,
    text_up,
    text_down,
    text_vectors,
    text_up_bias,
    pair_counts,
    pair_groups,
):
    dp, fsdp = lax.axis_size("dp"), lax.axis_size("fsdp")
    devices = dp * fsdp
    cap, length, width = text_tokens.shape
    hidden = image_up.shape[1]
    pairs = pair_groups.shape[0]
    me = lax.axis_index("dp") * fsdp + lax.axis_index("fsdp")

    grid_mesh = (dp, fsdp) == (PX, PF)
    packed = gather_packed(text_qkv, text_out, text_up, text_down, dp, fsdp)
    part = width // fsdp
    small = jnp.concatenate([text_vectors, text_up_bias.reshape(8, -1)], axis=1)
    if grid_mesh:
        small = jnp.broadcast_to(small[None], (fsdp,) + small.shape)
        small = lax.all_to_all(small, "fsdp", 0, 0, tiled=True)
    else:
        small = lax.all_gather(small, "fsdp", axis=0)
    vec = jnp.swapaxes(small[:, :, :part], 0, 1).reshape(8, width)
    ub = small[:, :, part:].reshape(1, hidden)
    bits = [lax.shift_right_logical(me, k) & 1 for k in range(5)]
    where = jnp.stack([bits[4], bits[1], 2 * bits[3] + bits[2], bits[0]])
    where = where if grid_mesh else jnp.zeros_like(where)

    image_low = image_forward(
        image_tokens, image_qkv, image_out, image_up, image_down, image_vectors, image_up_bias
    )
    if grid_mesh:
        images = image_low
        for change in (dict(z=1), dict(z=2), dict(x=1), dict(y=1), dict(core=1)):
            images = jnp.concatenate([images, hop(images, **change)], axis=0)
        far = jnp.arange(devices, dtype=jnp.int32) ^ me
        bit = lambda k: lax.shift_right_logical(far, k) & 1
        order = bit(2) + 2 * bit(3) + 4 * bit(4) + 8 * bit(1) + 16 * bit(0)
        images = jnp.take(images.reshape(devices, cap, width), order, axis=0).reshape(pairs, width)
    else:
        images = lax.all_gather(image_low, AXES, axis=0, tiled=True)

    slots = jnp.arange(cap, dtype=jnp.int32)
    live = (slots[None, :] < pair_counts[:, None]).reshape(pairs).astype(F32)
    same = jnp.maximum(
        jnp.sum(jnp.where(pair_groups[:, None] == pair_groups[None, :], live[None, :], 0.0), axis=1), 1.0
    )
    own_of = lambda array: lax.dynamic_slice_in_dim(array, me * cap, cap)
    own = jnp.stack([own_of(live), own_of(same)], axis=1)
    own_group = own_of(pair_groups).reshape(cap, 1)
    live_row, same_row, group_row = (a.reshape(1, pairs) for a in (live, same, pair_groups))
    live_total = jnp.sum(pair_counts).astype(F32)
    factor = jnp.broadcast_to(LOSS_WEIGHT / (2.0 * live_total), (1, 128))

    tokens = text_tokens.reshape(cap * length, width)
    h1, qkv, att, r1, h2, slope, acts, pooled, power, row_part, col_sum, loss_part = text_forward(
        tokens, packed, vec, ub, images, live_row, same_row, group_row, own, own_group, length, hidden,
        devices if grid_mesh else 1,
    )
    if grid_mesh:
        row_all = lax.all_to_all(row_part, AXES, 0, 0, tiled=True)
    else:
        row_all = lax.psum(row_part, AXES)
    h1_t, h2_t, att_t = relative_rows(where, h1, h2, att)
    factors, *up_parts, bias_up, down_bias, dr1, dz, da, sums, loss_rows = back_one(
        where, power, row_all, col_sum, images, live_row, same_row, group_row, own, own_group, factor, pooled,
        packed, vec, slope, h2_t, r1, acts, length, (dp, fsdp),
    )
    dqkv, *att_parts, bias_sums = back_two(where, qkv, da, dz, h1_t, att_t, length)

    both = lax.all_to_all(factors, AXES, 0, 0, tiled=True).reshape(pairs, width // dp + hidden // fsdp)
    grad_down = dot(both[:, width // dp :], both[:, : width // dp], 0, 0)

    if grid_mesh:
        up_parts = core_step(up_parts, *att_parts)
        (att_keep,) = after((att_parts[0],), *up_parts)
        att_parts = core_step([att_keep] + att_parts[1:])
        (dqkv,) = after((dqkv,), *att_parts)
        dx, share = back_third(
            dr1, dqkv, tokens, packed, vec, sums, bias_sums, down_bias, bias_up, loss_part, (dp, fsdp)
        )
        up_parts = first_step(up_parts, dx)
        att_parts = first_step(att_parts, grad_down, *up_parts)
        up_parts = second_step(up_parts, *att_parts)
        (share,) = after((share,), *att_parts)
        att_parts = second_step(att_parts, *up_parts)
        up_parts = third_step(up_parts, *att_parts)
        att_parts = third_step(att_parts, *up_parts)
        (grad_up,) = last_step(up_parts, (hidden // dp,))
        grad_qkv, grad_out = last_step(att_parts, (3 * width // dp, width // dp))
    else:
        dx, share = back_third(
            dr1, dqkv, tokens, packed, vec, sums, bias_sums, down_bias, bias_up, loss_part, (dp, fsdp)
        )
        grad_attn = natural_grad(*att_parts)
        grad_up = scatter_columns(natural_grad(*up_parts), dp, fsdp)
        grad_qkv = scatter_columns(grad_attn[:, :, : 3 * width // PX], dp, fsdp)
        grad_out = scatter_columns(grad_attn[:, :, 3 * width // PX :], dp, fsdp)

    share = jnp.sum(lax.all_to_all(share, AXES, 0, 0, tiled=True), axis=0)
    grad_vec = share[:, :part]
    tall = hidden // fsdp // 8
    grad_bias = share[:, part : part + tall].reshape(hidden // fsdp)
    loss = (share[0, part + tall] + loss_rows[0, 0]) / (2.0 * live_total)

    return (
        loss,
        dx.reshape(text_tokens.shape),
        grad_qkv,
        grad_out,
        grad_up,
        grad_down,
        grad_vec,
        grad_bias,
    )


def solution(mesh):
    return jax.shard_map(
        body,
        mesh=mesh,
        in_specs=(
            P(AXES, None, None),
            P(AXES, None, None),
            P(),
            P(),
            P(),
            P(),
            P(),
            P(),
            P("fsdp", "dp"),
            P("fsdp", "dp"),
            P("fsdp", "dp"),
            P("fsdp", "dp"),
            P(None, "fsdp"),
            P("fsdp"),
            P(),
            P(),
        ),
        out_specs=(
            P(),
            P(AXES, None, None),
            P("fsdp", "dp"),
            P("fsdp", "dp"),
            P("fsdp", "dp"),
            P("fsdp", "dp"),
            P(None, "fsdp"),
            P("fsdp"),
        ),
        check_vma=False,
    )
```

```python
import functools

import jax
import jax.numpy as jnp
from jax import lax
from jax.experimental import pallas as pl
from jax.experimental.pallas import tpu as pltpu
from jax.sharding import PartitionSpec as P

HEAD_DIM = 64
LOGIT_SCALE = 50.0
LOSS_WEIGHT = 32768.0
BF = jnp.bfloat16
F32 = jnp.float32
AXES = ("dp", "fsdp")
PX, PF = 2, 16

ANY = pl.BlockSpec(memory_space=pltpu.HBM)
WHOLE = pl.BlockSpec(memory_space=pltpu.VMEM)


def params(mebibytes=62):
    return pltpu.CompilerParams(vmem_limit_bytes=mebibytes * 1024 * 1024)


def dot(a, b, ca=1, cb=0):
    return lax.dot_general(a, b, (((ca,), (cb,)), ((), ())), preferred_element_type=F32)


def repeat(count, step, together=1):
    def turn(j, _):
        for k in range(together):
            step(j * together + k)
        return 0

    if together >= count:
        for i in range(count):
            step(i)
    else:
        lax.fori_loop(0, count // together, turn, 0)


def move(pairs, sem, base=0):
    copies = [pltpu.make_async_copy(a, b, sem.at[base + i]) for i, (a, b) in enumerate(pairs)]
    for copy in copies:
        copy.start()
    return copies


def normalize(values):
    centered = values - jnp.mean(values, axis=-1, keepdims=True)
    inverse = lax.rsqrt(jnp.mean(centered * centered, axis=-1, keepdims=True) + 1e-05)
    return centered * inverse, inverse


def norm_back(grad, hat, inverse, gain):
    scaled = grad * gain
    return inverse * (
        scaled
        - jnp.mean(scaled, axis=-1, keepdims=True)
        - hat * jnp.mean(scaled * hat, axis=-1, keepdims=True)
    )


def gauss_tail(u):
    size = jnp.abs(u)
    t = 1.0 / (1.0 + (0.3275911 * 0.7071067811865476) * size)
    bell = jnp.exp2(-0.7213475204444817 * (u * u))
    poly = 0.5 * 1.061405429 * t - 0.5 * 1.453152027
    poly = poly * t + 0.5 * 1.421413741
    poly = poly * t - 0.5 * 0.284496736
    poly = poly * t + 0.5 * 0.254829592
    return poly * t * bell, bell, size


def head_pair(block, low_lane):
    zero = jnp.zeros_like(block)
    return jnp.concatenate(
        [jnp.where(low_lane, block, zero), jnp.where(low_lane, zero, block)], axis=0
    )


def softmax_half(scores, bias):
    scores = scores + bias
    top = jnp.max(scores, axis=-1, keepdims=True)
    powers = jnp.exp(scores - top)
    return powers * (1.0 / jnp.sum(powers, axis=-1, keepdims=True))


def unit_rows(pooled):
    return pooled * lax.rsqrt(jnp.sum(pooled * pooled, axis=-1, keepdims=True) + 1e-06)


def mean_down(total, count, down):
    mean = total * (1.0 / count)
    high = mean.astype(BF)
    low = (mean - high.astype(F32)).astype(BF)
    both = dot(jnp.concatenate([high, low], axis=0), down)
    return both[: mean.shape[0]] + both[mean.shape[0] :]


def image_kernel(
    tok, wq_h, wo_h, wu_h, wd_h, vec, ub, out, wq, wo, wu, wd, x, h, qkv, att, act_sum, r1_sum, bias_row, stage, sem
):
    step, steps = pl.program_id(0), pl.num_programs(0)
    length, group, width = tok.shape
    rows = group * length
    hidden = wu.shape[1]
    copies = [
        pltpu.make_async_copy(src, dst, sem.at[i])
        for i, (src, dst) in enumerate(((wq_h, wq), (wo_h, wo), (wu_h, wu), (wd_h, wd)))
    ]

    @pl.when(step == 0)
    def _():
        for copy in copies:
            copy.start()

    def arrived(i):
        @pl.when(step == 0)
        def _():
            copies[i].wait()

    v = vec[...].astype(F32)
    bias_row[:, :width] = v[2:3]
    bias_row[:, width : 2 * width] = jnp.zeros((1, width), F32)
    bias_row[:, 2 * width :] = v[3:4]
    for k in range(width // 128):
        stage[k] = tok[:, :, k * 128 : (k + 1) * 128].astype(F32).reshape(rows, 128)
        for i in range(group):
            x[pl.ds(i * length, length), k * 128 : (k + 1) * 128] = stage[k, pl.ds(i, length, stride=group), :]

    def norm_rows(gain, shift):
        blk = 80

        def one(i):
            at = pl.ds(pl.multiple_of(i * blk, blk), blk)
            hat, _ = normalize(x[at, :])
            h[at, :] = (hat * gain + shift).astype(BF)

        repeat(rows // blk, one, 5)

    norm_rows(v[0:1], v[1:2])
    arrived(0)

    def project(i):
        at = pl.ds(pl.multiple_of(i * 256, 256), 256)
        qkv[:, at] = (dot(h[...], wq[:, at]) + bias_row[:, at]).astype(BF)

    repeat(3 * width // 256, project, 3)

    wins = rows // (2 * length)
    q_len = 112
    low_lane = lax.broadcasted_iota(jnp.int32, (128, 128), 1) < HEAD_DIM
    cols = range(0, width, 128)

    def window(w):
        q_at = pl.multiple_of((2 * length * w) // 16 * 16, 16)
        k_at = pl.multiple_of(jnp.minimum(q_at, rows - 128), 16)
        lo, mid, hi = 2 * w * length, (2 * w + 1) * length, (2 * w + 2) * length
        qi = q_at + lax.broadcasted_iota(jnp.int32, (q_len, 128), 0)
        ki = k_at + lax.broadcasted_iota(jnp.int32, (q_len, 128), 1)
        first = (qi >= lo) & (qi < mid) & (ki >= lo) & (ki < mid)
        second = (qi >= mid) & (qi < hi) & (ki >= mid) & (ki < hi)
        bias = jnp.where(first | second, 0.0, -1e30)
        q_rows, k_rows = pl.ds(q_at, q_len), pl.ds(k_at, 128)
        q2 = [qkv[q_rows, c : c + 128] * 0.125 for c in cols]
        k2 = [head_pair(qkv[k_rows, width + c : width + c + 128], low_lane) for c in cols]
        v2 = [head_pair(qkv[k_rows, 2 * width + c : 2 * width + c + 128], low_lane) for c in cols]
        scores = [dot(q, k, 1, 1) for q, k in zip(q2, k2)]
        probs = [
            jnp.concatenate(
                [softmax_half(s[:, :128], bias).astype(BF), softmax_half(s[:, 128:], bias).astype(BF)],
                axis=1,
            )
            for s in scores
        ]
        mine = (q_at + lax.broadcasted_iota(jnp.int32, (16, 128), 0)) >= lo
        for c, p, values in zip(cols, probs, v2):
            mixed = dot(p, values)
            old = att[pl.ds(q_at, 16), c : c + 128].astype(F32)
            att[pl.ds(q_at, 16), c : c + 128] = jnp.where(mine, mixed[:16], old).astype(BF)
            att[pl.ds(q_at + 16, q_len - 16), c : c + 128] = mixed[16:].astype(BF)

    repeat(wins, window, 2)

    arrived(1)
    for c in range(0, width, 256):
        x[:, c : c + 256] = x[:, c : c + 256] + (dot(att[...], wo[:, c : c + 256]) + v[4:5, c : c + 256])
    norm_rows(v[5:6], v[6:7])

    def image_sums(values):
        sums = []
        for i in range(group):
            lo, hi = i * length, (i + 1) * length
            a, b = lo // 8 * 8, -(-hi // 8) * 8
            part = values[a:b]
            row = a + lax.broadcasted_iota(jnp.int32, (b - a, 1), 0)
            if lo % 8 or hi % 8:
                part = jnp.where((row >= lo) & (row < hi), part, 0.0)
            sums.append(jnp.sum(part, axis=0, keepdims=True))
        return jnp.concatenate(sums, axis=0)

    place = pl.ds(pl.multiple_of(step * group, group), group)
    for c in range(0, width, 256):
        r1_sum[place, c : c + 256] = image_sums(x[:, c : c + 256])
    arrived(2)

    def expand(i):
        at = pl.ds(pl.multiple_of(i * 256, 256), 256)
        u = dot(h[...], wu[:, at]) + ub[:, at].astype(F32)
        tail, _, size = gauss_tail(u)
        act_sum[place, at] = image_sums(jnp.maximum(u, 0.0) - size * tail)

    repeat(hidden // 256, expand, 3)
    arrived(3)

    @pl.when(step == steps - 1)
    def _():
        pooled = r1_sum[...] * (1.0 / length) + mean_down(act_sum[...], length, wd[...]) + v[7:8]
        out[...] = unit_rows(pooled).astype(BF)


def image_forward(tokens, wq, wo, wu, wd, vec, ub):
    pairs, length, width = tokens.shape
    hidden = wu.shape[1]
    group = 16
    rows = group * length
    return pl.pallas_call(
        image_kernel,
        name="image_forward",
        grid=(pairs // group,),
        in_specs=[
            pl.BlockSpec((length, group, width), lambda i: (0, i, 0)),
            ANY,
            ANY,
            ANY,
            ANY,
            pl.BlockSpec((8, width), lambda i: (0, 0)),
            pl.BlockSpec((1, hidden), lambda i: (0, 0)),
        ],
        out_specs=pl.BlockSpec((pairs, width), lambda i: (0, 0)),
        out_shape=jax.ShapeDtypeStruct((pairs, width), BF),
        scratch_shapes=[
            pltpu.VMEM((width, 3 * width), BF),
            pltpu.VMEM((width, width), BF),
            pltpu.VMEM((width, hidden), BF),
            pltpu.VMEM((hidden, width), BF),
            pltpu.VMEM((rows, width), F32),
            pltpu.VMEM((rows, width), BF),
            pltpu.VMEM((rows, 3 * width), BF),
            pltpu.VMEM((rows, width), BF),
            pltpu.VMEM((pairs, hidden), F32),
            pltpu.VMEM((pairs, width), F32),
            pltpu.VMEM((1, 3 * width), F32),
            pltpu.VMEM((width // 128, rows, 128), F32),
            pltpu.SemaphoreType.DMA((4,)),
        ],
        compiler_params=params(),
        cost_estimate=pl.CostEstimate(
            flops=2 * pairs * length * width * (4 * width + hidden),
            bytes_accessed=2 * (4 * width * width + 2 * width * hidden + pairs * length * width),
            transcendentals=pairs * length * hidden,
        ),
    )(jnp.swapaxes(tokens, 0, 1), wq, wo, wu, wd, vec, ub.reshape(1, hidden))


def pack_rows(width, hidden):
    piece, rows = width // PX, width // PF
    return piece, rows, hidden // PF


def weight_copies(packed, which, dst, sem, base, width, hidden):
    piece, rows, frows = pack_rows(width, hidden)
    q_pieces, u_pieces = 3, hidden // width
    spans = {
        "qkv": (0, q_pieces, rows),
        "out": (q_pieces * rows, 1, rows),
        "up": ((q_pieces + 1) * rows, u_pieces, rows),
        "down": ((q_pieces + 1 + u_pieces) * rows, 1, frows),
    }
    start, count, tall = spans[which]
    copies = []
    for x in range(PX):
        for p in range(count):
            copies.append(
                pltpu.make_async_copy(
                    packed.at[pl.ds(x * PF, PF), pl.ds(start + p * tall, tall), :],
                    dst.at[:, :, pl.ds((x * count + p) * piece, piece)],
                    sem.at[base + len(copies)],
                )
            )
    return copies


def natural(ref):
    blocks, rows, cols = ref.shape
    return ref[...].reshape(blocks * rows, cols)


def weight_scratch(which, width, hidden):
    rows, frows = width // PF, hidden // PF
    shape = {
        "qkv": (PF, rows, 3 * width),
        "out": (PF, rows, width),
        "up": (PF, rows, hidden),
        "down": (PF, frows, width),
    }[which]
    return pltpu.VMEM(shape, BF)


def contrast(low, images, live, same, groups, own, own_group, power, row_part, col_sum, loss_part):
    scores = LOGIT_SCALE * dot(low, images[...], 1, 1)
    exps = jnp.exp(scores)
    live_own, same_own = own[:, 0:1], own[:, 1:2]
    power[...] = exps
    rows = jnp.sum(exps * live_own, axis=0, keepdims=True)
    tiled = jnp.concatenate(
        [rows[:, k * 128 : (k + 1) * 128] for k in range(rows.shape[1] // 128)], axis=0
    )
    for d in range(row_part.shape[0]):
        row_part[d] = tiled
    cols = jnp.sum(exps * live[...], axis=1, keepdims=True)
    col_sum[...] = cols
    pair = jnp.where(own_group[...] == groups[...], live_own * live[...], 0.0)
    linear = pair * scores * (1.0 / same_own + 1.0 / same[...])
    losses = live_own * jnp.log(cols) - jnp.sum(linear, axis=1, keepdims=True)
    loss_part[...] = jnp.broadcast_to(jnp.sum(losses, axis=0, keepdims=True), loss_part.shape)


def text_mask(size, length):
    row = lax.broadcasted_iota(jnp.int32, (size, size), 0) // length
    col = lax.broadcasted_iota(jnp.int32, (size, size), 1) // length
    return jnp.where(row == col, 0.0, -1e30)


def text_forward_kernel(
    length, tok, packed, vec, ub, images_i, live, same, groups, own, own_group,
    h1_o, qkv_o, att_o, r1_o, h2_o, slope_o, acts, pooled_out, power, row_part, col_sum, loss_part,
    wq, wo, wu, wd, total, bias_row, h1, qkv, att, r1, h2, slope, sem, images, out_sem
):
    rows, width = tok.shape
    hidden = slope.shape[1]
    texts = rows // length
    load = {}
    base = 0
    for which, dst in (("qkv", wq), ("out", wo), ("up", wu), ("down", wd)):
        load[which] = weight_copies(packed, which, dst, sem, base, width, hidden)
        base += len(load[which])
        for copy in load[which]:
            copy.start()
    v = vec[...].astype(F32)
    bias_row[:, :width] = v[2:3]
    bias_row[:, width : 2 * width] = jnp.zeros((1, width), F32)
    bias_row[:, 2 * width :] = v[3:4]
    blk = 128

    def norm_rows(src, dst, gain, shift):
        def one(i):
            at = pl.ds(pl.multiple_of(i * blk, blk), blk)
            hat, _ = normalize(src[at, :].astype(F32))
            dst[at, :] = (hat * gain + shift).astype(BF)

        repeat(rows // blk, one, 2)

    norm_rows(tok, h1, v[0:1], v[1:2])
    saves = move([(h1, h1_o)], out_sem)
    (gathered,) = move([(images_i, images)], out_sem, 6)
    for copy in load["qkv"]:
        copy.wait()

    def project(i):
        at = pl.ds(pl.multiple_of(i * 256, 256), 256)
        qkv[:, at] = (dot(h1[...], wq[:, :, at].reshape(width, 256)) + bias_row[:, at]).astype(BF)

    repeat(3 * width // 256, project, 3)
    saves += move([(qkv, qkv_o)], out_sem, 1)
    low_lane = lax.broadcasted_iota(jnp.int32, (blk, 128), 1) < HEAD_DIM
    bias = text_mask(blk, length)
    cols = range(0, width, 128)

    def attend(i):
        at = pl.ds(pl.multiple_of(i * blk, blk), blk)
        q2 = [qkv[at, c : c + 128] * 0.125 for c in cols]
        k2 = [head_pair(qkv[at, width + c : width + c + 128], low_lane) for c in cols]
        v2 = [head_pair(qkv[at, 2 * width + c : 2 * width + c + 128], low_lane) for c in cols]
        scores = [dot(q, k, 1, 1) for q, k in zip(q2, k2)]
        probs = [
            jnp.concatenate(
                [softmax_half(s[:, :blk], bias).astype(BF), softmax_half(s[:, blk:], bias).astype(BF)],
                axis=1,
            )
            for s in scores
        ]
        for c, p, values in zip(cols, probs, v2):
            att[at, c : c + 128] = dot(p, values).astype(BF)

    repeat(rows // blk, attend, 2)
    saves += move([(att, att_o)], out_sem, 2)
    for copy in load["out"]:
        copy.wait()
    for c in range(0, width, 256):
        r1[:, c : c + 256] = tok[:, c : c + 256].astype(F32) + (
            dot(att[...], wo[:, :, c : c + 256].reshape(width, 256)) + v[4:5, c : c + 256]
        )
    saves += move([(r1, r1_o)], out_sem, 3)
    norm_rows(r1, h2, v[5:6], v[6:7])
    saves += move([(h2, h2_o)], out_sem, 4)
    for copy in load["up"]:
        copy.wait()

    def expand(i):
        at = pl.ds(pl.multiple_of(i * 256, 256), 256)
        u = dot(h2[...], wu[:, :, at].reshape(width, 256)) + ub[:, at].astype(F32)
        tail, bell, _ = gauss_tail(u)
        phi = jnp.where(u >= 0.0, 1.0 - tail, tail)
        act = u * phi
        slope[:, at] = (phi + u * (bell * 0.3989422804014327)).astype(BF)
        sums = jnp.sum(act.reshape(texts, length, 256), axis=1)
        total[:, at] = sums
        acts[:, at] = sums.astype(BF)

    repeat(hidden // 256, expand, 3)
    saves += move([(slope, slope_o)], out_sem, 5)
    for copy in load["down"]:
        copy.wait()
    mean_r1 = jnp.sum(r1[...].reshape(texts, length, width), axis=1) * (1.0 / length)
    pooled = mean_r1 + mean_down(total[...], length, natural(wd)) + v[7:8]
    pooled_out[...] = pooled
    gathered.wait()
    contrast(
        unit_rows(pooled).astype(BF), images, live, same, groups, own, own_group, power, row_part, col_sum, loss_part
    )
    for copy in saves:
        copy.wait()


def text_forward(
    tokens, packed, vec, ub, images, live, same, groups, own, own_group, length, hidden, copies_of
):
    rows, width = tokens.shape
    texts = rows // length
    pairs = images.shape[0]
    shape = jax.ShapeDtypeStruct
    copies = PX * (3 + 1 + hidden // width + 1)
    return pl.pallas_call(
        functools.partial(text_forward_kernel, length),
        name="text_forward",
        in_specs=[WHOLE, ANY, WHOLE, WHOLE, ANY] + [WHOLE] * 5,
        out_specs=[ANY] * 6 + [WHOLE] * 6,
        out_shape=[
            shape((rows, width), BF),
            shape((rows, 3 * width), BF),
            shape((rows, width), BF),
            shape((rows, width), F32),
            shape((rows, width), BF),
            shape((rows, hidden), BF),
            shape((texts, hidden), BF),
            shape((texts, width), F32),
            shape((texts, pairs), F32),
            shape((copies_of, pairs // 128, 128), F32),
            shape((texts, 1), F32),
            shape((8, 128), F32),
        ],
        scratch_shapes=[weight_scratch(w, width, hidden) for w in ("qkv", "out", "up", "down")]
        + [
            pltpu.VMEM((texts, hidden), F32),
            pltpu.VMEM((1, 3 * width), F32),
            pltpu.VMEM((rows, width), BF),
            pltpu.VMEM((rows, 3 * width), BF),
            pltpu.VMEM((rows, width), BF),
            pltpu.VMEM((rows, width), F32),
            pltpu.VMEM((rows, width), BF),
            pltpu.VMEM((rows, hidden), BF),
            pltpu.SemaphoreType.DMA((copies,)),
            pltpu.VMEM((pairs, width), BF),
            pltpu.SemaphoreType.DMA((7,)),
        ],
        compiler_params=params(),
        cost_estimate=pl.CostEstimate(
            flops=2 * rows * width * (4 * width + hidden),
            bytes_accessed=2 * (4 * width * width + 2 * width * hidden + 12 * rows * width),
            transcendentals=rows * hidden,
        ),
    )(tokens, packed, vec, ub, images, live, same, groups, own, own_group)


def relative_kernel(where, h1_i, h2_i, att_i, h1_o, h2_o, att_o, h1, h2, att, h1_t, h2_t, att_t, sem):
    width = h1.shape[1]
    block = width // PF
    my, mz, mc = where[1], where[2], where[3]
    loads = move([(h2_i, h2), (h1_i, h1), (att_i, att)], sem)
    saves = []
    for n, (src, dst, out) in enumerate(((h2, h2_t, h2_o), (h1, h1_t, h1_o), (att, att_t, att_o))):
        loads[n].wait()
        turned = src[...].T
        for z in range(4):
            for y in range(2):
                for c in range(2):
                    f = (z * 2 + y) * 2 + c
                    place = (((c ^ mc) * 2 + (y ^ my)) * 4 + (z ^ mz)) * block
                    dst[pl.ds(pl.multiple_of(place, block), block), :] = turned[
                        f * block : (f + 1) * block
                    ]
        saves += move([(dst, out)], sem, 3 + n)
    for copy in saves:
        copy.wait()


SMEM = pl.BlockSpec(memory_space=pltpu.SMEM)


def relative_rows(where, h1, h2, att):
    rows, width = h1.shape
    return pl.pallas_call(
        relative_kernel,
        name="relative_rows",
        in_specs=[SMEM, ANY, ANY, ANY],
        out_specs=[ANY] * 3,
        out_shape=[jax.ShapeDtypeStruct((width, rows), BF)] * 3,
        scratch_shapes=[pltpu.VMEM((rows, width), BF)] * 3
        + [pltpu.VMEM((width, rows), BF)] * 3
        + [pltpu.SemaphoreType.DMA((6,))],
        compiler_params=params(),
        cost_estimate=pl.CostEstimate(flops=0, bytes_accessed=12 * rows * width, transcendentals=0),
    )(where, h1, h2, att)


def grad_shapes(width):
    block, half = width // PF, width
    return [jax.ShapeDtypeStruct((2, 2, 4, block, half), BF)] * 4


def put_grad(values, outs, x_rel, at, second):
    width, cols = values.shape
    block = width // PF
    low = values.astype(BF)
    for c in range(2):
        for y in range(2):
            piece = low[(c * 2 + y) * 4 * block : (c * 2 + y + 1) * 4 * block].reshape(4, block, cols)
            if second:
                outs[2 + c, y, x_rel, :, :, pl.ds(at, cols)] = piece
            else:
                outs[c, x_rel, y, :, :, pl.ds(at, cols)] = piece


def start_grads(parts, outs, sem, x):
    return move(
        [(parts.at[n, x], outs[n].at[x]) for n in range(2)]
        + [(parts.at[n, :, x], outs[n].at[:, x]) for n in range(2, 4)],
        sem,
        4 * x,
    )


def back_one_kernel(
    length, shard,
    where, power, row_all, col_sum, images_i, live, same, groups, own, own_group, factor, pooled, packed, vec,
    slope_i, h2_i, r1_i, acts,
    factors_o, keep_a, send_a, keep_b, send_b, bias_up, down_bias, dr1_o, dz_o, da_o, sums, loss_rows,
    factors, wd, wu, wo, dact, images, slope, h2_t, r1, du, dr1, dz_s, da_s, dy, parts, sem, in_sem, out_sem,
):
    rows, hidden = slope.shape
    texts = rows // length
    width = h2_t.shape[0]
    (gathered,) = move([(images_i, images)], in_sem)
    down = weight_copies(packed, "down", wd, sem, 0, width, hidden)
    up = weight_copies(packed, "up", wu, sem, len(down), width, hidden)
    out = weight_copies(packed, "out", wo, sem, len(down) + len(up), width, hidden)
    for copy in down:
        copy.start()
    saved = move([(slope_i, slope), (h2_i, h2_t)], in_sem, 1)
    for copy in up + out:
        copy.start()
    saved += move([(r1_i, r1)], in_sem, 3)
    totals = jnp.sum(row_all[...], axis=0)
    row_sum = jnp.concatenate([totals[k : k + 1] for k in range(totals.shape[0])], axis=1)
    live_own, same_own = own[:, 0:1], own[:, 1:2]
    pair = factor[0:1, 0:1] * live_own * live[...]
    match = jnp.where(own_group[...] == groups[...], 1.0 / same_own + 1.0 / same[...], 0.0)
    grad_scores = pair * (power[...] * (1.0 / row_sum + 1.0 / col_sum[...]) - match)
    gathered.wait()
    grad_low = LOGIT_SCALE * dot(grad_scores.astype(BF), images[...])
    pool = pooled[...]
    inverse = lax.rsqrt(jnp.sum(pool * pool, axis=-1, keepdims=True) + 1e-06)
    along = jnp.sum(pool * grad_low, axis=-1, keepdims=True)
    dy[...] = inverse * (grad_low - pool * (inverse * inverse * along)) * (1.0 / length)
    dm = dy[...].astype(BF)
    loss_rows[...] = jnp.broadcast_to(
        jnp.sum(live[...] * jnp.log(row_sum), axis=1, keepdims=True), loss_rows.shape
    )
    parts_x, parts_f = shard
    piece_x, piece_f = width // parts_x, hidden // parts_f
    for f in range(parts_f):
        left = acts[:, f * piece_f : (f + 1) * piece_f]
        for x in range(parts_x):
            factors[x * parts_f + f, :, piece_x:] = left
            factors[x * parts_f + f, :, :piece_x] = dm[:, x * piece_x : (x + 1) * piece_x]
    sent = move([(factors, factors_o)], out_sem, 11)
    down_bias[...] = length * jnp.sum(dm.astype(F32), axis=0, keepdims=True)
    for copy in down:
        copy.wait()
    dact[...] = dot(dm, natural(wd), 1, 1)
    saved[0].wait()

    saved[1].wait()
    half = hidden // PX
    outs = (keep_a, send_a, keep_b, send_b)
    for x in range(PX):
        first = (x ^ where[0]) * half

        def grads(i):
            c = pl.multiple_of(i * 256, 256)
            for second in range(2):
                at = pl.ds(pl.multiple_of(first + c + second * width, 256), 256)
                spread = jnp.broadcast_to(dact[:, at].reshape(texts, 1, 256), (texts, length, 256))
                part = (spread.reshape(rows, 256) * slope[:, at].astype(F32)).astype(BF)
                du[:, at] = part
                bias_up[:, at] = jnp.sum(part.astype(F32), axis=0, keepdims=True)
                put_grad(dot(h2_t[...], part), parts, x, c, second)

        repeat(width // 256, grads, 3)
        sent += start_grads(parts, outs, out_sem, x)

    v = vec[...].astype(F32)
    blk = 128
    for copy in up:
        copy.wait()

    def product(i):
        at = pl.ds(pl.multiple_of(i * (rows // 2), rows // 2), rows // 2)
        dr1[at, :] = dot(du[at, :], natural(wu), 1, 1)

    repeat(2, product)
    sums[...] = jnp.zeros((8, width), F32)
    some = blk // length
    saved[2].wait()

    def back(i):
        at = pl.ds(pl.multiple_of(i * blk, blk), blk)
        hat, inverse = normalize(r1[at, :])
        grad = dr1[at, :]
        sums[1:2, :] += jnp.sum(grad * hat, axis=0, keepdims=True)
        sums[2:3, :] += jnp.sum(grad, axis=0, keepdims=True)
        spread = jnp.broadcast_to(
            dy[pl.ds(pl.multiple_of(i * some, some), some), :].reshape(some, 1, width), (some, length, width)
        ).reshape(blk, width)
        grad = spread + norm_back(grad, hat, inverse, v[5:6])
        dr1[at, :] = grad
        low = grad.astype(BF)
        dz_s[at, :] = low
        sums[0:1, :] += jnp.sum(low.astype(F32), axis=0, keepdims=True)

    repeat(rows // blk, back, 2)
    sent += move([(dr1, dr1_o), (dz_s, dz_o)], out_sem, 8)
    for copy in out:
        copy.wait()
    da_s[...] = dot(dz_s[...], natural(wo), 1, 1).astype(BF)
    sent += move([(da_s, da_o)], out_sem, 10)
    for copy in sent:
        copy.wait()


def back_one(
    where, power, row_all, col_sum, images, live, same, groups, own, own_group, factor, pooled, packed, vec, slope,
    h2_t, r1, acts, length, shard,
):
    rows, hidden = slope.shape
    width = h2_t.shape[0]
    texts = rows // length
    payload = (shard[0] * shard[1], texts, width // shard[0] + hidden // shard[1])
    shape = jax.ShapeDtypeStruct
    return pl.pallas_call(
        functools.partial(back_one_kernel, length, shard),
        name="back_one",
        in_specs=[SMEM] + [WHOLE] * 3 + [ANY] + [WHOLE] * 7 + [ANY, WHOLE, ANY, ANY, ANY, WHOLE],
        out_specs=[ANY] * 5 + [WHOLE] * 2 + [ANY] * 3 + [WHOLE] * 2,
        out_shape=[
            shape(payload, BF),
            *grad_shapes(width),
            shape((1, hidden), F32),
            shape((1, width), F32),
            shape((rows, width), F32),
            shape((rows, width), BF),
            shape((rows, width), BF),
            shape((8, width), F32),
            shape((8, 128), F32),
        ],
        scratch_shapes=[
            pltpu.VMEM(payload, BF),
            weight_scratch("down", width, hidden),
            weight_scratch("up", width, hidden),
            weight_scratch("out", width, hidden),
            pltpu.VMEM((texts, hidden), F32),
            pltpu.VMEM(images.shape, BF),
            pltpu.VMEM((rows, hidden), BF),
            pltpu.VMEM((width, rows), BF),
            pltpu.VMEM((rows, width), F32),
            pltpu.VMEM((rows, hidden), BF),
            pltpu.VMEM((rows, width), F32),
            pltpu.VMEM((rows, width), BF),
            pltpu.VMEM((rows, width), BF),
            pltpu.VMEM((texts, width), F32),
            pltpu.VMEM((4,) + grad_shapes(width)[0].shape, BF),
            pltpu.SemaphoreType.DMA((PX * (2 + hidden // width),)),
            pltpu.SemaphoreType.DMA((4,)),
            pltpu.SemaphoreType.DMA((12,)),
        ],
        compiler_params=params(),
        cost_estimate=pl.CostEstimate(
            flops=2 * rows * width * (2 * hidden + width), bytes_accessed=16 * width * hidden, transcendentals=0
        ),
    )(
        where, power, row_all, col_sum, images, live, same, groups, own, own_group, factor, pooled, packed, vec,
        slope, h2_t, r1, acts,
    )


def back_two_kernel(
    length, where, qkv_i, da_i, dz_i, h1_i, att_i, dqkv_o, keep_a, send_a, keep_b, send_b, sums,
    qkv, da_s, dz, h1_t, att_t, dqkv, parts, sem, out_sem,
):
    rows, width = da_s.shape
    blk = 128
    loads = move([(qkv_i, qkv), (da_i, da_s), (att_i, att_t), (dz_i, dz), (h1_i, h1_t)], sem)
    for copy in loads[:2]:
        copy.wait()
    low_lane = lax.broadcasted_iota(jnp.int32, (blk, 128), 1) < HEAD_DIM
    bias = text_mask(blk, length)
    cols = range(0, width, 128)
    def group(i):
        at = pl.ds(pl.multiple_of(i * blk, blk), blk)
        take = lambda base, c: qkv[at, base + c : base + c + 128]
        q2 = [take(0, c) * 0.125 for c in cols]
        k2 = [head_pair(take(width, c), low_lane) for c in cols]
        v2 = [head_pair(take(2 * width, c), low_lane) for c in cols]
        da = [da_s[at, c : c + 128] for c in cols]
        scores = [dot(k, q, 1, 1) for k, q in zip(k2, q2)]
        grads = [dot(v, d, 1, 1) for v, d in zip(v2, da)]
        probs, deltas = [], []
        for score, grad in zip(scores, grads):
            p_low, d_low = [], []
            for half in range(2):
                s = score[half * blk : (half + 1) * blk] + bias
                g = grad[half * blk : (half + 1) * blk]
                powers = jnp.exp(s - jnp.max(s, axis=0, keepdims=True))
                soft = powers * (1.0 / jnp.sum(powers, axis=0, keepdims=True))
                p_low.append(soft.astype(BF))
                d_low.append((soft * (g - jnp.sum(g * soft, axis=0, keepdims=True))).astype(BF))
            probs.append(jnp.concatenate(p_low, axis=0))
            deltas.append(jnp.concatenate(d_low, axis=0))
        for n, c in enumerate(cols):
            dq = dot(deltas[n], k2[n], 0, 0) * 0.125
            dk = dot(deltas[n], q2[n])
            dv = dot(probs[n], da[n])
            dqkv[at, c : c + 128] = dq.astype(BF)
            dqkv[at, width + c : width + c + 128] = jnp.where(
                low_lane, dk[:blk], dk[blk:]
            ).astype(BF)
            dqkv[at, 2 * width + c : 2 * width + c + 128] = jnp.where(
                low_lane, dv[:blk], dv[blk:]
            ).astype(BF)

    repeat(rows // blk, group, 2)
    sums[0:1, :] = jnp.sum(dqkv[:, :width].astype(F32), axis=0, keepdims=True)
    sums[1:2, :] = jnp.sum(dqkv[:, 2 * width :].astype(F32), axis=0, keepdims=True)
    sums[2:8, :] = jnp.zeros((6, width), F32)
    sent = move([(dqkv, dqkv_o)], out_sem, 8)
    for copy in loads[2:]:
        copy.wait()
    piece = width // PX
    outs = (keep_a, send_a, keep_b, send_b)
    for x in range(PX):
        other = x ^ where[0]
        first = other * (3 * piece)

        def chunk(i):
            c = pl.multiple_of(i * 256, 256)
            part = dqkv[:, pl.ds(pl.multiple_of(first + c, 128), 256)]
            put_grad(dot(h1_t[...], part), parts, x, c, 0)

        repeat(width // 256, chunk, 3)
        part = dqkv[:, pl.ds(pl.multiple_of(first + width, 128), piece)]
        put_grad(dot(h1_t[...], part), parts, x, 0, 1)
        part = dz[:, pl.ds(pl.multiple_of(other * piece, 128), piece)]
        put_grad(dot(att_t[...], part), parts, x, piece, 1)
        sent += start_grads(parts, outs, out_sem, x)
    for copy in sent:
        copy.wait()


def back_two(where, qkv, da, dz, h1_t, att_t, length):
    rows, width = da.shape
    shape = jax.ShapeDtypeStruct
    return pl.pallas_call(
        functools.partial(back_two_kernel, length),
        name="back_two",
        in_specs=[SMEM] + [ANY] * 5,
        out_specs=[ANY] * 5 + [WHOLE],
        out_shape=[shape((rows, 3 * width), BF), *grad_shapes(width), shape((8, width), F32)],
        scratch_shapes=[
            pltpu.VMEM((rows, 3 * width), BF),
            pltpu.VMEM((rows, width), BF),
            pltpu.VMEM((rows, width), BF),
            pltpu.VMEM((width, rows), BF),
            pltpu.VMEM((width, rows), BF),
            pltpu.VMEM((rows, 3 * width), BF),
            pltpu.VMEM((4,) + grad_shapes(width)[0].shape, BF),
            pltpu.SemaphoreType.DMA((5,)),
            pltpu.SemaphoreType.DMA((9,)),
        ],
        compiler_params=params(),
        cost_estimate=pl.CostEstimate(
            flops=2 * rows * width * (1280 + 4 * width), bytes_accessed=20 * rows * width, transcendentals=rows * width
        ),
    )(where, qkv, da, dz, h1_t, att_t)


def back_third_kernel(
    parts_f, dr1_i, dqkv_i, tok_i, packed, vec, sums, bias_sums, down_bias, bias_up, loss_part, dx_o, share, all_sums, wq, dr1, tok, dx, sem, dqkv, own_sem
):
    rows, width = tok.shape
    loads = weight_copies(packed, "qkv", wq, sem, 0, width, width)
    for copy in loads:
        copy.start()
    saved = move([(dqkv_i, dqkv), (dr1_i, dr1), (tok_i, tok)], own_sem)
    saved[0].wait()
    v = vec[...].astype(F32)
    for copy in loads:
        copy.wait()
    half = rows // 2

    def product(i):
        at = pl.ds(pl.multiple_of(i * half, half), half)
        dx[at, :] = dot(dqkv[at, :], natural(wq), 1, 1)

    repeat(2, product)
    for copy in saved[1:]:
        copy.wait()
    all_sums[0:2, :] = jnp.zeros((2, width), F32)
    blk = 128

    def back(i):
        at = pl.ds(pl.multiple_of(i * blk, blk), blk)
        hat, inverse = normalize(tok[at, :].astype(F32))
        grad = dx[at, :]
        all_sums[0:1, :] += jnp.sum(grad * hat, axis=0, keepdims=True)
        all_sums[1:2, :] += jnp.sum(grad, axis=0, keepdims=True)
        dx[at, :] = dr1[at, :] + norm_back(grad, hat, inverse, v[0:1])

    repeat(rows // blk, back, 2)
    (save,) = move([(dx, dx_o)], own_sem, 3)
    all_sums[2:4, :] = bias_sums[0:2, :]
    all_sums[4:7, :] = sums[0:3, :]
    all_sums[7:8, :] = down_bias[...]
    every = all_sums[...]
    piece, tall = width // parts_f, bias_up.shape[1] // parts_f
    devices = share.shape[0]
    used = piece + tall // 8
    for f in range(parts_f):
        bias = bias_up[:, f * tall : (f + 1) * tall]
        bias = jnp.concatenate([bias[:, r * tall // 8 : (r + 1) * tall // 8] for r in range(8)], axis=0)
        block = jnp.concatenate(
            [every[:, f * piece : (f + 1) * piece], bias, loss_part[:, : 128 - used]], axis=1
        )
        for x in range(devices // parts_f):
            share[x * parts_f + f] = block
    save.wait()


def back_third(dr1, dqkv, tok, packed, vec, sums, bias_sums, down_bias, bias_up, loss_part, shard):
    rows, width = tok.shape
    shape = jax.ShapeDtypeStruct
    return pl.pallas_call(
        functools.partial(back_third_kernel, shard[1]),
        name="back_third",
        in_specs=[ANY, ANY, ANY, ANY] + [WHOLE] * 6,
        out_specs=[ANY, WHOLE],
        out_shape=[shape((rows, width), F32), shape((shard[0] * shard[1], 8, 128), F32)],
        scratch_shapes=[
            pltpu.VMEM((8, width), F32),
            weight_scratch("qkv", width, width),
            pltpu.VMEM((rows, width), F32),
            pltpu.VMEM((rows, width), BF),
            pltpu.VMEM((rows, width), F32),
            pltpu.SemaphoreType.DMA((PX * 3,)),
            pltpu.VMEM((rows, 3 * width), BF),
            pltpu.SemaphoreType.DMA((4,)),
        ],
        compiler_params=params(),
        cost_estimate=pl.CostEstimate(
            flops=6 * rows * width * width, bytes_accessed=14 * width * width, transcendentals=0
        ),
    )(dr1, dqkv, tok, packed, vec, sums, bias_sums, down_bias, bias_up, loss_part)


def fold_kernel(a_own, a_new, b_own, b_new, a_keep, a_send, b_keep, b_send):
    for own, new, keep, send in ((a_own, a_new, a_keep, a_send), (b_own, b_new, b_keep, b_send)):
        total = own[...].astype(F32) + new[...].astype(F32)
        keep[...] = total[0].astype(BF)
        send[...] = total[1].astype(BF)


def fold(a_own, a_new, b_own, b_new):
    shape = a_own.shape
    rest = 1
    for n in shape[1:-2]:
        rest *= n
    rows, cols = shape[-2:]
    view = lambda a: a.reshape(2, rest, rows, cols)
    steps = 2 if rest > 4 else 1
    pair = pl.BlockSpec((2, rest // steps, rows, cols), lambda i: (0, i, 0, 0))
    one = pl.BlockSpec((rest // steps, rows, cols), lambda i: (i, 0, 0))
    outs = pl.pallas_call(
        fold_kernel,
        name="fold",
        grid=(steps,),
        in_specs=[pair] * 4,
        out_specs=[one] * 4,
        out_shape=[jax.ShapeDtypeStruct((rest, rows, cols), BF)] * 4,
        compiler_params=params(18),
        cost_estimate=pl.CostEstimate(
            flops=4 * rest * rows * cols, bytes_accessed=24 * rest * rows * cols, transcendentals=0
        ),
    )(*(view(a) for a in (a_own, a_new, b_own, b_new)))
    return [o.reshape(shape[1:]) for o in outs]


def join_kernel(a_own, a_new, b_own, b_new, keep, send):
    half = a_own.shape[-1]
    for at, own, new in ((0, a_own, a_new), (half, b_own, b_new)):
        total = own[...].astype(F32) + new[...].astype(F32)
        for k in range(2):
            keep[k, :, at : at + half] = total[2 * k]
            send[k, :, at : at + half] = total[2 * k + 1].astype(BF)


def join(a_own, a_new, b_own, b_new):
    blocks, rows, cols = a_own.shape
    shape = jax.ShapeDtypeStruct
    return pl.pallas_call(
        join_kernel,
        name="join",
        in_specs=[WHOLE] * 4,
        out_specs=[WHOLE] * 2,
        out_shape=[shape((2, rows, 2 * cols), F32), shape((2, rows, 2 * cols), BF)],
        compiler_params=params(6),
        cost_estimate=pl.CostEstimate(
            flops=16 * rows * cols, bytes_accessed=40 * rows * cols, transcendentals=0
        ),
    )(a_own, a_new, b_own, b_new)


def turn_kernel(keep, new, stay, send):
    stay[...] = keep[0] + new[0].astype(F32)
    send[...] = (keep[1] + new[1].astype(F32)).astype(BF)


def turn(keep, new):
    blocks, rows, cols = keep.shape
    shape = jax.ShapeDtypeStruct
    return pl.pallas_call(
        turn_kernel,
        name="turn",
        in_specs=[WHOLE] * 2,
        out_specs=[WHOLE] * 2,
        out_shape=[shape((rows, cols), F32), shape((rows, cols), BF)],
        compiler_params=params(6),
        cost_estimate=pl.CostEstimate(
            flops=4 * rows * cols, bytes_accessed=18 * rows * cols, transcendentals=0
        ),
    )(keep, new)


def shifted(x, y, z, core):
    change = x * 16 + z * 4 + y * 2 + core
    return [(i, i ^ change) for i in range(32)]


def hop(array, x=0, y=0, z=0, core=0):
    return lax.ppermute(array, AXES, shifted(x, y, z, core))


def after(values, *others):
    return lax.optimization_barrier((tuple(values), others))[0]


def core_step(parts, *wait):
    keep_a, send_a, keep_b, send_b = parts
    new_a, new_b = hop(send_a, core=1), hop(send_b, core=1)
    keep_a, keep_b = after((keep_a, keep_b), *wait)
    return fold(keep_a, new_a, keep_b, new_b)


def first_step(parts, *wait):
    keep_a, send_a, keep_b, send_b = parts
    new_a, new_b = hop(send_a, x=1), hop(send_b, y=1)
    keep_a, keep_b = after((keep_a, keep_b), *wait)
    return fold(keep_a, new_a, keep_b, new_b)


def second_step(parts, *wait):
    keep_a, send_a, keep_b, send_b = parts
    new_a, new_b = hop(send_a, y=1), hop(send_b, x=1)
    keep_a, keep_b = after((keep_a, keep_b), *wait)
    return join(keep_a, new_a, keep_b, new_b)


def total_kernel(stay, new, *outs):
    total = stay[...] + new[...].astype(F32)
    at = 0
    for out in outs:
        out[...] = total[:, at : at + out.shape[1]]
        at += out.shape[1]


def third_step(parts, *wait):
    keep, send = parts
    new = hop(send, z=1)
    (keep,) = after((keep,), *wait)
    return turn(keep, new)


def last_step(parts, splits):
    stay, send = parts
    return pl.pallas_call(
        total_kernel,
        name="total",
        in_specs=[WHOLE] * 2,
        out_specs=[WHOLE] * len(splits),
        out_shape=[jax.ShapeDtypeStruct((stay.shape[0], n), F32) for n in splits],
        compiler_params=params(4),
    )(stay, hop(send, z=2))


def natural_grad(keep_a, send_a, keep_b, send_b):
    first = jnp.stack([keep_a, send_a])
    second = jnp.swapaxes(jnp.stack([keep_b, send_b]), 1, 2)
    whole = jnp.concatenate([first, second], axis=-1)
    core, x, y, z, rows, cols = whole.shape
    return whole.transpose(1, 3, 2, 0, 4, 5).reshape(x, z * y * core * rows, cols)


def pack_kernel(qkv, out, up, down, packed):
    rows, piece = out.shape
    at = 0
    for ref in (qkv, out, up, down):
        for c in range(0, ref.shape[1], piece):
            packed[at : at + ref.shape[0], :] = ref[:, c : c + piece]
            at += ref.shape[0]


def pack_block(qkv, out, up, down):
    piece = out.shape[1]
    total = sum(w.shape[0] * w.shape[1] for w in (qkv, out, up, down)) // piece
    return pl.pallas_call(
        pack_kernel,
        name="pack_block",
        in_specs=[WHOLE] * 4,
        out_specs=WHOLE,
        out_shape=jax.ShapeDtypeStruct((total, piece), BF),
        compiler_params=params(),
    )(qkv, out, up, down)


def gather_packed(qkv, out, up, down, dp, fsdp):
    if (dp, fsdp) == (PX, PF):
        return lax.all_gather(pack_block(qkv, out, up, down), AXES, axis=0)
    full = [
        lax.all_gather(lax.all_gather(w, "dp", axis=1, tiled=True), "fsdp", axis=0, tiled=True)
        for w in (qkv, out, up, down)
    ]
    blocks = []
    for x in range(PX):
        for f in range(PF):
            some = []
            for w in full:
                rows, cols = w.shape[0] // PF, w.shape[1] // PX
                some.append(w[f * rows : (f + 1) * rows, x * cols : (x + 1) * cols])
            blocks.append(pack_block(*some))
    return jnp.stack(blocks)


def scatter_columns(grad, dp, fsdp):
    parts, rows, cols = grad.shape
    if dp != parts:
        grad = jnp.swapaxes(grad, 0, 1).reshape(rows, dp, parts * cols // dp)
        grad = jnp.swapaxes(grad, 0, 1)
    return lax.psum_scatter(
        grad.reshape(dp * rows, -1), AXES, scatter_dimension=0, tiled=True
    ).astype(F32)


def body(
    image_tokens,
    text_tokens,
    image_qkv,
    image_out,
    image_up,
    image_down,
    image_vectors,
    image_up_bias,
    text_qkv,
    text_out,
    text_up,
    text_down,
    text_vectors,
    text_up_bias,
    pair_counts,
    pair_groups,
):
    dp, fsdp = lax.axis_size("dp"), lax.axis_size("fsdp")
    devices = dp * fsdp
    cap, length, width = text_tokens.shape
    hidden = image_up.shape[1]
    pairs = pair_groups.shape[0]
    me = lax.axis_index("dp") * fsdp + lax.axis_index("fsdp")

    grid_mesh = (dp, fsdp) == (PX, PF)
    packed = gather_packed(text_qkv, text_out, text_up, text_down, dp, fsdp)
    part = width // fsdp
    small = jnp.concatenate([text_vectors, text_up_bias.reshape(8, -1)], axis=1)
    if grid_mesh:
        small = jnp.broadcast_to(small[None], (fsdp,) + small.shape)
        small = lax.all_to_all(small, "fsdp", 0, 0, tiled=True)
    else:
        small = lax.all_gather(small, "fsdp", axis=0)
    vec = jnp.swapaxes(small[:, :, :part], 0, 1).reshape(8, width)
    ub = small[:, :, part:].reshape(1, hidden)
    bits = [lax.shift_right_logical(me, k) & 1 for k in range(5)]
    where = jnp.stack([bits[4], bits[1], 2 * bits[3] + bits[2], bits[0]])
    where = where if grid_mesh else jnp.zeros_like(where)

    image_low = image_forward(
        image_tokens, image_qkv, image_out, image_up, image_down, image_vectors, image_up_bias
    )
    if grid_mesh:
        images = image_low
        for change in (dict(z=1), dict(z=2), dict(x=1), dict(y=1), dict(core=1)):
            images = jnp.concatenate([images, hop(images, **change)], axis=0)
        far = jnp.arange(devices, dtype=jnp.int32) ^ me
        bit = lambda k: lax.shift_right_logical(far, k) & 1
        order = bit(2) + 2 * bit(3) + 4 * bit(4) + 8 * bit(1) + 16 * bit(0)
        images = jnp.take(images.reshape(devices, cap, width), order, axis=0).reshape(pairs, width)
    else:
        images = lax.all_gather(image_low, AXES, axis=0, tiled=True)

    slots = jnp.arange(cap, dtype=jnp.int32)
    live = (slots[None, :] < pair_counts[:, None]).reshape(pairs).astype(F32)
    same = jnp.maximum(
        jnp.sum(jnp.where(pair_groups[:, None] == pair_groups[None, :], live[None, :], 0.0), axis=1), 1.0
    )
    own_of = lambda array: lax.dynamic_slice_in_dim(array, me * cap, cap)
    own = jnp.stack([own_of(live), own_of(same)], axis=1)
    own_group = own_of(pair_groups).reshape(cap, 1)
    live_row, same_row, group_row = (a.reshape(1, pairs) for a in (live, same, pair_groups))
    live_total = jnp.sum(pair_counts).astype(F32)
    factor = jnp.broadcast_to(LOSS_WEIGHT / (2.0 * live_total), (1, 128))

    tokens = text_tokens.reshape(cap * length, width)
    h1, qkv, att, r1, h2, slope, acts, pooled, power, row_part, col_sum, loss_part = text_forward(
        tokens, packed, vec, ub, images, live_row, same_row, group_row, own, own_group, length, hidden,
        devices if grid_mesh else 1,
    )
    if grid_mesh:
        row_all = lax.all_to_all(row_part, AXES, 0, 0, tiled=True)
    else:
        row_all = lax.psum(row_part, AXES)
    h1_t, h2_t, att_t = relative_rows(where, h1, h2, att)
    factors, *up_parts, bias_up, down_bias, dr1, dz, da, sums, loss_rows = back_one(
        where, power, row_all, col_sum, images, live_row, same_row, group_row, own, own_group, factor, pooled,
        packed, vec, slope, h2_t, r1, acts, length, (dp, fsdp),
    )
    dqkv, *att_parts, bias_sums = back_two(where, qkv, da, dz, h1_t, att_t, length)

    both = lax.all_to_all(factors, AXES, 0, 0, tiled=True).reshape(pairs, width // dp + hidden // fsdp)
    grad_down = dot(both[:, width // dp :], both[:, : width // dp], 0, 0)

    if grid_mesh:
        up_parts = core_step(up_parts, *att_parts)
        (att_keep,) = after((att_parts[0],), *up_parts)
        att_parts = core_step([att_keep] + att_parts[1:])
        (dqkv,) = after((dqkv,), *att_parts)
        dx, share = back_third(
            dr1, dqkv, tokens, packed, vec, sums, bias_sums, down_bias, bias_up, loss_part, (dp, fsdp)
        )
        up_parts = first_step(up_parts, dx)
        att_parts = first_step(att_parts, grad_down, *up_parts)
        up_parts = second_step(up_parts, *att_parts)
        (share,) = after((share,), *att_parts)
        att_parts = second_step(att_parts, *up_parts)
        up_parts = third_step(up_parts, *att_parts)
        att_parts = third_step(att_parts, *up_parts)
        (grad_up,) = last_step(up_parts, (hidden // dp,))
        grad_qkv, grad_out = last_step(att_parts, (3 * width // dp, width // dp))
    else:
        dx, share = back_third(
            dr1, dqkv, tokens, packed, vec, sums, bias_sums, down_bias, bias_up, loss_part, (dp, fsdp)
        )
        grad_attn = natural_grad(*att_parts)
        grad_up = scatter_columns(natural_grad(*up_parts), dp, fsdp)
        grad_qkv = scatter_columns(grad_attn[:, :, : 3 * width // PX], dp, fsdp)
        grad_out = scatter_columns(grad_attn[:, :, 3 * width // PX :], dp, fsdp)

    share = jnp.sum(lax.all_to_all(share, AXES, 0, 0, tiled=True), axis=0)
    grad_vec = share[:, :part]
    tall = hidden // fsdp // 8
    grad_bias = share[:, part : part + tall].reshape(hidden // fsdp)
    loss = (share[0, part + tall] + loss_rows[0, 0]) / (2.0 * live_total)

    return (
        loss,
        dx.reshape(text_tokens.shape),
        grad_qkv,
        grad_out,
        grad_up,
        grad_down,
        grad_vec,
        grad_bias,
    )


def solution(mesh):
    return jax.shard_map(
        body,
        mesh=mesh,
        in_specs=(
            P(AXES, None, None),
            P(AXES, None, None),
            P(),
            P(),
            P(),
            P(),
            P(),
            P(),
            P("fsdp", "dp"),
            P("fsdp", "dp"),
            P("fsdp", "dp"),
            P("fsdp", "dp"),
            P(None, "fsdp"),
            P("fsdp"),
            P(),
            P(),
        ),
        out_specs=(
            P(),
            P(AXES, None, None),
            P("fsdp", "dp"),
            P("fsdp", "dp"),
            P("fsdp", "dp"),
            P("fsdp", "dp"),
            P(None, "fsdp"),
            P("fsdp"),
        ),
        check_vma=False,
    )
```

```python
import functools

import jax
import jax.numpy as jnp
from jax import lax
from jax.experimental import pallas as pl
from jax.experimental.pallas import tpu as pltpu
from jax.sharding import PartitionSpec as P

HEAD_DIM = 64
LOGIT_SCALE = 50.0
LOSS_WEIGHT = 32768.0
BF = jnp.bfloat16
F32 = jnp.float32
AXES = ("dp", "fsdp")
PX, PF = 2, 16

ANY = pl.BlockSpec(memory_space=pltpu.HBM)
WHOLE = pl.BlockSpec(memory_space=pltpu.VMEM)


def params(mebibytes=62):
    return pltpu.CompilerParams(vmem_limit_bytes=mebibytes * 1024 * 1024)


def dot(a, b, ca=1, cb=0):
    return lax.dot_general(a, b, (((ca,), (cb,)), ((), ())), preferred_element_type=F32)


def repeat(count, step, together=1):
    def turn(j, _):
        for k in range(together):
            step(j * together + k)
        return 0

    if together >= count:
        for i in range(count):
            step(i)
    else:
        lax.fori_loop(0, count // together, turn, 0)


def move(pairs, sem, base=0):
    copies = [pltpu.make_async_copy(a, b, sem.at[base + i]) for i, (a, b) in enumerate(pairs)]
    for copy in copies:
        copy.start()
    return copies


def normalize(values):
    centered = values - jnp.mean(values, axis=-1, keepdims=True)
    inverse = lax.rsqrt(jnp.mean(centered * centered, axis=-1, keepdims=True) + 1e-05)
    return centered * inverse, inverse


def norm_back(grad, hat, inverse, gain):
    scaled = grad * gain
    return inverse * (
        scaled
        - jnp.mean(scaled, axis=-1, keepdims=True)
        - hat * jnp.mean(scaled * hat, axis=-1, keepdims=True)
    )


def gauss_tail(u):
    size = jnp.abs(u)
    t = 1.0 / (1.0 + (0.3275911 * 0.7071067811865476) * size)
    bell = jnp.exp2(-0.7213475204444817 * (u * u))
    poly = 0.5 * 1.061405429 * t - 0.5 * 1.453152027
    poly = poly * t + 0.5 * 1.421413741
    poly = poly * t - 0.5 * 0.284496736
    poly = poly * t + 0.5 * 0.254829592
    return poly * t * bell, bell, size


def head_pair(block, low_lane):
    zero = jnp.zeros_like(block)
    return jnp.concatenate(
        [jnp.where(low_lane, block, zero), jnp.where(low_lane, zero, block)], axis=0
    )


def softmax_half(scores, bias):
    scores = scores + bias
    top = jnp.max(scores, axis=-1, keepdims=True)
    powers = jnp.exp(scores - top)
    return powers * (1.0 / jnp.sum(powers, axis=-1, keepdims=True))


def unit_rows(pooled):
    return pooled * lax.rsqrt(jnp.sum(pooled * pooled, axis=-1, keepdims=True) + 1e-06)


def mean_down(total, count, down):
    mean = total * (1.0 / count)
    high = mean.astype(BF)
    low = (mean - high.astype(F32)).astype(BF)
    both = dot(jnp.concatenate([high, low], axis=0), down)
    return both[: mean.shape[0]] + both[mean.shape[0] :]


def image_kernel(
    tok, wq_h, wo_h, wu_h, wd_h, vec, ub, out, wq, wo, wu, wd, x, h, qkv, att, act_sum, r1_sum, bias_row, stage, sem
):
    step, steps = pl.program_id(0), pl.num_programs(0)
    length, group, width = tok.shape
    rows = group * length
    hidden = wu.shape[1]
    copies = [
        pltpu.make_async_copy(src, dst, sem.at[i])
        for i, (src, dst) in enumerate(((wq_h, wq), (wo_h, wo), (wu_h, wu), (wd_h, wd)))
    ]

    @pl.when(step == 0)
    def _():
        for copy in copies:
            copy.start()

    def arrived(i):
        @pl.when(step == 0)
        def _():
            copies[i].wait()

    v = vec[...].astype(F32)
    bias_row[:, :width] = v[2:3]
    bias_row[:, width : 2 * width] = jnp.zeros((1, width), F32)
    bias_row[:, 2 * width :] = v[3:4]
    for k in range(width // 128):
        stage[k] = tok[:, :, k * 128 : (k + 1) * 128].astype(F32).reshape(rows, 128)
        for i in range(group):
            x[pl.ds(i * length, length), k * 128 : (k + 1) * 128] = stage[k, pl.ds(i, length, stride=group), :]

    def norm_rows(gain, shift):
        blk = 80

        def one(i):
            at = pl.ds(pl.multiple_of(i * blk, blk), blk)
            hat, _ = normalize(x[at, :])
            h[at, :] = (hat * gain + shift).astype(BF)

        repeat(rows // blk, one, 5)

    norm_rows(v[0:1], v[1:2])
    arrived(0)

    def project(i):
        at = pl.ds(pl.multiple_of(i * 256, 256), 256)
        qkv[:, at] = (dot(h[...], wq[:, at]) + bias_row[:, at]).astype(BF)

    repeat(3 * width // 256, project, 3)

    wins = rows // (2 * length)
    q_len = 112
    low_lane = lax.broadcasted_iota(jnp.int32, (128, 128), 1) < HEAD_DIM
    cols = range(0, width, 128)

    def window(w):
        q_at = pl.multiple_of((2 * length * w) // 16 * 16, 16)
        k_at = pl.multiple_of(jnp.minimum(q_at, rows - 128), 16)
        lo, mid, hi = 2 * w * length, (2 * w + 1) * length, (2 * w + 2) * length
        qi = q_at + lax.broadcasted_iota(jnp.int32, (q_len, 128), 0)
        ki = k_at + lax.broadcasted_iota(jnp.int32, (q_len, 128), 1)
        first = (qi >= lo) & (qi < mid) & (ki >= lo) & (ki < mid)
        second = (qi >= mid) & (qi < hi) & (ki >= mid) & (ki < hi)
        bias = jnp.where(first | second, 0.0, -1e30)
        q_rows, k_rows = pl.ds(q_at, q_len), pl.ds(k_at, 128)
        q2 = [qkv[q_rows, c : c + 128] * 0.125 for c in cols]
        k2 = [head_pair(qkv[k_rows, width + c : width + c + 128], low_lane) for c in cols]
        v2 = [head_pair(qkv[k_rows, 2 * width + c : 2 * width + c + 128], low_lane) for c in cols]
        scores = [dot(q, k, 1, 1) for q, k in zip(q2, k2)]
        probs = [
            jnp.concatenate(
                [softmax_half(s[:, :128], bias).astype(BF), softmax_half(s[:, 128:], bias).astype(BF)],
                axis=1,
            )
            for s in scores
        ]
        mine = (q_at + lax.broadcasted_iota(jnp.int32, (16, 128), 0)) >= lo
        for c, p, values in zip(cols, probs, v2):
            mixed = dot(p, values)
            old = att[pl.ds(q_at, 16), c : c + 128].astype(F32)
            att[pl.ds(q_at, 16), c : c + 128] = jnp.where(mine, mixed[:16], old).astype(BF)
            att[pl.ds(q_at + 16, q_len - 16), c : c + 128] = mixed[16:].astype(BF)

    repeat(wins, window, 2)

    arrived(1)
    for c in range(0, width, 256):
        x[:, c : c + 256] = x[:, c : c + 256] + (dot(att[...], wo[:, c : c + 256]) + v[4:5, c : c + 256])
    norm_rows(v[5:6], v[6:7])

    def image_sums(values):
        sums = []
        for i in range(group):
            lo, hi = i * length, (i + 1) * length
            a, b = lo // 8 * 8, -(-hi // 8) * 8
            part = values[a:b]
            row = a + lax.broadcasted_iota(jnp.int32, (b - a, 1), 0)
            if lo % 8 or hi % 8:
                part = jnp.where((row >= lo) & (row < hi), part, 0.0)
            sums.append(jnp.sum(part, axis=0, keepdims=True))
        return jnp.concatenate(sums, axis=0)

    place = pl.ds(pl.multiple_of(step * group, group), group)
    for c in range(0, width, 256):
        r1_sum[place, c : c + 256] = image_sums(x[:, c : c + 256])
    arrived(2)

    def expand(i):
        at = pl.ds(pl.multiple_of(i * 256, 256), 256)
        u = dot(h[...], wu[:, at]) + ub[:, at].astype(F32)
        tail, _, size = gauss_tail(u)
        act_sum[place, at] = image_sums(jnp.maximum(u, 0.0) - size * tail)

    repeat(hidden // 256, expand, 3)
    arrived(3)

    @pl.when(step == steps - 1)
    def _():
        pooled = r1_sum[...] * (1.0 / length) + mean_down(act_sum[...], length, wd[...]) + v[7:8]
        out[...] = unit_rows(pooled).astype(BF)


def image_forward(tokens, wq, wo, wu, wd, vec, ub):
    pairs, length, width = tokens.shape
    hidden = wu.shape[1]
    group = 16
    rows = group * length
    return pl.pallas_call(
        image_kernel,
        name="image_forward",
        grid=(pairs // group,),
        in_specs=[
            pl.BlockSpec((length, group, width), lambda i: (0, i, 0)),
            ANY,
            ANY,
            ANY,
            ANY,
            pl.BlockSpec((8, width), lambda i: (0, 0)),
            pl.BlockSpec((1, hidden), lambda i: (0, 0)),
        ],
        out_specs=pl.BlockSpec((pairs, width), lambda i: (0, 0)),
        out_shape=jax.ShapeDtypeStruct((pairs, width), BF),
        scratch_shapes=[
            pltpu.VMEM((width, 3 * width), BF),
            pltpu.VMEM((width, width), BF),
            pltpu.VMEM((width, hidden), BF),
            pltpu.VMEM((hidden, width), BF),
            pltpu.VMEM((rows, width), F32),
            pltpu.VMEM((rows, width), BF),
            pltpu.VMEM((rows, 3 * width), BF),
            pltpu.VMEM((rows, width), BF),
            pltpu.VMEM((pairs, hidden), F32),
            pltpu.VMEM((pairs, width), F32),
            pltpu.VMEM((1, 3 * width), F32),
            pltpu.VMEM((width // 128, rows, 128), F32),
            pltpu.SemaphoreType.DMA((4,)),
        ],
        compiler_params=params(),
        cost_estimate=pl.CostEstimate(
            flops=2 * pairs * length * width * (4 * width + hidden),
            bytes_accessed=2 * (4 * width * width + 2 * width * hidden + pairs * length * width),
            transcendentals=pairs * length * hidden,
        ),
    )(jnp.swapaxes(tokens, 0, 1), wq, wo, wu, wd, vec, ub.reshape(1, hidden))


def pack_rows(width, hidden):
    piece, rows = width // PX, width // PF
    return piece, rows, hidden // PF


def weight_copies(packed, which, dst, sem, base, width, hidden):
    piece, rows, frows = pack_rows(width, hidden)
    q_pieces, u_pieces = 3, hidden // width
    spans = {
        "qkv": (0, q_pieces, rows),
        "out": (q_pieces * rows, 1, rows),
        "up": ((q_pieces + 1) * rows, u_pieces, rows),
        "down": ((q_pieces + 1 + u_pieces) * rows, 1, frows),
    }
    start, count, tall = spans[which]
    copies = []
    for x in range(PX):
        for p in range(count):
            copies.append(
                pltpu.make_async_copy(
                    packed.at[pl.ds(x * PF, PF), pl.ds(start + p * tall, tall), :],
                    dst.at[:, :, pl.ds((x * count + p) * piece, piece)],
                    sem.at[base + len(copies)],
                )
            )
    return copies


def natural(ref):
    blocks, rows, cols = ref.shape
    return ref[...].reshape(blocks * rows, cols)


def weight_scratch(which, width, hidden):
    rows, frows = width // PF, hidden // PF
    shape = {
        "qkv": (PF, rows, 3 * width),
        "out": (PF, rows, width),
        "up": (PF, rows, hidden),
        "down": (PF, frows, width),
    }[which]
    return pltpu.VMEM(shape, BF)


def contrast(low, images, live, same, groups, own, own_group, power, row_part, col_sum, loss_part):
    scores = LOGIT_SCALE * dot(low, images[...], 1, 1)
    exps = jnp.exp(scores)
    live_own, same_own = own[:, 0:1], own[:, 1:2]
    power[...] = exps
    rows = jnp.sum(exps * live_own, axis=0, keepdims=True)
    tiled = jnp.concatenate(
        [rows[:, k * 128 : (k + 1) * 128] for k in range(rows.shape[1] // 128)], axis=0
    )
    for d in range(row_part.shape[0]):
        row_part[d] = tiled
    cols = jnp.sum(exps * live[...], axis=1, keepdims=True)
    col_sum[...] = cols
    pair = jnp.where(own_group[...] == groups[...], live_own * live[...], 0.0)
    linear = pair * scores * (1.0 / same_own + 1.0 / same[...])
    losses = live_own * jnp.log(cols) - jnp.sum(linear, axis=1, keepdims=True)
    loss_part[...] = jnp.broadcast_to(jnp.sum(losses, axis=0, keepdims=True), loss_part.shape)


def text_mask(size, length):
    row = lax.broadcasted_iota(jnp.int32, (size, size), 0) // length
    col = lax.broadcasted_iota(jnp.int32, (size, size), 1) // length
    return jnp.where(row == col, 0.0, -1e30)


def text_forward_kernel(
    length, tok, packed, vec, ub, images_i, live, same, groups, own, own_group,
    h1_o, qkv_o, att_o, r1_o, h2_o, slope_o, acts, pooled_out, power, row_part, col_sum, loss_part,
    wq, wo, wu, wd, total, bias_row, h1, qkv, att, r1, h2, slope, sem, images, out_sem
):
    rows, width = tok.shape
    hidden = slope.shape[1]
    texts = rows // length
    load = {}
    base = 0
    for which, dst in (("qkv", wq), ("out", wo), ("up", wu), ("down", wd)):
        load[which] = weight_copies(packed, which, dst, sem, base, width, hidden)
        base += len(load[which])
        for copy in load[which]:
            copy.start()
    v = vec[...].astype(F32)
    bias_row[:, :width] = v[2:3]
    bias_row[:, width : 2 * width] = jnp.zeros((1, width), F32)
    bias_row[:, 2 * width :] = v[3:4]
    blk = 128

    def norm_rows(src, dst, gain, shift):
        def one(i):
            at = pl.ds(pl.multiple_of(i * blk, blk), blk)
            hat, _ = normalize(src[at, :].astype(F32))
            dst[at, :] = (hat * gain + shift).astype(BF)

        repeat(rows // blk, one, 2)

    norm_rows(tok, h1, v[0:1], v[1:2])
    saves = move([(h1, h1_o)], out_sem)
    (gathered,) = move([(images_i, images)], out_sem, 6)
    for copy in load["qkv"]:
        copy.wait()

    def project(i):
        at = pl.ds(pl.multiple_of(i * 256, 256), 256)
        qkv[:, at] = (dot(h1[...], wq[:, :, at].reshape(width, 256)) + bias_row[:, at]).astype(BF)

    repeat(3 * width // 256, project, 3)
    saves += move([(qkv, qkv_o)], out_sem, 1)
    low_lane = lax.broadcasted_iota(jnp.int32, (blk, 128), 1) < HEAD_DIM
    bias = text_mask(blk, length)
    cols = range(0, width, 128)

    def attend(i):
        at = pl.ds(pl.multiple_of(i * blk, blk), blk)
        q2 = [qkv[at, c : c + 128] * 0.125 for c in cols]
        k2 = [head_pair(qkv[at, width + c : width + c + 128], low_lane) for c in cols]
        v2 = [head_pair(qkv[at, 2 * width + c : 2 * width + c + 128], low_lane) for c in cols]
        scores = [dot(q, k, 1, 1) for q, k in zip(q2, k2)]
        probs = [
            jnp.concatenate(
                [softmax_half(s[:, :blk], bias).astype(BF), softmax_half(s[:, blk:], bias).astype(BF)],
                axis=1,
            )
            for s in scores
        ]
        for c, p, values in zip(cols, probs, v2):
            att[at, c : c + 128] = dot(p, values).astype(BF)

    repeat(rows // blk, attend, 2)
    saves += move([(att, att_o)], out_sem, 2)
    for copy in load["out"]:
        copy.wait()
    for c in range(0, width, 256):
        r1[:, c : c + 256] = tok[:, c : c + 256].astype(F32) + (
            dot(att[...], wo[:, :, c : c + 256].reshape(width, 256)) + v[4:5, c : c + 256]
        )
    saves += move([(r1, r1_o)], out_sem, 3)
    norm_rows(r1, h2, v[5:6], v[6:7])
    saves += move([(h2, h2_o)], out_sem, 4)
    for copy in load["up"]:
        copy.wait()

    def expand(i):
        at = pl.ds(pl.multiple_of(i * 256, 256), 256)
        u = dot(h2[...], wu[:, :, at].reshape(width, 256)) + ub[:, at].astype(F32)
        tail, bell, _ = gauss_tail(u)
        phi = jnp.where(u >= 0.0, 1.0 - tail, tail)
        act = u * phi
        slope[:, at] = (phi + u * (bell * 0.3989422804014327)).astype(BF)
        sums = jnp.sum(act.reshape(texts, length, 256), axis=1)
        total[:, at] = sums
        acts[:, at] = sums.astype(BF)

    repeat(hidden // 256, expand, 6)
    saves += move([(slope, slope_o)], out_sem, 5)
    for copy in load["down"]:
        copy.wait()
    mean_r1 = jnp.sum(r1[...].reshape(texts, length, width), axis=1) * (1.0 / length)
    pooled = mean_r1 + mean_down(total[...], length, natural(wd)) + v[7:8]
    pooled_out[...] = pooled
    gathered.wait()
    contrast(
        unit_rows(pooled).astype(BF), images, live, same, groups, own, own_group, power, row_part, col_sum, loss_part
    )
    for copy in saves:
        copy.wait()


def text_forward(
    tokens, packed, vec, ub, images, live, same, groups, own, own_group, length, hidden, copies_of
):
    rows, width = tokens.shape
    texts = rows // length
    pairs = images.shape[0]
    shape = jax.ShapeDtypeStruct
    copies = PX * (3 + 1 + hidden // width + 1)
    return pl.pallas_call(
        functools.partial(text_forward_kernel, length),
        name="text_forward",
        in_specs=[WHOLE, ANY, WHOLE, WHOLE, ANY] + [WHOLE] * 5,
        out_specs=[ANY] * 6 + [WHOLE] * 6,
        out_shape=[
            shape((rows, width), BF),
            shape((rows, 3 * width), BF),
            shape((rows, width), BF),
            shape((rows, width), F32),
            shape((rows, width), BF),
            shape((rows, hidden), BF),
            shape((texts, hidden), BF),
            shape((texts, width), F32),
            shape((texts, pairs), F32),
            shape((copies_of, pairs // 128, 128), F32),
            shape((texts, 1), F32),
            shape((8, 128), F32),
        ],
        scratch_shapes=[weight_scratch(w, width, hidden) for w in ("qkv", "out", "up", "down")]
        + [
            pltpu.VMEM((texts, hidden), F32),
            pltpu.VMEM((1, 3 * width), F32),
            pltpu.VMEM((rows, width), BF),
            pltpu.VMEM((rows, 3 * width), BF),
            pltpu.VMEM((rows, width), BF),
            pltpu.VMEM((rows, width), F32),
            pltpu.VMEM((rows, width), BF),
            pltpu.VMEM((rows, hidden), BF),
            pltpu.SemaphoreType.DMA((copies,)),
            pltpu.VMEM((pairs, width), BF),
            pltpu.SemaphoreType.DMA((7,)),
        ],
        compiler_params=params(),
        cost_estimate=pl.CostEstimate(
            flops=2 * rows * width * (4 * width + hidden),
            bytes_accessed=2 * (4 * width * width + 2 * width * hidden + 12 * rows * width),
            transcendentals=rows * hidden,
        ),
    )(tokens, packed, vec, ub, images, live, same, groups, own, own_group)


def relative_kernel(where, h1_i, h2_i, att_i, h1_o, h2_o, att_o, h1, h2, att, h1_t, h2_t, att_t, sem):
    width = h1.shape[1]
    block = width // PF
    my, mz, mc = where[1], where[2], where[3]
    loads = move([(h2_i, h2), (h1_i, h1), (att_i, att)], sem)
    saves = []
    for n, (src, dst, out) in enumerate(((h2, h2_t, h2_o), (h1, h1_t, h1_o), (att, att_t, att_o))):
        loads[n].wait()
        turned = src[...].T
        for z in range(4):
            for y in range(2):
                for c in range(2):
                    f = (z * 2 + y) * 2 + c
                    place = (((c ^ mc) * 2 + (y ^ my)) * 4 + (z ^ mz)) * block
                    dst[pl.ds(pl.multiple_of(place, block), block), :] = turned[
                        f * block : (f + 1) * block
                    ]
        saves += move([(dst, out)], sem, 3 + n)
    for copy in saves:
        copy.wait()


SMEM = pl.BlockSpec(memory_space=pltpu.SMEM)


def relative_rows(where, h1, h2, att):
    rows, width = h1.shape
    return pl.pallas_call(
        relative_kernel,
        name="relative_rows",
        in_specs=[SMEM, ANY, ANY, ANY],
        out_specs=[ANY] * 3,
        out_shape=[jax.ShapeDtypeStruct((width, rows), BF)] * 3,
        scratch_shapes=[pltpu.VMEM((rows, width), BF)] * 3
        + [pltpu.VMEM((width, rows), BF)] * 3
        + [pltpu.SemaphoreType.DMA((6,))],
        compiler_params=params(),
        cost_estimate=pl.CostEstimate(flops=0, bytes_accessed=12 * rows * width, transcendentals=0),
    )(where, h1, h2, att)


def grad_shapes(width):
    block, half = width // PF, width
    return [jax.ShapeDtypeStruct((2, 2, 4, block, half), BF)] * 4


def put_grad(values, outs, x_rel, at, second):
    width, cols = values.shape
    block = width // PF
    low = values.astype(BF)
    for c in range(2):
        for y in range(2):
            piece = low[(c * 2 + y) * 4 * block : (c * 2 + y + 1) * 4 * block].reshape(4, block, cols)
            if second:
                outs[2 + c, y, x_rel, :, :, pl.ds(at, cols)] = piece
            else:
                outs[c, x_rel, y, :, :, pl.ds(at, cols)] = piece


def start_grads(parts, outs, sem, x):
    return move(
        [(parts.at[n, x], outs[n].at[x]) for n in range(2)]
        + [(parts.at[n, :, x], outs[n].at[:, x]) for n in range(2, 4)],
        sem,
        4 * x,
    )


def back_one_kernel(
    length, shard,
    where, power, row_all, col_sum, images_i, live, same, groups, own, own_group, pooled, packed, vec,
    slope_i, h2_i, r1_i, acts,
    factors_o, keep_a, send_a, keep_b, send_b, bias_up, down_bias, dr1_o, dz_o, da_o, sums, loss_rows,
    factors, wd, wu, wo, dact, images, slope, h2_t, r1, du, dr1, dz_s, da_s, dy, parts, sem, in_sem, out_sem,
):
    rows, hidden = slope.shape
    texts = rows // length
    width = h2_t.shape[0]
    (gathered,) = move([(images_i, images)], in_sem)
    down = weight_copies(packed, "down", wd, sem, 0, width, hidden)
    up = weight_copies(packed, "up", wu, sem, len(down), width, hidden)
    out = weight_copies(packed, "out", wo, sem, len(down) + len(up), width, hidden)
    for copy in down:
        copy.start()
    saved = move([(slope_i, slope), (h2_i, h2_t)], in_sem, 1)
    for copy in up + out:
        copy.start()
    saved += move([(r1_i, r1)], in_sem, 3)
    totals = jnp.sum(row_all[...], axis=0)
    row_sum = jnp.concatenate([totals[k : k + 1] for k in range(totals.shape[0])], axis=1)
    live_own, same_own = own[:, 0:1], own[:, 1:2]
    factor = LOSS_WEIGHT / (2.0 * jnp.sum(live[...], axis=1, keepdims=True))
    pair = factor * live_own * live[...]
    match = jnp.where(own_group[...] == groups[...], 1.0 / same_own + 1.0 / same[...], 0.0)
    grad_scores = pair * (power[...] * (1.0 / row_sum + 1.0 / col_sum[...]) - match)
    gathered.wait()
    grad_low = LOGIT_SCALE * dot(grad_scores.astype(BF), images[...])
    pool = pooled[...]
    inverse = lax.rsqrt(jnp.sum(pool * pool, axis=-1, keepdims=True) + 1e-06)
    along = jnp.sum(pool * grad_low, axis=-1, keepdims=True)
    dy[...] = inverse * (grad_low - pool * (inverse * inverse * along)) * (1.0 / length)
    dm = dy[...].astype(BF)
    loss_rows[...] = jnp.broadcast_to(
        jnp.sum(live[...] * jnp.log(row_sum), axis=1, keepdims=True), loss_rows.shape
    )
    parts_x, parts_f = shard
    piece_x, piece_f = width // parts_x, hidden // parts_f
    for f in range(parts_f):
        left = acts[:, f * piece_f : (f + 1) * piece_f]
        for x in range(parts_x):
            factors[x * parts_f + f, :, piece_x:] = left
            factors[x * parts_f + f, :, :piece_x] = dm[:, x * piece_x : (x + 1) * piece_x]
    sent = move([(factors, factors_o)], out_sem, 11)
    down_bias[...] = length * jnp.sum(dm.astype(F32), axis=0, keepdims=True)
    for copy in down:
        copy.wait()
    dact[...] = dot(dm, natural(wd), 1, 1)
    saved[0].wait()

    saved[1].wait()
    half = hidden // PX
    outs = (keep_a, send_a, keep_b, send_b)
    for x in range(PX):
        first = (x ^ where[0]) * half

        def grads(i):
            c = pl.multiple_of(i * 256, 256)
            for second in range(2):
                at = pl.ds(pl.multiple_of(first + c + second * width, 256), 256)
                spread = jnp.broadcast_to(dact[:, at].reshape(texts, 1, 256), (texts, length, 256))
                part = (spread.reshape(rows, 256) * slope[:, at].astype(F32)).astype(BF)
                du[:, at] = part
                bias_up[:, at] = jnp.sum(part.astype(F32), axis=0, keepdims=True)
                put_grad(dot(h2_t[...], part), parts, x, c, second)

        repeat(width // 256, grads, 3)
        sent += start_grads(parts, outs, out_sem, x)

    v = vec[...].astype(F32)
    blk = 128
    for copy in up:
        copy.wait()

    def product(i):
        at = pl.ds(pl.multiple_of(i * (rows // 2), rows // 2), rows // 2)
        dr1[at, :] = dot(du[at, :], natural(wu), 1, 1)

    repeat(2, product)
    sums[...] = jnp.zeros((8, width), F32)
    some = blk // length
    saved[2].wait()

    def back(i):
        at = pl.ds(pl.multiple_of(i * blk, blk), blk)
        hat, inverse = normalize(r1[at, :])
        grad = dr1[at, :]
        sums[1:2, :] += jnp.sum(grad * hat, axis=0, keepdims=True)
        sums[2:3, :] += jnp.sum(grad, axis=0, keepdims=True)
        spread = jnp.broadcast_to(
            dy[pl.ds(pl.multiple_of(i * some, some), some), :].reshape(some, 1, width), (some, length, width)
        ).reshape(blk, width)
        grad = spread + norm_back(grad, hat, inverse, v[5:6])
        dr1[at, :] = grad
        low = grad.astype(BF)
        dz_s[at, :] = low
        sums[0:1, :] += jnp.sum(low.astype(F32), axis=0, keepdims=True)

    repeat(rows // blk, back, 2)
    sent += move([(dr1, dr1_o), (dz_s, dz_o)], out_sem, 8)
    for copy in out:
        copy.wait()
    da_s[...] = dot(dz_s[...], natural(wo), 1, 1).astype(BF)
    sent += move([(da_s, da_o)], out_sem, 10)
    for copy in sent:
        copy.wait()


def back_one(
    where, power, row_all, col_sum, images, live, same, groups, own, own_group, pooled, packed, vec, slope,
    h2_t, r1, acts, length, shard,
):
    rows, hidden = slope.shape
    width = h2_t.shape[0]
    texts = rows // length
    payload = (shard[0] * shard[1], texts, width // shard[0] + hidden // shard[1])
    shape = jax.ShapeDtypeStruct
    return pl.pallas_call(
        functools.partial(back_one_kernel, length, shard),
        name="back_one",
        in_specs=[SMEM] + [WHOLE] * 3 + [ANY] + [WHOLE] * 6 + [ANY, WHOLE, ANY, ANY, ANY, WHOLE],
        out_specs=[ANY] * 5 + [WHOLE] * 2 + [ANY] * 3 + [WHOLE] * 2,
        out_shape=[
            shape(payload, BF),
            *grad_shapes(width),
            shape((1, hidden), F32),
            shape((1, width), F32),
            shape((rows, width), F32),
            shape((rows, width), BF),
            shape((rows, width), BF),
            shape((8, width), F32),
            shape((8, 128), F32),
        ],
        scratch_shapes=[
            pltpu.VMEM(payload, BF),
            weight_scratch("down", width, hidden),
            weight_scratch("up", width, hidden),
            weight_scratch("out", width, hidden),
            pltpu.VMEM((texts, hidden), F32),
            pltpu.VMEM(images.shape, BF),
            pltpu.VMEM((rows, hidden), BF),
            pltpu.VMEM((width, rows), BF),
            pltpu.VMEM((rows, width), F32),
            pltpu.VMEM((rows, hidden), BF),
            pltpu.VMEM((rows, width), F32),
            pltpu.VMEM((rows, width), BF),
            pltpu.VMEM((rows, width), BF),
            pltpu.VMEM((texts, width), F32),
            pltpu.VMEM((4,) + grad_shapes(width)[0].shape, BF),
            pltpu.SemaphoreType.DMA((PX * (2 + hidden // width),)),
            pltpu.SemaphoreType.DMA((4,)),
            pltpu.SemaphoreType.DMA((12,)),
        ],
        compiler_params=params(),
        cost_estimate=pl.CostEstimate(
            flops=2 * rows * width * (2 * hidden + width), bytes_accessed=16 * width * hidden, transcendentals=0
        ),
    )(
        where, power, row_all, col_sum, images, live, same, groups, own, own_group, pooled, packed, vec,
        slope, h2_t, r1, acts,
    )


def back_two_kernel(
    length, where, qkv_i, da_i, dz_i, h1_i, att_i, up_a, up_a_new, up_b, up_b_new,
    dqkv_o, keep_a, send_a, keep_b, send_b, up_a_keep, up_a_send, up_b_keep, up_b_send, sums,
    qkv, da_s, dz, h1_t, att_t, dqkv, parts, held, come, sem, out_sem, up_sem,
):
    rows, width = da_s.shape
    blk = 128
    loads = move([(qkv_i, qkv), (da_i, da_s), (att_i, att_t), (dz_i, dz), (h1_i, h1_t)], sem)
    arrivals = move(
        [(up_a, held.at[0]), (up_a_new, come.at[0]), (up_b, held.at[1]), (up_b_new, come.at[1])], up_sem
    )
    for copy in loads[:2]:
        copy.wait()
    low_lane = lax.broadcasted_iota(jnp.int32, (blk, 128), 1) < HEAD_DIM
    bias = text_mask(blk, length)
    cols = range(0, width, 128)
    def group(i):
        at = pl.ds(pl.multiple_of(i * blk, blk), blk)
        take = lambda base, c: qkv[at, base + c : base + c + 128]
        q2 = [take(0, c) * 0.125 for c in cols]
        k2 = [head_pair(take(width, c), low_lane) for c in cols]
        v2 = [head_pair(take(2 * width, c), low_lane) for c in cols]
        da = [da_s[at, c : c + 128] for c in cols]
        scores = [dot(k, q, 1, 1) for k, q in zip(k2, q2)]
        grads = [dot(v, d, 1, 1) for v, d in zip(v2, da)]
        probs, deltas = [], []
        for score, grad in zip(scores, grads):
            p_low, d_low = [], []
            for half in range(2):
                s = score[half * blk : (half + 1) * blk] + bias
                g = grad[half * blk : (half + 1) * blk]
                powers = jnp.exp(s - jnp.max(s, axis=0, keepdims=True))
                soft = powers * (1.0 / jnp.sum(powers, axis=0, keepdims=True))
                p_low.append(soft.astype(BF))
                d_low.append((soft * (g - jnp.sum(g * soft, axis=0, keepdims=True))).astype(BF))
            probs.append(jnp.concatenate(p_low, axis=0))
            deltas.append(jnp.concatenate(d_low, axis=0))
        for n, c in enumerate(cols):
            dq = dot(deltas[n], k2[n], 0, 0) * 0.125
            dk = dot(deltas[n], q2[n])
            dv = dot(probs[n], da[n])
            dqkv[at, c : c + 128] = dq.astype(BF)
            dqkv[at, width + c : width + c + 128] = jnp.where(
                low_lane, dk[:blk], dk[blk:]
            ).astype(BF)
            dqkv[at, 2 * width + c : 2 * width + c + 128] = jnp.where(
                low_lane, dv[:blk], dv[blk:]
            ).astype(BF)

    repeat(rows // blk, group, 2)
    sums[0:1, :] = jnp.sum(dqkv[:, :width].astype(F32), axis=0, keepdims=True)
    sums[1:2, :] = jnp.sum(dqkv[:, 2 * width :].astype(F32), axis=0, keepdims=True)
    sums[2:8, :] = jnp.zeros((6, width), F32)
    sent = move([(dqkv, dqkv_o)], out_sem, 8)
    for copy in arrivals:
        copy.wait()

    def add(i):
        n, first, second = i // 4, i // 2 % 2, i % 2
        held[n, first, second] = (
            held[n, first, second].astype(F32) + come[n, first, second].astype(F32)
        ).astype(BF)

    repeat(8, add)
    sent += move(
        [
            (held.at[0, 0], up_a_keep),
            (held.at[0, 1], up_a_send),
            (held.at[1, 0], up_b_keep),
            (held.at[1, 1], up_b_send),
        ],
        up_sem,
        4,
    )
    for copy in loads[2:]:
        copy.wait()
    piece = width // PX
    outs = (keep_a, send_a, keep_b, send_b)
    for x in range(PX):
        other = x ^ where[0]
        first = other * (3 * piece)

        def chunk(i):
            c = pl.multiple_of(i * 256, 256)
            part = dqkv[:, pl.ds(pl.multiple_of(first + c, 128), 256)]
            put_grad(dot(h1_t[...], part), parts, x, c, 0)

        repeat(width // 256, chunk, 3)
        part = dqkv[:, pl.ds(pl.multiple_of(first + width, 128), piece)]
        put_grad(dot(h1_t[...], part), parts, x, 0, 1)
        part = dz[:, pl.ds(pl.multiple_of(other * piece, 128), piece)]
        put_grad(dot(att_t[...], part), parts, x, piece, 1)
        sent += start_grads(parts, outs, out_sem, x)
    for copy in sent:
        copy.wait()


def back_two(where, qkv, da, dz, h1_t, att_t, up_parts, length):
    rows, width = da.shape
    shape = jax.ShapeDtypeStruct
    whole = grad_shapes(width)
    return pl.pallas_call(
        functools.partial(back_two_kernel, length),
        name="back_two",
        in_specs=[SMEM] + [ANY] * 9,
        out_specs=[ANY] * 9 + [WHOLE],
        out_shape=[shape((rows, 3 * width), BF), *whole, *[shape(whole[0].shape[1:], BF)] * 4, shape((8, width), F32)],
        scratch_shapes=[
            pltpu.VMEM((rows, 3 * width), BF),
            pltpu.VMEM((rows, width), BF),
            pltpu.VMEM((rows, width), BF),
            pltpu.VMEM((width, rows), BF),
            pltpu.VMEM((width, rows), BF),
            pltpu.VMEM((rows, 3 * width), BF),
            pltpu.VMEM((4,) + whole[0].shape, BF),
            pltpu.VMEM((2,) + whole[0].shape, BF),
            pltpu.VMEM((2,) + whole[0].shape, BF),
            pltpu.SemaphoreType.DMA((5,)),
            pltpu.SemaphoreType.DMA((9,)),
            pltpu.SemaphoreType.DMA((8,)),
        ],
        compiler_params=params(),
        cost_estimate=pl.CostEstimate(
            flops=2 * rows * width * (1280 + 4 * width), bytes_accessed=20 * rows * width, transcendentals=rows * width
        ),
    )(where, qkv, da, dz, h1_t, att_t, *up_parts)


def back_third_kernel(
    parts_f, dr1_i, dqkv_i, tok_i, packed, vec, sums, bias_sums, down_bias, bias_up, loss_part, dx_o, share, all_sums, wq, dr1, tok, dx, sem, dqkv, own_sem
):
    rows, width = tok.shape
    loads = weight_copies(packed, "qkv", wq, sem, 0, width, width)
    for copy in loads:
        copy.start()
    saved = move([(dqkv_i, dqkv), (dr1_i, dr1), (tok_i, tok)], own_sem)
    saved[0].wait()
    v = vec[...].astype(F32)
    for copy in loads:
        copy.wait()
    half = rows // 2

    def product(i):
        at = pl.ds(pl.multiple_of(i * half, half), half)
        dx[at, :] = dot(dqkv[at, :], natural(wq), 1, 1)

    repeat(2, product)
    for copy in saved[1:]:
        copy.wait()
    all_sums[0:2, :] = jnp.zeros((2, width), F32)
    blk = 128

    def back(i):
        at = pl.ds(pl.multiple_of(i * blk, blk), blk)
        hat, inverse = normalize(tok[at, :].astype(F32))
        grad = dx[at, :]
        all_sums[0:1, :] += jnp.sum(grad * hat, axis=0, keepdims=True)
        all_sums[1:2, :] += jnp.sum(grad, axis=0, keepdims=True)
        dx[at, :] = dr1[at, :] + norm_back(grad, hat, inverse, v[0:1])

    repeat(rows // blk, back, 2)
    (save,) = move([(dx, dx_o)], own_sem, 3)
    all_sums[2:4, :] = bias_sums[0:2, :]
    all_sums[4:7, :] = sums[0:3, :]
    all_sums[7:8, :] = down_bias[...]
    every = all_sums[...]
    piece, tall = width // parts_f, bias_up.shape[1] // parts_f
    devices = share.shape[0]
    used = piece + tall // 8
    for f in range(parts_f):
        bias = bias_up[:, f * tall : (f + 1) * tall]
        bias = jnp.concatenate([bias[:, r * tall // 8 : (r + 1) * tall // 8] for r in range(8)], axis=0)
        block = jnp.concatenate(
            [every[:, f * piece : (f + 1) * piece], bias, loss_part[:, : 128 - used]], axis=1
        )
        for x in range(devices // parts_f):
            share[x * parts_f + f] = block
    save.wait()


def back_third(dr1, dqkv, tok, packed, vec, sums, bias_sums, down_bias, bias_up, loss_part, shard):
    rows, width = tok.shape
    shape = jax.ShapeDtypeStruct
    return pl.pallas_call(
        functools.partial(back_third_kernel, shard[1]),
        name="back_third",
        in_specs=[ANY, ANY, ANY, ANY] + [WHOLE] * 6,
        out_specs=[ANY, WHOLE],
        out_shape=[shape((rows, width), F32), shape((shard[0] * shard[1], 8, 128), F32)],
        scratch_shapes=[
            pltpu.VMEM((8, width), F32),
            weight_scratch("qkv", width, width),
            pltpu.VMEM((rows, width), F32),
            pltpu.VMEM((rows, width), BF),
            pltpu.VMEM((rows, width), F32),
            pltpu.SemaphoreType.DMA((PX * 3,)),
            pltpu.VMEM((rows, 3 * width), BF),
            pltpu.SemaphoreType.DMA((4,)),
        ],
        compiler_params=params(),
        cost_estimate=pl.CostEstimate(
            flops=6 * rows * width * width, bytes_accessed=14 * width * width, transcendentals=0
        ),
    )(dr1, dqkv, tok, packed, vec, sums, bias_sums, down_bias, bias_up, loss_part)


def fold_kernel(a_own, a_new, b_own, b_new, a_keep, a_send, b_keep, b_send):
    for own, new, keep, send in ((a_own, a_new, a_keep, a_send), (b_own, b_new, b_keep, b_send)):
        total = own[...].astype(F32) + new[...].astype(F32)
        keep[...] = total[0].astype(BF)
        send[...] = total[1].astype(BF)


def fold(a_own, a_new, b_own, b_new):
    shape = a_own.shape
    rest = 1
    for n in shape[1:-2]:
        rest *= n
    rows, cols = shape[-2:]
    view = lambda a: a.reshape(2, rest, rows, cols)
    steps = 2 if rest > 4 else 1
    pair = pl.BlockSpec((2, rest // steps, rows, cols), lambda i: (0, i, 0, 0))
    one = pl.BlockSpec((rest // steps, rows, cols), lambda i: (i, 0, 0))
    outs = pl.pallas_call(
        fold_kernel,
        name="fold",
        grid=(steps,),
        in_specs=[pair] * 4,
        out_specs=[one] * 4,
        out_shape=[jax.ShapeDtypeStruct((rest, rows, cols), BF)] * 4,
        compiler_params=params(18),
        cost_estimate=pl.CostEstimate(
            flops=4 * rest * rows * cols, bytes_accessed=24 * rest * rows * cols, transcendentals=0
        ),
    )(*(view(a) for a in (a_own, a_new, b_own, b_new)))
    return [o.reshape(shape[1:]) for o in outs]


def join_kernel(a_own, a_new, b_own, b_new, keep, send):
    half = a_own.shape[-1]
    for at, own, new in ((0, a_own, a_new), (half, b_own, b_new)):
        total = own[...].astype(F32) + new[...].astype(F32)
        for k in range(2):
            keep[k, :, at : at + half] = total[2 * k]
            send[k, :, at : at + half] = total[2 * k + 1].astype(BF)


def join(a_own, a_new, b_own, b_new):
    blocks, rows, cols = a_own.shape
    shape = jax.ShapeDtypeStruct
    return pl.pallas_call(
        join_kernel,
        name="join",
        in_specs=[WHOLE] * 4,
        out_specs=[WHOLE] * 2,
        out_shape=[shape((2, rows, 2 * cols), F32), shape((2, rows, 2 * cols), BF)],
        compiler_params=params(6),
        cost_estimate=pl.CostEstimate(
            flops=16 * rows * cols, bytes_accessed=40 * rows * cols, transcendentals=0
        ),
    )(a_own, a_new, b_own, b_new)


def turn_kernel(keep, new, stay, send):
    stay[...] = keep[0] + new[0].astype(F32)
    send[...] = (keep[1] + new[1].astype(F32)).astype(BF)


def turn(keep, new):
    blocks, rows, cols = keep.shape
    shape = jax.ShapeDtypeStruct
    return pl.pallas_call(
        turn_kernel,
        name="turn",
        in_specs=[WHOLE] * 2,
        out_specs=[WHOLE] * 2,
        out_shape=[shape((rows, cols), F32), shape((rows, cols), BF)],
        compiler_params=params(6),
        cost_estimate=pl.CostEstimate(
            flops=4 * rows * cols, bytes_accessed=18 * rows * cols, transcendentals=0
        ),
    )(keep, new)


def shifted(x, y, z, core):
    change = x * 16 + z * 4 + y * 2 + core
    return [(i, i ^ change) for i in range(32)]


def hop(array, x=0, y=0, z=0, core=0):
    return lax.ppermute(array, AXES, shifted(x, y, z, core))


def after(values, *others):
    return lax.optimization_barrier((tuple(values), others))[0]


def core_step(parts, *wait):
    keep_a, send_a, keep_b, send_b = parts
    new_a, new_b = hop(send_a, core=1), hop(send_b, core=1)
    keep_a, keep_b = after((keep_a, keep_b), *wait)
    return fold(keep_a, new_a, keep_b, new_b)


def first_step(parts, *wait):
    keep_a, send_a, keep_b, send_b = parts
    new_a, new_b = hop(send_a, x=1), hop(send_b, y=1)
    keep_a, keep_b = after((keep_a, keep_b), *wait)
    return fold(keep_a, new_a, keep_b, new_b)


def second_step(parts, *wait):
    keep_a, send_a, keep_b, send_b = parts
    new_a, new_b = hop(send_a, y=1), hop(send_b, x=1)
    keep_a, keep_b = after((keep_a, keep_b), *wait)
    return join(keep_a, new_a, keep_b, new_b)


def total_kernel(stay, new, *outs):
    total = stay[...] + new[...].astype(F32)
    at = 0
    for out in outs:
        out[...] = total[:, at : at + out.shape[1]]
        at += out.shape[1]


def third_step(parts, *wait):
    keep, send = parts
    new = hop(send, z=1)
    (keep,) = after((keep,), *wait)
    return turn(keep, new)


def last_step(parts, splits):
    stay, send = parts
    return pl.pallas_call(
        total_kernel,
        name="total",
        in_specs=[WHOLE] * 2,
        out_specs=[WHOLE] * len(splits),
        out_shape=[jax.ShapeDtypeStruct((stay.shape[0], n), F32) for n in splits],
        compiler_params=params(4),
    )(stay, hop(send, z=2))


def natural_grad(keep_a, send_a, keep_b, send_b):
    first = jnp.stack([keep_a, send_a])
    second = jnp.swapaxes(jnp.stack([keep_b, send_b]), 1, 2)
    whole = jnp.concatenate([first, second], axis=-1)
    core, x, y, z, rows, cols = whole.shape
    return whole.transpose(1, 3, 2, 0, 4, 5).reshape(x, z * y * core * rows, cols)


def pack_kernel(qkv, out, up, down, packed):
    rows, piece = out.shape
    at = 0
    for ref in (qkv, out, up, down):
        for c in range(0, ref.shape[1], piece):
            packed[at : at + ref.shape[0], :] = ref[:, c : c + piece]
            at += ref.shape[0]


def pack_block(qkv, out, up, down):
    piece = out.shape[1]
    total = sum(w.shape[0] * w.shape[1] for w in (qkv, out, up, down)) // piece
    return pl.pallas_call(
        pack_kernel,
        name="pack_block",
        in_specs=[WHOLE] * 4,
        out_specs=WHOLE,
        out_shape=jax.ShapeDtypeStruct((total, piece), BF),
        compiler_params=params(),
    )(qkv, out, up, down)


def gather_packed(qkv, out, up, down, dp, fsdp):
    if (dp, fsdp) == (PX, PF):
        return lax.all_gather(pack_block(qkv, out, up, down), AXES, axis=0)
    full = [
        lax.all_gather(lax.all_gather(w, "dp", axis=1, tiled=True), "fsdp", axis=0, tiled=True)
        for w in (qkv, out, up, down)
    ]
    blocks = []
    for x in range(PX):
        for f in range(PF):
            some = []
            for w in full:
                rows, cols = w.shape[0] // PF, w.shape[1] // PX
                some.append(w[f * rows : (f + 1) * rows, x * cols : (x + 1) * cols])
            blocks.append(pack_block(*some))
    return jnp.stack(blocks)


def scatter_columns(grad, dp, fsdp):
    parts, rows, cols = grad.shape
    if dp != parts:
        grad = jnp.swapaxes(grad, 0, 1).reshape(rows, dp, parts * cols // dp)
        grad = jnp.swapaxes(grad, 0, 1)
    return lax.psum_scatter(
        grad.reshape(dp * rows, -1), AXES, scatter_dimension=0, tiled=True
    ).astype(F32)


def body(
    image_tokens,
    text_tokens,
    image_qkv,
    image_out,
    image_up,
    image_down,
    image_vectors,
    image_up_bias,
    text_qkv,
    text_out,
    text_up,
    text_down,
    text_vectors,
    text_up_bias,
    pair_counts,
    pair_groups,
):
    dp, fsdp = lax.axis_size("dp"), lax.axis_size("fsdp")
    devices = dp * fsdp
    cap, length, width = text_tokens.shape
    hidden = image_up.shape[1]
    pairs = pair_groups.shape[0]
    me = lax.axis_index("dp") * fsdp + lax.axis_index("fsdp")

    grid_mesh = (dp, fsdp) == (PX, PF)
    packed = gather_packed(text_qkv, text_out, text_up, text_down, dp, fsdp)
    part = width // fsdp
    small = jnp.concatenate([text_vectors, text_up_bias.reshape(8, -1)], axis=1)
    if grid_mesh:
        small = jnp.broadcast_to(small[None], (fsdp,) + small.shape)
        small = lax.all_to_all(small, "fsdp", 0, 0, tiled=True)
    else:
        small = lax.all_gather(small, "fsdp", axis=0)
    vec = jnp.swapaxes(small[:, :, :part], 0, 1).reshape(8, width)
    ub = small[:, :, part:].reshape(1, hidden)
    bits = [lax.shift_right_logical(me, k) & 1 for k in range(5)]
    where = jnp.stack([bits[4], bits[1], 2 * bits[3] + bits[2], bits[0]])
    where = where if grid_mesh else jnp.zeros_like(where)

    image_low = image_forward(
        image_tokens, image_qkv, image_out, image_up, image_down, image_vectors, image_up_bias
    )
    if grid_mesh:
        images = image_low
        for change in (dict(z=1), dict(z=2), dict(x=1), dict(y=1), dict(core=1)):
            images = jnp.concatenate([images, hop(images, **change)], axis=0)
        far = jnp.arange(devices, dtype=jnp.int32) ^ me
        bit = lambda k: lax.shift_right_logical(far, k) & 1
        order = bit(2) + 2 * bit(3) + 4 * bit(4) + 8 * bit(1) + 16 * bit(0)
        images = jnp.take(images.reshape(devices, cap, width), order, axis=0).reshape(pairs, width)
    else:
        images = lax.all_gather(image_low, AXES, axis=0, tiled=True)

    slots = jnp.arange(cap, dtype=jnp.int32)
    live = (slots[None, :] < pair_counts[:, None]).reshape(pairs).astype(F32)
    same = jnp.maximum(
        jnp.sum(jnp.where(pair_groups[:, None] == pair_groups[None, :], live[None, :], 0.0), axis=1), 1.0
    )
    own_of = lambda array: lax.dynamic_slice_in_dim(array, me * cap, cap)
    own = jnp.stack([own_of(live), own_of(same)], axis=1)
    own_group = own_of(pair_groups).reshape(cap, 1)
    live_row, same_row, group_row = (a.reshape(1, pairs) for a in (live, same, pair_groups))
    live_total = jnp.sum(pair_counts).astype(F32)

    tokens = text_tokens.reshape(cap * length, width)
    h1, qkv, att, r1, h2, slope, acts, pooled, power, row_part, col_sum, loss_part = text_forward(
        tokens, packed, vec, ub, images, live_row, same_row, group_row, own, own_group, length, hidden,
        devices if grid_mesh else 1,
    )
    if grid_mesh:
        row_all = lax.all_to_all(row_part, AXES, 0, 0, tiled=True)
    else:
        row_all = lax.psum(row_part, AXES)
    h1_t, h2_t, att_t = relative_rows(where, h1, h2, att)
    factors, *up_parts, bias_up, down_bias, dr1, dz, da, sums, loss_rows = back_one(
        where, power, row_all, col_sum, images, live_row, same_row, group_row, own, own_group, pooled,
        packed, vec, slope, h2_t, r1, acts, length, (dp, fsdp),
    )
    keep_a, send_a, keep_b, send_b = up_parts
    if grid_mesh:
        travel = (keep_a, hop(send_a, core=1), keep_b, hop(send_b, core=1))
    else:
        travel = (keep_a, send_a, keep_b, send_b)
    dqkv, *both_parts, bias_sums = back_two(where, qkv, da, dz, h1_t, att_t, travel, length)
    att_parts = both_parts[:4]

    both = lax.all_to_all(factors, AXES, 0, 0, tiled=True).reshape(pairs, width // dp + hidden // fsdp)
    grad_down = dot(both[:, width // dp :], both[:, : width // dp], 0, 0)

    if grid_mesh:
        up_parts = both_parts[4:]
        att_parts = core_step(att_parts)
        (dqkv,) = after((dqkv,), *att_parts)
        dx, share = back_third(
            dr1, dqkv, tokens, packed, vec, sums, bias_sums, down_bias, bias_up, loss_part, (dp, fsdp)
        )
        up_parts = first_step(up_parts, dx)
        att_parts = first_step(att_parts, grad_down, *up_parts)
        up_parts = second_step(up_parts, *att_parts)
        (share,) = after((share,), *att_parts)
        att_parts = second_step(att_parts, *up_parts)
        up_parts = third_step(up_parts, *att_parts)
        att_parts = third_step(att_parts, *up_parts)
        (grad_up,) = last_step(up_parts, (hidden // dp,))
        grad_qkv, grad_out = last_step(att_parts, (3 * width // dp, width // dp))
    else:
        dx, share = back_third(
            dr1, dqkv, tokens, packed, vec, sums, bias_sums, down_bias, bias_up, loss_part, (dp, fsdp)
        )
        grad_attn = natural_grad(*att_parts)
        grad_up = scatter_columns(natural_grad(*up_parts), dp, fsdp)
        grad_qkv = scatter_columns(grad_attn[:, :, : 3 * width // PX], dp, fsdp)
        grad_out = scatter_columns(grad_attn[:, :, 3 * width // PX :], dp, fsdp)

    share = jnp.sum(lax.all_to_all(share, AXES, 0, 0, tiled=True), axis=0)
    grad_vec = share[:, :part]
    tall = hidden // fsdp // 8
    grad_bias = share[:, part : part + tall].reshape(hidden // fsdp)
    loss = (share[0, part + tall] + loss_rows[0, 0]) / (2.0 * live_total)

    return (
        loss,
        dx.reshape(text_tokens.shape),
        grad_qkv,
        grad_out,
        grad_up,
        grad_down,
        grad_vec,
        grad_bias,
    )


def solution(mesh):
    return jax.shard_map(
        body,
        mesh=mesh,
        in_specs=(
            P(AXES, None, None),
            P(AXES, None, None),
            P(),
            P(),
            P(),
            P(),
            P(),
            P(),
            P("fsdp", "dp"),
            P("fsdp", "dp"),
            P("fsdp", "dp"),
            P("fsdp", "dp"),
            P(None, "fsdp"),
            P("fsdp"),
            P(),
            P(),
        ),
        out_specs=(
            P(),
            P(AXES, None, None),
            P("fsdp", "dp"),
            P("fsdp", "dp"),
            P("fsdp", "dp"),
            P("fsdp", "dp"),
            P(None, "fsdp"),
            P("fsdp"),
        ),
        check_vma=False,
    )
```

```python
import functools

import jax
import jax.numpy as jnp
from jax import lax
from jax.experimental import pallas as pl
from jax.experimental.pallas import tpu as pltpu
from jax.sharding import PartitionSpec as P

HEAD_DIM = 64
LOGIT_SCALE = 50.0
LOSS_WEIGHT = 32768.0
BF = jnp.bfloat16
F32 = jnp.float32
AXES = ("dp", "fsdp")
PX, PF = 2, 16

ANY = pl.BlockSpec(memory_space=pltpu.HBM)
WHOLE = pl.BlockSpec(memory_space=pltpu.VMEM)


def params(mebibytes=62):
    return pltpu.CompilerParams(vmem_limit_bytes=mebibytes * 1024 * 1024)


def dot(a, b, ca=1, cb=0):
    return lax.dot_general(a, b, (((ca,), (cb,)), ((), ())), preferred_element_type=F32)


def repeat(count, step, together=1):
    def turn(j, _):
        for k in range(together):
            step(j * together + k)
        return 0

    if together >= count:
        for i in range(count):
            step(i)
    else:
        lax.fori_loop(0, count // together, turn, 0)


def move(pairs, sem, base=0):
    copies = [pltpu.make_async_copy(a, b, sem.at[base + i]) for i, (a, b) in enumerate(pairs)]
    for copy in copies:
        copy.start()
    return copies


def normalize(values):
    centered = values - jnp.mean(values, axis=-1, keepdims=True)
    inverse = lax.rsqrt(jnp.mean(centered * centered, axis=-1, keepdims=True) + 1e-05)
    return centered * inverse, inverse


def norm_back(grad, hat, inverse, gain):
    scaled = grad * gain
    return inverse * (
        scaled
        - jnp.mean(scaled, axis=-1, keepdims=True)
        - hat * jnp.mean(scaled * hat, axis=-1, keepdims=True)
    )


def gauss_tail(u):
    size = jnp.abs(u)
    t = 1.0 / (1.0 + (0.3275911 * 0.7071067811865476) * size)
    bell = jnp.exp2(-0.7213475204444817 * (u * u))
    poly = 0.5 * 1.061405429 * t - 0.5 * 1.453152027
    poly = poly * t + 0.5 * 1.421413741
    poly = poly * t - 0.5 * 0.284496736
    poly = poly * t + 0.5 * 0.254829592
    return poly * t * bell, bell, size


def head_pair(block, low_lane):
    zero = jnp.zeros_like(block)
    return jnp.concatenate(
        [jnp.where(low_lane, block, zero), jnp.where(low_lane, zero, block)], axis=0
    )


def softmax_half(scores, bias):
    scores = scores + bias
    top = jnp.max(scores, axis=-1, keepdims=True)
    powers = jnp.exp(scores - top)
    return powers * (1.0 / jnp.sum(powers, axis=-1, keepdims=True))


def unit_rows(pooled):
    return pooled * lax.rsqrt(jnp.sum(pooled * pooled, axis=-1, keepdims=True) + 1e-06)


def mean_down(total, count, down):
    mean = total * (1.0 / count)
    high = mean.astype(BF)
    low = (mean - high.astype(F32)).astype(BF)
    both = dot(jnp.concatenate([high, low], axis=0), down)
    return both[: mean.shape[0]] + both[mean.shape[0] :]


def image_kernel(
    tok, wq_h, wo_h, wu_h, wd_h, vec, ub, out, wq, wo, wu, wd, x, h, qkv, att, act_sum, r1_sum, bias_row, stage, sem
):
    step, steps = pl.program_id(0), pl.num_programs(0)
    length, group, width = tok.shape
    rows = group * length
    hidden = wu.shape[1]
    copies = [
        pltpu.make_async_copy(src, dst, sem.at[i])
        for i, (src, dst) in enumerate(((wq_h, wq), (wo_h, wo), (wu_h, wu), (wd_h, wd)))
    ]

    @pl.when(step == 0)
    def _():
        for copy in copies:
            copy.start()

    def arrived(i):
        @pl.when(step == 0)
        def _():
            copies[i].wait()

    v = vec[...].astype(F32)
    bias_row[:, :width] = v[2:3]
    bias_row[:, width : 2 * width] = jnp.zeros((1, width), F32)
    bias_row[:, 2 * width :] = v[3:4]
    for k in range(width // 128):
        stage[k] = tok[:, :, k * 128 : (k + 1) * 128].astype(F32).reshape(rows, 128)
        for i in range(group):
            x[pl.ds(i * length, length), k * 128 : (k + 1) * 128] = stage[k, pl.ds(i, length, stride=group), :]

    def norm_rows(gain, shift):
        blk = 80

        def one(i):
            at = pl.ds(pl.multiple_of(i * blk, blk), blk)
            hat, _ = normalize(x[at, :])
            h[at, :] = (hat * gain + shift).astype(BF)

        repeat(rows // blk, one, 5)

    norm_rows(v[0:1], v[1:2])
    arrived(0)

    def project(i):
        at = pl.ds(pl.multiple_of(i * 256, 256), 256)
        qkv[:, at] = (dot(h[...], wq[:, at]) + bias_row[:, at]).astype(BF)

    repeat(3 * width // 256, project, 3)

    wins = rows // (2 * length)
    q_len = 112
    low_lane = lax.broadcasted_iota(jnp.int32, (128, 128), 1) < HEAD_DIM
    cols = range(0, width, 128)

    def window(w):
        q_at = pl.multiple_of((2 * length * w) // 16 * 16, 16)
        k_at = pl.multiple_of(jnp.minimum(q_at, rows - 128), 16)
        lo, mid, hi = 2 * w * length, (2 * w + 1) * length, (2 * w + 2) * length
        qi = q_at + lax.broadcasted_iota(jnp.int32, (q_len, 128), 0)
        ki = k_at + lax.broadcasted_iota(jnp.int32, (q_len, 128), 1)
        first = (qi >= lo) & (qi < mid) & (ki >= lo) & (ki < mid)
        second = (qi >= mid) & (qi < hi) & (ki >= mid) & (ki < hi)
        bias = jnp.where(first | second, 0.0, -1e30)
        q_rows, k_rows = pl.ds(q_at, q_len), pl.ds(k_at, 128)
        q2 = [qkv[q_rows, c : c + 128] * 0.125 for c in cols]
        k2 = [head_pair(qkv[k_rows, width + c : width + c + 128], low_lane) for c in cols]
        v2 = [head_pair(qkv[k_rows, 2 * width + c : 2 * width + c + 128], low_lane) for c in cols]
        scores = [dot(q, k, 1, 1) for q, k in zip(q2, k2)]
        probs = [
            jnp.concatenate(
                [softmax_half(s[:, :128], bias).astype(BF), softmax_half(s[:, 128:], bias).astype(BF)],
                axis=1,
            )
            for s in scores
        ]
        mine = (q_at + lax.broadcasted_iota(jnp.int32, (16, 128), 0)) >= lo
        for c, p, values in zip(cols, probs, v2):
            mixed = dot(p, values)
            old = att[pl.ds(q_at, 16), c : c + 128].astype(F32)
            att[pl.ds(q_at, 16), c : c + 128] = jnp.where(mine, mixed[:16], old).astype(BF)
            att[pl.ds(q_at + 16, q_len - 16), c : c + 128] = mixed[16:].astype(BF)

    repeat(wins, window, 2)

    arrived(1)
    for c in range(0, width, 256):
        x[:, c : c + 256] = x[:, c : c + 256] + (dot(att[...], wo[:, c : c + 256]) + v[4:5, c : c + 256])
    norm_rows(v[5:6], v[6:7])

    def image_sums(values):
        sums = []
        for i in range(group):
            lo, hi = i * length, (i + 1) * length
            a, b = lo // 8 * 8, -(-hi // 8) * 8
            part = values[a:b]
            row = a + lax.broadcasted_iota(jnp.int32, (b - a, 1), 0)
            if lo % 8 or hi % 8:
                part = jnp.where((row >= lo) & (row < hi), part, 0.0)
            sums.append(jnp.sum(part, axis=0, keepdims=True))
        return jnp.concatenate(sums, axis=0)

    place = pl.ds(pl.multiple_of(step * group, group), group)
    for c in range(0, width, 256):
        r1_sum[place, c : c + 256] = image_sums(x[:, c : c + 256])
    arrived(2)

    def expand(i):
        at = pl.ds(pl.multiple_of(i * 256, 256), 256)
        u = dot(h[...], wu[:, at]) + ub[:, at].astype(F32)
        tail, _, size = gauss_tail(u)
        act_sum[place, at] = image_sums(jnp.maximum(u, 0.0) - size * tail)

    repeat(hidden // 256, expand, 3)
    arrived(3)

    @pl.when(step == steps - 1)
    def _():
        pooled = r1_sum[...] * (1.0 / length) + mean_down(act_sum[...], length, wd[...]) + v[7:8]
        out[...] = unit_rows(pooled).astype(BF)


def image_forward(tokens, wq, wo, wu, wd, vec, ub):
    pairs, length, width = tokens.shape
    hidden = wu.shape[1]
    group = 16
    rows = group * length
    return pl.pallas_call(
        image_kernel,
        name="image_forward",
        grid=(pairs // group,),
        in_specs=[
            pl.BlockSpec((length, group, width), lambda i: (0, i, 0)),
            ANY,
            ANY,
            ANY,
            ANY,
            pl.BlockSpec((8, width), lambda i: (0, 0)),
            pl.BlockSpec((1, hidden), lambda i: (0, 0)),
        ],
        out_specs=pl.BlockSpec((pairs, width), lambda i: (0, 0)),
        out_shape=jax.ShapeDtypeStruct((pairs, width), BF),
        scratch_shapes=[
            pltpu.VMEM((width, 3 * width), BF),
            pltpu.VMEM((width, width), BF),
            pltpu.VMEM((width, hidden), BF),
            pltpu.VMEM((hidden, width), BF),
            pltpu.VMEM((rows, width), F32),
            pltpu.VMEM((rows, width), BF),
            pltpu.VMEM((rows, 3 * width), BF),
            pltpu.VMEM((rows, width), BF),
            pltpu.VMEM((pairs, hidden), F32),
            pltpu.VMEM((pairs, width), F32),
            pltpu.VMEM((1, 3 * width), F32),
            pltpu.VMEM((width // 128, rows, 128), F32),
            pltpu.SemaphoreType.DMA((4,)),
        ],
        compiler_params=params(),
        cost_estimate=pl.CostEstimate(
            flops=2 * pairs * length * width * (4 * width + hidden),
            bytes_accessed=2 * (4 * width * width + 2 * width * hidden + pairs * length * width),
            transcendentals=pairs * length * hidden,
        ),
    )(jnp.swapaxes(tokens, 0, 1), wq, wo, wu, wd, vec, ub.reshape(1, hidden))


def pack_rows(width, hidden):
    piece, rows = width // PX, width // PF
    return piece, rows, hidden // PF


def weight_copies(packed, which, dst, sem, base, width, hidden):
    piece, rows, frows = pack_rows(width, hidden)
    q_pieces, u_pieces = 3, hidden // width
    spans = {
        "qkv": (0, q_pieces, rows),
        "out": (q_pieces * rows, 1, rows),
        "up": ((q_pieces + 1) * rows, u_pieces, rows),
        "down": ((q_pieces + 1 + u_pieces) * rows, 1, frows),
    }
    start, count, tall = spans[which]
    copies = []
    for x in range(PX):
        for p in range(count):
            copies.append(
                pltpu.make_async_copy(
                    packed.at[pl.ds(x * PF, PF), pl.ds(start + p * tall, tall), :],
                    dst.at[:, :, pl.ds((x * count + p) * piece, piece)],
                    sem.at[base + len(copies)],
                )
            )
    return copies


def natural(ref):
    blocks, rows, cols = ref.shape
    return ref[...].reshape(blocks * rows, cols)


def weight_scratch(which, width, hidden):
    rows, frows = width // PF, hidden // PF
    shape = {
        "qkv": (PF, rows, 3 * width),
        "out": (PF, rows, width),
        "up": (PF, rows, hidden),
        "down": (PF, frows, width),
    }[which]
    return pltpu.VMEM(shape, BF)


def contrast(low, images, live, same, groups, own, own_group, power, row_part, col_sum, loss_part):
    scores = LOGIT_SCALE * dot(low, images[...], 1, 1)
    exps = jnp.exp(scores)
    live_own, same_own = own[:, 0:1], own[:, 1:2]
    power[...] = exps
    rows = jnp.sum(exps * live_own, axis=0, keepdims=True)
    tiled = jnp.concatenate(
        [rows[:, k * 128 : (k + 1) * 128] for k in range(rows.shape[1] // 128)], axis=0
    )
    for d in range(row_part.shape[0]):
        row_part[d] = tiled
    cols = jnp.sum(exps * live[...], axis=1, keepdims=True)
    col_sum[...] = cols
    pair = jnp.where(own_group[...] == groups[...], live_own * live[...], 0.0)
    linear = pair * scores * (1.0 / same_own + 1.0 / same[...])
    losses = live_own * jnp.log(cols) - jnp.sum(linear, axis=1, keepdims=True)
    loss_part[...] = jnp.broadcast_to(jnp.sum(losses, axis=0, keepdims=True), loss_part.shape)


def text_mask(size, length):
    row = lax.broadcasted_iota(jnp.int32, (size, size), 0) // length
    col = lax.broadcasted_iota(jnp.int32, (size, size), 1) // length
    return jnp.where(row == col, 0.0, -1e30)


def text_forward_kernel(
    length, tok, packed, vec, ub, images_i, live, same, groups, own, own_group,
    h1_o, qkv_o, att_o, r1_o, h2_o, slope_o, acts, pooled_out, power, row_part, col_sum, loss_part,
    wq, wo, wu, wd, total, bias_row, h1, qkv, att, r1, h2, slope, sem, images, out_sem
):
    rows, width = tok.shape
    hidden = slope.shape[1]
    texts = rows // length
    load = {}
    base = 0
    for which, dst in (("qkv", wq), ("out", wo), ("up", wu), ("down", wd)):
        load[which] = weight_copies(packed, which, dst, sem, base, width, hidden)
        base += len(load[which])
        for copy in load[which]:
            copy.start()
    v = vec[...].astype(F32)
    bias_row[:, :width] = v[2:3]
    bias_row[:, width : 2 * width] = jnp.zeros((1, width), F32)
    bias_row[:, 2 * width :] = v[3:4]
    blk = 128

    def norm_rows(src, dst, gain, shift):
        def one(i):
            at = pl.ds(pl.multiple_of(i * blk, blk), blk)
            hat, _ = normalize(src[at, :].astype(F32))
            dst[at, :] = (hat * gain + shift).astype(BF)

        repeat(rows // blk, one, 2)

    norm_rows(tok, h1, v[0:1], v[1:2])
    saves = move([(h1, h1_o)], out_sem)
    (gathered,) = move([(images_i, images)], out_sem, 6)
    for copy in load["qkv"]:
        copy.wait()

    def project(i):
        at = pl.ds(pl.multiple_of(i * 256, 256), 256)
        qkv[:, at] = (dot(h1[...], wq[:, :, at].reshape(width, 256)) + bias_row[:, at]).astype(BF)

    repeat(3 * width // 256, project, 3)
    saves += move([(qkv, qkv_o)], out_sem, 1)
    low_lane = lax.broadcasted_iota(jnp.int32, (blk, 128), 1) < HEAD_DIM
    bias = text_mask(blk, length)
    cols = range(0, width, 128)

    def attend(i):
        at = pl.ds(pl.multiple_of(i * blk, blk), blk)
        q2 = [qkv[at, c : c + 128] * 0.125 for c in cols]
        k2 = [head_pair(qkv[at, width + c : width + c + 128], low_lane) for c in cols]
        v2 = [head_pair(qkv[at, 2 * width + c : 2 * width + c + 128], low_lane) for c in cols]
        scores = [dot(q, k, 1, 1) for q, k in zip(q2, k2)]
        probs = [
            jnp.concatenate(
                [softmax_half(s[:, :blk], bias).astype(BF), softmax_half(s[:, blk:], bias).astype(BF)],
                axis=1,
            )
            for s in scores
        ]
        for c, p, values in zip(cols, probs, v2):
            att[at, c : c + 128] = dot(p, values).astype(BF)

    repeat(rows // blk, attend, 2)
    saves += move([(att, att_o)], out_sem, 2)
    for copy in load["out"]:
        copy.wait()
    for c in range(0, width, 256):
        r1[:, c : c + 256] = tok[:, c : c + 256].astype(F32) + (
            dot(att[...], wo[:, :, c : c + 256].reshape(width, 256)) + v[4:5, c : c + 256]
        )
    saves += move([(r1, r1_o)], out_sem, 3)
    norm_rows(r1, h2, v[5:6], v[6:7])
    saves += move([(h2, h2_o)], out_sem, 4)
    for copy in load["up"]:
        copy.wait()

    def expand(i):
        at = pl.ds(pl.multiple_of(i * 256, 256), 256)
        u = dot(h2[...], wu[:, :, at].reshape(width, 256)) + ub[:, at].astype(F32)
        tail, bell, _ = gauss_tail(u)
        phi = jnp.where(u >= 0.0, 1.0 - tail, tail)
        act = u * phi
        slope[:, at] = (phi + u * (bell * 0.3989422804014327)).astype(BF)
        sums = jnp.sum(act.reshape(texts, length, 256), axis=1)
        total[:, at] = sums
        acts[:, at] = sums.astype(BF)

    repeat(hidden // 256, expand, 3)
    saves += move([(slope, slope_o)], out_sem, 5)
    for copy in load["down"]:
        copy.wait()
    mean_r1 = jnp.sum(r1[...].reshape(texts, length, width), axis=1) * (1.0 / length)
    pooled = mean_r1 + mean_down(total[...], length, natural(wd)) + v[7:8]
    pooled_out[...] = pooled
    gathered.wait()
    contrast(
        unit_rows(pooled).astype(BF), images, live, same, groups, own, own_group, power, row_part, col_sum, loss_part
    )
    for copy in saves:
        copy.wait()


def text_forward(
    tokens, packed, vec, ub, images, live, same, groups, own, own_group, length, hidden, copies_of
):
    rows, width = tokens.shape
    texts = rows // length
    pairs = images.shape[0]
    shape = jax.ShapeDtypeStruct
    copies = PX * (3 + 1 + hidden // width + 1)
    return pl.pallas_call(
        functools.partial(text_forward_kernel, length),
        name="text_forward",
        in_specs=[WHOLE, ANY, WHOLE, WHOLE, ANY] + [WHOLE] * 5,
        out_specs=[ANY] * 6 + [WHOLE] * 6,
        out_shape=[
            shape((rows, width), BF),
            shape((rows, 3 * width), BF),
            shape((rows, width), BF),
            shape((rows, width), F32),
            shape((rows, width), BF),
            shape((rows, hidden), BF),
            shape((texts, hidden), BF),
            shape((texts, width), F32),
            shape((texts, pairs), F32),
            shape((copies_of, pairs // 128, 128), F32),
            shape((texts, 1), F32),
            shape((8, 128), F32),
        ],
        scratch_shapes=[weight_scratch(w, width, hidden) for w in ("qkv", "out", "up", "down")]
        + [
            pltpu.VMEM((texts, hidden), F32),
            pltpu.VMEM((1, 3 * width), F32),
            pltpu.VMEM((rows, width), BF),
            pltpu.VMEM((rows, 3 * width), BF),
            pltpu.VMEM((rows, width), BF),
            pltpu.VMEM((rows, width), F32),
            pltpu.VMEM((rows, width), BF),
            pltpu.VMEM((rows, hidden), BF),
            pltpu.SemaphoreType.DMA((copies,)),
            pltpu.VMEM((pairs, width), BF),
            pltpu.SemaphoreType.DMA((7,)),
        ],
        compiler_params=params(),
        cost_estimate=pl.CostEstimate(
            flops=2 * rows * width * (4 * width + hidden),
            bytes_accessed=2 * (4 * width * width + 2 * width * hidden + 12 * rows * width),
            transcendentals=rows * hidden,
        ),
    )(tokens, packed, vec, ub, images, live, same, groups, own, own_group)


def relative_kernel(where, h1_i, h2_i, att_i, h1_o, h2_o, att_o, h1, h2, att, h1_t, h2_t, att_t, sem):
    width = h1.shape[1]
    block = width // PF
    my, mz, mc = where[1], where[2], where[3]
    loads = move([(h2_i, h2), (h1_i, h1), (att_i, att)], sem)
    saves = []
    for n, (src, dst, out) in enumerate(((h2, h2_t, h2_o), (h1, h1_t, h1_o), (att, att_t, att_o))):
        loads[n].wait()
        turned = src[...].T
        for z in range(4):
            for y in range(2):
                for c in range(2):
                    f = (z * 2 + y) * 2 + c
                    place = (((c ^ mc) * 2 + (y ^ my)) * 4 + (z ^ mz)) * block
                    dst[pl.ds(pl.multiple_of(place, block), block), :] = turned[
                        f * block : (f + 1) * block
                    ]
        saves += move([(dst, out)], sem, 3 + n)
    for copy in saves:
        copy.wait()


SMEM = pl.BlockSpec(memory_space=pltpu.SMEM)


def relative_rows(where, h1, h2, att):
    rows, width = h1.shape
    return pl.pallas_call(
        relative_kernel,
        name="relative_rows",
        in_specs=[SMEM, ANY, ANY, ANY],
        out_specs=[ANY] * 3,
        out_shape=[jax.ShapeDtypeStruct((width, rows), BF)] * 3,
        scratch_shapes=[pltpu.VMEM((rows, width), BF)] * 3
        + [pltpu.VMEM((width, rows), BF)] * 3
        + [pltpu.SemaphoreType.DMA((6,))],
        compiler_params=params(),
        cost_estimate=pl.CostEstimate(flops=0, bytes_accessed=12 * rows * width, transcendentals=0),
    )(where, h1, h2, att)


def grad_shapes(width):
    block, half = width // PF, width
    return [jax.ShapeDtypeStruct((2, 2, 4, block, half), BF)] * 4


def put_grad(values, outs, x_rel, at, second):
    width, cols = values.shape
    block = width // PF
    low = values.astype(BF)
    for c in range(2):
        for y in range(2):
            piece = low[(c * 2 + y) * 4 * block : (c * 2 + y + 1) * 4 * block].reshape(4, block, cols)
            if second:
                outs[2 + c, y, x_rel, :, :, pl.ds(at, cols)] = piece
            else:
                outs[c, x_rel, y, :, :, pl.ds(at, cols)] = piece


def start_grads(parts, outs, sem, x):
    return move(
        [(parts.at[n, x], outs[n].at[x]) for n in range(2)]
        + [(parts.at[n, :, x], outs[n].at[:, x]) for n in range(2, 4)],
        sem,
        4 * x,
    )


def back_one_kernel(
    length, shard,
    where, power, row_all, col_sum, images_i, live, same, groups, own, own_group, pooled, packed, vec,
    slope_i, h2_i, r1_i, acts,
    factors_o, keep_a, send_a, keep_b, send_b, bias_up, down_bias, dr1_o, dz_o, da_o, sums, loss_rows,
    factors, wd, wu, wo, dact, images, slope, h2_t, r1, du, dr1, dz_s, da_s, dy, parts, sem, in_sem, out_sem,
):
    rows, hidden = slope.shape
    texts = rows // length
    width = h2_t.shape[0]
    (gathered,) = move([(images_i, images)], in_sem)
    down = weight_copies(packed, "down", wd, sem, 0, width, hidden)
    up = weight_copies(packed, "up", wu, sem, len(down), width, hidden)
    out = weight_copies(packed, "out", wo, sem, len(down) + len(up), width, hidden)
    for copy in down:
        copy.start()
    saved = move([(slope_i, slope), (h2_i, h2_t)], in_sem, 1)
    for copy in up + out:
        copy.start()
    saved += move([(r1_i, r1)], in_sem, 3)
    totals = jnp.sum(row_all[...], axis=0)
    row_sum = jnp.concatenate([totals[k : k + 1] for k in range(totals.shape[0])], axis=1)
    live_own, same_own = own[:, 0:1], own[:, 1:2]
    factor = LOSS_WEIGHT / (2.0 * jnp.sum(live[...], axis=1, keepdims=True))
    pair = factor * live_own * live[...]
    match = jnp.where(own_group[...] == groups[...], 1.0 / same_own + 1.0 / same[...], 0.0)
    grad_scores = pair * (power[...] * (1.0 / row_sum + 1.0 / col_sum[...]) - match)
    gathered.wait()
    grad_low = LOGIT_SCALE * dot(grad_scores.astype(BF), images[...])
    pool = pooled[...]
    inverse = lax.rsqrt(jnp.sum(pool * pool, axis=-1, keepdims=True) + 1e-06)
    along = jnp.sum(pool * grad_low, axis=-1, keepdims=True)
    dy[...] = inverse * (grad_low - pool * (inverse * inverse * along)) * (1.0 / length)
    dm = dy[...].astype(BF)
    loss_rows[...] = jnp.broadcast_to(
        jnp.sum(live[...] * jnp.log(row_sum), axis=1, keepdims=True), loss_rows.shape
    )
    parts_x, parts_f = shard
    piece_x, piece_f = width // parts_x, hidden // parts_f
    for f in range(parts_f):
        left = acts[:, f * piece_f : (f + 1) * piece_f]
        for x in range(parts_x):
            factors[x * parts_f + f, :, piece_x:] = left
            factors[x * parts_f + f, :, :piece_x] = dm[:, x * piece_x : (x + 1) * piece_x]
    sent = move([(factors, factors_o)], out_sem, 11)
    down_bias[...] = length * jnp.sum(dm.astype(F32), axis=0, keepdims=True)
    for copy in down:
        copy.wait()
    dact[...] = dot(dm, natural(wd), 1, 1)
    saved[0].wait()

    saved[1].wait()
    half = hidden // PX
    outs = (keep_a, send_a, keep_b, send_b)
    for x in range(PX):
        first = (x ^ where[0]) * half

        def grads(i):
            c = pl.multiple_of(i * 256, 256)
            for second in range(2):
                at = pl.ds(pl.multiple_of(first + c + second * width, 256), 256)
                spread = jnp.broadcast_to(dact[:, at].reshape(texts, 1, 256), (texts, length, 256))
                part = (spread.reshape(rows, 256) * slope[:, at].astype(F32)).astype(BF)
                du[:, at] = part
                bias_up[:, at] = jnp.sum(part.astype(F32), axis=0, keepdims=True)
                put_grad(dot(h2_t[...], part), parts, x, c, second)

        repeat(width // 256, grads, 3)
        sent += start_grads(parts, outs, out_sem, x)

    v = vec[...].astype(F32)
    blk = 128
    for copy in up:
        copy.wait()

    def product(i):
        at = pl.ds(pl.multiple_of(i * (rows // 2), rows // 2), rows // 2)
        dr1[at, :] = dot(du[at, :], natural(wu), 1, 1)

    repeat(2, product)
    sums[...] = jnp.zeros((8, width), F32)
    some = blk // length
    saved[2].wait()

    def back(i):
        at = pl.ds(pl.multiple_of(i * blk, blk), blk)
        hat, inverse = normalize(r1[at, :])
        grad = dr1[at, :]
        sums[1:2, :] += jnp.sum(grad * hat, axis=0, keepdims=True)
        sums[2:3, :] += jnp.sum(grad, axis=0, keepdims=True)
        spread = jnp.broadcast_to(
            dy[pl.ds(pl.multiple_of(i * some, some), some), :].reshape(some, 1, width), (some, length, width)
        ).reshape(blk, width)
        grad = spread + norm_back(grad, hat, inverse, v[5:6])
        dr1[at, :] = grad
        low = grad.astype(BF)
        dz_s[at, :] = low
        sums[0:1, :] += jnp.sum(low.astype(F32), axis=0, keepdims=True)

    repeat(rows // blk, back)
    sent += move([(dr1, dr1_o), (dz_s, dz_o)], out_sem, 8)
    for copy in out:
        copy.wait()
    da_s[...] = dot(dz_s[...], natural(wo), 1, 1).astype(BF)
    sent += move([(da_s, da_o)], out_sem, 10)
    for copy in sent:
        copy.wait()


def back_one(
    where, power, row_all, col_sum, images, live, same, groups, own, own_group, pooled, packed, vec, slope,
    h2_t, r1, acts, length, shard,
):
    rows, hidden = slope.shape
    width = h2_t.shape[0]
    texts = rows // length
    payload = (shard[0] * shard[1], texts, width // shard[0] + hidden // shard[1])
    shape = jax.ShapeDtypeStruct
    return pl.pallas_call(
        functools.partial(back_one_kernel, length, shard),
        name="back_one",
        in_specs=[SMEM] + [WHOLE] * 3 + [ANY] + [WHOLE] * 6 + [ANY, WHOLE, ANY, ANY, ANY, WHOLE],
        out_specs=[ANY] * 5 + [WHOLE] * 2 + [ANY] * 3 + [WHOLE] * 2,
        out_shape=[
            shape(payload, BF),
            *grad_shapes(width),
            shape((1, hidden), F32),
            shape((1, width), F32),
            shape((rows, width), F32),
            shape((rows, width), BF),
            shape((rows, width), BF),
            shape((8, width), F32),
            shape((8, 128), F32),
        ],
        scratch_shapes=[
            pltpu.VMEM(payload, BF),
            weight_scratch("down", width, hidden),
            weight_scratch("up", width, hidden),
            weight_scratch("out", width, hidden),
            pltpu.VMEM((texts, hidden), F32),
            pltpu.VMEM(images.shape, BF),
            pltpu.VMEM((rows, hidden), BF),
            pltpu.VMEM((width, rows), BF),
            pltpu.VMEM((rows, width), F32),
            pltpu.VMEM((rows, hidden), BF),
            pltpu.VMEM((rows, width), F32),
            pltpu.VMEM((rows, width), BF),
            pltpu.VMEM((rows, width), BF),
            pltpu.VMEM((texts, width), F32),
            pltpu.VMEM((4,) + grad_shapes(width)[0].shape, BF),
            pltpu.SemaphoreType.DMA((PX * (2 + hidden // width),)),
            pltpu.SemaphoreType.DMA((4,)),
            pltpu.SemaphoreType.DMA((12,)),
        ],
        compiler_params=params(),
        cost_estimate=pl.CostEstimate(
            flops=2 * rows * width * (2 * hidden + width), bytes_accessed=16 * width * hidden, transcendentals=0
        ),
    )(
        where, power, row_all, col_sum, images, live, same, groups, own, own_group, pooled, packed, vec,
        slope, h2_t, r1, acts,
    )


def back_two_kernel(
    length, where, qkv_i, da_i, dz_i, h1_i, att_i, up_a, up_a_new, up_b, up_b_new,
    dqkv_o, keep_a, send_a, keep_b, send_b, up_a_keep, up_a_send, up_b_keep, up_b_send, sums,
    qkv, da_s, dz, h1_t, att_t, dqkv, parts, held, come, sem, out_sem, up_sem,
):
    rows, width = da_s.shape
    blk = 128
    loads = move([(qkv_i, qkv), (da_i, da_s), (att_i, att_t), (dz_i, dz), (h1_i, h1_t)], sem)
    arrivals = move(
        [(up_a, held.at[0]), (up_a_new, come.at[0]), (up_b, held.at[1]), (up_b_new, come.at[1])], up_sem
    )
    for copy in loads[:2]:
        copy.wait()
    low_lane = lax.broadcasted_iota(jnp.int32, (blk, 128), 1) < HEAD_DIM
    bias = text_mask(blk, length)
    cols = range(0, width, 128)
    def group(i):
        at = pl.ds(pl.multiple_of(i * blk, blk), blk)
        take = lambda base, c: qkv[at, base + c : base + c + 128]
        q2 = [take(0, c) * 0.125 for c in cols]
        k2 = [head_pair(take(width, c), low_lane) for c in cols]
        v2 = [head_pair(take(2 * width, c), low_lane) for c in cols]
        da = [da_s[at, c : c + 128] for c in cols]
        scores = [dot(k, q, 1, 1) for k, q in zip(k2, q2)]
        grads = [dot(v, d, 1, 1) for v, d in zip(v2, da)]
        probs, deltas = [], []
        for score, grad in zip(scores, grads):
            p_low, d_low = [], []
            for half in range(2):
                s = score[half * blk : (half + 1) * blk] + bias
                g = grad[half * blk : (half + 1) * blk]
                powers = jnp.exp(s - jnp.max(s, axis=0, keepdims=True))
                soft = powers * (1.0 / jnp.sum(powers, axis=0, keepdims=True))
                p_low.append(soft.astype(BF))
                d_low.append((soft * (g - jnp.sum(g * soft, axis=0, keepdims=True))).astype(BF))
            probs.append(jnp.concatenate(p_low, axis=0))
            deltas.append(jnp.concatenate(d_low, axis=0))
        for n, c in enumerate(cols):
            dq = dot(deltas[n], k2[n], 0, 0) * 0.125
            dk = dot(deltas[n], q2[n])
            dv = dot(probs[n], da[n])
            dqkv[at, c : c + 128] = dq.astype(BF)
            dqkv[at, width + c : width + c + 128] = jnp.where(
                low_lane, dk[:blk], dk[blk:]
            ).astype(BF)
            dqkv[at, 2 * width + c : 2 * width + c + 128] = jnp.where(
                low_lane, dv[:blk], dv[blk:]
            ).astype(BF)

    repeat(rows // blk, group, 2)
    sums[0:1, :] = jnp.sum(dqkv[:, :width].astype(F32), axis=0, keepdims=True)
    sums[1:2, :] = jnp.sum(dqkv[:, 2 * width :].astype(F32), axis=0, keepdims=True)
    sums[2:8, :] = jnp.zeros((6, width), F32)
    sent = move([(dqkv, dqkv_o)], out_sem, 8)
    for copy in arrivals:
        copy.wait()

    def add(i):
        n, first, second = i // 4, i // 2 % 2, i % 2
        held[n, first, second] = (
            held[n, first, second].astype(F32) + come[n, first, second].astype(F32)
        ).astype(BF)

    repeat(8, add)
    sent += move(
        [
            (held.at[0, 0], up_a_keep),
            (held.at[0, 1], up_a_send),
            (held.at[1, 0], up_b_keep),
            (held.at[1, 1], up_b_send),
        ],
        up_sem,
        4,
    )
    for copy in loads[2:]:
        copy.wait()
    piece = width // PX
    outs = (keep_a, send_a, keep_b, send_b)
    for x in range(PX):
        other = x ^ where[0]
        first = other * (3 * piece)

        def chunk(i):
            c = pl.multiple_of(i * 256, 256)
            part = dqkv[:, pl.ds(pl.multiple_of(first + c, 128), 256)]
            put_grad(dot(h1_t[...], part), parts, x, c, 0)

        repeat(width // 256, chunk, 3)
        part = dqkv[:, pl.ds(pl.multiple_of(first + width, 128), piece)]
        put_grad(dot(h1_t[...], part), parts, x, 0, 1)
        part = dz[:, pl.ds(pl.multiple_of(other * piece, 128), piece)]
        put_grad(dot(att_t[...], part), parts, x, piece, 1)
        sent += start_grads(parts, outs, out_sem, x)
    for copy in sent:
        copy.wait()


def back_two(where, qkv, da, dz, h1_t, att_t, up_parts, length):
    rows, width = da.shape
    shape = jax.ShapeDtypeStruct
    whole = grad_shapes(width)
    return pl.pallas_call(
        functools.partial(back_two_kernel, length),
        name="back_two",
        in_specs=[SMEM] + [ANY] * 9,
        out_specs=[ANY] * 9 + [WHOLE],
        out_shape=[shape((rows, 3 * width), BF), *whole, *[shape(whole[0].shape[1:], BF)] * 4, shape((8, width), F32)],
        scratch_shapes=[
            pltpu.VMEM((rows, 3 * width), BF),
            pltpu.VMEM((rows, width), BF),
            pltpu.VMEM((rows, width), BF),
            pltpu.VMEM((width, rows), BF),
            pltpu.VMEM((width, rows), BF),
            pltpu.VMEM((rows, 3 * width), BF),
            pltpu.VMEM((4,) + whole[0].shape, BF),
            pltpu.VMEM((2,) + whole[0].shape, BF),
            pltpu.VMEM((2,) + whole[0].shape, BF),
            pltpu.SemaphoreType.DMA((5,)),
            pltpu.SemaphoreType.DMA((9,)),
            pltpu.SemaphoreType.DMA((8,)),
        ],
        compiler_params=params(),
        cost_estimate=pl.CostEstimate(
            flops=2 * rows * width * (1280 + 4 * width), bytes_accessed=20 * rows * width, transcendentals=rows * width
        ),
    )(where, qkv, da, dz, h1_t, att_t, *up_parts)


def back_third_kernel(
    parts_f, dr1_i, dqkv_i, tok_i, packed, vec, sums, bias_sums, down_bias, bias_up, loss_part, dx_o, share, all_sums, wq, dr1, tok, dx, sem, dqkv, own_sem
):
    rows, width = tok.shape
    loads = weight_copies(packed, "qkv", wq, sem, 0, width, width)
    for copy in loads:
        copy.start()
    saved = move([(dqkv_i, dqkv), (dr1_i, dr1), (tok_i, tok)], own_sem)
    saved[0].wait()
    v = vec[...].astype(F32)
    for copy in loads:
        copy.wait()
    half = rows // 2

    def product(i):
        at = pl.ds(pl.multiple_of(i * half, half), half)
        dx[at, :] = dot(dqkv[at, :], natural(wq), 1, 1)

    repeat(2, product)
    for copy in saved[1:]:
        copy.wait()
    all_sums[0:2, :] = jnp.zeros((2, width), F32)
    blk = 128

    def back(i):
        at = pl.ds(pl.multiple_of(i * blk, blk), blk)
        hat, inverse = normalize(tok[at, :].astype(F32))
        grad = dx[at, :]
        all_sums[0:1, :] += jnp.sum(grad * hat, axis=0, keepdims=True)
        all_sums[1:2, :] += jnp.sum(grad, axis=0, keepdims=True)
        dx[at, :] = dr1[at, :] + norm_back(grad, hat, inverse, v[0:1])

    repeat(rows // blk, back)
    (save,) = move([(dx, dx_o)], own_sem, 3)
    all_sums[2:4, :] = bias_sums[0:2, :]
    all_sums[4:7, :] = sums[0:3, :]
    all_sums[7:8, :] = down_bias[...]
    every = all_sums[...]
    piece, tall = width // parts_f, bias_up.shape[1] // parts_f
    devices = share.shape[0]
    used = piece + tall // 8
    for f in range(parts_f):
        bias = bias_up[:, f * tall : (f + 1) * tall]
        bias = jnp.concatenate([bias[:, r * tall // 8 : (r + 1) * tall // 8] for r in range(8)], axis=0)
        block = jnp.concatenate(
            [every[:, f * piece : (f + 1) * piece], bias, loss_part[:, : 128 - used]], axis=1
        )
        for x in range(devices // parts_f):
            share[x * parts_f + f] = block
    save.wait()


def back_third(dr1, dqkv, tok, packed, vec, sums, bias_sums, down_bias, bias_up, loss_part, shard):
    rows, width = tok.shape
    shape = jax.ShapeDtypeStruct
    return pl.pallas_call(
        functools.partial(back_third_kernel, shard[1]),
        name="back_third",
        in_specs=[ANY, ANY, ANY, ANY] + [WHOLE] * 6,
        out_specs=[ANY, WHOLE],
        out_shape=[shape((rows, width), F32), shape((shard[0] * shard[1], 8, 128), F32)],
        scratch_shapes=[
            pltpu.VMEM((8, width), F32),
            weight_scratch("qkv", width, width),
            pltpu.VMEM((rows, width), F32),
            pltpu.VMEM((rows, width), BF),
            pltpu.VMEM((rows, width), F32),
            pltpu.SemaphoreType.DMA((PX * 3,)),
            pltpu.VMEM((rows, 3 * width), BF),
            pltpu.SemaphoreType.DMA((4,)),
        ],
        compiler_params=params(),
        cost_estimate=pl.CostEstimate(
            flops=6 * rows * width * width, bytes_accessed=14 * width * width, transcendentals=0
        ),
    )(dr1, dqkv, tok, packed, vec, sums, bias_sums, down_bias, bias_up, loss_part)


def fold_kernel(a_own, a_new, b_own, b_new, a_keep, a_send, b_keep, b_send):
    for own, new, keep, send in ((a_own, a_new, a_keep, a_send), (b_own, b_new, b_keep, b_send)):
        total = own[...].astype(F32) + new[...].astype(F32)
        keep[...] = total[0].astype(BF)
        send[...] = total[1].astype(BF)


def fold(a_own, a_new, b_own, b_new):
    shape = a_own.shape
    rest = 1
    for n in shape[1:-2]:
        rest *= n
    rows, cols = shape[-2:]
    view = lambda a: a.reshape(2, rest, rows, cols)
    steps = 2 if rest > 4 else 1
    pair = pl.BlockSpec((2, rest // steps, rows, cols), lambda i: (0, i, 0, 0))
    one = pl.BlockSpec((rest // steps, rows, cols), lambda i: (i, 0, 0))
    outs = pl.pallas_call(
        fold_kernel,
        name="fold",
        grid=(steps,),
        in_specs=[pair] * 4,
        out_specs=[one] * 4,
        out_shape=[jax.ShapeDtypeStruct((rest, rows, cols), BF)] * 4,
        compiler_params=params(18),
        cost_estimate=pl.CostEstimate(
            flops=4 * rest * rows * cols, bytes_accessed=24 * rest * rows * cols, transcendentals=0
        ),
    )(*(view(a) for a in (a_own, a_new, b_own, b_new)))
    return [o.reshape(shape[1:]) for o in outs]


def join_kernel(a_own, a_new, b_own, b_new, keep, send):
    half = a_own.shape[-1]
    for at, own, new in ((0, a_own, a_new), (half, b_own, b_new)):
        total = own[...].astype(F32) + new[...].astype(F32)
        for k in range(2):
            keep[k, :, at : at + half] = total[2 * k]
            send[k, :, at : at + half] = total[2 * k + 1].astype(BF)


def join(a_own, a_new, b_own, b_new):
    blocks, rows, cols = a_own.shape
    shape = jax.ShapeDtypeStruct
    return pl.pallas_call(
        join_kernel,
        name="join",
        in_specs=[WHOLE] * 4,
        out_specs=[WHOLE] * 2,
        out_shape=[shape((2, rows, 2 * cols), F32), shape((2, rows, 2 * cols), BF)],
        compiler_params=params(6),
        cost_estimate=pl.CostEstimate(
            flops=16 * rows * cols, bytes_accessed=40 * rows * cols, transcendentals=0
        ),
    )(a_own, a_new, b_own, b_new)


def turn_kernel(keep, new, stay, send):
    stay[...] = keep[0] + new[0].astype(F32)
    send[...] = (keep[1] + new[1].astype(F32)).astype(BF)


def turn(keep, new):
    blocks, rows, cols = keep.shape
    shape = jax.ShapeDtypeStruct
    return pl.pallas_call(
        turn_kernel,
        name="turn",
        in_specs=[WHOLE] * 2,
        out_specs=[WHOLE] * 2,
        out_shape=[shape((rows, cols), F32), shape((rows, cols), BF)],
        compiler_params=params(6),
        cost_estimate=pl.CostEstimate(
            flops=4 * rows * cols, bytes_accessed=18 * rows * cols, transcendentals=0
        ),
    )(keep, new)


def shifted(x, y, z, core):
    change = x * 16 + z * 4 + y * 2 + core
    return [(i, i ^ change) for i in range(32)]


def hop(array, x=0, y=0, z=0, core=0):
    return lax.ppermute(array, AXES, shifted(x, y, z, core))


def after(values, *others):
    return lax.optimization_barrier((tuple(values), others))[0]


def core_step(parts, *wait):
    keep_a, send_a, keep_b, send_b = parts
    new_a, new_b = hop(send_a, core=1), hop(send_b, core=1)
    keep_a, keep_b = after((keep_a, keep_b), *wait)
    return fold(keep_a, new_a, keep_b, new_b)


def first_step(parts, *wait):
    keep_a, send_a, keep_b, send_b = parts
    new_a, new_b = hop(send_a, x=1), hop(send_b, y=1)
    keep_a, keep_b = after((keep_a, keep_b), *wait)
    return fold(keep_a, new_a, keep_b, new_b)


def second_step(parts, *wait):
    keep_a, send_a, keep_b, send_b = parts
    new_a, new_b = hop(send_a, y=1), hop(send_b, x=1)
    keep_a, keep_b = after((keep_a, keep_b), *wait)
    return join(keep_a, new_a, keep_b, new_b)


def total_kernel(stay, new, *outs):
    total = stay[...] + new[...].astype(F32)
    at = 0
    for out in outs:
        out[...] = total[:, at : at + out.shape[1]]
        at += out.shape[1]


def third_step(parts, *wait):
    keep, send = parts
    new = hop(send, z=1)
    (keep,) = after((keep,), *wait)
    return turn(keep, new)


def last_step(parts, splits):
    stay, send = parts
    return pl.pallas_call(
        total_kernel,
        name="total",
        in_specs=[WHOLE] * 2,
        out_specs=[WHOLE] * len(splits),
        out_shape=[jax.ShapeDtypeStruct((stay.shape[0], n), F32) for n in splits],
        compiler_params=params(4),
    )(stay, hop(send, z=2))


def natural_grad(keep_a, send_a, keep_b, send_b):
    first = jnp.stack([keep_a, send_a])
    second = jnp.swapaxes(jnp.stack([keep_b, send_b]), 1, 2)
    whole = jnp.concatenate([first, second], axis=-1)
    core, x, y, z, rows, cols = whole.shape
    return whole.transpose(1, 3, 2, 0, 4, 5).reshape(x, z * y * core * rows, cols)


def pack_kernel(qkv, out, up, down, packed):
    rows, piece = out.shape
    at = 0
    for ref in (qkv, out, up, down):
        for c in range(0, ref.shape[1], piece):
            packed[at : at + ref.shape[0], :] = ref[:, c : c + piece]
            at += ref.shape[0]


def pack_block(qkv, out, up, down):
    piece = out.shape[1]
    total = sum(w.shape[0] * w.shape[1] for w in (qkv, out, up, down)) // piece
    return pl.pallas_call(
        pack_kernel,
        name="pack_block",
        in_specs=[WHOLE] * 4,
        out_specs=WHOLE,
        out_shape=jax.ShapeDtypeStruct((total, piece), BF),
        compiler_params=params(),
    )(qkv, out, up, down)


def gather_packed(qkv, out, up, down, dp, fsdp):
    if (dp, fsdp) == (PX, PF):
        return lax.all_gather(pack_block(qkv, out, up, down), AXES, axis=0)
    full = [
        lax.all_gather(lax.all_gather(w, "dp", axis=1, tiled=True), "fsdp", axis=0, tiled=True)
        for w in (qkv, out, up, down)
    ]
    blocks = []
    for x in range(PX):
        for f in range(PF):
            some = []
            for w in full:
                rows, cols = w.shape[0] // PF, w.shape[1] // PX
                some.append(w[f * rows : (f + 1) * rows, x * cols : (x + 1) * cols])
            blocks.append(pack_block(*some))
    return jnp.stack(blocks)


def scatter_columns(grad, dp, fsdp):
    parts, rows, cols = grad.shape
    if dp != parts:
        grad = jnp.swapaxes(grad, 0, 1).reshape(rows, dp, parts * cols // dp)
        grad = jnp.swapaxes(grad, 0, 1)
    return lax.psum_scatter(
        grad.reshape(dp * rows, -1), AXES, scatter_dimension=0, tiled=True
    ).astype(F32)


def body(
    image_tokens,
    text_tokens,
    image_qkv,
    image_out,
    image_up,
    image_down,
    image_vectors,
    image_up_bias,
    text_qkv,
    text_out,
    text_up,
    text_down,
    text_vectors,
    text_up_bias,
    pair_counts,
    pair_groups,
):
    dp, fsdp = lax.axis_size("dp"), lax.axis_size("fsdp")
    devices = dp * fsdp
    cap, length, width = text_tokens.shape
    hidden = image_up.shape[1]
    pairs = pair_groups.shape[0]
    me = lax.axis_index("dp") * fsdp + lax.axis_index("fsdp")

    grid_mesh = (dp, fsdp) == (PX, PF)
    packed = gather_packed(text_qkv, text_out, text_up, text_down, dp, fsdp)
    part = width // fsdp
    small = jnp.concatenate([text_vectors, text_up_bias.reshape(8, -1)], axis=1)
    if grid_mesh:
        small = jnp.broadcast_to(small[None], (fsdp,) + small.shape)
        small = lax.all_to_all(small, "fsdp", 0, 0, tiled=True)
    else:
        small = lax.all_gather(small, "fsdp", axis=0)
    vec = jnp.swapaxes(small[:, :, :part], 0, 1).reshape(8, width)
    ub = small[:, :, part:].reshape(1, hidden)
    bits = [lax.shift_right_logical(me, k) & 1 for k in range(5)]
    where = jnp.stack([bits[4], bits[1], 2 * bits[3] + bits[2], bits[0]])
    where = where if grid_mesh else jnp.zeros_like(where)

    image_low = image_forward(
        image_tokens, image_qkv, image_out, image_up, image_down, image_vectors, image_up_bias
    )
    if grid_mesh:
        images = image_low
        for change in (dict(z=1), dict(z=2), dict(x=1), dict(y=1), dict(core=1)):
            images = jnp.concatenate([images, hop(images, **change)], axis=0)
        far = jnp.arange(devices, dtype=jnp.int32) ^ me
        bit = lambda k: lax.shift_right_logical(far, k) & 1
        order = bit(2) + 2 * bit(3) + 4 * bit(4) + 8 * bit(1) + 16 * bit(0)
        images = jnp.take(images.reshape(devices, cap, width), order, axis=0).reshape(pairs, width)
    else:
        images = lax.all_gather(image_low, AXES, axis=0, tiled=True)

    slots = jnp.arange(cap, dtype=jnp.int32)
    live = (slots[None, :] < pair_counts[:, None]).reshape(pairs).astype(F32)
    same = jnp.maximum(
        jnp.sum(jnp.where(pair_groups[:, None] == pair_groups[None, :], live[None, :], 0.0), axis=1), 1.0
    )
    own_of = lambda array: lax.dynamic_slice_in_dim(array, me * cap, cap)
    own = jnp.stack([own_of(live), own_of(same)], axis=1)
    own_group = own_of(pair_groups).reshape(cap, 1)
    live_row, same_row, group_row = (a.reshape(1, pairs) for a in (live, same, pair_groups))
    live_total = jnp.sum(pair_counts).astype(F32)

    tokens = text_tokens.reshape(cap * length, width)
    h1, qkv, att, r1, h2, slope, acts, pooled, power, row_part, col_sum, loss_part = text_forward(
        tokens, packed, vec, ub, images, live_row, same_row, group_row, own, own_group, length, hidden,
        devices if grid_mesh else 1,
    )
    if grid_mesh:
        row_all = lax.all_to_all(row_part, AXES, 0, 0, tiled=True)
    else:
        row_all = lax.psum(row_part, AXES)
    h1_t, h2_t, att_t = relative_rows(where, h1, h2, att)
    factors, *up_parts, bias_up, down_bias, dr1, dz, da, sums, loss_rows = back_one(
        where, power, row_all, col_sum, images, live_row, same_row, group_row, own, own_group, pooled,
        packed, vec, slope, h2_t, r1, acts, length, (dp, fsdp),
    )
    keep_a, send_a, keep_b, send_b = up_parts
    if grid_mesh:
        travel = (keep_a, hop(send_a, core=1), keep_b, hop(send_b, core=1))
    else:
        travel = (keep_a, send_a, keep_b, send_b)
    dqkv, *both_parts, bias_sums = back_two(where, qkv, da, dz, h1_t, att_t, travel, length)
    att_parts = both_parts[:4]

    both = lax.all_to_all(factors, AXES, 0, 0, tiled=True).reshape(pairs, width // dp + hidden // fsdp)
    grad_down = dot(both[:, width // dp :], both[:, : width // dp], 0, 0)

    if grid_mesh:
        up_parts = both_parts[4:]
        att_parts = core_step(att_parts)
        (dqkv,) = after((dqkv,), *att_parts)
        dx, share = back_third(
            dr1, dqkv, tokens, packed, vec, sums, bias_sums, down_bias, bias_up, loss_part, (dp, fsdp)
        )
        up_parts = first_step(up_parts, dx)
        att_parts = first_step(att_parts, grad_down, *up_parts)
        up_parts = second_step(up_parts, *att_parts)
        (share,) = after((share,), *att_parts)
        att_parts = second_step(att_parts, *up_parts)
        up_parts = third_step(up_parts, *att_parts)
        att_parts = third_step(att_parts, *up_parts)
        (grad_up,) = last_step(up_parts, (hidden // dp,))
        grad_qkv, grad_out = last_step(att_parts, (3 * width // dp, width // dp))
    else:
        dx, share = back_third(
            dr1, dqkv, tokens, packed, vec, sums, bias_sums, down_bias, bias_up, loss_part, (dp, fsdp)
        )
        grad_attn = natural_grad(*att_parts)
        grad_up = scatter_columns(natural_grad(*up_parts), dp, fsdp)
        grad_qkv = scatter_columns(grad_attn[:, :, : 3 * width // PX], dp, fsdp)
        grad_out = scatter_columns(grad_attn[:, :, 3 * width // PX :], dp, fsdp)

    share = jnp.sum(lax.all_to_all(share, AXES, 0, 0, tiled=True), axis=0)
    grad_vec = share[:, :part]
    tall = hidden // fsdp // 8
    grad_bias = share[:, part : part + tall].reshape(hidden // fsdp)
    loss = (share[0, part + tall] + loss_rows[0, 0]) / (2.0 * live_total)

    return (
        loss,
        dx.reshape(text_tokens.shape),
        grad_qkv,
        grad_out,
        grad_up,
        grad_down,
        grad_vec,
        grad_bias,
    )


def solution(mesh):
    return jax.shard_map(
        body,
        mesh=mesh,
        in_specs=(
            P(AXES, None, None),
            P(AXES, None, None),
            P(),
            P(),
            P(),
            P(),
            P(),
            P(),
            P("fsdp", "dp"),
            P("fsdp", "dp"),
            P("fsdp", "dp"),
            P("fsdp", "dp"),
            P(None, "fsdp"),
            P("fsdp"),
            P(),
            P(),
        ),
        out_specs=(
            P(),
            P(AXES, None, None),
            P("fsdp", "dp"),
            P("fsdp", "dp"),
            P("fsdp", "dp"),
            P("fsdp", "dp"),
            P(None, "fsdp"),
            P("fsdp"),
        ),
        check_vma=False,
    )
```

```python
import functools

import jax
import jax.numpy as jnp
from jax import lax
from jax.experimental import pallas as pl
from jax.experimental.pallas import tpu as pltpu
from jax.sharding import PartitionSpec as P

HEAD_DIM = 64
LOGIT_SCALE = 50.0
LOSS_WEIGHT = 32768.0
BF = jnp.bfloat16
F32 = jnp.float32
AXES = ("dp", "fsdp")
PX, PF = 2, 16

ANY = pl.BlockSpec(memory_space=pltpu.HBM)
WHOLE = pl.BlockSpec(memory_space=pltpu.VMEM)


def params(mebibytes=62):
    return pltpu.CompilerParams(vmem_limit_bytes=mebibytes * 1024 * 1024)


def dot(a, b, ca=1, cb=0):
    return lax.dot_general(a, b, (((ca,), (cb,)), ((), ())), preferred_element_type=F32)


def repeat(count, step, together=1):
    def turn(j, _):
        for k in range(together):
            step(j * together + k)
        return 0

    if together >= count:
        for i in range(count):
            step(i)
    else:
        lax.fori_loop(0, count // together, turn, 0)


def move(pairs, sem, base=0):
    copies = [pltpu.make_async_copy(a, b, sem.at[base + i]) for i, (a, b) in enumerate(pairs)]
    for copy in copies:
        copy.start()
    return copies


def normalize(values):
    centered = values - jnp.mean(values, axis=-1, keepdims=True)
    inverse = lax.rsqrt(jnp.mean(centered * centered, axis=-1, keepdims=True) + 1e-05)
    return centered * inverse, inverse


def norm_back(grad, hat, inverse, gain):
    scaled = grad * gain
    return inverse * (
        scaled
        - jnp.mean(scaled, axis=-1, keepdims=True)
        - hat * jnp.mean(scaled * hat, axis=-1, keepdims=True)
    )


def gauss_tail(u):
    size = jnp.abs(u)
    t = 1.0 / (1.0 + (0.3275911 * 0.7071067811865476) * size)
    bell = jnp.exp2(-0.7213475204444817 * (u * u))
    poly = 0.5 * 1.061405429 * t - 0.5 * 1.453152027
    poly = poly * t + 0.5 * 1.421413741
    poly = poly * t - 0.5 * 0.284496736
    poly = poly * t + 0.5 * 0.254829592
    return poly * t * bell, bell, size


def head_pair(block, low_lane):
    zero = jnp.zeros_like(block)
    return jnp.concatenate(
        [jnp.where(low_lane, block, zero), jnp.where(low_lane, zero, block)], axis=0
    )


def softmax_half(scores, bias):
    scores = scores + bias
    top = jnp.max(scores, axis=-1, keepdims=True)
    powers = jnp.exp(scores - top)
    return powers * (1.0 / jnp.sum(powers, axis=-1, keepdims=True))


def unit_rows(pooled):
    return pooled * lax.rsqrt(jnp.sum(pooled * pooled, axis=-1, keepdims=True) + 1e-06)


def mean_down(total, count, down):
    mean = total * (1.0 / count)
    high = mean.astype(BF)
    low = (mean - high.astype(F32)).astype(BF)
    both = dot(jnp.concatenate([high, low], axis=0), down)
    return both[: mean.shape[0]] + both[mean.shape[0] :]


def image_kernel(
    tok, wq_h, wo_h, wu_h, wd_h, vec, ub, out, wq, wo, wu, wd, x, h, qkv, att, act_sum, r1_sum, bias_row, stage, sem
):
    step, steps = pl.program_id(0), pl.num_programs(0)
    length, group, width = tok.shape
    rows = group * length
    hidden = wu.shape[1]
    copies = [
        pltpu.make_async_copy(src, dst, sem.at[i])
        for i, (src, dst) in enumerate(((wq_h, wq), (wo_h, wo), (wu_h, wu), (wd_h, wd)))
    ]

    @pl.when(step == 0)
    def _():
        for copy in copies:
            copy.start()

    def arrived(i):
        @pl.when(step == 0)
        def _():
            copies[i].wait()

    v = vec[...].astype(F32)
    bias_row[:, :width] = v[2:3]
    bias_row[:, width : 2 * width] = jnp.zeros((1, width), F32)
    bias_row[:, 2 * width :] = v[3:4]
    for k in range(width // 128):
        stage[k] = tok[:, :, k * 128 : (k + 1) * 128].astype(F32).reshape(rows, 128)
        for i in range(group):
            x[pl.ds(i * length, length), k * 128 : (k + 1) * 128] = stage[k, pl.ds(i, length, stride=group), :]

    def norm_rows(gain, shift):
        blk = 80

        def one(i):
            at = pl.ds(pl.multiple_of(i * blk, blk), blk)
            hat, _ = normalize(x[at, :])
            h[at, :] = (hat * gain + shift).astype(BF)

        repeat(rows // blk, one, 5)

    norm_rows(v[0:1], v[1:2])
    arrived(0)

    def project(i):
        at = pl.ds(pl.multiple_of(i * 256, 256), 256)
        qkv[:, at] = (dot(h[...], wq[:, at]) + bias_row[:, at]).astype(BF)

    repeat(3 * width // 256, project, 3)

    wins = rows // (2 * length)
    q_len = 112
    low_lane = lax.broadcasted_iota(jnp.int32, (128, 128), 1) < HEAD_DIM
    cols = range(0, width, 128)

    def window(w):
        q_at = pl.multiple_of((2 * length * w) // 16 * 16, 16)
        k_at = pl.multiple_of(jnp.minimum(q_at, rows - 128), 16)
        lo, mid, hi = 2 * w * length, (2 * w + 1) * length, (2 * w + 2) * length
        qi = q_at + lax.broadcasted_iota(jnp.int32, (q_len, 128), 0)
        ki = k_at + lax.broadcasted_iota(jnp.int32, (q_len, 128), 1)
        first = (qi >= lo) & (qi < mid) & (ki >= lo) & (ki < mid)
        second = (qi >= mid) & (qi < hi) & (ki >= mid) & (ki < hi)
        bias = jnp.where(first | second, 0.0, -1e30)
        q_rows, k_rows = pl.ds(q_at, q_len), pl.ds(k_at, 128)
        q2 = [qkv[q_rows, c : c + 128] * 0.125 for c in cols]
        k2 = [head_pair(qkv[k_rows, width + c : width + c + 128], low_lane) for c in cols]
        v2 = [head_pair(qkv[k_rows, 2 * width + c : 2 * width + c + 128], low_lane) for c in cols]
        scores = [dot(q, k, 1, 1) for q, k in zip(q2, k2)]
        probs = [
            jnp.concatenate(
                [softmax_half(s[:, :128], bias).astype(BF), softmax_half(s[:, 128:], bias).astype(BF)],
                axis=1,
            )
            for s in scores
        ]
        mine = (q_at + lax.broadcasted_iota(jnp.int32, (16, 128), 0)) >= lo
        for c, p, values in zip(cols, probs, v2):
            mixed = dot(p, values)
            old = att[pl.ds(q_at, 16), c : c + 128].astype(F32)
            att[pl.ds(q_at, 16), c : c + 128] = jnp.where(mine, mixed[:16], old).astype(BF)
            att[pl.ds(q_at + 16, q_len - 16), c : c + 128] = mixed[16:].astype(BF)

    repeat(wins, window, 2)

    arrived(1)
    for c in range(0, width, 256):
        x[:, c : c + 256] = x[:, c : c + 256] + (dot(att[...], wo[:, c : c + 256]) + v[4:5, c : c + 256])
    norm_rows(v[5:6], v[6:7])

    def image_sums(values):
        sums = []
        for i in range(group):
            lo, hi = i * length, (i + 1) * length
            a, b = lo // 8 * 8, -(-hi // 8) * 8
            part = values[a:b]
            row = a + lax.broadcasted_iota(jnp.int32, (b - a, 1), 0)
            if lo % 8 or hi % 8:
                part = jnp.where((row >= lo) & (row < hi), part, 0.0)
            sums.append(jnp.sum(part, axis=0, keepdims=True))
        return jnp.concatenate(sums, axis=0)

    place = pl.ds(pl.multiple_of(step * group, group), group)
    for c in range(0, width, 256):
        r1_sum[place, c : c + 256] = image_sums(x[:, c : c + 256])
    arrived(2)

    def expand(i):
        at = pl.ds(pl.multiple_of(i * 256, 256), 256)
        u = dot(h[...], wu[:, at]) + ub[:, at].astype(F32)
        tail, _, size = gauss_tail(u)
        act_sum[place, at] = image_sums(jnp.maximum(u, 0.0) - size * tail)

    repeat(hidden // 256, expand, 3)
    arrived(3)

    @pl.when(step == steps - 1)
    def _():
        pooled = r1_sum[...] * (1.0 / length) + mean_down(act_sum[...], length, wd[...]) + v[7:8]
        out[...] = unit_rows(pooled).astype(BF)


def image_forward(tokens, wq, wo, wu, wd, vec, ub):
    pairs, length, width = tokens.shape
    hidden = wu.shape[1]
    group = 16
    rows = group * length
    return pl.pallas_call(
        image_kernel,
        name="image_forward",
        grid=(pairs // group,),
        in_specs=[
            pl.BlockSpec((length, group, width), lambda i: (0, i, 0)),
            ANY,
            ANY,
            ANY,
            ANY,
            pl.BlockSpec((8, width), lambda i: (0, 0)),
            pl.BlockSpec((1, hidden), lambda i: (0, 0)),
        ],
        out_specs=pl.BlockSpec((pairs, width), lambda i: (0, 0)),
        out_shape=jax.ShapeDtypeStruct((pairs, width), BF),
        scratch_shapes=[
            pltpu.VMEM((width, 3 * width), BF),
            pltpu.VMEM((width, width), BF),
            pltpu.VMEM((width, hidden), BF),
            pltpu.VMEM((hidden, width), BF),
            pltpu.VMEM((rows, width), F32),
            pltpu.VMEM((rows, width), BF),
            pltpu.VMEM((rows, 3 * width), BF),
            pltpu.VMEM((rows, width), BF),
            pltpu.VMEM((pairs, hidden), F32),
            pltpu.VMEM((pairs, width), F32),
            pltpu.VMEM((1, 3 * width), F32),
            pltpu.VMEM((width // 128, rows, 128), F32),
            pltpu.SemaphoreType.DMA((4,)),
        ],
        compiler_params=params(),
        cost_estimate=pl.CostEstimate(
            flops=2 * pairs * length * width * (4 * width + hidden),
            bytes_accessed=2 * (4 * width * width + 2 * width * hidden + pairs * length * width),
            transcendentals=pairs * length * hidden,
        ),
    )(jnp.swapaxes(tokens, 0, 1), wq, wo, wu, wd, vec, ub.reshape(1, hidden))


def pack_rows(width, hidden):
    piece, rows = width // PX, width // PF
    return piece, rows, hidden // PF


def weight_copies(packed, which, dst, sem, base, width, hidden):
    piece, rows, frows = pack_rows(width, hidden)
    q_pieces, u_pieces = 3, hidden // width
    spans = {
        "qkv": (0, q_pieces, rows),
        "out": (q_pieces * rows, 1, rows),
        "up": ((q_pieces + 1) * rows, u_pieces, rows),
        "down": ((q_pieces + 1 + u_pieces) * rows, 1, frows),
    }
    start, count, tall = spans[which]
    copies = []
    for x in range(PX):
        for p in range(count):
            copies.append(
                pltpu.make_async_copy(
                    packed.at[pl.ds(x * PF, PF), pl.ds(start + p * tall, tall), :],
                    dst.at[:, :, pl.ds((x * count + p) * piece, piece)],
                    sem.at[base + len(copies)],
                )
            )
    return copies


def natural(ref):
    blocks, rows, cols = ref.shape
    return ref[...].reshape(blocks * rows, cols)


def weight_scratch(which, width, hidden):
    rows, frows = width // PF, hidden // PF
    shape = {
        "qkv": (PF, rows, 3 * width),
        "out": (PF, rows, width),
        "up": (PF, rows, hidden),
        "down": (PF, frows, width),
    }[which]
    return pltpu.VMEM(shape, BF)


def contrast(low, images, live, same, groups, own, own_group, power, row_part, col_sum, loss_part):
    scores = LOGIT_SCALE * dot(low, images[...], 1, 1)
    exps = jnp.exp(scores)
    live_own, same_own = own[:, 0:1], own[:, 1:2]
    power[...] = exps
    rows = jnp.sum(exps * live_own, axis=0, keepdims=True)
    tiled = jnp.concatenate(
        [rows[:, k * 128 : (k + 1) * 128] for k in range(rows.shape[1] // 128)], axis=0
    )
    for d in range(row_part.shape[0]):
        row_part[d] = tiled
    cols = jnp.sum(exps * live[...], axis=1, keepdims=True)
    col_sum[...] = cols
    pair = jnp.where(own_group[...] == groups[...], live_own * live[...], 0.0)
    linear = pair * scores * (1.0 / same_own + 1.0 / same[...])
    losses = live_own * jnp.log(cols) - jnp.sum(linear, axis=1, keepdims=True)
    loss_part[...] = jnp.broadcast_to(jnp.sum(losses, axis=0, keepdims=True), loss_part.shape)


def text_mask(size, length):
    row = lax.broadcasted_iota(jnp.int32, (size, size), 0) // length
    col = lax.broadcasted_iota(jnp.int32, (size, size), 1) // length
    return jnp.where(row == col, 0.0, -1e30)


def text_forward_kernel(
    length, tok, packed, vec, ub, images_i, live, same, groups, own, own_group,
    h1_o, qkv_o, att_o, r1_o, h2_o, slope_o, acts, pooled_out, power, row_part, col_sum, loss_part,
    wq, wo, wu, wd, total, bias_row, h1, qkv, att, r1, h2, slope, sem, images, out_sem
):
    rows, width = tok.shape
    hidden = slope.shape[1]
    texts = rows // length
    load = {}
    base = 0
    for which, dst in (("qkv", wq), ("out", wo), ("up", wu), ("down", wd)):
        load[which] = weight_copies(packed, which, dst, sem, base, width, hidden)
        base += len(load[which])
        for copy in load[which]:
            copy.start()
    v = vec[...].astype(F32)
    bias_row[:, :width] = v[2:3]
    bias_row[:, width : 2 * width] = jnp.zeros((1, width), F32)
    bias_row[:, 2 * width :] = v[3:4]
    blk = 128

    def norm_rows(src, dst, gain, shift):
        def one(i):
            at = pl.ds(pl.multiple_of(i * blk, blk), blk)
            hat, _ = normalize(src[at, :].astype(F32))
            dst[at, :] = (hat * gain + shift).astype(BF)

        repeat(rows // blk, one, 2)

    norm_rows(tok, h1, v[0:1], v[1:2])
    saves = move([(h1, h1_o)], out_sem)
    (gathered,) = move([(images_i, images)], out_sem, 6)
    for copy in load["qkv"]:
        copy.wait()

    def project(i):
        at = pl.ds(pl.multiple_of(i * 256, 256), 256)
        qkv[:, at] = (dot(h1[...], wq[:, :, at].reshape(width, 256)) + bias_row[:, at]).astype(BF)

    repeat(3 * width // 256, project, 3)
    saves += move([(qkv, qkv_o)], out_sem, 1)
    low_lane = lax.broadcasted_iota(jnp.int32, (blk, 128), 1) < HEAD_DIM
    bias = text_mask(blk, length)
    cols = range(0, width, 128)

    def attend(i):
        at = pl.ds(pl.multiple_of(i * blk, blk), blk)
        q2 = [qkv[at, c : c + 128] * 0.125 for c in cols]
        k2 = [head_pair(qkv[at, width + c : width + c + 128], low_lane) for c in cols]
        v2 = [head_pair(qkv[at, 2 * width + c : 2 * width + c + 128], low_lane) for c in cols]
        scores = [dot(q, k, 1, 1) for q, k in zip(q2, k2)]
        probs = [
            jnp.concatenate(
                [softmax_half(s[:, :blk], bias).astype(BF), softmax_half(s[:, blk:], bias).astype(BF)],
                axis=1,
            )
            for s in scores
        ]
        for c, p, values in zip(cols, probs, v2):
            att[at, c : c + 128] = dot(p, values).astype(BF)

    repeat(rows // blk, attend, 2)
    saves += move([(att, att_o)], out_sem, 2)
    for copy in load["out"]:
        copy.wait()
    for c in range(0, width, 256):
        r1[:, c : c + 256] = tok[:, c : c + 256].astype(F32) + (
            dot(att[...], wo[:, :, c : c + 256].reshape(width, 256)) + v[4:5, c : c + 256]
        )
    saves += move([(r1, r1_o)], out_sem, 3)
    norm_rows(r1, h2, v[5:6], v[6:7])
    saves += move([(h2, h2_o)], out_sem, 4)
    for copy in load["up"]:
        copy.wait()

    def expand(i):
        at = pl.ds(pl.multiple_of(i * 256, 256), 256)
        u = dot(h2[...], wu[:, :, at].reshape(width, 256)) + ub[:, at].astype(F32)
        tail, bell, _ = gauss_tail(u)
        phi = jnp.where(u >= 0.0, 1.0 - tail, tail)
        act = u * phi
        slope[:, at] = (phi + u * (bell * 0.3989422804014327)).astype(BF)
        sums = jnp.sum(act.reshape(texts, length, 256), axis=1)
        total[:, at] = sums
        acts[:, at] = sums.astype(BF)

    repeat(hidden // 256, expand, 3)
    saves += move([(slope, slope_o)], out_sem, 5)
    for copy in load["down"]:
        copy.wait()
    mean_r1 = jnp.sum(r1[...].reshape(texts, length, width), axis=1) * (1.0 / length)
    pooled = mean_r1 + mean_down(total[...], length, natural(wd)) + v[7:8]
    pooled_out[...] = pooled
    gathered.wait()
    contrast(
        unit_rows(pooled).astype(BF), images, live, same, groups, own, own_group, power, row_part, col_sum, loss_part
    )
    for copy in saves:
        copy.wait()


def text_forward(
    tokens, packed, vec, ub, images, live, same, groups, own, own_group, length, hidden, copies_of
):
    rows, width = tokens.shape
    texts = rows // length
    pairs = images.shape[0]
    shape = jax.ShapeDtypeStruct
    copies = PX * (3 + 1 + hidden // width + 1)
    return pl.pallas_call(
        functools.partial(text_forward_kernel, length),
        name="text_forward",
        in_specs=[WHOLE, ANY, WHOLE, WHOLE, ANY] + [WHOLE] * 5,
        out_specs=[ANY] * 6 + [WHOLE] * 6,
        out_shape=[
            shape((rows, width), BF),
            shape((rows, 3 * width), BF),
            shape((rows, width), BF),
            shape((rows, width), F32),
            shape((rows, width), BF),
            shape((rows, hidden), BF),
            shape((texts, hidden), BF),
            shape((texts, width), F32),
            shape((texts, pairs), F32),
            shape((copies_of, pairs // 128, 128), F32),
            shape((texts, 1), F32),
            shape((8, 128), F32),
        ],
        scratch_shapes=[weight_scratch(w, width, hidden) for w in ("qkv", "out", "up", "down")]
        + [
            pltpu.VMEM((texts, hidden), F32),
            pltpu.VMEM((1, 3 * width), F32),
            pltpu.VMEM((rows, width), BF),
            pltpu.VMEM((rows, 3 * width), BF),
            pltpu.VMEM((rows, width), BF),
            pltpu.VMEM((rows, width), F32),
            pltpu.VMEM((rows, width), BF),
            pltpu.VMEM((rows, hidden), BF),
            pltpu.SemaphoreType.DMA((copies,)),
            pltpu.VMEM((pairs, width), BF),
            pltpu.SemaphoreType.DMA((7,)),
        ],
        compiler_params=params(),
        cost_estimate=pl.CostEstimate(
            flops=2 * rows * width * (4 * width + hidden),
            bytes_accessed=2 * (4 * width * width + 2 * width * hidden + 12 * rows * width),
            transcendentals=rows * hidden,
        ),
    )(tokens, packed, vec, ub, images, live, same, groups, own, own_group)


def relative_kernel(where, h1_i, h2_i, att_i, h1_o, h2_o, att_o, h1, h2, att, h1_t, h2_t, att_t, sem):
    width = h1.shape[1]
    block = width // PF
    my, mz, mc = where[1], where[2], where[3]
    loads = move([(h2_i, h2), (h1_i, h1), (att_i, att)], sem)
    saves = []
    for n, (src, dst, out) in enumerate(((h2, h2_t, h2_o), (h1, h1_t, h1_o), (att, att_t, att_o))):
        loads[n].wait()
        turned = src[...].T
        for z in range(4):
            for y in range(2):
                for c in range(2):
                    f = (z * 2 + y) * 2 + c
                    place = (((c ^ mc) * 2 + (y ^ my)) * 4 + (z ^ mz)) * block
                    dst[pl.ds(pl.multiple_of(place, block), block), :] = turned[
                        f * block : (f + 1) * block
                    ]
        saves += move([(dst, out)], sem, 3 + n)
    for copy in saves:
        copy.wait()


SMEM = pl.BlockSpec(memory_space=pltpu.SMEM)


def relative_rows(where, h1, h2, att):
    rows, width = h1.shape
    return pl.pallas_call(
        relative_kernel,
        name="relative_rows",
        in_specs=[SMEM, ANY, ANY, ANY],
        out_specs=[ANY] * 3,
        out_shape=[jax.ShapeDtypeStruct((width, rows), BF)] * 3,
        scratch_shapes=[pltpu.VMEM((rows, width), BF)] * 3
        + [pltpu.VMEM((width, rows), BF)] * 3
        + [pltpu.SemaphoreType.DMA((6,))],
        compiler_params=params(),
        cost_estimate=pl.CostEstimate(flops=0, bytes_accessed=12 * rows * width, transcendentals=0),
    )(where, h1, h2, att)


def grad_shapes(width):
    block, half = width // PF, width
    return [jax.ShapeDtypeStruct((2, 2, 4, block, half), BF)] * 4


def put_grad(values, outs, x_rel, at, second):
    width, cols = values.shape
    block = width // PF
    low = values.astype(BF)
    for c in range(2):
        for y in range(2):
            piece = low[(c * 2 + y) * 4 * block : (c * 2 + y + 1) * 4 * block].reshape(4, block, cols)
            if second:
                outs[2 + c, y, x_rel, :, :, pl.ds(at, cols)] = piece
            else:
                outs[c, x_rel, y, :, :, pl.ds(at, cols)] = piece


def start_grads(parts, outs, sem, x):
    return move(
        [(parts.at[n, x], outs[n].at[x]) for n in range(2)]
        + [(parts.at[n, :, x], outs[n].at[:, x]) for n in range(2, 4)],
        sem,
        4 * x,
    )


def back_one_kernel(
    length, shard,
    where, power, row_all, col_sum, images_i, live, same, groups, own, own_group, pooled, packed, vec,
    slope_i, h2_i, r1_i, acts,
    factors_o, keep_a, send_a, keep_b, send_b, bias_up, down_bias, dr1_o, dz_o, da_o, sums, loss_rows,
    factors, wd, wu, wo, dact, images, slope, h2_t, r1, du, dr1, dz_s, da_s, dy, parts, sem, in_sem, out_sem,
):
    rows, hidden = slope.shape
    texts = rows // length
    width = h2_t.shape[0]
    (gathered,) = move([(images_i, images)], in_sem)
    down = weight_copies(packed, "down", wd, sem, 0, width, hidden)
    up = weight_copies(packed, "up", wu, sem, len(down), width, hidden)
    out = weight_copies(packed, "out", wo, sem, len(down) + len(up), width, hidden)
    for copy in down:
        copy.start()
    saved = move([(slope_i, slope), (h2_i, h2_t)], in_sem, 1)
    for copy in up + out:
        copy.start()
    saved += move([(r1_i, r1)], in_sem, 3)
    totals = jnp.sum(row_all[...], axis=0)
    row_sum = jnp.concatenate([totals[k : k + 1] for k in range(totals.shape[0])], axis=1)
    live_own, same_own = own[:, 0:1], own[:, 1:2]
    factor = LOSS_WEIGHT / (2.0 * jnp.sum(live[...], axis=1, keepdims=True))
    pair = factor * live_own * live[...]
    match = jnp.where(own_group[...] == groups[...], 1.0 / same_own + 1.0 / same[...], 0.0)
    grad_scores = pair * (power[...] * (1.0 / row_sum + 1.0 / col_sum[...]) - match)
    gathered.wait()
    grad_low = LOGIT_SCALE * dot(grad_scores.astype(BF), images[...])
    pool = pooled[...]
    inverse = lax.rsqrt(jnp.sum(pool * pool, axis=-1, keepdims=True) + 1e-06)
    along = jnp.sum(pool * grad_low, axis=-1, keepdims=True)
    dy[...] = inverse * (grad_low - pool * (inverse * inverse * along)) * (1.0 / length)
    dm = dy[...].astype(BF)
    loss_rows[...] = jnp.broadcast_to(
        jnp.sum(live[...] * jnp.log(row_sum), axis=1, keepdims=True), loss_rows.shape
    )
    parts_x, parts_f = shard
    piece_x, piece_f = width // parts_x, hidden // parts_f
    for f in range(parts_f):
        left = acts[:, f * piece_f : (f + 1) * piece_f]
        for x in range(parts_x):
            factors[x * parts_f + f, :, piece_x:] = left
            factors[x * parts_f + f, :, :piece_x] = dm[:, x * piece_x : (x + 1) * piece_x]
    sent = move([(factors, factors_o)], out_sem, 11)
    down_bias[...] = length * jnp.sum(dm.astype(F32), axis=0, keepdims=True)
    for copy in down:
        copy.wait()
    dact[...] = dot(dm, natural(wd), 1, 1)
    saved[0].wait()

    saved[1].wait()
    half = hidden // PX
    outs = (keep_a, send_a, keep_b, send_b)
    for x in range(PX):
        first = (x ^ where[0]) * half

        def grads(i):
            c = pl.multiple_of(i * 256, 256)
            for second in range(2):
                at = pl.ds(pl.multiple_of(first + c + second * width, 256), 256)
                spread = jnp.broadcast_to(dact[:, at].reshape(texts, 1, 256), (texts, length, 256))
                part = (spread.reshape(rows, 256) * slope[:, at].astype(F32)).astype(BF)
                du[:, at] = part
                bias_up[:, at] = jnp.sum(part.astype(F32), axis=0, keepdims=True)
                put_grad(dot(h2_t[...], part), parts, x, c, second)

        repeat(width // 256, grads, 3)
        sent += start_grads(parts, outs, out_sem, x)

    v = vec[...].astype(F32)
    blk = 128
    for copy in up:
        copy.wait()

    def product(i):
        at = pl.ds(pl.multiple_of(i * (rows // 2), rows // 2), rows // 2)
        dr1[at, :] = dot(du[at, :], natural(wu), 1, 1)

    repeat(2, product)
    sums[...] = jnp.zeros((8, width), F32)
    some = blk // length
    saved[2].wait()

    def back(i):
        at = pl.ds(pl.multiple_of(i * blk, blk), blk)
        hat, inverse = normalize(r1[at, :])
        grad = dr1[at, :]
        sums[1:2, :] += jnp.sum(grad * hat, axis=0, keepdims=True)
        sums[2:3, :] += jnp.sum(grad, axis=0, keepdims=True)
        spread = jnp.broadcast_to(
            dy[pl.ds(pl.multiple_of(i * some, some), some), :].reshape(some, 1, width), (some, length, width)
        ).reshape(blk, width)
        grad = spread + norm_back(grad, hat, inverse, v[5:6])
        dr1[at, :] = grad
        low = grad.astype(BF)
        dz_s[at, :] = low
        sums[0:1, :] += jnp.sum(low.astype(F32), axis=0, keepdims=True)

    repeat(rows // blk, back)
    sent += move([(dr1, dr1_o), (dz_s, dz_o)], out_sem, 8)
    for copy in out:
        copy.wait()
    da_s[...] = dot(dz_s[...], natural(wo), 1, 1).astype(BF)
    sent += move([(da_s, da_o)], out_sem, 10)
    for copy in sent:
        copy.wait()


def back_one(
    where, power, row_all, col_sum, images, live, same, groups, own, own_group, pooled, packed, vec, slope,
    h2_t, r1, acts, length, shard,
):
    rows, hidden = slope.shape
    width = h2_t.shape[0]
    texts = rows // length
    payload = (shard[0] * shard[1], texts, width // shard[0] + hidden // shard[1])
    shape = jax.ShapeDtypeStruct
    return pl.pallas_call(
        functools.partial(back_one_kernel, length, shard),
        name="back_one",
        in_specs=[SMEM] + [WHOLE] * 3 + [ANY] + [WHOLE] * 6 + [ANY, WHOLE, ANY, ANY, ANY, WHOLE],
        out_specs=[ANY] * 5 + [WHOLE] * 2 + [ANY] * 3 + [WHOLE] * 2,
        out_shape=[
            shape(payload, BF),
            *grad_shapes(width),
            shape((1, hidden), F32),
            shape((1, width), F32),
            shape((rows, width), F32),
            shape((rows, width), BF),
            shape((rows, width), BF),
            shape((8, width), F32),
            shape((8, 128), F32),
        ],
        scratch_shapes=[
            pltpu.VMEM(payload, BF),
            weight_scratch("down", width, hidden),
            weight_scratch("up", width, hidden),
            weight_scratch("out", width, hidden),
            pltpu.VMEM((texts, hidden), F32),
            pltpu.VMEM(images.shape, BF),
            pltpu.VMEM((rows, hidden), BF),
            pltpu.VMEM((width, rows), BF),
            pltpu.VMEM((rows, width), F32),
            pltpu.VMEM((rows, hidden), BF),
            pltpu.VMEM((rows, width), F32),
            pltpu.VMEM((rows, width), BF),
            pltpu.VMEM((rows, width), BF),
            pltpu.VMEM((texts, width), F32),
            pltpu.VMEM((4,) + grad_shapes(width)[0].shape, BF),
            pltpu.SemaphoreType.DMA((PX * (2 + hidden // width),)),
            pltpu.SemaphoreType.DMA((4,)),
            pltpu.SemaphoreType.DMA((12,)),
        ],
        compiler_params=params(),
        cost_estimate=pl.CostEstimate(
            flops=2 * rows * width * (2 * hidden + width), bytes_accessed=16 * width * hidden, transcendentals=0
        ),
    )(
        where, power, row_all, col_sum, images, live, same, groups, own, own_group, pooled, packed, vec,
        slope, h2_t, r1, acts,
    )


def back_two_kernel(
    length, where, qkv_i, da_i, dz_i, h1_i, att_i, up_a, up_a_new, up_b, up_b_new,
    dqkv_o, keep_a, send_a, keep_b, send_b, up_a_keep, up_a_send, up_b_keep, up_b_send, sums,
    qkv, da_s, dz, h1_t, att_t, dqkv, parts, held, come, sem, out_sem, up_sem,
):
    rows, width = da_s.shape
    blk = 128
    loads = move([(qkv_i, qkv), (da_i, da_s), (att_i, att_t), (dz_i, dz), (h1_i, h1_t)], sem)
    arrivals = move(
        [(up_a, held.at[0]), (up_a_new, come.at[0]), (up_b, held.at[1]), (up_b_new, come.at[1])], up_sem
    )
    for copy in loads[:2]:
        copy.wait()
    low_lane = lax.broadcasted_iota(jnp.int32, (blk, 128), 1) < HEAD_DIM
    bias = text_mask(blk, length)
    cols = range(0, width, 128)
    def group(i):
        at = pl.ds(pl.multiple_of(i * blk, blk), blk)
        take = lambda base, c: qkv[at, base + c : base + c + 128]
        q2 = [take(0, c) * 0.125 for c in cols]
        k2 = [head_pair(take(width, c), low_lane) for c in cols]
        v2 = [head_pair(take(2 * width, c), low_lane) for c in cols]
        da = [da_s[at, c : c + 128] for c in cols]
        scores = [dot(k, q, 1, 1) for k, q in zip(k2, q2)]
        grads = [dot(v, d, 1, 1) for v, d in zip(v2, da)]
        probs, deltas = [], []
        for score, grad in zip(scores, grads):
            p_low, d_low = [], []
            for half in range(2):
                s = score[half * blk : (half + 1) * blk] + bias
                g = grad[half * blk : (half + 1) * blk]
                powers = jnp.exp(s - jnp.max(s, axis=0, keepdims=True))
                soft = powers * (1.0 / jnp.sum(powers, axis=0, keepdims=True))
                p_low.append(soft.astype(BF))
                d_low.append((soft * (g - jnp.sum(g * soft, axis=0, keepdims=True))).astype(BF))
            probs.append(jnp.concatenate(p_low, axis=0))
            deltas.append(jnp.concatenate(d_low, axis=0))
        for n, c in enumerate(cols):
            dq = dot(deltas[n], k2[n], 0, 0) * 0.125
            dk = dot(deltas[n], q2[n])
            dv = dot(probs[n], da[n])
            dqkv[at, c : c + 128] = dq.astype(BF)
            dqkv[at, width + c : width + c + 128] = jnp.where(
                low_lane, dk[:blk], dk[blk:]
            ).astype(BF)
            dqkv[at, 2 * width + c : 2 * width + c + 128] = jnp.where(
                low_lane, dv[:blk], dv[blk:]
            ).astype(BF)

    repeat(rows // blk, group)
    sums[0:1, :] = jnp.sum(dqkv[:, :width].astype(F32), axis=0, keepdims=True)
    sums[1:2, :] = jnp.sum(dqkv[:, 2 * width :].astype(F32), axis=0, keepdims=True)
    sums[2:8, :] = jnp.zeros((6, width), F32)
    sent = move([(dqkv, dqkv_o)], out_sem, 8)
    for copy in arrivals:
        copy.wait()

    def add(i):
        n, first, second = i // 4, i // 2 % 2, i % 2
        held[n, first, second] = (
            held[n, first, second].astype(F32) + come[n, first, second].astype(F32)
        ).astype(BF)

    repeat(8, add)
    sent += move(
        [
            (held.at[0, 0], up_a_keep),
            (held.at[0, 1], up_a_send),
            (held.at[1, 0], up_b_keep),
            (held.at[1, 1], up_b_send),
        ],
        up_sem,
        4,
    )
    for copy in loads[2:]:
        copy.wait()
    piece = width // PX
    outs = (keep_a, send_a, keep_b, send_b)
    for x in range(PX):
        other = x ^ where[0]
        first = other * (3 * piece)

        def chunk(i):
            c = pl.multiple_of(i * 256, 256)
            part = dqkv[:, pl.ds(pl.multiple_of(first + c, 128), 256)]
            put_grad(dot(h1_t[...], part), parts, x, c, 0)

        repeat(width // 256, chunk)
        part = dqkv[:, pl.ds(pl.multiple_of(first + width, 128), piece)]
        put_grad(dot(h1_t[...], part), parts, x, 0, 1)
        part = dz[:, pl.ds(pl.multiple_of(other * piece, 128), piece)]
        put_grad(dot(att_t[...], part), parts, x, piece, 1)
        sent += start_grads(parts, outs, out_sem, x)
    for copy in sent:
        copy.wait()


def back_two(where, qkv, da, dz, h1_t, att_t, up_parts, length):
    rows, width = da.shape
    shape = jax.ShapeDtypeStruct
    whole = grad_shapes(width)
    return pl.pallas_call(
        functools.partial(back_two_kernel, length),
        name="back_two",
        in_specs=[SMEM] + [ANY] * 9,
        out_specs=[ANY] * 9 + [WHOLE],
        out_shape=[shape((rows, 3 * width), BF), *whole, *[shape(whole[0].shape[1:], BF)] * 4, shape((8, width), F32)],
        scratch_shapes=[
            pltpu.VMEM((rows, 3 * width), BF),
            pltpu.VMEM((rows, width), BF),
            pltpu.VMEM((rows, width), BF),
            pltpu.VMEM((width, rows), BF),
            pltpu.VMEM((width, rows), BF),
            pltpu.VMEM((rows, 3 * width), BF),
            pltpu.VMEM((4,) + whole[0].shape, BF),
            pltpu.VMEM((2,) + whole[0].shape, BF),
            pltpu.VMEM((2,) + whole[0].shape, BF),
            pltpu.SemaphoreType.DMA((5,)),
            pltpu.SemaphoreType.DMA((9,)),
            pltpu.SemaphoreType.DMA((8,)),
        ],
        compiler_params=params(),
        cost_estimate=pl.CostEstimate(
            flops=2 * rows * width * (1280 + 4 * width), bytes_accessed=20 * rows * width, transcendentals=rows * width
        ),
    )(where, qkv, da, dz, h1_t, att_t, *up_parts)


def back_third_kernel(
    parts_f, dr1_i, dqkv_i, tok_i, packed, vec, sums, bias_sums, down_bias, bias_up, loss_part, dx_o, share, all_sums, wq, dr1, tok, dx, sem, dqkv, own_sem
):
    rows, width = tok.shape
    loads = weight_copies(packed, "qkv", wq, sem, 0, width, width)
    for copy in loads:
        copy.start()
    saved = move([(dqkv_i, dqkv), (dr1_i, dr1), (tok_i, tok)], own_sem)
    saved[0].wait()
    v = vec[...].astype(F32)
    for copy in loads:
        copy.wait()
    half = rows // 2

    def product(i):
        at = pl.ds(pl.multiple_of(i * half, half), half)
        dx[at, :] = dot(dqkv[at, :], natural(wq), 1, 1)

    repeat(2, product)
    for copy in saved[1:]:
        copy.wait()
    all_sums[0:2, :] = jnp.zeros((2, width), F32)
    blk = 128

    def back(i):
        at = pl.ds(pl.multiple_of(i * blk, blk), blk)
        hat, inverse = normalize(tok[at, :].astype(F32))
        grad = dx[at, :]
        all_sums[0:1, :] += jnp.sum(grad * hat, axis=0, keepdims=True)
        all_sums[1:2, :] += jnp.sum(grad, axis=0, keepdims=True)
        dx[at, :] = dr1[at, :] + norm_back(grad, hat, inverse, v[0:1])

    repeat(rows // blk, back)
    (save,) = move([(dx, dx_o)], own_sem, 3)
    all_sums[2:4, :] = bias_sums[0:2, :]
    all_sums[4:7, :] = sums[0:3, :]
    all_sums[7:8, :] = down_bias[...]
    every = all_sums[...]
    piece, tall = width // parts_f, bias_up.shape[1] // parts_f
    devices = share.shape[0]
    used = piece + tall // 8
    for f in range(parts_f):
        bias = bias_up[:, f * tall : (f + 1) * tall]
        bias = jnp.concatenate([bias[:, r * tall // 8 : (r + 1) * tall // 8] for r in range(8)], axis=0)
        block = jnp.concatenate(
            [every[:, f * piece : (f + 1) * piece], bias, loss_part[:, : 128 - used]], axis=1
        )
        for x in range(devices // parts_f):
            share[x * parts_f + f] = block
    save.wait()


def back_third(dr1, dqkv, tok, packed, vec, sums, bias_sums, down_bias, bias_up, loss_part, shard):
    rows, width = tok.shape
    shape = jax.ShapeDtypeStruct
    return pl.pallas_call(
        functools.partial(back_third_kernel, shard[1]),
        name="back_third",
        in_specs=[ANY, ANY, ANY, ANY] + [WHOLE] * 6,
        out_specs=[ANY, WHOLE],
        out_shape=[shape((rows, width), F32), shape((shard[0] * shard[1], 8, 128), F32)],
        scratch_shapes=[
            pltpu.VMEM((8, width), F32),
            weight_scratch("qkv", width, width),
            pltpu.VMEM((rows, width), F32),
            pltpu.VMEM((rows, width), BF),
            pltpu.VMEM((rows, width), F32),
            pltpu.SemaphoreType.DMA((PX * 3,)),
            pltpu.VMEM((rows, 3 * width), BF),
            pltpu.SemaphoreType.DMA((4,)),
        ],
        compiler_params=params(),
        cost_estimate=pl.CostEstimate(
            flops=6 * rows * width * width, bytes_accessed=14 * width * width, transcendentals=0
        ),
    )(dr1, dqkv, tok, packed, vec, sums, bias_sums, down_bias, bias_up, loss_part)


def fold_kernel(a_own, a_new, b_own, b_new, a_keep, a_send, b_keep, b_send):
    for own, new, keep, send in ((a_own, a_new, a_keep, a_send), (b_own, b_new, b_keep, b_send)):
        total = own[...].astype(F32) + new[...].astype(F32)
        keep[...] = total[0].astype(BF)
        send[...] = total[1].astype(BF)


def fold(a_own, a_new, b_own, b_new):
    shape = a_own.shape
    rest = 1
    for n in shape[1:-2]:
        rest *= n
    rows, cols = shape[-2:]
    view = lambda a: a.reshape(2, rest, rows, cols)
    steps = 2 if rest > 4 else 1
    pair = pl.BlockSpec((2, rest // steps, rows, cols), lambda i: (0, i, 0, 0))
    one = pl.BlockSpec((rest // steps, rows, cols), lambda i: (i, 0, 0))
    outs = pl.pallas_call(
        fold_kernel,
        name="fold",
        grid=(steps,),
        in_specs=[pair] * 4,
        out_specs=[one] * 4,
        out_shape=[jax.ShapeDtypeStruct((rest, rows, cols), BF)] * 4,
        compiler_params=params(18),
        cost_estimate=pl.CostEstimate(
            flops=4 * rest * rows * cols, bytes_accessed=24 * rest * rows * cols, transcendentals=0
        ),
    )(*(view(a) for a in (a_own, a_new, b_own, b_new)))
    return [o.reshape(shape[1:]) for o in outs]


def join_kernel(a_own, a_new, b_own, b_new, keep, send):
    half = a_own.shape[-1]
    for at, own, new in ((0, a_own, a_new), (half, b_own, b_new)):
        total = own[...].astype(F32) + new[...].astype(F32)
        for k in range(2):
            keep[k, :, at : at + half] = total[2 * k]
            send[k, :, at : at + half] = total[2 * k + 1].astype(BF)


def join(a_own, a_new, b_own, b_new):
    blocks, rows, cols = a_own.shape
    shape = jax.ShapeDtypeStruct
    return pl.pallas_call(
        join_kernel,
        name="join",
        in_specs=[WHOLE] * 4,
        out_specs=[WHOLE] * 2,
        out_shape=[shape((2, rows, 2 * cols), F32), shape((2, rows, 2 * cols), BF)],
        compiler_params=params(6),
        cost_estimate=pl.CostEstimate(
            flops=16 * rows * cols, bytes_accessed=40 * rows * cols, transcendentals=0
        ),
    )(a_own, a_new, b_own, b_new)


def turn_kernel(keep, new, stay, send):
    stay[...] = keep[0] + new[0].astype(F32)
    send[...] = (keep[1] + new[1].astype(F32)).astype(BF)


def turn(keep, new):
    blocks, rows, cols = keep.shape
    shape = jax.ShapeDtypeStruct
    return pl.pallas_call(
        turn_kernel,
        name="turn",
        in_specs=[WHOLE] * 2,
        out_specs=[WHOLE] * 2,
        out_shape=[shape((rows, cols), F32), shape((rows, cols), BF)],
        compiler_params=params(6),
        cost_estimate=pl.CostEstimate(
            flops=4 * rows * cols, bytes_accessed=18 * rows * cols, transcendentals=0
        ),
    )(keep, new)


def shifted(x, y, z, core):
    change = x * 16 + z * 4 + y * 2 + core
    return [(i, i ^ change) for i in range(32)]


def hop(array, x=0, y=0, z=0, core=0):
    return lax.ppermute(array, AXES, shifted(x, y, z, core))


def after(values, *others):
    return lax.optimization_barrier((tuple(values), others))[0]


def core_step(parts, *wait):
    keep_a, send_a, keep_b, send_b = parts
    new_a, new_b = hop(send_a, core=1), hop(send_b, core=1)
    keep_a, keep_b = after((keep_a, keep_b), *wait)
    return fold(keep_a, new_a, keep_b, new_b)


def first_step(parts, *wait):
    keep_a, send_a, keep_b, send_b = parts
    new_a, new_b = hop(send_a, x=1), hop(send_b, y=1)
    keep_a, keep_b = after((keep_a, keep_b), *wait)
    return fold(keep_a, new_a, keep_b, new_b)


def second_step(parts, *wait):
    keep_a, send_a, keep_b, send_b = parts
    new_a, new_b = hop(send_a, y=1), hop(send_b, x=1)
    keep_a, keep_b = after((keep_a, keep_b), *wait)
    return join(keep_a, new_a, keep_b, new_b)


def total_kernel(stay, new, *outs):
    total = stay[...] + new[...].astype(F32)
    at = 0
    for out in outs:
        out[...] = total[:, at : at + out.shape[1]]
        at += out.shape[1]


def third_step(parts, *wait):
    keep, send = parts
    new = hop(send, z=1)
    (keep,) = after((keep,), *wait)
    return turn(keep, new)


def last_step(parts, splits):
    stay, send = parts
    return pl.pallas_call(
        total_kernel,
        name="total",
        in_specs=[WHOLE] * 2,
        out_specs=[WHOLE] * len(splits),
        out_shape=[jax.ShapeDtypeStruct((stay.shape[0], n), F32) for n in splits],
        compiler_params=params(4),
    )(stay, hop(send, z=2))


def natural_grad(keep_a, send_a, keep_b, send_b):
    first = jnp.stack([keep_a, send_a])
    second = jnp.swapaxes(jnp.stack([keep_b, send_b]), 1, 2)
    whole = jnp.concatenate([first, second], axis=-1)
    core, x, y, z, rows, cols = whole.shape
    return whole.transpose(1, 3, 2, 0, 4, 5).reshape(x, z * y * core * rows, cols)


def pack_kernel(qkv, out, up, down, packed):
    rows, piece = out.shape
    at = 0
    for ref in (qkv, out, up, down):
        for c in range(0, ref.shape[1], piece):
            packed[at : at + ref.shape[0], :] = ref[:, c : c + piece]
            at += ref.shape[0]


def pack_block(qkv, out, up, down):
    piece = out.shape[1]
    total = sum(w.shape[0] * w.shape[1] for w in (qkv, out, up, down)) // piece
    return pl.pallas_call(
        pack_kernel,
        name="pack_block",
        in_specs=[WHOLE] * 4,
        out_specs=WHOLE,
        out_shape=jax.ShapeDtypeStruct((total, piece), BF),
        compiler_params=params(),
    )(qkv, out, up, down)


def gather_packed(qkv, out, up, down, dp, fsdp):
    if (dp, fsdp) == (PX, PF):
        return lax.all_gather(pack_block(qkv, out, up, down), AXES, axis=0)
    full = [
        lax.all_gather(lax.all_gather(w, "dp", axis=1, tiled=True), "fsdp", axis=0, tiled=True)
        for w in (qkv, out, up, down)
    ]
    blocks = []
    for x in range(PX):
        for f in range(PF):
            some = []
            for w in full:
                rows, cols = w.shape[0] // PF, w.shape[1] // PX
                some.append(w[f * rows : (f + 1) * rows, x * cols : (x + 1) * cols])
            blocks.append(pack_block(*some))
    return jnp.stack(blocks)


def scatter_columns(grad, dp, fsdp):
    parts, rows, cols = grad.shape
    if dp != parts:
        grad = jnp.swapaxes(grad, 0, 1).reshape(rows, dp, parts * cols // dp)
        grad = jnp.swapaxes(grad, 0, 1)
    return lax.psum_scatter(
        grad.reshape(dp * rows, -1), AXES, scatter_dimension=0, tiled=True
    ).astype(F32)


def body(
    image_tokens,
    text_tokens,
    image_qkv,
    image_out,
    image_up,
    image_down,
    image_vectors,
    image_up_bias,
    text_qkv,
    text_out,
    text_up,
    text_down,
    text_vectors,
    text_up_bias,
    pair_counts,
    pair_groups,
):
    dp, fsdp = lax.axis_size("dp"), lax.axis_size("fsdp")
    devices = dp * fsdp
    cap, length, width = text_tokens.shape
    hidden = image_up.shape[1]
    pairs = pair_groups.shape[0]
    me = lax.axis_index("dp") * fsdp + lax.axis_index("fsdp")

    grid_mesh = (dp, fsdp) == (PX, PF)
    packed = gather_packed(text_qkv, text_out, text_up, text_down, dp, fsdp)
    part = width // fsdp
    small = jnp.concatenate([text_vectors, text_up_bias.reshape(8, -1)], axis=1)
    if grid_mesh:
        small = jnp.broadcast_to(small[None], (fsdp,) + small.shape)
        small = lax.all_to_all(small, "fsdp", 0, 0, tiled=True)
    else:
        small = lax.all_gather(small, "fsdp", axis=0)
    vec = jnp.swapaxes(small[:, :, :part], 0, 1).reshape(8, width)
    ub = small[:, :, part:].reshape(1, hidden)
    bits = [lax.shift_right_logical(me, k) & 1 for k in range(5)]
    where = jnp.stack([bits[4], bits[1], 2 * bits[3] + bits[2], bits[0]])
    where = where if grid_mesh else jnp.zeros_like(where)

    image_low = image_forward(
        image_tokens, image_qkv, image_out, image_up, image_down, image_vectors, image_up_bias
    )
    if grid_mesh:
        images = image_low
        for change in (dict(z=1), dict(z=2), dict(x=1), dict(y=1), dict(core=1)):
            images = jnp.concatenate([images, hop(images, **change)], axis=0)
        far = jnp.arange(devices, dtype=jnp.int32) ^ me
        bit = lambda k: lax.shift_right_logical(far, k) & 1
        order = bit(2) + 2 * bit(3) + 4 * bit(4) + 8 * bit(1) + 16 * bit(0)
        images = jnp.take(images.reshape(devices, cap, width), order, axis=0).reshape(pairs, width)
    else:
        images = lax.all_gather(image_low, AXES, axis=0, tiled=True)

    slots = jnp.arange(cap, dtype=jnp.int32)
    live = (slots[None, :] < pair_counts[:, None]).reshape(pairs).astype(F32)
    same = jnp.maximum(
        jnp.sum(jnp.where(pair_groups[:, None] == pair_groups[None, :], live[None, :], 0.0), axis=1), 1.0
    )
    own_of = lambda array: lax.dynamic_slice_in_dim(array, me * cap, cap)
    own = jnp.stack([own_of(live), own_of(same)], axis=1)
    own_group = own_of(pair_groups).reshape(cap, 1)
    live_row, same_row, group_row = (a.reshape(1, pairs) for a in (live, same, pair_groups))
    live_total = jnp.sum(pair_counts).astype(F32)

    tokens = text_tokens.reshape(cap * length, width)
    h1, qkv, att, r1, h2, slope, acts, pooled, power, row_part, col_sum, loss_part = text_forward(
        tokens, packed, vec, ub, images, live_row, same_row, group_row, own, own_group, length, hidden,
        devices if grid_mesh else 1,
    )
    if grid_mesh:
        row_all = lax.all_to_all(row_part, AXES, 0, 0, tiled=True)
    else:
        row_all = lax.psum(row_part, AXES)
    h1_t, h2_t, att_t = relative_rows(where, h1, h2, att)
    factors, *up_parts, bias_up, down_bias, dr1, dz, da, sums, loss_rows = back_one(
        where, power, row_all, col_sum, images, live_row, same_row, group_row, own, own_group, pooled,
        packed, vec, slope, h2_t, r1, acts, length, (dp, fsdp),
    )
    keep_a, send_a, keep_b, send_b = up_parts
    if grid_mesh:
        travel = (keep_a, hop(send_a, core=1), keep_b, hop(send_b, core=1))
    else:
        travel = (keep_a, send_a, keep_b, send_b)
    dqkv, *both_parts, bias_sums = back_two(where, qkv, da, dz, h1_t, att_t, travel, length)
    att_parts = both_parts[:4]

    both = lax.all_to_all(factors, AXES, 0, 0, tiled=True).reshape(pairs, width // dp + hidden // fsdp)
    grad_down = dot(both[:, width // dp :], both[:, : width // dp], 0, 0)

    if grid_mesh:
        up_parts = both_parts[4:]
        att_parts = core_step(att_parts)
        (dqkv,) = after((dqkv,), *att_parts)
        dx, share = back_third(
            dr1, dqkv, tokens, packed, vec, sums, bias_sums, down_bias, bias_up, loss_part, (dp, fsdp)
        )
        up_parts = first_step(up_parts, dx)
        att_parts = first_step(att_parts, grad_down, *up_parts)
        up_parts = second_step(up_parts, *att_parts)
        (share,) = after((share,), *att_parts)
        att_parts = second_step(att_parts, *up_parts)
        up_parts = third_step(up_parts, *att_parts)
        att_parts = third_step(att_parts, *up_parts)
        (grad_up,) = last_step(up_parts, (hidden // dp,))
        grad_qkv, grad_out = last_step(att_parts, (3 * width // dp, width // dp))
    else:
        dx, share = back_third(
            dr1, dqkv, tokens, packed, vec, sums, bias_sums, down_bias, bias_up, loss_part, (dp, fsdp)
        )
        grad_attn = natural_grad(*att_parts)
        grad_up = scatter_columns(natural_grad(*up_parts), dp, fsdp)
        grad_qkv = scatter_columns(grad_attn[:, :, : 3 * width // PX], dp, fsdp)
        grad_out = scatter_columns(grad_attn[:, :, 3 * width // PX :], dp, fsdp)

    share = jnp.sum(lax.all_to_all(share, AXES, 0, 0, tiled=True), axis=0)
    grad_vec = share[:, :part]
    tall = hidden // fsdp // 8
    grad_bias = share[:, part : part + tall].reshape(hidden // fsdp)
    loss = (share[0, part + tall] + loss_rows[0, 0]) / (2.0 * live_total)

    return (
        loss,
        dx.reshape(text_tokens.shape),
        grad_qkv,
        grad_out,
        grad_up,
        grad_down,
        grad_vec,
        grad_bias,
    )


def solution(mesh):
    return jax.shard_map(
        body,
        mesh=mesh,
        in_specs=(
            P(AXES, None, None),
            P(AXES, None, None),
            P(),
            P(),
            P(),
            P(),
            P(),
            P(),
            P("fsdp", "dp"),
            P("fsdp", "dp"),
            P("fsdp", "dp"),
            P("fsdp", "dp"),
            P(None, "fsdp"),
            P("fsdp"),
            P(),
            P(),
        ),
        out_specs=(
            P(),
            P(AXES, None, None),
            P("fsdp", "dp"),
            P("fsdp", "dp"),
            P("fsdp", "dp"),
            P("fsdp", "dp"),
            P(None, "fsdp"),
            P("fsdp"),
        ),
        check_vma=False,
    )
```
